32 devices in a mesh: seq: 2 (over x), fsdp: 16 (over z, y, core).
Axes of the slice: x: 2, y: 2, z: 4, core: 2. Of those that a mesh axis runs over, the one named last changes fastest.
Arguments:
- hidden_in: bfloat16 [2, 2048, 768], P(None, ('seq', 'fsdp')), may hold values from -6 to 6
- time_index: int32 [2], replicated, may hold values from 0 to 999, as said below
- cotangent: bfloat16 [2, 2048, 768], P(None, ('seq', 'fsdp')), may hold values from -6 to 6
- w_qkv: bfloat16 [768, 2304], P('fsdp'), may hold values from -0.21875 to 0.21875
- w_attn_out: bfloat16 [768, 768], P('fsdp'), may hold values from -2 to 2
- w_mlp_in: bfloat16 [768, 3072], P('fsdp'), may hold values from -0.21875 to 0.21875
- w_mlp_out: bfloat16 [3072, 768], P('fsdp'), may hold values from -0.109375 to 0.109375
- w_ada: bfloat16 [4608, 128], P('fsdp'), may hold values from -0.5 to 0.5
- bias_ada: bfloat16 [4608], P('fsdp'), may hold values from -3 to 3
- gain_attn: bfloat16 [768], P('fsdp'), may hold values from 0.5 to 1.5
- gain_mlp: bfloat16 [768], P('fsdp'), may hold values from 0.5 to 1.5
- bias_mlp_in: bfloat16 [3072], P('fsdp'), may hold values from -3 to 3
- bias_mlp_out: bfloat16 [768], P('fsdp'), may hold values from -3 to 3
Outputs:
- output: bfloat16 [2, 2048, 768], P(None, ('seq', 'fsdp'))
- grad_hidden_in: float32 [2, 2048, 768], P(None, ('seq', 'fsdp'))
- grad_w_qkv: float32 [768, 2304], P('fsdp')
- grad_w_attn_out: float32 [768, 768], P('fsdp')
- grad_w_mlp_in: float32 [768, 3072], P('fsdp')
- gradient_mlp_output_weight: float32 [3072, 768], P('fsdp')
- grad_w_ada: float32 [4608, 128], P('fsdp')
- grad_bias_ada: float32 [4608], P('fsdp')
- grad_gain_attn: float32 [768], P('fsdp')
- grad_gain_mlp: float32 [768], P('fsdp')
- grad_bias_mlp_in: float32 [3072], P('fsdp')
- grad_bias_mlp_out: float32 [768], P('fsdp')
The draws below stay inside these ranges and needn't reach their ends.
Inputs may be any that keep to these rules, and one draw needn't show every extreme that they name: `time_index`: the 2 sequences have different time indices.
All inputs are finite; a program needn't handle non-finite values.
Results may differ from the reference program's by a relative error of at most 0.015.
The reference program's roundings to bfloat16 on the way count: a program that leaves them out, or rounds other values in their place, can miss the bound.
Values may be sent and summed in bfloat16 or wider, within the bound.
No kernel may reach another device: no remote copies, remote signals or barrier semaphores. Data moves between devices by JAX's collectives and lax.ppermute only.
A program may use at most 576 MiB of HBM per device.

```python
import math
import jax
import jax.numpy as jnp
from jax import lax

D = 768
HEADS = 12
HDIM = 64
FF = 3072
CDIM = 128
SEQS = 2
LEN = 2048


def draw_time_index(key, part):
    return jax.random.permutation(key, 1000)[:SEQS].astype(jnp.int32)


def block_levels(own_key, shape, pieces, smallest, high):
    factor_of, own = 1.0, jax.random.fold_in(own_key, 6)
    for dim, parts in pieces:
        steps = jnp.exp(jax.random.uniform(jax.random.fold_in(own, dim), (parts,), jnp.float32, smallest / len(pieces), high / len(pieces)))
        factor_of = factor_of * jnp.repeat(steps, shape[dim] // parts).reshape([-1 if axis == dim else 1 for axis in range(len(shape))])
    return factor_of


def normal_values(own_key, shape, scale, most, shards=(), kind=jnp.bfloat16):
    entries = scale * jax.random.normal(own_key, shape, jnp.float32)
    if shards:
        entries = entries * block_levels(own_key, shape, shards, -0.22, 0.18)
    return jnp.clip(entries, -most, most).astype(kind)


def setup_inputs(seed: int = 0) -> dict:
    key_list = jax.random.split(jax.random.key(seed), 14)
    hidden_in = normal_values(key_list[0], (SEQS, LEN, D), 1.0, 6.0, ((1, 32),))
    time_index = draw_time_index(jax.random.fold_in(key_list[13], 71), 0)
    cotangent = normal_values(key_list[2], (SEQS, LEN, D), 1.0, 6.0, ((1, 32),))
    w_qkv = normal_values(key_list[3], (D, 3 * D), D ** -0.5, 0.21875, ((0, 16),))
    w_attn_out = normal_values(key_list[4], (D, D), (max(1, D * D // (LEN * 32))) ** -0.5, 2.0, ((0, 16),))
    w_mlp_in = normal_values(key_list[5], (D, FF), D ** -0.5, 0.21875, ((0, 16),))
    w_mlp_out = normal_values(key_list[6], (FF, D), FF ** -0.5, 0.109375, ((0, 16),))
    w_ada = normal_values(key_list[7], (6 * D, CDIM), CDIM ** -0.5, 0.5, ((0, 16),))
    bias_ada = normal_values(key_list[8], (6 * D,), 0.3, 3.0, ((0, 16),))
    gain_attn = jnp.clip(1.0 + 0.1 * jax.random.normal(key_list[9], (D,), jnp.float32), 0.5, 1.5).astype(jnp.bfloat16)
    gain_mlp = jnp.clip(1.0 + 0.1 * jax.random.normal(key_list[10], (D,), jnp.float32), 0.5, 1.5).astype(jnp.bfloat16)
    bias_mlp_in = normal_values(key_list[11], (FF,), 0.3, 3.0, ((0, 16),))
    bias_mlp_out = normal_values(key_list[12], (D,), 0.3, 3.0, ((0, 16),))
    return dict(hidden_in=hidden_in, time_index=time_index, cotangent=cotangent, w_qkv=w_qkv, w_attn_out=w_attn_out, w_mlp_in=w_mlp_in, w_mlp_out=w_mlp_out, w_ada=w_ada, bias_ada=bias_ada, gain_attn=gain_attn, gain_mlp=gain_mlp, bias_mlp_in=bias_mlp_in, bias_mlp_out=bias_mlp_out)


highest_precision = lax.Precision.HIGHEST

@jax.custom_vjp
def low(v):
    return lax.optimization_barrier(v.astype(jnp.bfloat16)).astype(jnp.float32)

@jax.custom_vjp
def low_back(v):
    return v

def low_keep(v):
    return (low(v), None)

def low_pass(kept, grad):
    return (grad,)

def back_keep(v):
    return (v, None)

def back_low(kept, grad):
    return (low(grad),)
low.defvjp(low_keep, low_pass)
low_back.defvjp(back_keep, back_low)

def normalize(values):
    center = values - lax.optimization_barrier(jnp.mean(values, -1, keepdims=True))
    return center * lax.rsqrt(lax.optimization_barrier(jnp.mean(center * center, -1, keepdims=True)) + 1e-05)

def adapt(values, gain, shift, scale):
    return normalize(values) * gain * (1.0 + scale) + shift

def time_features(time_index, width):
    half_width = width // 2
    frequency = jnp.exp(-math.log(10000.0) * jnp.arange(half_width, dtype=jnp.float32) / half_width)
    angles = time_index.astype(jnp.float32)[:, None] * frequency[None, :]
    return jnp.concatenate([jnp.cos(angles), jnp.sin(angles)], -1)

def rotary_tables(positions, head_dim):
    inverse = jnp.exp(-math.log(10000.0) * jnp.arange(0, head_dim, 2, dtype=jnp.float32) / head_dim)
    angles = positions.astype(jnp.float32)[:, None] * inverse[None, :]
    angles = jnp.concatenate([angles, angles], -1)
    return (jnp.cos(angles), jnp.sin(angles))

def rotate(values, cosine, sine):
    first_half, second_half = jnp.split(values, 2, axis=-1)
    turned = jnp.concatenate([-second_half, first_half], -1)
    return values * cosine[:, None, :] + turned * sine[:, None, :]

def attend(queries, keys, values):
    length = queries.shape[0]
    block_rows = min(256, length)

    def block_out(query_block):
        logits = low_back(jnp.einsum('qhd,khd->hqk', query_block, keys, precision=highest_precision) * HDIM ** (-0.5))
        probs = jax.nn.softmax(logits, axis=-1)
        return jnp.einsum('hqk,khd->qhd', low(probs), values, precision=highest_precision)
    block_list = queries.reshape(length // block_rows, block_rows, HEADS, HDIM)
    return lax.map(jax.checkpoint(block_out), block_list).reshape(length, HEADS, HDIM)

def project(left_neighbor, right_neighbor):
    return jnp.einsum('rum,mv->ruv', left_neighbor, right_neighbor, precision=highest_precision)

def reference(hidden_in, time_index, cotangent, w_qkv, w_attn_out, w_mlp_in, w_mlp_out, w_ada, bias_ada, gain_attn, gain_mlp, bias_mlp_in, bias_mlp_out):
    params = tuple((member.astype(jnp.float32) for member in (w_qkv, w_attn_out, w_mlp_in, w_mlp_out, w_ada, bias_ada, gain_attn, gain_mlp, bias_mlp_in, bias_mlp_out)))
    cond = jax.nn.silu(time_features(time_index, CDIM))
    seqs_here = hidden_in.shape[0]
    length = hidden_in.shape[1]
    cosine, sine = rotary_tables(jnp.arange(length, dtype=jnp.int32), HDIM)

    def layer(source, weight_qkv, weight_out, weight_in, weight_down, weight_ada, bias_mod, gain_first, gain_second, bias_in, bias_down):
        modulation = jnp.dot(cond, weight_ada.T, precision=highest_precision) + bias_mod
        shift_attn, scale_attn, gate_attn, shift_mlp, scale_mlp, gate_mlp = jnp.split(modulation[:, None, :], 6, axis=-1)
        attn_in = low(adapt(source, gain_first, shift_attn, scale_attn))
        qkv = low_back(project(attn_in, weight_qkv))
        split_three = qkv.reshape(seqs_here, length, 3, HEADS, HDIM)
        queries = low_back(low(rotate(split_three[:, :, 0], cosine, sine)))
        keys = low_back(low(rotate(split_three[:, :, 1], cosine, sine)))
        values = low_back(low(split_three[:, :, 2]))
        attended = jnp.stack([attend(queries[number], keys[number], values[number]) for number in range(seqs_here)])
        attn_low = low_back(low(attended.reshape(seqs_here, length, HEADS * HDIM)))
        projected = low_back(project(attn_low, weight_out))
        middle = source + gate_attn * projected
        mlp_in = low(adapt(middle, gain_second, shift_mlp, scale_mlp))
        pre_act = low_back(project(mlp_in, weight_in) + bias_in)
        active = low(jax.nn.gelu(pre_act, approximate=True))
        branch = low_back(project(active, weight_down) + bias_down)
        return middle + gate_mlp * branch
    result, pullback = jax.vjp(layer, hidden_in.astype(jnp.float32), *params)
    grads = pullback(cotangent.astype(jnp.float32))
    return (result.astype(jnp.bfloat16), grads[0], grads[1], grads[2], grads[3], grads[4], grads[5], grads[6], grads[7], grads[8], grads[9], grads[10])
```

```python
import math

import jax
import jax.numpy as jnp
from jax import lax
from jax.experimental import pallas as pl
from jax.experimental.pallas import tpu as pltpu
from jax.sharding import PartitionSpec as P

HEADS = 12
HDIM = 64


highest_precision = lax.Precision.HIGHEST


def normalize(values):
    center = values - jnp.mean(values, -1, keepdims=True)
    return center * lax.rsqrt(jnp.mean(center * center, -1, keepdims=True) + 1e-05)


def adapt(values, gain, shift, scale):
    return normalize(values) * gain * (1.0 + scale) + shift


def time_features(time_index, width):
    half_width = width // 2
    frequency = jnp.exp(-math.log(10000.0) * jnp.arange(half_width, dtype=jnp.float32) / half_width)
    angles = time_index.astype(jnp.float32)[:, None] * frequency[None, :]
    return jnp.concatenate([jnp.cos(angles), jnp.sin(angles)], -1)


def rotary_tables(positions, head_dim):
    inverse = jnp.exp(-math.log(10000.0) * jnp.arange(0, head_dim, 2, dtype=jnp.float32) / head_dim)
    angles = positions.astype(jnp.float32)[:, None] * inverse[None, :]
    angles = jnp.concatenate([angles, angles], -1)
    return (jnp.cos(angles), jnp.sin(angles))


def rotate(values, cosine, sine):
    first_half, second_half = jnp.split(values, 2, axis=-1)
    turned = jnp.concatenate([-second_half, first_half], -1)
    return values * cosine[:, None, :] + turned * sine[:, None, :]


def contract_rows(left_neighbor, right_neighbor):
    return lax.dot_general(
        left_neighbor, right_neighbor, (((0,), (0,)), ((), ())), preferred_element_type=jnp.float32
    )


def contract_cols(left_neighbor, right_neighbor):
    return lax.dot_general(
        left_neighbor, right_neighbor, (((1,), (1,)), ((), ())), preferred_element_type=jnp.float32
    )


def gelu_tanh(values):
    return jax.nn.gelu(values, approximate=True)


def local(
    hidden_in,
    time_index,
    cotangent,
    w_qkv,
    w_attn_out,
    w_mlp_in,
    w_mlp_out,
    w_ada,
    bias_ada,
    gain_attn,
    gain_mlp,
    bias_mlp_in,
    bias_mlp_out,
):
    seqs_here, row_count, width = hidden_in.shape
    flat_rows = seqs_here * row_count
    gathered = (
        lax.all_gather(w_qkv, "fsdp", axis=0, tiled=True),
        lax.all_gather(w_attn_out, "fsdp", axis=0, tiled=True),
        lax.all_gather(w_mlp_in, "fsdp", axis=0, tiled=True),
        lax.all_gather(w_mlp_out, "fsdp", axis=0, tiled=True),
        lax.all_gather(w_ada, "fsdp", axis=0, tiled=True),
        lax.all_gather(bias_ada, "fsdp", axis=0, tiled=True),
        lax.all_gather(gain_attn, "fsdp", axis=0, tiled=True),
        lax.all_gather(gain_mlp, "fsdp", axis=0, tiled=True),
        lax.all_gather(bias_mlp_in, "fsdp", axis=0, tiled=True),
        lax.all_gather(bias_mlp_out, "fsdp", axis=0, tiled=True),
    )
    (
        full_qkv,
        gathered_output,
        full_in,
        full_down,
        full_ada,
        full_bias_ada,
        full_gain_attn,
        full_gain_mlp,
        full_bias_in,
        full_bias_down,
    ) = gathered
    gain_first = full_gain_attn.astype(jnp.float32)
    gain_second = full_gain_mlp.astype(jnp.float32)
    cond = jax.nn.silu(time_features(time_index, full_ada.shape[1]))
    modulation = jnp.dot(
        cond, full_ada.astype(jnp.float32).T, precision=highest_precision
    ) + full_bias_ada.astype(jnp.float32)
    shift_attn, scale_attn, gate_attn, shift_mlp, scale_mlp, gate_mlp = jnp.split(
        modulation[:, None, :], 6, axis=-1
    )
    source = hidden_in.astype(jnp.float32)
    attn_in = adapt(source, gain_first, shift_attn, scale_attn)
    attn_low = attn_in.astype(jnp.bfloat16).reshape(flat_rows, width)
    qkv = jnp.dot(attn_low, full_qkv, preferred_element_type=jnp.float32).reshape(
        seqs_here, row_count, 3 * width
    )
    device_number = lax.axis_index("seq") * lax.axis_size("fsdp") + lax.axis_index("fsdp")
    positions = device_number * row_count + jnp.arange(row_count, dtype=jnp.int32)
    cosine, sine = rotary_tables(positions, HDIM)

    def turn_all(packed):
        split_three = packed.reshape(seqs_here, row_count, 3, HEADS, HDIM)
        query_turned = rotate(split_three[:, :, 0], cosine, sine).reshape(
            seqs_here, row_count, width
        )
        key_turned = rotate(split_three[:, :, 1], cosine, sine).reshape(seqs_here, row_count, width)
        return (query_turned, key_turned, split_three[:, :, 2].reshape(seqs_here, row_count, width))

    query_rot, key_rot, value_raw = turn_all(qkv)
    queries, keys, values = (
        lax.all_to_all(
            query_rot.astype(jnp.bfloat16), "seq", split_axis=2, concat_axis=1, tiled=True
        ),
        lax.all_to_all(
            key_rot.astype(jnp.bfloat16), "seq", split_axis=2, concat_axis=1, tiled=True
        ),
        lax.all_to_all(
            value_raw.astype(jnp.bfloat16), "seq", split_axis=2, concat_axis=1, tiled=True
        ),
    )
    local_heads = HEADS // lax.axis_size("seq")
    span = queries.shape[1]
    query_heads = queries.reshape(seqs_here, span, local_heads, HDIM)
    scale = HDIM ** (-0.5)

    def score_block(key_piece):
        key_heads = key_piece.reshape(seqs_here, key_piece.shape[1], local_heads, HDIM)
        logits = (
            jnp.einsum(
                "sqhd,skhd->shqk", query_heads, key_heads, preferred_element_type=jnp.float32
            )
            * scale
        )
        return (logits, key_heads)

    pieces = (
        lax.all_gather(keys, "fsdp", axis=1, tiled=True),
        lax.all_gather(values, "fsdp", axis=1, tiled=True),
    )
    best = jnp.full((seqs_here, local_heads, span), -1e30, jnp.float32)
    logits, unused = score_block(pieces[0])
    value_heads = pieces[1].reshape(seqs_here, pieces[1].shape[1], local_heads, HDIM)
    newest = jnp.maximum(best, jnp.max(logits, -1))
    raised = jnp.exp(logits - newest[..., None])
    total = jnp.sum(raised, -1)
    accum = jnp.einsum(
        "shqk,skhd->sqhd",
        raised.astype(jnp.bfloat16),
        value_heads,
        preferred_element_type=jnp.float32,
    )
    best, total, accum = (newest, total, accum)
    log_total = best + jnp.log(total)
    attended = accum / jnp.transpose(total, (0, 2, 1))[..., None]
    attended_low = attended.reshape(seqs_here, span, local_heads * HDIM).astype(jnp.bfloat16)
    attn_rows = lax.all_to_all(attended_low, "seq", split_axis=1, concat_axis=2, tiled=True)
    attn_flat = attn_rows.reshape(flat_rows, width)
    projected = jnp.dot(attn_flat, gathered_output, preferred_element_type=jnp.float32).reshape(
        seqs_here, row_count, width
    )
    middle = source + gate_attn * projected
    mlp_in = adapt(middle, gain_second, shift_mlp, scale_mlp)
    mlp_low = mlp_in.astype(jnp.bfloat16).reshape(flat_rows, width)
    pre_act = jnp.dot(mlp_low, full_in, preferred_element_type=jnp.float32) + full_bias_in.astype(
        jnp.float32
    )
    active = gelu_tanh(pre_act).astype(jnp.bfloat16)
    branch = (
        jnp.dot(active, full_down, preferred_element_type=jnp.float32)
        + full_bias_down.astype(jnp.float32)
    ).reshape(seqs_here, row_count, width)
    output = (middle + gate_mlp * branch).astype(jnp.bfloat16)
    grad_result = cotangent.astype(jnp.float32)
    grad_gate_mlp = jnp.sum(grad_result * branch, 1, keepdims=True)
    grad_branch = (gate_mlp * grad_result).astype(jnp.bfloat16).reshape(flat_rows, width)
    grad_bias_down = jnp.sum(grad_branch.astype(jnp.float32), 0)
    grad_down = contract_rows(active, grad_branch)
    grad_active = contract_cols(grad_branch, full_down)
    unused_gelu, gelu_back = jax.vjp(gelu_tanh, pre_act)
    grad_pre = gelu_back(grad_active)[0].astype(jnp.bfloat16)
    grad_bias_in = jnp.sum(grad_pre.astype(jnp.float32), 0)
    grad_in = contract_rows(mlp_low, grad_pre)
    grad_mlp_in = contract_cols(grad_pre, full_in).reshape(seqs_here, row_count, width)
    unused_second, second_back = jax.vjp(adapt, middle, gain_second, shift_mlp, scale_mlp)
    grad_middle_norm, grad_gain_mlp, grad_shift_mlp, grad_scale_mlp = second_back(grad_mlp_in)
    grad_middle = grad_result + grad_middle_norm
    grad_gate_attn = jnp.sum(grad_middle * projected, 1, keepdims=True)
    grad_proj = (gate_attn * grad_middle).astype(jnp.bfloat16).reshape(flat_rows, width)
    grad_attn_weight = contract_rows(attn_flat, grad_proj)
    grad_attn_rows = (
        contract_cols(grad_proj, gathered_output)
        .astype(jnp.bfloat16)
        .reshape(seqs_here, row_count, width)
    )
    grad_heads = lax.all_to_all(grad_attn_rows, "seq", split_axis=2, concat_axis=1, tiled=True)
    grad_head_parts = grad_heads.reshape(seqs_here, span, local_heads, HDIM)
    delta = jnp.transpose(jnp.sum(grad_head_parts.astype(jnp.float32) * attended, -1), (0, 2, 1))
    pieces = (
        lax.all_gather(keys, "fsdp", axis=1, tiled=True),
        lax.all_gather(values, "fsdp", axis=1, tiled=True),
    )
    logits, key_heads = score_block(pieces[0])
    piece_rows = pieces[1].shape[1]
    value_heads = pieces[1].reshape(seqs_here, piece_rows, local_heads, HDIM)
    probs = jnp.exp(logits - log_total[..., None])
    grad_weights = jnp.einsum(
        "sqhd,skhd->shqk", grad_head_parts, value_heads, preferred_element_type=jnp.float32
    )
    probs, grad_logits = (probs, (probs * (grad_weights - delta[..., None])).astype(jnp.bfloat16))
    grad_query = (
        jnp.einsum("shqk,skhd->sqhd", grad_logits, key_heads, preferred_element_type=jnp.float32)
        * scale
    )
    key_part = (
        jnp.einsum("shqk,sqhd->skhd", grad_logits, query_heads, preferred_element_type=jnp.float32)
        * scale
    )
    value_part = jnp.einsum(
        "shqk,sqhd->skhd",
        probs.astype(jnp.bfloat16),
        grad_head_parts,
        preferred_element_type=jnp.float32,
    )
    grad_key_all = key_part.reshape(seqs_here, piece_rows, local_heads * HDIM)
    grad_value_all = value_part.reshape(seqs_here, piece_rows, local_heads * HDIM)
    folded_rows = (grad_query, grad_key_all, grad_value_all)
    grad_query, grad_key_all, grad_value_all = folded_rows
    grad_keys, grad_values = (
        lax.psum_scatter(grad_key_all, "fsdp", scatter_dimension=1, tiled=True),
        lax.psum_scatter(grad_value_all, "fsdp", scatter_dimension=1, tiled=True),
    )
    grad_parts = (
        lax.all_to_all(
            grad_query.reshape(seqs_here, span, local_heads * HDIM).astype(jnp.bfloat16),
            "seq",
            split_axis=1,
            concat_axis=2,
            tiled=True,
        ),
        lax.all_to_all(
            grad_keys.astype(jnp.bfloat16), "seq", split_axis=1, concat_axis=2, tiled=True
        ),
        lax.all_to_all(
            grad_values.astype(jnp.bfloat16), "seq", split_axis=1, concat_axis=2, tiled=True
        ),
    )
    unused_turn, reverse_rotation = jax.vjp(turn_all, qkv)
    grad_qkv = (
        reverse_rotation(tuple((member.astype(jnp.float32) for member in grad_parts)))[0]
        .astype(jnp.bfloat16)
        .reshape(flat_rows, 3 * width)
    )
    grad_qkv_weight = contract_rows(attn_low, grad_qkv)
    grad_attn_in = contract_cols(grad_qkv, full_qkv).reshape(seqs_here, row_count, width)
    unused_first, first_back = jax.vjp(adapt, source, gain_first, shift_attn, scale_attn)
    grad_source_norm, grad_gain_attn, grad_shift_attn, grad_scale_attn = first_back(grad_attn_in)
    grad_hidden = grad_middle + grad_source_norm
    grad_mod = jnp.concatenate(
        [
            grad_shift_attn,
            grad_scale_attn,
            grad_gate_attn,
            grad_shift_mlp,
            grad_scale_mlp,
            grad_gate_mlp,
        ],
        -1,
    )[:, 0, :]
    grad_ada = jnp.dot(grad_mod.T, cond, precision=highest_precision)
    grad_bias_mod = jnp.sum(grad_mod, 0)
    summed = (
        lax.psum_scatter(grad_qkv_weight, "fsdp", scatter_dimension=0, tiled=True),
        lax.psum_scatter(grad_attn_weight, "fsdp", scatter_dimension=0, tiled=True),
        lax.psum_scatter(grad_in, "fsdp", scatter_dimension=0, tiled=True),
        lax.psum_scatter(grad_down, "fsdp", scatter_dimension=0, tiled=True),
        lax.psum_scatter(grad_ada, "fsdp", scatter_dimension=0, tiled=True),
        lax.psum_scatter(grad_bias_mod, "fsdp", scatter_dimension=0, tiled=True),
        lax.psum_scatter(grad_gain_attn, "fsdp", scatter_dimension=0, tiled=True),
        lax.psum_scatter(grad_gain_mlp, "fsdp", scatter_dimension=0, tiled=True),
        lax.psum_scatter(grad_bias_in, "fsdp", scatter_dimension=0, tiled=True),
        lax.psum_scatter(grad_bias_down, "fsdp", scatter_dimension=0, tiled=True),
    )
    totals = (
        lax.psum(summed[0].astype(jnp.bfloat16), "seq").astype(jnp.float32),
        lax.psum(summed[1].astype(jnp.bfloat16), "seq").astype(jnp.float32),
        lax.psum(summed[2].astype(jnp.bfloat16), "seq").astype(jnp.float32),
        lax.psum(summed[3].astype(jnp.bfloat16), "seq").astype(jnp.float32),
        lax.psum(summed[4].astype(jnp.bfloat16), "seq").astype(jnp.float32),
        lax.psum(summed[5].astype(jnp.bfloat16), "seq").astype(jnp.float32),
        lax.psum(summed[6].astype(jnp.bfloat16), "seq").astype(jnp.float32),
        lax.psum(summed[7].astype(jnp.bfloat16), "seq").astype(jnp.float32),
        lax.psum(summed[8].astype(jnp.bfloat16), "seq").astype(jnp.float32),
        lax.psum(summed[9].astype(jnp.bfloat16), "seq").astype(jnp.float32),
    )
    return (output, grad_hidden) + tuple(totals)


AXES = ("seq", "fsdp")
SEQ_BIT, HALF_BIT, LOW_BIT, ROW_BIT, CORE_BIT = 16, 8, 4, 2, 1
STREAM = ((ROW_BIT, SEQ_BIT), (LOW_BIT, ROW_BIT), (SEQ_BIT, LOW_BIT))
SHARED = ((LOW_BIT, LOW_BIT), (SEQ_BIT, SEQ_BIT), (ROW_BIT, ROW_BIT))
VMEM_LIMIT = 62 * 1024 * 1024


def swap_bits(values, even, odd=None):
    odd = even if odd is None else odd
    return lax.ppermute(values, AXES, [(i, i ^ (odd if i & 1 else even)) for i in range(32)])


def spread(values, order):
    for even, odd in order:
        values = jnp.concatenate([values, swap_bits(values, even, odd)], 0)
    return values


def collect(arrays, order):
    for even, odd in reversed(order):
        half = arrays[0].shape[0] // 2
        sent = jnp.concatenate([member[half:] for member in arrays], 1) if len(arrays) > 1 else arrays[0][half:]
        came = swap_bits(sent, even, odd)
        begin, summed = 0, []
        for member in arrays:
            part = came[:, begin : begin + member.shape[1]]
            begin += member.shape[1]
            summed.append((member[:half].astype(jnp.float32) + part.astype(jnp.float32)).astype(jnp.bfloat16))
        arrays = summed
    return arrays


def slot_masks(order, core):
    masks = [jnp.int32(0)]
    for even, odd in order:
        step = jnp.where(core == 0, even, odd).astype(jnp.int32)
        masks = masks + [mask ^ step for mask in masks]
    return jnp.stack(masks)


def quad_exchange(parts):
    came = swap_bits(parts[:, 1], ROW_BIT)
    parts = jnp.stack([parts[:, 0], came], 1)
    came = swap_bits(parts[1], LOW_BIT)
    return jnp.stack([parts[0], came], 0)


def pick(values, index, axis=0):
    return lax.dynamic_index_in_dim(values, index, axis, keepdims=False)


def pair_up(mine, other, position):
    return jnp.where(position == 0, jnp.stack([mine, other]), jnp.stack([other, mine]))


def dot_nn(left, right):
    return lax.dot_general(left, right, (((1,), (0,)), ((), ())), preferred_element_type=jnp.float32)


def row_norm(values):
    center = values - jnp.mean(values, -1, keepdims=True)
    return center * lax.rsqrt(jnp.mean(center * center, -1, keepdims=True) + 1e-05)


def head_select(width, head):
    lane = lax.broadcasted_iota(jnp.int32, (1, width), 1)
    return (lane % 128) // 32 == head


def order_weight_kernel(meta, pieces, chooser, out, gathered):
    rows = pieces.shape[0] // 16
    for slot in range(16):
        start = pl.multiple_of(meta[48 + slot] * rows, 16)
        gathered[pl.ds(start, rows), :] = pieces[slot * rows : (slot + 1) * rows, :]
    out[...] = dot_nn(gathered[...], chooser[...]).astype(jnp.bfloat16)


def attend_kernel(
    meta, own_rows, other_rows, weight, vectors, cosine, sine, query_out, key_out, value_out, out_turned, log_out, out, low
):
    gain, scale, shift = vectors[0:1, :], vectors[1:2, :], vectors[2:3, :]
    span = own_rows.shape[0]

    def project(source, base):
        def body(i, carry):
            here = pl.multiple_of(i * 256, 256)
            rows = pl.ds(pl.multiple_of(base + i * 256, 256), 256)
            norm = row_norm(source[pl.ds(here, 256), :].astype(jnp.float32))
            attn_in = (norm * gain * scale + shift).astype(jnp.bfloat16)
            low[rows, :] = attn_in
            packed = dot_nn(attn_in, weight[:, 256:768])
            first, second = packed[:, 0:128], packed[:, 128:256]
            turn_c, turn_s = cosine[rows, :], sine[rows, :]
            key_out[rows, 0:128] = (first * turn_c - second * turn_s).astype(jnp.bfloat16)
            key_out[rows, 128:256] = (second * turn_c + first * turn_s).astype(jnp.bfloat16)
            value_out[rows, :] = packed[:, 256:512].astype(jnp.bfloat16)
            return carry

        lax.fori_loop(0, span // 256, body, 0)

    project(own_rows, 0)
    project(other_rows, span)
    block = span // 8
    stride = 1 + meta[64]
    for j in range(4):
        rows = pl.ds(pl.multiple_of(j * stride * block, 128), block)
        packed = dot_nn(low[rows, :], weight[:, 0:256]) * (HDIM ** (-0.5))
        first, second = packed[:, 0:128], packed[:, 128:256]
        turn_c, turn_s = cosine[rows, :], sine[rows, :]
        here = slice(j * block, (j + 1) * block)
        query_out[here, 0:128] = (first * turn_c - second * turn_s).astype(jnp.bfloat16)
        query_out[here, 128:256] = (second * turn_c + first * turn_s).astype(jnp.bfloat16)
    keys = key_out[...]
    value_turned = value_out[...].T
    log_out[...] = jnp.zeros(log_out.shape, jnp.float32)
    out_turned[...] = jnp.zeros(out_turned.shape, jnp.float32)
    for head in range(3):
        for q_start in range(0, 4 * block, 256):
            here = slice(q_start, q_start + 256)
            query = query_out[here, :]
            query = jnp.where(head_select(256, head), query, jnp.zeros_like(query))
            scores = contract_cols(keys, query)
            best = jnp.max(scores, 0, keepdims=True)
            raised = jnp.exp(scores - best)
            total = jnp.sum(raised, 0, keepdims=True)
            mixed = dot_nn(value_turned[head * 64 : (head + 1) * 64, :], raised.astype(jnp.bfloat16))
            out_turned[head * 64 : (head + 1) * 64, here] = mixed / total
            log_out[head : head + 1, here] = best + jnp.log(total)
    turned_back = out_turned[...].T.astype(jnp.bfloat16)
    for j in range(4):
        out[j, :, :] = turned_back[j * block : (j + 1) * block, 0:192]


def attend_back_kernel(
    meta, own_rows, other_rows, weight, chooser, vectors, cosine, sine, query_in, key_in, value_in, out_turned, log_in, grad_in,
    grad_rows, grad_weight, sums, low, low_queries, grad_packed, key_sum, value_sum, weight_sum
):
    gain, scale, shift = vectors[0:1, :], vectors[1:2, :], vectors[2:3, :]
    span = own_rows.shape[0]
    block = span // 8
    width = own_rows.shape[1]
    stride = 1 + meta[64]
    keys, values = key_in[...], value_in[...]
    key_turned = keys.T
    lane_pad = jnp.zeros((4 * block, 64), jnp.bfloat16)
    grad_out = jnp.concatenate([jnp.concatenate([grad_in[j, :, :] for j in range(4)], 0), lane_pad], 1)
    grad_turned = grad_out.astype(jnp.float32).T
    key_sum[...] = jnp.zeros(key_sum.shape, jnp.float32)
    value_sum[...] = jnp.zeros(value_sum.shape, jnp.float32)
    product = grad_turned * out_turned[...]
    lane = lax.broadcasted_iota(jnp.int32, (1, 256), 1)
    query_parts = []
    for q_start in range(0, 4 * block, 256):
        here = slice(q_start, q_start + 256)
        query_sum = jnp.zeros((256, 256), jnp.float32)
        sub = lax.broadcasted_iota(jnp.int32, (256, 1), 0)
        for head in range(3):
            query = query_in[here, :]
            query = jnp.where(head_select(256, head), query, jnp.zeros_like(query))
            head_grad = grad_out[q_start : q_start + 256, :]
            head_grad = jnp.where(lane // 64 == head, head_grad, jnp.zeros_like(head_grad))
            probs = jnp.exp(contract_cols(keys, query) - log_in[head : head + 1, here])
            delta = jnp.sum(product[head * 64 : (head + 1) * 64, here], 0, keepdims=True)
            grad_scores = (probs * (contract_cols(values, head_grad) - delta)).astype(jnp.bfloat16)
            value_sum[...] += dot_nn(probs.astype(jnp.bfloat16), head_grad)
            key_sum[...] += dot_nn(grad_scores, query)
            part = dot_nn(key_turned, grad_scores)
            query_sum = jnp.where((sub % 128) // 32 == head, part, query_sum)
        query_parts.append(query_sum.T * (HDIM ** (-0.5)))
    for j in range(4):
        rows = pl.ds(pl.multiple_of(j * stride * block, 128), block)
        q_part = query_parts[(j * block) // 256][(j * block) % 256 : (j * block) % 256 + block, :]
        first, second = q_part[:, 0:128], q_part[:, 128:256]
        turn_c, turn_s = cosine[rows, :], sine[rows, :]
        here = slice(j * block, (j + 1) * block)
        grad_packed[here, 0:128] = (first * turn_c + second * turn_s).astype(jnp.bfloat16)
        grad_packed[here, 128:256] = (second * turn_c - first * turn_s).astype(jnp.bfloat16)
    weight_sum[...] = jnp.zeros((width, 512), jnp.float32)
    shift_sum = jnp.zeros((1, width), jnp.float32)
    norm_sum = jnp.zeros((1, width), jnp.float32)
    query_back = contract_cols(grad_packed[...], weight[:, 0:256])
    for i in range(2 * span // 256):
        rows = slice(i * 256, (i + 1) * 256)
        source, start = (own_rows, i * 256) if i * 256 < span else (other_rows, i * 256 - span)
        norm = row_norm(source[start : start + 256, :].astype(jnp.float32))
        attn_in = (norm * gain * scale + shift).astype(jnp.bfloat16)
        low[rows, :] = attn_in
        first, second = key_sum[rows, 0:128], key_sum[rows, 128:256]
        turn_c, turn_s = cosine[rows, :], sine[rows, :]
        pair = jnp.concatenate(
            [first * turn_c + second * turn_s, second * turn_c - first * turn_s, value_sum[rows, :]], 1
        ).astype(jnp.bfloat16)
        back = contract_cols(pair, weight[:, 256:768])
        grad_rows[rows, :] = back.astype(jnp.bfloat16)
        shift_sum += jnp.sum(back, 0, keepdims=True)
        norm_sum += jnp.sum(back * norm, 0, keepdims=True)
        weight_sum[...] += contract_rows(attn_in, pair)
    for j in range(4):
        rows = pl.ds(pl.multiple_of(j * stride * block, 128), block)
        here = slice(j * block, (j + 1) * block)
        back = query_back[here, :]
        norm = row_norm(own_rows[rows, :].astype(jnp.float32))
        shift_sum += jnp.sum(back, 0, keepdims=True)
        norm_sum += jnp.sum(back * norm, 0, keepdims=True)
        grad_rows[rows, :] = (grad_rows[rows, :].astype(jnp.float32) + back).astype(jnp.bfloat16)
        low_queries[here, :] = low[rows, :]
    query_weight = contract_rows(low_queries[...], grad_packed[...])
    whole = jnp.concatenate([query_weight, weight_sum[...]], 1).astype(jnp.bfloat16)
    grad_weight[...] = contract_cols(whole, chooser[...]).astype(jnp.bfloat16)
    sums[...] = jnp.concatenate([shift_sum, norm_sum, jnp.zeros((6, width), jnp.float32)], 0)


def middle_kernel(
    meta, attended, part_a, part_b, other, own_rows, vectors, projected_out, middle_out, low_out, weight_out
):
    core = meta[64]
    mine = pl.multiple_of(core * 384, 128)
    theirs = pl.multiple_of(384 - core * 384, 128)
    for slot in range(16):
        rows_a = pl.ds(pl.multiple_of(meta[slot] * 48, 16), 48)
        rows_b = pl.ds(pl.multiple_of(meta[16 + slot] * 48, 16), 48)
        rows_p = pl.ds(pl.multiple_of(meta[32 + slot] * 48, 16), 48)
        weight_out[rows_a, pl.ds(mine, 256)] = part_a[slot, :, :]
        weight_out[rows_b, pl.ds(pl.multiple_of(mine + 256, 128), 128)] = part_b[slot, :, :]
        weight_out[rows_p, pl.ds(theirs, 256)] = other[slot, :, 0:256]
        weight_out[rows_b, pl.ds(pl.multiple_of(theirs + 256, 128), 128)] = other[slot, :, 256:384]
    projected = dot_nn(attended[...], weight_out[...])
    projected_out[...] = projected
    middle = own_rows[...].astype(jnp.float32) + vectors[3:4, :] * projected
    middle_out[...] = middle
    low_out[...] = (row_norm(middle) * vectors[4:5, :] * vectors[5:6, :] + vectors[6:7, :]).astype(jnp.bfloat16)


def mlp_kernel(
    meta, low_own, low_other, grad_own, grad_other, part_a, part_b, bias, branch_own, branch_other, back_own, back_other,
    grad_a, grad_b, grad_bias, weight_in, weight_down, grad_in, grad_down, branch, back
):
    for slot in range(16):
        for lane_start, size, part, index in ((0, 256, part_a, meta[slot]), (256, 128, part_b, meta[16 + slot])):
            rows = pl.ds(pl.multiple_of(index * 48, 16), 48)
            for i in range(4):
                lanes = slice(i * 384 + lane_start, i * 384 + lane_start + size)
                weight_in[rows, lanes] = part[slot, i * 48 : (i + 1) * 48, :]
            rows = pl.ds(pl.multiple_of(index * 96, 16), 96)
            for i in range(2):
                lanes = slice(i * 384 + lane_start, i * 384 + lane_start + size)
                weight_down[rows, lanes] = part[slot, 192 + i * 96 : 192 + (i + 1) * 96, :]
    low = jnp.concatenate([low_own[...], low_other[...]], 0)
    grad = jnp.concatenate([grad_own[...], grad_other[...]], 0)
    tokens = low_own.shape[0]
    branch[...] = jnp.zeros(branch.shape, jnp.float32)
    back[...] = jnp.zeros(back.shape, jnp.float32)
    root, cubic = math.sqrt(2.0 / math.pi), 0.044715
    for i in range(4):
        hidden = slice(i * 384, (i + 1) * 384)
        pre_act = dot_nn(low, weight_in[:, hidden]) + bias[:, hidden]
        square = pre_act * pre_act
        bend = jnp.tanh(root * (pre_act + cubic * square * pre_act))
        active = (0.5 * pre_act * (1.0 + bend)).astype(jnp.bfloat16)
        slope = 0.5 * (1.0 + bend) + 0.5 * pre_act * (1.0 - bend * bend) * (root * (1.0 + 3.0 * cubic * square))
        branch[...] += dot_nn(active, weight_down[hidden, :])
        grad_pre = (contract_cols(grad, weight_down[hidden, :]) * slope).astype(jnp.bfloat16)
        grad_bias[:, hidden] = jnp.sum(grad_pre.astype(jnp.float32), 0, keepdims=True)
        back[...] += contract_cols(grad_pre, weight_in[:, hidden])
        grad_in[:, hidden] = contract_rows(low, grad_pre).astype(jnp.bfloat16)
        grad_down[hidden, :] = contract_rows(active, grad).astype(jnp.bfloat16)
    branch_own[...] = branch[:tokens, :]
    branch_other[...] = branch[tokens:, :]
    back_own[...] = back[:tokens, :]
    back_other[...] = back[tokens:, :]
    for slot in range(16):
        for lane_start, size, part, index in ((0, 256, grad_a, meta[slot]), (256, 128, grad_b, meta[16 + slot])):
            rows = pl.ds(pl.multiple_of(index * 48, 16), 48)
            for i in range(4):
                lanes = slice(i * 384 + lane_start, i * 384 + lane_start + size)
                part[slot, i * 48 : (i + 1) * 48, :] = grad_in[rows, lanes]
            rows = pl.ds(pl.multiple_of(index * 96, 16), 96)
            for i in range(2):
                lanes = slice(i * 384 + lane_start, i * 384 + lane_start + size)
                part[slot, 192 + i * 96 : 192 + (i + 1) * 96, :] = grad_down[rows, lanes]


def turn_kernel(
    meta, branch_own, branch_other, back_own, back_other, bias, middle_in, projected_in, cotangent, grad_branch, weight,
    attended, vectors, output, grad_middle_out, grad_attn_out, keep_a, keep_b, send_a, send_b, sums, grad_weight
):
    width = middle_in.shape[1]
    core = meta[64]
    mine = pl.multiple_of(core * 384, 128)
    theirs = pl.multiple_of(384 - core * 384, 128)
    branch = branch_own[...] + branch_other[...] + bias[...]
    middle = middle_in[...]
    grad = cotangent[...].astype(jnp.float32)
    output[...] = (middle + vectors[7:8, :] * branch).astype(jnp.bfloat16)
    back = back_own[...] + back_other[...]
    center = middle - jnp.mean(middle, -1, keepdims=True)
    inverse = lax.rsqrt(jnp.mean(center * center, -1, keepdims=True) + 1e-05)
    norm = center * inverse
    scaled = back * vectors[5:6, :] * vectors[4:5, :]
    grad_middle = grad + inverse * (
        scaled - jnp.mean(scaled, -1, keepdims=True) - norm * jnp.mean(scaled * norm, -1, keepdims=True)
    )
    grad_middle_out[...] = grad_middle
    grad_proj = (vectors[3:4, :] * grad_middle).astype(jnp.bfloat16)
    grad_attn_out[...] = contract_cols(grad_proj, weight[...]).astype(jnp.bfloat16)
    grad_weight[...] = contract_rows(attended[...], grad_proj).astype(jnp.bfloat16)
    for slot in range(16):
        rows_a = pl.ds(pl.multiple_of(meta[slot] * 48, 16), 48)
        rows_b = pl.ds(pl.multiple_of(meta[16 + slot] * 48, 16), 48)
        rows_p = pl.ds(pl.multiple_of(meta[32 + slot] * 48, 16), 48)
        keep_a[slot, :, :] = grad_weight[rows_a, pl.ds(mine, 256)]
        keep_b[slot, :, :] = grad_weight[rows_b, pl.ds(pl.multiple_of(mine + 256, 128), 128)]
        send_a[slot, :, :] = grad_weight[rows_p, pl.ds(theirs, 256)]
        send_b[slot, :, :] = grad_weight[rows_b, pl.ds(pl.multiple_of(theirs + 256, 128), 128)]

    def total(values):
        return jnp.sum(values, 0, keepdims=True)

    sums[...] = jnp.concatenate(
        [
            total(grad_middle * projected_in[...]),
            total(back),
            total(back * norm),
            total(grad * branch),
            total(grad_branch[...].astype(jnp.float32)),
            jnp.zeros((3, width), jnp.float32),
        ],
        0,
    )


def call(body, outs, args, scratch=(), flops=0, moved=0):
    whole = pl.BlockSpec(memory_space=pltpu.VMEM)
    in_specs = [pl.BlockSpec(memory_space=pltpu.SMEM)] + [whole] * (len(args) - 1)
    return pl.pallas_call(
        body,
        out_shape=[jax.ShapeDtypeStruct(*member) for member in outs],
        in_specs=in_specs,
        out_specs=[whole] * len(outs),
        scratch_shapes=[pltpu.VMEM(*member) for member in scratch],
        compiler_params=pltpu.CompilerParams(vmem_limit_bytes=VMEM_LIMIT),
        cost_estimate=pl.CostEstimate(flops=flops, bytes_accessed=moved, transcendentals=0),
    )(*args)


def cube_local(
    hidden_in, time_index, cotangent, w_qkv, w_attn_out, w_mlp_in, w_mlp_out, w_ada, bias_ada, gain_attn, gain_mlp,
    bias_mlp_in, bias_mlp_out
):
    f32, bf16 = jnp.float32, jnp.bfloat16
    rows, width = hidden_in.shape[1:]
    tokens = 2 * rows
    place = lax.axis_index("fsdp")
    side = lax.axis_index("seq")
    device = side * 16 + place
    core, half, group = place & 1, place >> 3, (place >> 1) & 3
    x_own = jnp.concatenate(
        [pick(hidden_in, half), swap_bits(pick(hidden_in, 1 - half), HALF_BIT)], 0
    )
    x_a = spread(x_own, STREAM)
    x_b = swap_bits(x_a, CORE_BIT)
    cond = jax.nn.silu(time_features(time_index, w_ada.shape[1]))
    modulation = jnp.dot(cond, w_ada.astype(f32).T, precision=highest_precision) + bias_ada.astype(f32)
    vector = jnp.concatenate(
        [modulation.reshape(-1)]
        + [member.astype(f32) for member in (gain_attn, gain_mlp, bias_mlp_in, bias_mlp_out)]
    )[None]
    for bit in (CORE_BIT, ROW_BIT, LOW_BIT, HALF_BIT):
        vector = jnp.concatenate([vector, swap_bits(vector, bit)], 0)
    vector = vector[place ^ jnp.arange(16)]
    parts, begin = [], 0
    for size in (288, 288, 48, 48, 192, 48):
        parts.append(vector[:, begin : begin + size])
        begin += size
    modulation = jnp.stack([parts[0].reshape(6, width), parts[1].reshape(6, width)])
    shift_attn, scale_attn, gate_attn, shift_mlp, scale_mlp, gate_mlp = [
        row for row in pick(modulation, half)
    ]
    full_gain_attn, full_gain_mlp = parts[2].reshape(-1), parts[3].reshape(-1)
    bias_in = pick(parts[4].reshape(8, 2, 192), core, 1).reshape(1, -1)
    bias_down = parts[5].reshape(1, -1)
    vectors = jnp.stack(
        [full_gain_attn, 1.0 + scale_attn, shift_attn, gate_attn, full_gain_mlp, 1.0 + scale_mlp, shift_mlp, gate_mlp]
    )
    stream_own, stream_other = slot_masks(STREAM, core), slot_masks(STREAM, 1 - core)
    shared = slot_masks(SHARED, core)

    def weight_slots(masks):
        moved = ((masks & 6) | (masks >> 4))[:, None] ^ jnp.array([0, 8], jnp.int32)[None]
        return (((place & 14) + side) ^ moved).reshape(-1)

    quad = jnp.array([0, ROW_BIT, LOW_BIT, LOW_BIT | ROW_BIT], jnp.int32)
    oct_masks = jnp.concatenate([quad, quad ^ HALF_BIT])
    row_slots = place ^ jnp.concatenate([oct_masks, oct_masks ^ CORE_BIT])
    meta = jnp.concatenate(
        [weight_slots(stream_own), weight_slots(shared), weight_slots(stream_other), row_slots, core[None]]
    ).astype(jnp.int32)
    blocks = jnp.concatenate([device ^ stream_own, device ^ CORE_BIT ^ stream_other])
    blocks = jnp.stack([blocks, blocks ^ HALF_BIT], 1)
    positions = (blocks[:, :, None] * rows + jnp.arange(rows, dtype=jnp.int32)).reshape(-1)
    inverse = jnp.exp(-math.log(10000.0) * jnp.arange(0, HDIM, 2, dtype=f32) / HDIM)
    angles = positions.astype(f32)[:, None] * inverse[None, :]
    cosine, sine = jnp.tile(jnp.cos(angles), (1, 4)), jnp.tile(jnp.sin(angles), (1, 4))
    lane = jnp.arange(768)
    inner = lane % 128
    wanted = jnp.where(
        lane < 512,
        jnp.where(inner < 96, (lane // 256) * 192 + (inner // 32) * 64 + ((lane % 256) // 128) * 32 + inner % 32, -1),
        jnp.where(lane < 704, lane - 128, -1),
    )
    chooser = (jnp.arange(576)[:, None] == wanted[None, :]).astype(bf16)
    grouped = w_qkv.reshape(48, 3, 4, 192).transpose(2, 0, 1, 3).reshape(4, 48, 576)
    grouped = grouped[group ^ jnp.arange(4)].reshape(2, 2, 48, 576)
    grouped = quad_exchange(grouped).reshape(4, 48, 576)
    grouped = jnp.concatenate([grouped, swap_bits(grouped, HALF_BIT)], 0)
    grouped = jnp.concatenate([grouped, swap_bits(grouped, CORE_BIT)], 0).reshape(768, 576)
    (weight_qkv,) = call(
        order_weight_kernel,
        [((768, 768), bf16)],
        [meta, grouped, chooser],
        [((768, 576), bf16)],
        flops=2 * 768 * 768 * 576,
        moved=3_000_000,
    )
    in_columns = w_mlp_in.reshape(48, 8, 2, 192)

    def in_blocks(columns):
        return columns.reshape(48, 4, 384).transpose(1, 0, 2).reshape(192, 384)

    own_share = jnp.concatenate(
        [in_blocks(pick(in_columns, core, 2)), pick(w_attn_out.reshape(48, 2, 384), core, 1)], 0
    )
    sent_share = jnp.concatenate(
        [in_blocks(pick(in_columns, 1 - core, 2)), pick(w_attn_out.reshape(48, 2, 384), 1 - core, 1)], 0
    )
    share = jnp.where(core == side, own_share, swap_bits(sent_share, CORE_BIT))
    down_share = pick(w_mlp_out.reshape(2, 96, 2, 384), side).transpose(1, 0, 2).reshape(192, 384)
    share = jnp.concatenate([share[:192], down_share, share[192:]], 0)
    share = jnp.stack([share, swap_bits(share, HALF_BIT)])[None]
    part_a = spread(share[..., :256], STREAM).reshape(16, 432, 256)
    part_b = spread(share[..., 256:], SHARED).reshape(16, 432, 128)
    out_share = jnp.concatenate([part_a[:, 384:], part_b[:, 384:]], 2)
    other_out = swap_bits(out_share, CORE_BIT)
    span = 16 * tokens
    queries, keys, values, out_turned, log_total, heads_out = call(
        attend_kernel,
        [
            ((4 * tokens, 256), bf16),
            ((span, 256), bf16),
            ((span, 256), bf16),
            ((256, 4 * tokens), f32),
            ((8, 4 * tokens), f32),
            ((4, tokens, 192), bf16),
        ],
        [meta, x_a, x_b, weight_qkv, vectors, cosine, sine],
        [((span, width), bf16)],
        flops=8_000_000_000,
        moved=10_000_000,
    )
    by_group = quad_exchange(heads_out.reshape(2, 2, tokens, 192)).reshape(4, tokens, 192)
    attended = by_group[group ^ jnp.arange(4)].transpose(1, 0, 2).reshape(tokens, width)
    projected, middle, mlp_own, weight_out = call(
        middle_kernel,
        [((tokens, width), f32), ((tokens, width), f32), ((tokens, width), bf16), ((768, 768), bf16)],
        [meta, attended, part_a[:, 384:], part_b[:, 384:], other_out, x_own, vectors],
        flops=150_000_000,
        moved=3_000_000,
    )
    grad_own = jnp.concatenate(
        [pick(cotangent, half), swap_bits(pick(cotangent, 1 - half), HALF_BIT)], 0
    )
    branch_grad = (gate_mlp[None] * grad_own.astype(f32)).astype(bf16)
    branch_grad_other = swap_bits(branch_grad, CORE_BIT)
    mlp_other = swap_bits(mlp_own, CORE_BIT)
    branch_own, branch_sent, back_own, back_sent, grad_a, grad_b, grad_bias_in = call(
        mlp_kernel,
        [((tokens, width), f32)] * 4
        + [((16, 384, 256), bf16), ((16, 384, 128), bf16), ((1, 1536), f32)],
        [meta, mlp_own, mlp_other, branch_grad, branch_grad_other, part_a, part_b, bias_in],
        [((768, 1536), bf16), ((1536, 768), bf16), ((768, 1536), bf16), ((1536, 768), bf16)]
        + [((2 * tokens, width), f32)] * 2,
        flops=3_600_000_000,
        moved=12_000_000,
    )
    came = swap_bits(jnp.stack([branch_sent, back_sent]), CORE_BIT)
    output_rows, grad_middle, grad_attn, keep_a, keep_b, send_a, send_b, sums_mlp = call(
        turn_kernel,
        [
            ((tokens, width), bf16),
            ((tokens, width), f32),
            ((tokens, width), bf16),
            ((16, 48, 256), bf16),
            ((16, 48, 128), bf16),
            ((16, 48, 256), bf16),
            ((16, 48, 128), bf16),
            ((8, width), f32),
        ],
        [meta, branch_own, came[0], back_own, came[1], bias_down, middle, projected, grad_own, branch_grad, weight_out]
        + [attended, vectors],
        [((768, 768), bf16)],
        flops=300_000_000,
        moved=5_000_000,
    )
    grad_heads = grad_attn.reshape(tokens, 4, 192).transpose(1, 0, 2)[group ^ jnp.arange(4)]
    grad_heads = quad_exchange(grad_heads.reshape(2, 2, tokens, 192)).reshape(4, tokens, 192)
    grad_rows, grad_qkv, sums_attn = call(
        attend_back_kernel,
        [((span, width), bf16), ((768, 576), bf16), ((8, width), f32)],
        [meta, x_a, x_b, weight_qkv, chooser, vectors, cosine, sine, queries, keys, values, out_turned, log_total]
        + [grad_heads],
        [
            ((span, width), bf16),
            ((4 * tokens, width), bf16),
            ((4 * tokens, 256), bf16),
            ((span, 256), f32),
            ((span, 256), f32),
            ((width, 512), f32),
        ],
        flops=16_000_000_000,
        moved=16_000_000,
    )
    grad_rows = grad_rows.reshape(2, 8, tokens, width)
    came_rows = swap_bits(grad_rows[1], CORE_BIT)
    own_sum = (grad_rows[0].astype(f32) + came_rows.astype(f32)).astype(bf16)
    (own_sum,) = collect([own_sum], STREAM)
    grad_in = own_sum[0].astype(f32)
    source = x_own.astype(f32)
    center = source - jnp.mean(source, -1, keepdims=True)
    inverse = lax.rsqrt(jnp.mean(center * center, -1, keepdims=True) + 1e-05)
    norm = center * inverse
    scaled = grad_in * vectors[1:2] * vectors[0:1]
    grad_hidden = grad_middle + inverse * (
        scaled - jnp.mean(scaled, -1, keepdims=True) - norm * jnp.mean(scaled * norm, -1, keepdims=True)
    )
    output = pair_up(output_rows[:rows], swap_bits(output_rows[rows:], HALF_BIT), half)
    grad_hidden = pair_up(
        grad_hidden[:rows], swap_bits(grad_hidden[rows:].astype(bf16), HALF_BIT).astype(f32), half
    )

    def plus(left, right):
        return (left.astype(f32) + right.astype(f32)).astype(bf16)

    came = swap_bits(jnp.concatenate([send_a, send_b], 2), CORE_BIT)
    out_a, out_b = plus(keep_a, came[..., :256]), plus(keep_b, came[..., 256:])
    sum_a = collect([grad_a.reshape(8, 768, 256), out_a.reshape(8, 96, 256)], STREAM)
    sum_b = collect([grad_b.reshape(8, 768, 128), out_b.reshape(8, 96, 128)], SHARED)
    total = jnp.concatenate(
        [
            jnp.concatenate([sum_a[0].reshape(2, 384, 256), sum_b[0].reshape(2, 384, 128)], 2),
            jnp.concatenate([sum_a[1].reshape(2, 48, 256), sum_b[1].reshape(2, 48, 128)], 2),
        ],
        1,
    )
    total = plus(total[0], swap_bits(total[1], HALF_BIT))
    across = swap_bits(total, SEQ_BIT)
    grad_down = pair_up(total[192:384], across[192:384], side).reshape(2, 2, 96, 384)
    grad_down = grad_down.transpose(0, 2, 1, 3).reshape(192, 768).astype(f32)
    pieces = [jnp.concatenate([member[:192], member[384:]], 0) for member in (total, across)]
    mine = jnp.where(core == side, pieces[0], pieces[1])
    theirs = swap_bits(jnp.where(core == side, pieces[1], pieces[0]), CORE_BIT)

    def in_columns_back(blocks):
        return blocks.reshape(4, 48, 384).transpose(1, 0, 2).reshape(48, 8, 192)

    grad_w_in = pair_up(in_columns_back(mine[:192]), in_columns_back(theirs[:192]), core)
    grad_w_in = grad_w_in.transpose(1, 2, 0, 3).reshape(48, 3072).astype(f32)
    grad_w_out = pair_up(mine[192:], theirs[192:], core).transpose(1, 0, 2).reshape(48, 768).astype(f32)
    by_core = grad_qkv.reshape(8, 2, 48, 576)
    kept = plus(pick(by_core, core, 1), swap_bits(pick(by_core, 1 - core, 1), CORE_BIT))
    by_side = kept.reshape(8, 2, 24, 576)
    kept = plus(pick(by_side, side, 1), swap_bits(pick(by_side, 1 - side, 1), SEQ_BIT))
    by_half = kept.reshape(2, 4, 24, 576)
    kept = plus(pick(by_half, half), swap_bits(pick(by_half, 1 - half), HALF_BIT))
    kept = quad_exchange(kept[group ^ jnp.arange(4)].reshape(2, 2, 24, 576)).reshape(4, 24, 576)
    kept = kept[group ^ jnp.arange(4)].reshape(4, 24, 3, 192).transpose(1, 2, 0, 3).reshape(24, 2304)
    grad_w_qkv = pair_up(kept, swap_bits(kept, SEQ_BIT), side).reshape(48, 2304).astype(f32)
    small = jnp.concatenate([sums_attn[0:2], sums_mlp[0:5]], 0)
    small = small + swap_bits(small, CORE_BIT)
    small = jnp.concatenate([small, grad_bias_in.reshape(2, width)], 0)
    for bit in (ROW_BIT, LOW_BIT, SEQ_BIT):
        small = small + swap_bits(small, bit)
    both = pair_up(small, swap_bits(small, HALF_BIT), half)
    plus_scale = 1.0 + modulation[:, 1], 1.0 + modulation[:, 4]
    grad_mod = jnp.stack(
        [both[:, 0], both[:, 1] * full_gain_attn, both[:, 2], both[:, 3], both[:, 4] * full_gain_mlp, both[:, 5]], 1
    ).reshape(2, 16, 288)
    grad_mod = pick(grad_mod, place, 1)
    grad_ada = grad_mod[0][:, None] * cond[0][None] + grad_mod[1][:, None] * cond[1][None]
    gain_first = pick(jnp.sum(both[:, 1] * plus_scale[0], 0).reshape(16, 48), place)
    gain_second = pick(jnp.sum(both[:, 4] * plus_scale[1], 0).reshape(16, 48), place)
    summed = both[0] + both[1]
    bias_in_grad = pick(summed[7:9].reshape(8, 192), place >> 1)
    bias_down_grad = pick(summed[6].reshape(16, 48), place)
    return (
        output,
        grad_hidden,
        grad_w_qkv,
        grad_w_out,
        grad_w_in,
        grad_down,
        grad_ada,
        jnp.sum(grad_mod, 0),
        gain_first,
        gain_second,
        bias_in_grad,
        bias_down_grad,
    )


def solution(mesh):
    return jax.shard_map(
        cube_local if dict(mesh.shape) == {"seq": 2, "fsdp": 16} else local,
        mesh=mesh,
        in_specs=(
            P(None, ("seq", "fsdp"), None),
            P(),
            P(None, ("seq", "fsdp"), None),
            P("fsdp", None),
            P("fsdp", None),
            P("fsdp", None),
            P("fsdp", None),
            P("fsdp", None),
            P("fsdp"),
            P("fsdp"),
            P("fsdp"),
            P("fsdp"),
            P("fsdp"),
        ),
        out_specs=(
            P(None, ("seq", "fsdp"), None),
            P(None, ("seq", "fsdp"), None),
            P("fsdp", None),
            P("fsdp", None),
            P("fsdp", None),
            P("fsdp", None),
            P("fsdp", None),
            P("fsdp"),
            P("fsdp"),
            P("fsdp"),
            P("fsdp"),
            P("fsdp"),
        ),
        check_vma=False,
    )
```

```python
import math

import jax
import jax.numpy as jnp
from jax import lax
from jax.experimental import pallas as pl
from jax.experimental.pallas import tpu as pltpu
from jax.sharding import PartitionSpec as P

HEADS = 12
HDIM = 64


highest_precision = lax.Precision.HIGHEST


def normalize(values):
    center = values - jnp.mean(values, -1, keepdims=True)
    return center * lax.rsqrt(jnp.mean(center * center, -1, keepdims=True) + 1e-05)


def adapt(values, gain, shift, scale):
    return normalize(values) * gain * (1.0 + scale) + shift


def time_features(time_index, width):
    half_width = width // 2
    frequency = jnp.exp(-math.log(10000.0) * jnp.arange(half_width, dtype=jnp.float32) / half_width)
    angles = time_index.astype(jnp.float32)[:, None] * frequency[None, :]
    return jnp.concatenate([jnp.cos(angles), jnp.sin(angles)], -1)


def rotary_tables(positions, head_dim):
    inverse = jnp.exp(-math.log(10000.0) * jnp.arange(0, head_dim, 2, dtype=jnp.float32) / head_dim)
    angles = positions.astype(jnp.float32)[:, None] * inverse[None, :]
    angles = jnp.concatenate([angles, angles], -1)
    return (jnp.cos(angles), jnp.sin(angles))


def rotate(values, cosine, sine):
    first_half, second_half = jnp.split(values, 2, axis=-1)
    turned = jnp.concatenate([-second_half, first_half], -1)
    return values * cosine[:, None, :] + turned * sine[:, None, :]


def contract_rows(left_neighbor, right_neighbor):
    return lax.dot_general(
        left_neighbor, right_neighbor, (((0,), (0,)), ((), ())), preferred_element_type=jnp.float32
    )


def contract_cols(left_neighbor, right_neighbor):
    return lax.dot_general(
        left_neighbor, right_neighbor, (((1,), (1,)), ((), ())), preferred_element_type=jnp.float32
    )


def gelu_tanh(values):
    return jax.nn.gelu(values, approximate=True)


def local(
    hidden_in,
    time_index,
    cotangent,
    w_qkv,
    w_attn_out,
    w_mlp_in,
    w_mlp_out,
    w_ada,
    bias_ada,
    gain_attn,
    gain_mlp,
    bias_mlp_in,
    bias_mlp_out,
):
    seqs_here, row_count, width = hidden_in.shape
    flat_rows = seqs_here * row_count
    gathered = (
        lax.all_gather(w_qkv, "fsdp", axis=0, tiled=True),
        lax.all_gather(w_attn_out, "fsdp", axis=0, tiled=True),
        lax.all_gather(w_mlp_in, "fsdp", axis=0, tiled=True),
        lax.all_gather(w_mlp_out, "fsdp", axis=0, tiled=True),
        lax.all_gather(w_ada, "fsdp", axis=0, tiled=True),
        lax.all_gather(bias_ada, "fsdp", axis=0, tiled=True),
        lax.all_gather(gain_attn, "fsdp", axis=0, tiled=True),
        lax.all_gather(gain_mlp, "fsdp", axis=0, tiled=True),
        lax.all_gather(bias_mlp_in, "fsdp", axis=0, tiled=True),
        lax.all_gather(bias_mlp_out, "fsdp", axis=0, tiled=True),
    )
    (
        full_qkv,
        gathered_output,
        full_in,
        full_down,
        full_ada,
        full_bias_ada,
        full_gain_attn,
        full_gain_mlp,
        full_bias_in,
        full_bias_down,
    ) = gathered
    gain_first = full_gain_attn.astype(jnp.float32)
    gain_second = full_gain_mlp.astype(jnp.float32)
    cond = jax.nn.silu(time_features(time_index, full_ada.shape[1]))
    modulation = jnp.dot(
        cond, full_ada.astype(jnp.float32).T, precision=highest_precision
    ) + full_bias_ada.astype(jnp.float32)
    shift_attn, scale_attn, gate_attn, shift_mlp, scale_mlp, gate_mlp = jnp.split(
        modulation[:, None, :], 6, axis=-1
    )
    source = hidden_in.astype(jnp.float32)
    attn_in = adapt(source, gain_first, shift_attn, scale_attn)
    attn_low = attn_in.astype(jnp.bfloat16).reshape(flat_rows, width)
    qkv = jnp.dot(attn_low, full_qkv, preferred_element_type=jnp.float32).reshape(
        seqs_here, row_count, 3 * width
    )
    device_number = lax.axis_index("seq") * lax.axis_size("fsdp") + lax.axis_index("fsdp")
    positions = device_number * row_count + jnp.arange(row_count, dtype=jnp.int32)
    cosine, sine = rotary_tables(positions, HDIM)

    def turn_all(packed):
        split_three = packed.reshape(seqs_here, row_count, 3, HEADS, HDIM)
        query_turned = rotate(split_three[:, :, 0], cosine, sine).reshape(
            seqs_here, row_count, width
        )
        key_turned = rotate(split_three[:, :, 1], cosine, sine).reshape(seqs_here, row_count, width)
        return (query_turned, key_turned, split_three[:, :, 2].reshape(seqs_here, row_count, width))

    query_rot, key_rot, value_raw = turn_all(qkv)
    queries, keys, values = (
        lax.all_to_all(
            query_rot.astype(jnp.bfloat16), "seq", split_axis=2, concat_axis=1, tiled=True
        ),
        lax.all_to_all(
            key_rot.astype(jnp.bfloat16), "seq", split_axis=2, concat_axis=1, tiled=True
        ),
        lax.all_to_all(
            value_raw.astype(jnp.bfloat16), "seq", split_axis=2, concat_axis=1, tiled=True
        ),
    )
    local_heads = HEADS // lax.axis_size("seq")
    span = queries.shape[1]
    query_heads = queries.reshape(seqs_here, span, local_heads, HDIM)
    scale = HDIM ** (-0.5)

    def score_block(key_piece):
        key_heads = key_piece.reshape(seqs_here, key_piece.shape[1], local_heads, HDIM)
        logits = (
            jnp.einsum(
                "sqhd,skhd->shqk", query_heads, key_heads, preferred_element_type=jnp.float32
            )
            * scale
        )
        return (logits, key_heads)

    pieces = (
        lax.all_gather(keys, "fsdp", axis=1, tiled=True),
        lax.all_gather(values, "fsdp", axis=1, tiled=True),
    )
    best = jnp.full((seqs_here, local_heads, span), -1e30, jnp.float32)
    logits, unused = score_block(pieces[0])
    value_heads = pieces[1].reshape(seqs_here, pieces[1].shape[1], local_heads, HDIM)
    newest = jnp.maximum(best, jnp.max(logits, -1))
    raised = jnp.exp(logits - newest[..., None])
    total = jnp.sum(raised, -1)
    accum = jnp.einsum(
        "shqk,skhd->sqhd",
        raised.astype(jnp.bfloat16),
        value_heads,
        preferred_element_type=jnp.float32,
    )
    best, total, accum = (newest, total, accum)
    log_total = best + jnp.log(total)
    attended = accum / jnp.transpose(total, (0, 2, 1))[..., None]
    attended_low = attended.reshape(seqs_here, span, local_heads * HDIM).astype(jnp.bfloat16)
    attn_rows = lax.all_to_all(attended_low, "seq", split_axis=1, concat_axis=2, tiled=True)
    attn_flat = attn_rows.reshape(flat_rows, width)
    projected = jnp.dot(attn_flat, gathered_output, preferred_element_type=jnp.float32).reshape(
        seqs_here, row_count, width
    )
    middle = source + gate_attn * projected
    mlp_in = adapt(middle, gain_second, shift_mlp, scale_mlp)
    mlp_low = mlp_in.astype(jnp.bfloat16).reshape(flat_rows, width)
    pre_act = jnp.dot(mlp_low, full_in, preferred_element_type=jnp.float32) + full_bias_in.astype(
        jnp.float32
    )
    active = gelu_tanh(pre_act).astype(jnp.bfloat16)
    branch = (
        jnp.dot(active, full_down, preferred_element_type=jnp.float32)
        + full_bias_down.astype(jnp.float32)
    ).reshape(seqs_here, row_count, width)
    output = (middle + gate_mlp * branch).astype(jnp.bfloat16)
    grad_result = cotangent.astype(jnp.float32)
    grad_gate_mlp = jnp.sum(grad_result * branch, 1, keepdims=True)
    grad_branch = (gate_mlp * grad_result).astype(jnp.bfloat16).reshape(flat_rows, width)
    grad_bias_down = jnp.sum(grad_branch.astype(jnp.float32), 0)
    grad_down = contract_rows(active, grad_branch)
    grad_active = contract_cols(grad_branch, full_down)
    unused_gelu, gelu_back = jax.vjp(gelu_tanh, pre_act)
    grad_pre = gelu_back(grad_active)[0].astype(jnp.bfloat16)
    grad_bias_in = jnp.sum(grad_pre.astype(jnp.float32), 0)
    grad_in = contract_rows(mlp_low, grad_pre)
    grad_mlp_in = contract_cols(grad_pre, full_in).reshape(seqs_here, row_count, width)
    unused_second, second_back = jax.vjp(adapt, middle, gain_second, shift_mlp, scale_mlp)
    grad_middle_norm, grad_gain_mlp, grad_shift_mlp, grad_scale_mlp = second_back(grad_mlp_in)
    grad_middle = grad_result + grad_middle_norm
    grad_gate_attn = jnp.sum(grad_middle * projected, 1, keepdims=True)
    grad_proj = (gate_attn * grad_middle).astype(jnp.bfloat16).reshape(flat_rows, width)
    grad_attn_weight = contract_rows(attn_flat, grad_proj)
    grad_attn_rows = (
        contract_cols(grad_proj, gathered_output)
        .astype(jnp.bfloat16)
        .reshape(seqs_here, row_count, width)
    )
    grad_heads = lax.all_to_all(grad_attn_rows, "seq", split_axis=2, concat_axis=1, tiled=True)
    grad_head_parts = grad_heads.reshape(seqs_here, span, local_heads, HDIM)
    delta = jnp.transpose(jnp.sum(grad_head_parts.astype(jnp.float32) * attended, -1), (0, 2, 1))
    pieces = (
        lax.all_gather(keys, "fsdp", axis=1, tiled=True),
        lax.all_gather(values, "fsdp", axis=1, tiled=True),
    )
    logits, key_heads = score_block(pieces[0])
    piece_rows = pieces[1].shape[1]
    value_heads = pieces[1].reshape(seqs_here, piece_rows, local_heads, HDIM)
    probs = jnp.exp(logits - log_total[..., None])
    grad_weights = jnp.einsum(
        "sqhd,skhd->shqk", grad_head_parts, value_heads, preferred_element_type=jnp.float32
    )
    probs, grad_logits = (probs, (probs * (grad_weights - delta[..., None])).astype(jnp.bfloat16))
    grad_query = (
        jnp.einsum("shqk,skhd->sqhd", grad_logits, key_heads, preferred_element_type=jnp.float32)
        * scale
    )
    key_part = (
        jnp.einsum("shqk,sqhd->skhd", grad_logits, query_heads, preferred_element_type=jnp.float32)
        * scale
    )
    value_part = jnp.einsum(
        "shqk,sqhd->skhd",
        probs.astype(jnp.bfloat16),
        grad_head_parts,
        preferred_element_type=jnp.float32,
    )
    grad_key_all = key_part.reshape(seqs_here, piece_rows, local_heads * HDIM)
    grad_value_all = value_part.reshape(seqs_here, piece_rows, local_heads * HDIM)
    folded_rows = (grad_query, grad_key_all, grad_value_all)
    grad_query, grad_key_all, grad_value_all = folded_rows
    grad_keys, grad_values = (
        lax.psum_scatter(grad_key_all, "fsdp", scatter_dimension=1, tiled=True),
        lax.psum_scatter(grad_value_all, "fsdp", scatter_dimension=1, tiled=True),
    )
    grad_parts = (
        lax.all_to_all(
            grad_query.reshape(seqs_here, span, local_heads * HDIM).astype(jnp.bfloat16),
            "seq",
            split_axis=1,
            concat_axis=2,
            tiled=True,
        ),
        lax.all_to_all(
            grad_keys.astype(jnp.bfloat16), "seq", split_axis=1, concat_axis=2, tiled=True
        ),
        lax.all_to_all(
            grad_values.astype(jnp.bfloat16), "seq", split_axis=1, concat_axis=2, tiled=True
        ),
    )
    unused_turn, reverse_rotation = jax.vjp(turn_all, qkv)
    grad_qkv = (
        reverse_rotation(tuple((member.astype(jnp.float32) for member in grad_parts)))[0]
        .astype(jnp.bfloat16)
        .reshape(flat_rows, 3 * width)
    )
    grad_qkv_weight = contract_rows(attn_low, grad_qkv)
    grad_attn_in = contract_cols(grad_qkv, full_qkv).reshape(seqs_here, row_count, width)
    unused_first, first_back = jax.vjp(adapt, source, gain_first, shift_attn, scale_attn)
    grad_source_norm, grad_gain_attn, grad_shift_attn, grad_scale_attn = first_back(grad_attn_in)
    grad_hidden = grad_middle + grad_source_norm
    grad_mod = jnp.concatenate(
        [
            grad_shift_attn,
            grad_scale_attn,
            grad_gate_attn,
            grad_shift_mlp,
            grad_scale_mlp,
            grad_gate_mlp,
        ],
        -1,
    )[:, 0, :]
    grad_ada = jnp.dot(grad_mod.T, cond, precision=highest_precision)
    grad_bias_mod = jnp.sum(grad_mod, 0)
    summed = (
        lax.psum_scatter(grad_qkv_weight, "fsdp", scatter_dimension=0, tiled=True),
        lax.psum_scatter(grad_attn_weight, "fsdp", scatter_dimension=0, tiled=True),
        lax.psum_scatter(grad_in, "fsdp", scatter_dimension=0, tiled=True),
        lax.psum_scatter(grad_down, "fsdp", scatter_dimension=0, tiled=True),
        lax.psum_scatter(grad_ada, "fsdp", scatter_dimension=0, tiled=True),
        lax.psum_scatter(grad_bias_mod, "fsdp", scatter_dimension=0, tiled=True),
        lax.psum_scatter(grad_gain_attn, "fsdp", scatter_dimension=0, tiled=True),
        lax.psum_scatter(grad_gain_mlp, "fsdp", scatter_dimension=0, tiled=True),
        lax.psum_scatter(grad_bias_in, "fsdp", scatter_dimension=0, tiled=True),
        lax.psum_scatter(grad_bias_down, "fsdp", scatter_dimension=0, tiled=True),
    )
    totals = (
        lax.psum(summed[0].astype(jnp.bfloat16), "seq").astype(jnp.float32),
        lax.psum(summed[1].astype(jnp.bfloat16), "seq").astype(jnp.float32),
        lax.psum(summed[2].astype(jnp.bfloat16), "seq").astype(jnp.float32),
        lax.psum(summed[3].astype(jnp.bfloat16), "seq").astype(jnp.float32),
        lax.psum(summed[4].astype(jnp.bfloat16), "seq").astype(jnp.float32),
        lax.psum(summed[5].astype(jnp.bfloat16), "seq").astype(jnp.float32),
        lax.psum(summed[6].astype(jnp.bfloat16), "seq").astype(jnp.float32),
        lax.psum(summed[7].astype(jnp.bfloat16), "seq").astype(jnp.float32),
        lax.psum(summed[8].astype(jnp.bfloat16), "seq").astype(jnp.float32),
        lax.psum(summed[9].astype(jnp.bfloat16), "seq").astype(jnp.float32),
    )
    return (output, grad_hidden) + tuple(totals)


AXES = ("seq", "fsdp")
SEQ_BIT, HALF_BIT, LOW_BIT, ROW_BIT, CORE_BIT = 16, 8, 4, 2, 1
STREAM = ((ROW_BIT, SEQ_BIT), (LOW_BIT, ROW_BIT), (SEQ_BIT, LOW_BIT))
SHARED = ((LOW_BIT, LOW_BIT), (SEQ_BIT, SEQ_BIT), (ROW_BIT, ROW_BIT))
VMEM_LIMIT = 62 * 1024 * 1024


def swap_bits(values, even, odd=None):
    odd = even if odd is None else odd
    return lax.ppermute(values, AXES, [(i, i ^ (odd if i & 1 else even)) for i in range(32)])


def spread(values, order):
    for even, odd in order:
        values = jnp.concatenate([values, swap_bits(values, even, odd)], 0)
    return values


def collect(arrays, order):
    for even, odd in reversed(order):
        half = arrays[0].shape[0] // 2
        sent = jnp.concatenate([member[half:] for member in arrays], 1) if len(arrays) > 1 else arrays[0][half:]
        came = swap_bits(sent, even, odd)
        begin, summed = 0, []
        for member in arrays:
            part = came[:, begin : begin + member.shape[1]]
            begin += member.shape[1]
            summed.append((member[:half].astype(jnp.float32) + part.astype(jnp.float32)).astype(jnp.bfloat16))
        arrays = summed
    return arrays


def slot_masks(order, core):
    masks = [jnp.int32(0)]
    for even, odd in order:
        step = jnp.where(core == 0, even, odd).astype(jnp.int32)
        masks = masks + [mask ^ step for mask in masks]
    return jnp.stack(masks)


def quad_exchange(parts):
    came = swap_bits(parts[:, 1], ROW_BIT)
    parts = jnp.stack([parts[:, 0], came], 1)
    came = swap_bits(parts[1], LOW_BIT)
    return jnp.stack([parts[0], came], 0)


def after(values, *others):
    return lax.optimization_barrier((values,) + others)[0]


def pick(values, index, axis=0):
    return lax.dynamic_index_in_dim(values, index, axis, keepdims=False)


def pair_up(mine, other, position):
    return jnp.where(position == 0, jnp.stack([mine, other]), jnp.stack([other, mine]))


def dot_nn(left, right):
    return lax.dot_general(left, right, (((1,), (0,)), ((), ())), preferred_element_type=jnp.float32)


def row_norm(values):
    center = values - jnp.mean(values, -1, keepdims=True)
    return center * lax.rsqrt(jnp.mean(center * center, -1, keepdims=True) + 1e-05)


def head_select(width, head):
    lane = lax.broadcasted_iota(jnp.int32, (1, width), 1)
    return (lane % 128) // 32 == head


def order_weight_kernel(meta, pieces, chooser, out, gathered):
    rows = pieces.shape[0] // 16
    for slot in range(16):
        start = pl.multiple_of(meta[48 + slot] * rows, 16)
        gathered[pl.ds(start, rows), :] = pieces[slot * rows : (slot + 1) * rows, :]
    out[...] = dot_nn(gathered[...], chooser[...]).astype(jnp.bfloat16)


def project_kernel(meta, own_rows, other_rows, weight, vectors, cosine, sine, query_out, key_out, value_out, low):
    gain, scale, shift = vectors[0:1, :], vectors[1:2, :], vectors[2:3, :]
    span = own_rows.shape[0]

    def project(source, base):
        def body(i, carry):
            here = pl.multiple_of(i * 256, 256)
            rows = pl.ds(pl.multiple_of(base + i * 256, 256), 256)
            norm = row_norm(source[pl.ds(here, 256), :].astype(jnp.float32))
            attn_in = (norm * gain * scale + shift).astype(jnp.bfloat16)
            low[rows, :] = attn_in
            packed = dot_nn(attn_in, weight[:, 256:768])
            first, second = packed[:, 0:128], packed[:, 128:256]
            turn_c, turn_s = cosine[rows, :], sine[rows, :]
            key_out[rows, 0:128] = (first * turn_c - second * turn_s).astype(jnp.bfloat16)
            key_out[rows, 128:256] = (second * turn_c + first * turn_s).astype(jnp.bfloat16)
            value_out[rows, :] = packed[:, 256:512].astype(jnp.bfloat16)
            return carry

        lax.fori_loop(0, span // 256, body, 0)

    project(own_rows, 0)
    project(other_rows, span)
    block = span // 8
    stride = 1 + meta[64]
    for j in range(4):
        rows = pl.ds(pl.multiple_of(j * stride * block, 128), block)
        packed = dot_nn(low[rows, :], weight[:, 0:256]) * (HDIM ** (-0.5))
        first, second = packed[:, 0:128], packed[:, 128:256]
        turn_c, turn_s = cosine[rows, :], sine[rows, :]
        here = slice(j * block, (j + 1) * block)
        query_out[here, 0:128] = (first * turn_c - second * turn_s).astype(jnp.bfloat16)
        query_out[here, 128:256] = (second * turn_c + first * turn_s).astype(jnp.bfloat16)


def attend_kernel(meta, query_in, key_in, value_in, out_turned, log_out, out):
    block = query_in.shape[0] // 4
    keys = key_in[...]
    value_turned = value_in[...].T
    log_out[...] = jnp.zeros(log_out.shape, jnp.float32)
    out_turned[...] = jnp.zeros(out_turned.shape, jnp.float32)
    for head in range(3):
        for q_start in range(0, 4 * block, 256):
            here = slice(q_start, q_start + 256)
            query = query_in[here, :]
            query = jnp.where(head_select(256, head), query, jnp.zeros_like(query))
            scores = contract_cols(keys, query)
            best = jnp.max(scores, 0, keepdims=True)
            raised = jnp.exp(scores - best)
            total = jnp.sum(raised, 0, keepdims=True)
            mixed = dot_nn(value_turned[head * 64 : (head + 1) * 64, :], raised.astype(jnp.bfloat16))
            out_turned[head * 64 : (head + 1) * 64, here] = mixed / total
            log_out[head : head + 1, here] = best + jnp.log(total)
    turned_back = out_turned[...].T.astype(jnp.bfloat16)
    for j in range(4):
        out[j, :, :] = turned_back[j * block : (j + 1) * block, 0:192]


def attend_back_kernel(
    meta, cosine, sine, query_in, key_in, value_in, out_turned, log_in, grad_in, grad_packed, key_sum, value_sum
):
    block = query_in.shape[0] // 4
    stride = 1 + meta[64]
    keys, values = key_in[...], value_in[...]
    key_turned = keys.T
    lane_pad = jnp.zeros((4 * block, 64), jnp.bfloat16)
    grad_out = jnp.concatenate([jnp.concatenate([grad_in[j, :, :] for j in range(4)], 0), lane_pad], 1)
    grad_turned = grad_out.astype(jnp.float32).T
    key_sum[...] = jnp.zeros(key_sum.shape, jnp.float32)
    value_sum[...] = jnp.zeros(value_sum.shape, jnp.float32)
    product = grad_turned * out_turned[...]
    lane = lax.broadcasted_iota(jnp.int32, (1, 256), 1)
    query_parts = []
    for q_start in range(0, 4 * block, 256):
        here = slice(q_start, q_start + 256)
        query_sum = jnp.zeros((256, 256), jnp.float32)
        sub = lax.broadcasted_iota(jnp.int32, (256, 1), 0)
        for head in range(3):
            query = query_in[here, :]
            query = jnp.where(head_select(256, head), query, jnp.zeros_like(query))
            head_grad = grad_out[q_start : q_start + 256, :]
            head_grad = jnp.where(lane // 64 == head, head_grad, jnp.zeros_like(head_grad))
            probs = jnp.exp(contract_cols(keys, query) - log_in[head : head + 1, here])
            delta = jnp.sum(product[head * 64 : (head + 1) * 64, here], 0, keepdims=True)
            grad_scores = (probs * (contract_cols(values, head_grad) - delta)).astype(jnp.bfloat16)
            value_sum[...] += dot_nn(probs.astype(jnp.bfloat16), head_grad)
            key_sum[...] += dot_nn(grad_scores, query)
            part = dot_nn(key_turned, grad_scores)
            query_sum = jnp.where((sub % 128) // 32 == head, part, query_sum)
        query_parts.append(query_sum.T * (HDIM ** (-0.5)))
    for j in range(4):
        rows = pl.ds(pl.multiple_of(j * stride * block, 128), block)
        q_part = query_parts[(j * block) // 256][(j * block) % 256 : (j * block) % 256 + block, :]
        first, second = q_part[:, 0:128], q_part[:, 128:256]
        turn_c, turn_s = cosine[rows, :], sine[rows, :]
        here = slice(j * block, (j + 1) * block)
        grad_packed[here, 0:128] = (first * turn_c + second * turn_s).astype(jnp.bfloat16)
        grad_packed[here, 128:256] = (second * turn_c - first * turn_s).astype(jnp.bfloat16)


def project_back_kernel(
    meta, own_rows, other_rows, weight, chooser, vectors, cosine, sine, grad_packed, key_sum, value_sum,
    grad_rows, grad_weight, sums, low, low_queries, weight_sum
):
    gain, scale, shift = vectors[0:1, :], vectors[1:2, :], vectors[2:3, :]
    span = own_rows.shape[0]
    block = span // 8
    width = own_rows.shape[1]
    stride = 1 + meta[64]
    weight_sum[...] = jnp.zeros((width, 512), jnp.float32)
    shift_sum = jnp.zeros((1, width), jnp.float32)
    norm_sum = jnp.zeros((1, width), jnp.float32)
    query_back = contract_cols(grad_packed[...], weight[:, 0:256])
    for i in range(2 * span // 256):
        rows = slice(i * 256, (i + 1) * 256)
        source, start = (own_rows, i * 256) if i * 256 < span else (other_rows, i * 256 - span)
        norm = row_norm(source[start : start + 256, :].astype(jnp.float32))
        attn_in = (norm * gain * scale + shift).astype(jnp.bfloat16)
        low[rows, :] = attn_in
        first, second = key_sum[rows, 0:128], key_sum[rows, 128:256]
        turn_c, turn_s = cosine[rows, :], sine[rows, :]
        pair = jnp.concatenate(
            [first * turn_c + second * turn_s, second * turn_c - first * turn_s, value_sum[rows, :]], 1
        ).astype(jnp.bfloat16)
        back = contract_cols(pair, weight[:, 256:768])
        grad_rows[rows, :] = back.astype(jnp.bfloat16)
        shift_sum += jnp.sum(back, 0, keepdims=True)
        norm_sum += jnp.sum(back * norm, 0, keepdims=True)
        weight_sum[...] += contract_rows(attn_in, pair)
    for j in range(4):
        rows = pl.ds(pl.multiple_of(j * stride * block, 128), block)
        here = slice(j * block, (j + 1) * block)
        back = query_back[here, :]
        norm = row_norm(own_rows[rows, :].astype(jnp.float32))
        shift_sum += jnp.sum(back, 0, keepdims=True)
        norm_sum += jnp.sum(back * norm, 0, keepdims=True)
        grad_rows[rows, :] = (grad_rows[rows, :].astype(jnp.float32) + back).astype(jnp.bfloat16)
        low_queries[here, :] = low[rows, :]
    query_weight = contract_rows(low_queries[...], grad_packed[...])
    whole = jnp.concatenate([query_weight, weight_sum[...]], 1).astype(jnp.bfloat16)
    grad_weight[...] = contract_cols(whole, chooser[...]).astype(jnp.bfloat16)
    sums[...] = jnp.concatenate([shift_sum, norm_sum, jnp.zeros((6, width), jnp.float32)], 0)


def middle_kernel(
    meta, attended, part_a, part_b, other, own_rows, vectors, projected_out, middle_out, low_out, weight_out
):
    core = meta[64]
    mine = pl.multiple_of(core * 384, 128)
    theirs = pl.multiple_of(384 - core * 384, 128)
    for slot in range(16):
        rows_a = pl.ds(pl.multiple_of(meta[slot] * 48, 16), 48)
        rows_b = pl.ds(pl.multiple_of(meta[16 + slot] * 48, 16), 48)
        rows_p = pl.ds(pl.multiple_of(meta[32 + slot] * 48, 16), 48)
        weight_out[rows_a, pl.ds(mine, 256)] = part_a[slot, :, :]
        weight_out[rows_b, pl.ds(pl.multiple_of(mine + 256, 128), 128)] = part_b[slot, :, :]
        weight_out[rows_p, pl.ds(theirs, 256)] = other[slot, :, 0:256]
        weight_out[rows_b, pl.ds(pl.multiple_of(theirs + 256, 128), 128)] = other[slot, :, 256:384]
    projected = dot_nn(attended[...], weight_out[...])
    projected_out[...] = projected
    middle = own_rows[...].astype(jnp.float32) + vectors[3:4, :] * projected
    middle_out[...] = middle
    low_out[...] = (row_norm(middle) * vectors[4:5, :] * vectors[5:6, :] + vectors[6:7, :]).astype(jnp.bfloat16)


def mlp_kernel(
    meta, low_own, low_other, grad_own, grad_other, part_a, part_b, bias, branch_own, branch_other, back_own, back_other,
    grad_a, grad_b, grad_bias, weight_in, weight_down, grad_in, grad_down, branch, back
):
    for slot in range(16):
        for lane_start, size, part, index in ((0, 256, part_a, meta[slot]), (256, 128, part_b, meta[16 + slot])):
            rows = pl.ds(pl.multiple_of(index * 48, 16), 48)
            for i in range(4):
                lanes = slice(i * 384 + lane_start, i * 384 + lane_start + size)
                weight_in[rows, lanes] = part[slot, i * 48 : (i + 1) * 48, :]
            rows = pl.ds(pl.multiple_of(index * 96, 16), 96)
            for i in range(2):
                lanes = slice(i * 384 + lane_start, i * 384 + lane_start + size)
                weight_down[rows, lanes] = part[slot, 192 + i * 96 : 192 + (i + 1) * 96, :]
    low = jnp.concatenate([low_own[...], low_other[...]], 0)
    grad = jnp.concatenate([grad_own[...], grad_other[...]], 0)
    tokens = low_own.shape[0]
    branch[...] = jnp.zeros(branch.shape, jnp.float32)
    back[...] = jnp.zeros(back.shape, jnp.float32)
    root, cubic = math.sqrt(2.0 / math.pi), 0.044715
    for i in range(4):
        hidden = slice(i * 384, (i + 1) * 384)
        pre_act = dot_nn(low, weight_in[:, hidden]) + bias[:, hidden]
        square = pre_act * pre_act
        bend = jnp.tanh(root * (pre_act + cubic * square * pre_act))
        active = (0.5 * pre_act * (1.0 + bend)).astype(jnp.bfloat16)
        slope = 0.5 * (1.0 + bend) + 0.5 * pre_act * (1.0 - bend * bend) * (root * (1.0 + 3.0 * cubic * square))
        branch[...] += dot_nn(active, weight_down[hidden, :])
        grad_pre = (contract_cols(grad, weight_down[hidden, :]) * slope).astype(jnp.bfloat16)
        grad_bias[:, hidden] = jnp.sum(grad_pre.astype(jnp.float32), 0, keepdims=True)
        back[...] += contract_cols(grad_pre, weight_in[:, hidden])
        grad_in[:, hidden] = contract_rows(low, grad_pre).astype(jnp.bfloat16)
        grad_down[hidden, :] = contract_rows(active, grad).astype(jnp.bfloat16)
    branch_own[...] = branch[:tokens, :]
    branch_other[...] = branch[tokens:, :]
    back_own[...] = back[:tokens, :]
    back_other[...] = back[tokens:, :]
    for slot in range(16):
        for lane_start, size, part, index in ((0, 256, grad_a, meta[slot]), (256, 128, grad_b, meta[16 + slot])):
            rows = pl.ds(pl.multiple_of(index * 48, 16), 48)
            for i in range(4):
                lanes = slice(i * 384 + lane_start, i * 384 + lane_start + size)
                part[slot, i * 48 : (i + 1) * 48, :] = grad_in[rows, lanes]
            rows = pl.ds(pl.multiple_of(index * 96, 16), 96)
            for i in range(2):
                lanes = slice(i * 384 + lane_start, i * 384 + lane_start + size)
                part[slot, 192 + i * 96 : 192 + (i + 1) * 96, :] = grad_down[rows, lanes]


def turn_kernel(
    meta, branch_own, branch_other, back_own, back_other, bias, middle_in, projected_in, cotangent, grad_branch, weight,
    attended, vectors, output, grad_middle_out, grad_attn_out, grad_weight, sums
):
    width = middle_in.shape[1]
    branch = branch_own[...] + branch_other[...] + bias[...]
    middle = middle_in[...]
    grad = cotangent[...].astype(jnp.float32)
    output[...] = (middle + vectors[7:8, :] * branch).astype(jnp.bfloat16)
    back = back_own[...] + back_other[...]
    center = middle - jnp.mean(middle, -1, keepdims=True)
    inverse = lax.rsqrt(jnp.mean(center * center, -1, keepdims=True) + 1e-05)
    norm = center * inverse
    scaled = back * vectors[5:6, :] * vectors[4:5, :]
    grad_middle = grad + inverse * (
        scaled - jnp.mean(scaled, -1, keepdims=True) - norm * jnp.mean(scaled * norm, -1, keepdims=True)
    )
    grad_middle_out[...] = grad_middle
    grad_proj = (vectors[3:4, :] * grad_middle).astype(jnp.bfloat16)
    grad_attn_out[...] = contract_cols(grad_proj, weight[...]).astype(jnp.bfloat16)
    grad_weight[...] = contract_rows(attended[...], grad_proj).astype(jnp.bfloat16)
    def total(values):
        return jnp.sum(values, 0, keepdims=True)

    sums[...] = jnp.concatenate(
        [
            total(grad_middle * projected_in[...]),
            total(back),
            total(back * norm),
            total(grad * branch),
            total(grad_branch[...].astype(jnp.float32)),
            jnp.zeros((3, width), jnp.float32),
        ],
        0,
    )


def call(body, outs, args, scratch=(), flops=0, moved=0):
    whole = pl.BlockSpec(memory_space=pltpu.VMEM)
    in_specs = [pl.BlockSpec(memory_space=pltpu.SMEM)] + [whole] * (len(args) - 1)
    return pl.pallas_call(
        body,
        out_shape=[jax.ShapeDtypeStruct(*member) for member in outs],
        in_specs=in_specs,
        out_specs=[whole] * len(outs),
        scratch_shapes=[pltpu.VMEM(*member) for member in scratch],
        compiler_params=pltpu.CompilerParams(vmem_limit_bytes=VMEM_LIMIT),
        cost_estimate=pl.CostEstimate(flops=flops, bytes_accessed=moved, transcendentals=0),
    )(*args)


def cube_local(
    hidden_in, time_index, cotangent, w_qkv, w_attn_out, w_mlp_in, w_mlp_out, w_ada, bias_ada, gain_attn, gain_mlp,
    bias_mlp_in, bias_mlp_out
):
    f32, bf16 = jnp.float32, jnp.bfloat16
    rows, width = hidden_in.shape[1:]
    tokens = 2 * rows
    place = lax.axis_index("fsdp")
    side = lax.axis_index("seq")
    device = side * 16 + place
    core, half, group = place & 1, place >> 3, (place >> 1) & 3
    x_own = jnp.concatenate(
        [pick(hidden_in, half), swap_bits(pick(hidden_in, 1 - half), HALF_BIT)], 0
    )
    both_qkv = jnp.stack([w_qkv, swap_bits(w_qkv, HALF_BIT)])
    x_kept, w_mlp_in, w_attn_out, w_mlp_out, w_ada = lax.optimization_barrier(
        (x_own, w_mlp_in, w_attn_out, w_mlp_out, w_ada)
    )
    x_one = spread(x_own, STREAM[:1])
    cond = jax.nn.silu(time_features(time_index, w_ada.shape[1]))
    modulation = jnp.dot(cond, w_ada.astype(f32).T, precision=highest_precision) + bias_ada.astype(f32)
    vector = jnp.concatenate(
        [modulation.reshape(-1)]
        + [member.astype(f32) for member in (gain_attn, gain_mlp, bias_mlp_in, bias_mlp_out)]
    )[None]
    in_columns = w_mlp_in.reshape(48, 8, 2, 192)

    def in_blocks(columns):
        return columns.reshape(48, 4, 384).transpose(1, 0, 2).reshape(192, 384)

    own_share = jnp.concatenate(
        [in_blocks(pick(in_columns, core, 2)), pick(w_attn_out.reshape(48, 2, 384), core, 1)], 0
    )
    sent_share = jnp.concatenate(
        [in_blocks(pick(in_columns, 1 - core, 2)), pick(w_attn_out.reshape(48, 2, 384), 1 - core, 1)], 0
    )
    down_share = pick(w_mlp_out.reshape(2, 96, 2, 384), side).transpose(1, 0, 2).reshape(192, 384)
    share = jnp.where(core == side, own_share, swap_bits(sent_share, CORE_BIT))
    share = jnp.concatenate([share[:192], down_share, share[192:]], 0)
    share = jnp.stack([share, swap_bits(share, HALF_BIT)])[None]
    place_kept, x_one_kept = lax.optimization_barrier((place, x_one))
    x_two = spread(x_one, STREAM[1:2])
    x_a = spread(x_two, STREAM[2:])
    x_b = swap_bits(x_a, CORE_BIT)
    vector = jnp.concatenate([vector, swap_bits(vector, CORE_BIT)], 0)
    vector = after(vector, x_two)
    for bit in (ROW_BIT, LOW_BIT, HALF_BIT):
        vector = jnp.concatenate([vector, swap_bits(vector, bit)], 0)
    vector = vector[place ^ jnp.arange(16)]
    parts, begin = [], 0
    for size in (288, 288, 48, 48, 192, 48):
        parts.append(vector[:, begin : begin + size])
        begin += size
    modulation = jnp.stack([parts[0].reshape(6, width), parts[1].reshape(6, width)])
    shift_attn, scale_attn, gate_attn, shift_mlp, scale_mlp, gate_mlp = [
        row for row in pick(modulation, half)
    ]
    full_gain_attn, full_gain_mlp = parts[2].reshape(-1), parts[3].reshape(-1)
    bias_in = pick(parts[4].reshape(8, 2, 192), core, 1).reshape(1, -1)
    bias_down = parts[5].reshape(1, -1)
    vectors = jnp.stack(
        [full_gain_attn, 1.0 + scale_attn, shift_attn, gate_attn, full_gain_mlp, 1.0 + scale_mlp, shift_mlp, gate_mlp]
    )
    place = place_kept
    device, core = side * 16 + place, place & 1
    stream_own, stream_other = slot_masks(STREAM, core), slot_masks(STREAM, 1 - core)
    shared = slot_masks(SHARED, core)

    def weight_slots(masks):
        moved = ((masks & 6) | (masks >> 4))[:, None] ^ jnp.array([0, 8], jnp.int32)[None]
        return (((place & 14) + side) ^ moved).reshape(-1)

    quad = jnp.array([0, ROW_BIT, LOW_BIT, LOW_BIT | ROW_BIT], jnp.int32)
    oct_masks = (quad[:, None] ^ jnp.array([0, HALF_BIT], jnp.int32)).reshape(-1)
    row_slots = place ^ jnp.concatenate([oct_masks, oct_masks ^ CORE_BIT])
    meta = jnp.concatenate(
        [weight_slots(stream_own), weight_slots(shared), weight_slots(stream_other), row_slots, core[None]]
    ).astype(jnp.int32)
    blocks = jnp.concatenate([device ^ stream_own, device ^ CORE_BIT ^ stream_other])
    blocks = jnp.stack([blocks, blocks ^ HALF_BIT], 1)
    positions = (blocks[:, :, None] * rows + jnp.arange(rows, dtype=jnp.int32)).reshape(-1)
    inverse = jnp.exp(-math.log(10000.0) * jnp.arange(0, HDIM, 2, dtype=f32) / HDIM)
    angles = positions.astype(f32)[:, None] * inverse[None, :]
    cosine, sine = jnp.tile(jnp.cos(angles), (1, 4)), jnp.tile(jnp.sin(angles), (1, 4))
    lane = jnp.arange(768)
    inner = lane % 128
    wanted = jnp.where(
        lane < 512,
        jnp.where(inner < 96, (lane // 256) * 192 + (inner // 32) * 64 + ((lane % 256) // 128) * 32 + inner % 32, -1),
        jnp.where(lane < 704, lane - 128, -1),
    )
    chooser = (jnp.arange(576)[:, None] == wanted[None, :]).astype(bf16)
    grouped = both_qkv.reshape(96, 3, 4, 192).transpose(2, 0, 1, 3).reshape(4, 96, 576)
    grouped = grouped[group ^ jnp.arange(4)].reshape(2, 2, 96, 576)
    grouped = quad_exchange(grouped).reshape(8, 48, 576)
    grouped = jnp.concatenate([grouped, swap_bits(grouped, CORE_BIT)], 0).reshape(768, 576)
    share = after(share, grouped)
    part_a, part_b = spread(share[..., :256], STREAM[:1]), spread(share[..., 256:], SHARED[:1])
    (weight_qkv,) = call(
        order_weight_kernel,
        [((768, 768), bf16)],
        [meta, grouped, chooser],
        [((768, 576), bf16)],
        flops=2 * 768 * 768 * 576,
        moved=3_000_000,
    )
    span = 16 * tokens
    x_last, part_a, part_b = lax.optimization_barrier((x_b, part_a, part_b))
    part_a, part_b = spread(part_a, STREAM[1:2]), spread(part_b, SHARED[1:2])
    queries, keys, values = call(
        project_kernel,
        [((4 * tokens, 256), bf16), ((span, 256), bf16), ((span, 256), bf16)],
        [meta, x_a, x_last, weight_qkv, vectors, cosine, sine],
        [((span, width), bf16)],
        flops=2_000_000_000,
        moved=8_000_000,
    )
    keys, part_a, part_b = lax.optimization_barrier((keys, part_a, part_b))
    part_a, part_b = spread(part_a, STREAM[2:]), spread(part_b, SHARED[2:])
    out_turned, log_total, heads_out = call(
        attend_kernel,
        [((256, 4 * tokens), f32), ((8, 4 * tokens), f32), ((4, tokens, 192), bf16)],
        [meta, queries, keys, values],
        flops=8_000_000_000,
        moved=4_000_000,
    )
    part_a, part_b = part_a.reshape(16, 432, 256), part_b.reshape(16, 432, 128)
    out_share = jnp.concatenate([part_a[:, 384:], part_b[:, 384:]], 2)
    other_out = swap_bits(out_share, CORE_BIT)
    by_group = quad_exchange(heads_out.reshape(2, 2, tokens, 192)).reshape(4, tokens, 192)
    attended = by_group[group ^ jnp.arange(4)].transpose(1, 0, 2).reshape(tokens, width)
    projected, middle, mlp_own, weight_out = call(
        middle_kernel,
        [((tokens, width), f32), ((tokens, width), f32), ((tokens, width), bf16), ((768, 768), bf16)],
        [meta, attended, part_a[:, 384:], part_b[:, 384:], other_out, x_kept, vectors],
        flops=150_000_000,
        moved=3_000_000,
    )
    grad_own = jnp.concatenate(
        [pick(cotangent, half), swap_bits(pick(cotangent, 1 - half), HALF_BIT)], 0
    )
    branch_grad = (gate_mlp[None] * grad_own.astype(f32)).astype(bf16)
    branch_grad_other = swap_bits(branch_grad, CORE_BIT)
    mlp_other = swap_bits(mlp_own, CORE_BIT)
    branch_own, branch_sent, back_own, back_sent, grad_a, grad_b, grad_bias_in = call(
        mlp_kernel,
        [((tokens, width), f32)] * 4
        + [((16, 384, 256), bf16), ((16, 384, 128), bf16), ((1, 1536), f32)],
        [meta, mlp_own, mlp_other, branch_grad, branch_grad_other, part_a, part_b, bias_in],
        [((768, 1536), bf16), ((1536, 768), bf16), ((768, 1536), bf16), ((1536, 768), bf16)]
        + [((2 * tokens, width), f32)] * 2,
        flops=3_600_000_000,
        moved=12_000_000,
    )
    came = swap_bits(jnp.stack([branch_sent, back_sent]), CORE_BIT)
    sum_a = collect([grad_a.reshape(8, 768, 256)], STREAM[2:])[0]
    sum_b = collect([grad_b.reshape(8, 768, 128)], SHARED[2:])[0]
    output_rows, grad_middle, grad_attn, grad_w_out, sums_mlp = call(
        turn_kernel,
        [((tokens, width), bf16), ((tokens, width), f32), ((tokens, width), bf16), ((768, 768), bf16), ((8, width), f32)],
        [meta, branch_own, came[0], back_own, came[1], bias_down, middle, projected, grad_own, branch_grad, weight_out]
        + [attended, vectors],
        flops=300_000_000,
        moved=5_000_000,
    )

    def plus(left, right):
        return (left.astype(f32) + right.astype(f32)).astype(bf16)

    grad_heads = grad_attn.reshape(tokens, 4, 192).transpose(1, 0, 2)[group ^ jnp.arange(4)]
    grad_heads = quad_exchange(grad_heads.reshape(2, 2, tokens, 192)).reshape(4, tokens, 192)
    by_core = grad_w_out.reshape(8, 2, 48, width)
    sum_out = plus(pick(by_core, core, 1), swap_bits(pick(by_core, 1 - core, 1), CORE_BIT))
    output = pair_up(output_rows[:rows], swap_bits(output_rows[rows:], HALF_BIT), half)
    grad_heads, sum_a, sum_b, sum_out, output = lax.optimization_barrier((grad_heads, sum_a, sum_b, sum_out, output))
    sum_a = collect([sum_a], STREAM[1:2])[0]
    sum_b = collect([sum_b], SHARED[1:2])[0]
    by_side = sum_out.reshape(8, 2, 24, width)
    sum_out = plus(pick(by_side, side, 1), swap_bits(pick(by_side, 1 - side, 1), SEQ_BIT))
    grad_packed, key_sum, value_sum = call(
        attend_back_kernel,
        [((4 * tokens, 256), bf16), ((span, 256), f32), ((span, 256), f32)],
        [meta, cosine, sine, queries, keys, values, out_turned, log_total, grad_heads],
        flops=14_000_000_000,
        moved=8_000_000,
    )
    key_sum, sum_a, sum_b, sum_out = lax.optimization_barrier((key_sum, sum_a, sum_b, sum_out))
    sum_a = collect([sum_a], STREAM[:1])[0]
    sum_b = collect([sum_b], SHARED[:1])[0]
    by_half = sum_out.reshape(2, 4, 24, width)
    sum_out = plus(pick(by_half, half), swap_bits(pick(by_half, 1 - half), HALF_BIT))
    grad_rows, grad_qkv, sums_attn = call(
        project_back_kernel,
        [((span, width), bf16), ((768, 576), bf16), ((8, width), f32)],
        [meta, x_a, x_b, weight_qkv, chooser, vectors, cosine, sine, grad_packed, key_sum, value_sum],
        [((span, width), bf16), ((4 * tokens, width), bf16), ((width, 512), f32)],
        flops=6_000_000_000,
        moved=16_000_000,
    )
    grad_rows, grad_qkv, sums_attn, sum_a, sum_b, sum_out = lax.optimization_barrier(
        (grad_rows, grad_qkv, sums_attn, sum_a, sum_b, sum_out)
    )
    grad_rows = grad_rows.reshape(2, 8, tokens, width)
    came_rows = swap_bits(grad_rows[1], CORE_BIT)
    came_rows, grad_qkv = lax.optimization_barrier((came_rows, grad_qkv))
    small = jnp.concatenate([sums_attn[0:2], sums_mlp[0:5]], 0)
    own_sum = plus(grad_rows[0], came_rows)
    (own_sum,) = collect([own_sum], STREAM[2:])
    total = jnp.concatenate([sum_a.reshape(2, 384, 256), sum_b.reshape(2, 384, 128)], 2)
    total = plus(total[0], swap_bits(total[1], HALF_BIT))
    by_core = grad_qkv.reshape(8, 2, 48, 576)
    kept = plus(pick(by_core, core, 1), swap_bits(pick(by_core, 1 - core, 1), CORE_BIT))
    own_sum, total, kept = lax.optimization_barrier((own_sum, total, kept))
    (own_sum,) = collect([own_sum], STREAM[1:2])
    across = swap_bits(total, SEQ_BIT)
    by_side = kept.reshape(8, 2, 24, 576)
    kept = plus(pick(by_side, side, 1), swap_bits(pick(by_side, 1 - side, 1), SEQ_BIT))
    own_sum, across, kept, small = lax.optimization_barrier((own_sum, across, kept, small))
    (own_sum,) = collect([own_sum], STREAM[:1])
    grad_in = own_sum[0].astype(f32)
    source = x_kept.astype(f32)
    center = source - jnp.mean(source, -1, keepdims=True)
    inverse = lax.rsqrt(jnp.mean(center * center, -1, keepdims=True) + 1e-05)
    norm = center * inverse
    scaled = grad_in * vectors[1:2] * vectors[0:1]
    grad_hidden = grad_middle + inverse * (
        scaled - jnp.mean(scaled, -1, keepdims=True) - norm * jnp.mean(scaled * norm, -1, keepdims=True)
    )
    grad_hidden = pair_up(
        grad_hidden[:rows], swap_bits(grad_hidden[rows:].astype(bf16), HALF_BIT).astype(f32), half
    )

    grad_down = pair_up(total[192:], across[192:], side).reshape(2, 2, 96, 384)
    grad_down = grad_down.transpose(0, 2, 1, 3).reshape(192, 768).astype(f32)
    mine = jnp.where(core == side, total[:192], across[:192])
    theirs = swap_bits(jnp.where(core == side, across[:192], total[:192]), CORE_BIT)

    def in_columns_back(blocks):
        return blocks.reshape(4, 48, 384).transpose(1, 0, 2).reshape(48, 8, 192)

    grad_w_in = pair_up(in_columns_back(mine), in_columns_back(theirs), core)
    grad_w_in = grad_w_in.transpose(1, 2, 0, 3).reshape(48, 3072).astype(f32)
    by_half = kept.reshape(2, 4, 24, 576)
    kept = plus(pick(by_half, half), swap_bits(pick(by_half, 1 - half), HALF_BIT))
    kept = kept[group ^ jnp.arange(4)].reshape(2, 2, 24, 576)
    sum_out = sum_out[group ^ jnp.arange(4)].reshape(2, 2, 24, width)
    came = swap_bits(jnp.concatenate([kept[:, 1], sum_out[:, 1]], 2), ROW_BIT)
    sum_out = plus(sum_out[:, 0], came[:, :, 576:])
    near, far = [kept[0, 0], came[0, :, :576]], [kept[1, 0], came[1, :, :576]]
    came = swap_bits(jnp.concatenate(far + [sum_out[1]], 1), LOW_BIT)
    sum_out = plus(sum_out[0], came[:, 1152:])
    kept = jnp.stack(near + [came[:, :576], came[:, 576:1152]])
    kept = kept[group ^ jnp.arange(4)].reshape(4, 24, 3, 192).transpose(1, 2, 0, 3).reshape(24, 2304)
    kept = jnp.concatenate([kept, sum_out], 1)
    kept = pair_up(kept, swap_bits(kept, SEQ_BIT), side).reshape(48, 3072).astype(f32)
    grad_w_qkv, grad_w_out = kept[:, :2304], kept[:, 2304:]
    small = small + swap_bits(small, CORE_BIT)
    small = jnp.concatenate([small, grad_bias_in.reshape(2, width)], 0)
    for bit in (ROW_BIT, LOW_BIT, SEQ_BIT):
        small = small + swap_bits(small, bit)
    both = pair_up(small, swap_bits(small, HALF_BIT), half)
    plus_scale = 1.0 + modulation[:, 1], 1.0 + modulation[:, 4]
    grad_mod = jnp.stack(
        [both[:, 0], both[:, 1] * full_gain_attn, both[:, 2], both[:, 3], both[:, 4] * full_gain_mlp, both[:, 5]], 1
    ).reshape(2, 16, 288)
    grad_mod = pick(grad_mod, place, 1)
    grad_ada = grad_mod[0][:, None] * cond[0][None] + grad_mod[1][:, None] * cond[1][None]
    gain_first = pick(jnp.sum(both[:, 1] * plus_scale[0], 0).reshape(16, 48), place)
    gain_second = pick(jnp.sum(both[:, 4] * plus_scale[1], 0).reshape(16, 48), place)
    summed = both[0] + both[1]
    bias_in_grad = pick(summed[7:9].reshape(8, 192), place >> 1)
    bias_down_grad = pick(summed[6].reshape(16, 48), place)
    return (
        output,
        grad_hidden,
        grad_w_qkv,
        grad_w_out,
        grad_w_in,
        grad_down,
        grad_ada,
        jnp.sum(grad_mod, 0),
        gain_first,
        gain_second,
        bias_in_grad,
        bias_down_grad,
    )


def solution(mesh):
    return jax.shard_map(
        cube_local if dict(mesh.shape) == {"seq": 2, "fsdp": 16} else local,
        mesh=mesh,
        in_specs=(
            P(None, ("seq", "fsdp"), None),
            P(),
            P(None, ("seq", "fsdp"), None),
            P("fsdp", None),
            P("fsdp", None),
            P("fsdp", None),
            P("fsdp", None),
            P("fsdp", None),
            P("fsdp"),
            P("fsdp"),
            P("fsdp"),
            P("fsdp"),
            P("fsdp"),
        ),
        out_specs=(
            P(None, ("seq", "fsdp"), None),
            P(None, ("seq", "fsdp"), None),
            P("fsdp", None),
            P("fsdp", None),
            P("fsdp", None),
            P("fsdp", None),
            P("fsdp", None),
            P("fsdp"),
            P("fsdp"),
            P("fsdp"),
            P("fsdp"),
            P("fsdp"),
        ),
        check_vma=False,
    )
```

```python
import math

import jax
import jax.numpy as jnp
from jax import lax
from jax.experimental import pallas as pl
from jax.experimental.pallas import tpu as pltpu
from jax.sharding import PartitionSpec as P

HEADS = 12
HDIM = 64


highest_precision = lax.Precision.HIGHEST


def normalize(values):
    center = values - jnp.mean(values, -1, keepdims=True)
    return center * lax.rsqrt(jnp.mean(center * center, -1, keepdims=True) + 1e-05)


def adapt(values, gain, shift, scale):
    return normalize(values) * gain * (1.0 + scale) + shift


def time_features(time_index, width):
    half_width = width // 2
    frequency = jnp.exp(-math.log(10000.0) * jnp.arange(half_width, dtype=jnp.float32) / half_width)
    angles = time_index.astype(jnp.float32)[:, None] * frequency[None, :]
    return jnp.concatenate([jnp.cos(angles), jnp.sin(angles)], -1)


def rotary_tables(positions, head_dim):
    inverse = jnp.exp(-math.log(10000.0) * jnp.arange(0, head_dim, 2, dtype=jnp.float32) / head_dim)
    angles = positions.astype(jnp.float32)[:, None] * inverse[None, :]
    angles = jnp.concatenate([angles, angles], -1)
    return (jnp.cos(angles), jnp.sin(angles))


def rotate(values, cosine, sine):
    first_half, second_half = jnp.split(values, 2, axis=-1)
    turned = jnp.concatenate([-second_half, first_half], -1)
    return values * cosine[:, None, :] + turned * sine[:, None, :]


def contract_rows(left_neighbor, right_neighbor):
    return lax.dot_general(
        left_neighbor, right_neighbor, (((0,), (0,)), ((), ())), preferred_element_type=jnp.float32
    )


def contract_cols(left_neighbor, right_neighbor):
    return lax.dot_general(
        left_neighbor, right_neighbor, (((1,), (1,)), ((), ())), preferred_element_type=jnp.float32
    )


def gelu_tanh(values):
    return jax.nn.gelu(values, approximate=True)


def local(
    hidden_in,
    time_index,
    cotangent,
    w_qkv,
    w_attn_out,
    w_mlp_in,
    w_mlp_out,
    w_ada,
    bias_ada,
    gain_attn,
    gain_mlp,
    bias_mlp_in,
    bias_mlp_out,
):
    seqs_here, row_count, width = hidden_in.shape
    flat_rows = seqs_here * row_count
    gathered = (
        lax.all_gather(w_qkv, "fsdp", axis=0, tiled=True),
        lax.all_gather(w_attn_out, "fsdp", axis=0, tiled=True),
        lax.all_gather(w_mlp_in, "fsdp", axis=0, tiled=True),
        lax.all_gather(w_mlp_out, "fsdp", axis=0, tiled=True),
        lax.all_gather(w_ada, "fsdp", axis=0, tiled=True),
        lax.all_gather(bias_ada, "fsdp", axis=0, tiled=True),
        lax.all_gather(gain_attn, "fsdp", axis=0, tiled=True),
        lax.all_gather(gain_mlp, "fsdp", axis=0, tiled=True),
        lax.all_gather(bias_mlp_in, "fsdp", axis=0, tiled=True),
        lax.all_gather(bias_mlp_out, "fsdp", axis=0, tiled=True),
    )
    (
        full_qkv,
        gathered_output,
        full_in,
        full_down,
        full_ada,
        full_bias_ada,
        full_gain_attn,
        full_gain_mlp,
        full_bias_in,
        full_bias_down,
    ) = gathered
    gain_first = full_gain_attn.astype(jnp.float32)
    gain_second = full_gain_mlp.astype(jnp.float32)
    cond = jax.nn.silu(time_features(time_index, full_ada.shape[1]))
    modulation = jnp.dot(
        cond, full_ada.astype(jnp.float32).T, precision=highest_precision
    ) + full_bias_ada.astype(jnp.float32)
    shift_attn, scale_attn, gate_attn, shift_mlp, scale_mlp, gate_mlp = jnp.split(
        modulation[:, None, :], 6, axis=-1
    )
    source = hidden_in.astype(jnp.float32)
    attn_in = adapt(source, gain_first, shift_attn, scale_attn)
    attn_low = attn_in.astype(jnp.bfloat16).reshape(flat_rows, width)
    qkv = jnp.dot(attn_low, full_qkv, preferred_element_type=jnp.float32).reshape(
        seqs_here, row_count, 3 * width
    )
    device_number = lax.axis_index("seq") * lax.axis_size("fsdp") + lax.axis_index("fsdp")
    positions = device_number * row_count + jnp.arange(row_count, dtype=jnp.int32)
    cosine, sine = rotary_tables(positions, HDIM)

    def turn_all(packed):
        split_three = packed.reshape(seqs_here, row_count, 3, HEADS, HDIM)
        query_turned = rotate(split_three[:, :, 0], cosine, sine).reshape(
            seqs_here, row_count, width
        )
        key_turned = rotate(split_three[:, :, 1], cosine, sine).reshape(seqs_here, row_count, width)
        return (query_turned, key_turned, split_three[:, :, 2].reshape(seqs_here, row_count, width))

    query_rot, key_rot, value_raw = turn_all(qkv)
    queries, keys, values = (
        lax.all_to_all(
            query_rot.astype(jnp.bfloat16), "seq", split_axis=2, concat_axis=1, tiled=True
        ),
        lax.all_to_all(
            key_rot.astype(jnp.bfloat16), "seq", split_axis=2, concat_axis=1, tiled=True
        ),
        lax.all_to_all(
            value_raw.astype(jnp.bfloat16), "seq", split_axis=2, concat_axis=1, tiled=True
        ),
    )
    local_heads = HEADS // lax.axis_size("seq")
    span = queries.shape[1]
    query_heads = queries.reshape(seqs_here, span, local_heads, HDIM)
    scale = HDIM ** (-0.5)

    def score_block(key_piece):
        key_heads = key_piece.reshape(seqs_here, key_piece.shape[1], local_heads, HDIM)
        logits = (
            jnp.einsum(
                "sqhd,skhd->shqk", query_heads, key_heads, preferred_element_type=jnp.float32
            )
            * scale
        )
        return (logits, key_heads)

    pieces = (
        lax.all_gather(keys, "fsdp", axis=1, tiled=True),
        lax.all_gather(values, "fsdp", axis=1, tiled=True),
    )
    best = jnp.full((seqs_here, local_heads, span), -1e30, jnp.float32)
    logits, unused = score_block(pieces[0])
    value_heads = pieces[1].reshape(seqs_here, pieces[1].shape[1], local_heads, HDIM)
    newest = jnp.maximum(best, jnp.max(logits, -1))
    raised = jnp.exp(logits - newest[..., None])
    total = jnp.sum(raised, -1)
    accum = jnp.einsum(
        "shqk,skhd->sqhd",
        raised.astype(jnp.bfloat16),
        value_heads,
        preferred_element_type=jnp.float32,
    )
    best, total, accum = (newest, total, accum)
    log_total = best + jnp.log(total)
    attended = accum / jnp.transpose(total, (0, 2, 1))[..., None]
    attended_low = attended.reshape(seqs_here, span, local_heads * HDIM).astype(jnp.bfloat16)
    attn_rows = lax.all_to_all(attended_low, "seq", split_axis=1, concat_axis=2, tiled=True)
    attn_flat = attn_rows.reshape(flat_rows, width)
    projected = jnp.dot(attn_flat, gathered_output, preferred_element_type=jnp.float32).reshape(
        seqs_here, row_count, width
    )
    middle = source + gate_attn * projected
    mlp_in = adapt(middle, gain_second, shift_mlp, scale_mlp)
    mlp_low = mlp_in.astype(jnp.bfloat16).reshape(flat_rows, width)
    pre_act = jnp.dot(mlp_low, full_in, preferred_element_type=jnp.float32) + full_bias_in.astype(
        jnp.float32
    )
    active = gelu_tanh(pre_act).astype(jnp.bfloat16)
    branch = (
        jnp.dot(active, full_down, preferred_element_type=jnp.float32)
        + full_bias_down.astype(jnp.float32)
    ).reshape(seqs_here, row_count, width)
    output = (middle + gate_mlp * branch).astype(jnp.bfloat16)
    grad_result = cotangent.astype(jnp.float32)
    grad_gate_mlp = jnp.sum(grad_result * branch, 1, keepdims=True)
    grad_branch = (gate_mlp * grad_result).astype(jnp.bfloat16).reshape(flat_rows, width)
    grad_bias_down = jnp.sum(grad_branch.astype(jnp.float32), 0)
    grad_down = contract_rows(active, grad_branch)
    grad_active = contract_cols(grad_branch, full_down)
    unused_gelu, gelu_back = jax.vjp(gelu_tanh, pre_act)
    grad_pre = gelu_back(grad_active)[0].astype(jnp.bfloat16)
    grad_bias_in = jnp.sum(grad_pre.astype(jnp.float32), 0)
    grad_in = contract_rows(mlp_low, grad_pre)
    grad_mlp_in = contract_cols(grad_pre, full_in).reshape(seqs_here, row_count, width)
    unused_second, second_back = jax.vjp(adapt, middle, gain_second, shift_mlp, scale_mlp)
    grad_middle_norm, grad_gain_mlp, grad_shift_mlp, grad_scale_mlp = second_back(grad_mlp_in)
    grad_middle = grad_result + grad_middle_norm
    grad_gate_attn = jnp.sum(grad_middle * projected, 1, keepdims=True)
    grad_proj = (gate_attn * grad_middle).astype(jnp.bfloat16).reshape(flat_rows, width)
    grad_attn_weight = contract_rows(attn_flat, grad_proj)
    grad_attn_rows = (
        contract_cols(grad_proj, gathered_output)
        .astype(jnp.bfloat16)
        .reshape(seqs_here, row_count, width)
    )
    grad_heads = lax.all_to_all(grad_attn_rows, "seq", split_axis=2, concat_axis=1, tiled=True)
    grad_head_parts = grad_heads.reshape(seqs_here, span, local_heads, HDIM)
    delta = jnp.transpose(jnp.sum(grad_head_parts.astype(jnp.float32) * attended, -1), (0, 2, 1))
    pieces = (
        lax.all_gather(keys, "fsdp", axis=1, tiled=True),
        lax.all_gather(values, "fsdp", axis=1, tiled=True),
    )
    logits, key_heads = score_block(pieces[0])
    piece_rows = pieces[1].shape[1]
    value_heads = pieces[1].reshape(seqs_here, piece_rows, local_heads, HDIM)
    probs = jnp.exp(logits - log_total[..., None])
    grad_weights = jnp.einsum(
        "sqhd,skhd->shqk", grad_head_parts, value_heads, preferred_element_type=jnp.float32
    )
    probs, grad_logits = (probs, (probs * (grad_weights - delta[..., None])).astype(jnp.bfloat16))
    grad_query = (
        jnp.einsum("shqk,skhd->sqhd", grad_logits, key_heads, preferred_element_type=jnp.float32)
        * scale
    )
    key_part = (
        jnp.einsum("shqk,sqhd->skhd", grad_logits, query_heads, preferred_element_type=jnp.float32)
        * scale
    )
    value_part = jnp.einsum(
        "shqk,sqhd->skhd",
        probs.astype(jnp.bfloat16),
        grad_head_parts,
        preferred_element_type=jnp.float32,
    )
    grad_key_all = key_part.reshape(seqs_here, piece_rows, local_heads * HDIM)
    grad_value_all = value_part.reshape(seqs_here, piece_rows, local_heads * HDIM)
    folded_rows = (grad_query, grad_key_all, grad_value_all)
    grad_query, grad_key_all, grad_value_all = folded_rows
    grad_keys, grad_values = (
        lax.psum_scatter(grad_key_all, "fsdp", scatter_dimension=1, tiled=True),
        lax.psum_scatter(grad_value_all, "fsdp", scatter_dimension=1, tiled=True),
    )
    grad_parts = (
        lax.all_to_all(
            grad_query.reshape(seqs_here, span, local_heads * HDIM).astype(jnp.bfloat16),
            "seq",
            split_axis=1,
            concat_axis=2,
            tiled=True,
        ),
        lax.all_to_all(
            grad_keys.astype(jnp.bfloat16), "seq", split_axis=1, concat_axis=2, tiled=True
        ),
        lax.all_to_all(
            grad_values.astype(jnp.bfloat16), "seq", split_axis=1, concat_axis=2, tiled=True
        ),
    )
    unused_turn, reverse_rotation = jax.vjp(turn_all, qkv)
    grad_qkv = (
        reverse_rotation(tuple((member.astype(jnp.float32) for member in grad_parts)))[0]
        .astype(jnp.bfloat16)
        .reshape(flat_rows, 3 * width)
    )
    grad_qkv_weight = contract_rows(attn_low, grad_qkv)
    grad_attn_in = contract_cols(grad_qkv, full_qkv).reshape(seqs_here, row_count, width)
    unused_first, first_back = jax.vjp(adapt, source, gain_first, shift_attn, scale_attn)
    grad_source_norm, grad_gain_attn, grad_shift_attn, grad_scale_attn = first_back(grad_attn_in)
    grad_hidden = grad_middle + grad_source_norm
    grad_mod = jnp.concatenate(
        [
            grad_shift_attn,
            grad_scale_attn,
            grad_gate_attn,
            grad_shift_mlp,
            grad_scale_mlp,
            grad_gate_mlp,
        ],
        -1,
    )[:, 0, :]
    grad_ada = jnp.dot(grad_mod.T, cond, precision=highest_precision)
    grad_bias_mod = jnp.sum(grad_mod, 0)
    summed = (
        lax.psum_scatter(grad_qkv_weight, "fsdp", scatter_dimension=0, tiled=True),
        lax.psum_scatter(grad_attn_weight, "fsdp", scatter_dimension=0, tiled=True),
        lax.psum_scatter(grad_in, "fsdp", scatter_dimension=0, tiled=True),
        lax.psum_scatter(grad_down, "fsdp", scatter_dimension=0, tiled=True),
        lax.psum_scatter(grad_ada, "fsdp", scatter_dimension=0, tiled=True),
        lax.psum_scatter(grad_bias_mod, "fsdp", scatter_dimension=0, tiled=True),
        lax.psum_scatter(grad_gain_attn, "fsdp", scatter_dimension=0, tiled=True),
        lax.psum_scatter(grad_gain_mlp, "fsdp", scatter_dimension=0, tiled=True),
        lax.psum_scatter(grad_bias_in, "fsdp", scatter_dimension=0, tiled=True),
        lax.psum_scatter(grad_bias_down, "fsdp", scatter_dimension=0, tiled=True),
    )
    totals = (
        lax.psum(summed[0].astype(jnp.bfloat16), "seq").astype(jnp.float32),
        lax.psum(summed[1].astype(jnp.bfloat16), "seq").astype(jnp.float32),
        lax.psum(summed[2].astype(jnp.bfloat16), "seq").astype(jnp.float32),
        lax.psum(summed[3].astype(jnp.bfloat16), "seq").astype(jnp.float32),
        lax.psum(summed[4].astype(jnp.bfloat16), "seq").astype(jnp.float32),
        lax.psum(summed[5].astype(jnp.bfloat16), "seq").astype(jnp.float32),
        lax.psum(summed[6].astype(jnp.bfloat16), "seq").astype(jnp.float32),
        lax.psum(summed[7].astype(jnp.bfloat16), "seq").astype(jnp.float32),
        lax.psum(summed[8].astype(jnp.bfloat16), "seq").astype(jnp.float32),
        lax.psum(summed[9].astype(jnp.bfloat16), "seq").astype(jnp.float32),
    )
    return (output, grad_hidden) + tuple(totals)


AXES = ("seq", "fsdp")
SEQ_BIT, HALF_BIT, LOW_BIT, ROW_BIT, CORE_BIT = 16, 8, 4, 2, 1
STREAM = ((ROW_BIT, SEQ_BIT), (LOW_BIT, ROW_BIT), (SEQ_BIT, LOW_BIT))
TOKENS = ((LOW_BIT, LOW_BIT), (ROW_BIT, SEQ_BIT), (SEQ_BIT, ROW_BIT))
SHARED = ((LOW_BIT, LOW_BIT), (SEQ_BIT, SEQ_BIT), (ROW_BIT, ROW_BIT))
VMEM_LIMIT = 62 * 1024 * 1024


def swap_bits(values, even, odd=None):
    odd = even if odd is None else odd
    return lax.ppermute(values, AXES, [(i, i ^ (odd if i & 1 else even)) for i in range(32)])


def spread(values, order):
    for even, odd in order:
        values = jnp.concatenate([values, swap_bits(values, even, odd)], 0)
    return values


def collect(arrays, order):
    for even, odd in reversed(order):
        half = arrays[0].shape[0] // 2
        sent = jnp.concatenate([member[half:] for member in arrays], 1) if len(arrays) > 1 else arrays[0][half:]
        came = swap_bits(sent, even, odd)
        begin, summed = 0, []
        for member in arrays:
            part = came[:, begin : begin + member.shape[1]]
            begin += member.shape[1]
            summed.append((member[:half].astype(jnp.float32) + part.astype(jnp.float32)).astype(jnp.bfloat16))
        arrays = summed
    return arrays


def slot_masks(order, core):
    masks = [jnp.int32(0)]
    for even, odd in order:
        step = jnp.where(core == 0, even, odd).astype(jnp.int32)
        masks = masks + [mask ^ step for mask in masks]
    return jnp.stack(masks)


def quad_exchange(parts):
    came = swap_bits(parts[:, 1], ROW_BIT)
    parts = jnp.stack([parts[:, 0], came], 1)
    came = swap_bits(parts[1], LOW_BIT)
    return jnp.stack([parts[0], came], 0)


def after(values, *others):
    return lax.optimization_barrier((values,) + others)[0]


def pick(values, index, axis=0):
    return lax.dynamic_index_in_dim(values, index, axis, keepdims=False)


def pair_up(mine, other, position):
    return jnp.where(position == 0, jnp.stack([mine, other]), jnp.stack([other, mine]))


def dot_nn(left, right):
    return lax.dot_general(left, right, (((1,), (0,)), ((), ())), preferred_element_type=jnp.float32)


def row_norm(values):
    center = values - jnp.mean(values, -1, keepdims=True)
    return center * lax.rsqrt(jnp.mean(center * center, -1, keepdims=True) + 1e-05)


def head_select(width, head):
    lane = lax.broadcasted_iota(jnp.int32, (1, width), 1)
    return (lane % 128) // 32 == head


def order_weight_kernel(meta, own, other, chooser, out, gathered):
    for slot in range(16):
        start = pl.multiple_of(meta[48 + slot] * own.shape[1], 16)
        gathered[pl.ds(start, own.shape[1]), :] = (own if slot < 8 else other)[slot % 8, :, :]
    out[...] = dot_nn(gathered[...], chooser[...]).astype(jnp.bfloat16)


def project_kernel(
    meta, near, far, other_near, other_far, weight, vectors, cosine, sine, query_out, key_out, value_out, norm_out, all_queries
):
    step = pl.program_id(0)
    rows = near.shape[0]

    def project(source):
        norm = row_norm(source[...].astype(jnp.float32))
        norm_out[...] = norm.astype(jnp.bfloat16)
        attn_in = (norm * vectors[8:9, :] + vectors[2:3, :]).astype(jnp.bfloat16)
        packed = dot_nn(attn_in, weight[:, 256:768])
        first, second = packed[:, 0:128], packed[:, 128:256]
        turn_c, turn_s = cosine[...], sine[...]
        key_out[:, 0:128] = (first * turn_c - second * turn_s).astype(jnp.bfloat16)
        key_out[:, 128:256] = (second * turn_c + first * turn_s).astype(jnp.bfloat16)
        value_out[...] = packed[:, 256:512].astype(jnp.bfloat16)
        return attn_in

    def project_queries(attn_in):
        packed = dot_nn(attn_in, weight[:, 0:256]) * (HDIM ** (-0.5))
        first, second = packed[:, 0:128], packed[:, 128:256]
        turn_c, turn_s = cosine[...], sine[...]
        here = pl.ds(pl.multiple_of(step * rows, 256), rows)
        all_queries[here, 0:128] = (first * turn_c - second * turn_s).astype(jnp.bfloat16)
        all_queries[here, 128:256] = (second * turn_c + first * turn_s).astype(jnp.bfloat16)

    for number, source in enumerate((near, far, other_near, other_far)):

        @pl.when(step // 2 == number)
        def _(number=number, source=source):
            attn_in = project(source)
            if number < 2:
                project_queries(attn_in)

    @pl.when(step == 3)
    def _():
        block = query_out.shape[0] // 4
        stride = 1 + meta[64]
        for j in range(4):
            chosen = pl.ds(pl.multiple_of(((j >> 1) + (j & 1) * 2 * stride) * block, 128), block)
            query_out[j * block : (j + 1) * block, :] = all_queries[chosen, :]


def attend_kernel(meta, query_in, key_in, value_in, out_turned, log_out, out):
    block = query_in.shape[0] // 4
    keys = key_in[...]
    value_turned = value_in[...].T
    log_out[...] = jnp.zeros(log_out.shape, jnp.float32)
    out_turned[...] = jnp.zeros(out_turned.shape, jnp.float32)
    for head in range(3):
        for q_start in range(0, 4 * block, 256):
            here = slice(q_start, q_start + 256)
            query = query_in[here, :]
            query = jnp.where(head_select(256, head), query, jnp.zeros_like(query))
            scores = contract_cols(keys, query)
            best = jnp.max(scores, 0, keepdims=True)
            raised = jnp.exp(scores - best)
            total = jnp.sum(raised, 0, keepdims=True)
            mixed = dot_nn(value_turned[head * 64 : (head + 1) * 64, :], raised.astype(jnp.bfloat16))
            out_turned[head * 64 : (head + 1) * 64, here] = mixed / total
            log_out[head : head + 1, here] = best + jnp.log(total)
    turned_back = out_turned[...].T.astype(jnp.bfloat16)
    for j in range(4):
        out[j, :, :] = turned_back[j * block : (j + 1) * block, 0:192]


def attend_back_kernel(
    meta, cosine, sine, query_in, key_in, value_in, out_turned, log_in, grad_in, grad_packed, key_sum, value_sum
):
    block = query_in.shape[0] // 4
    stride = 1 + meta[64]
    keys, values = key_in[...], value_in[...]
    key_turned = keys.T
    lane_pad = jnp.zeros((4 * block, 64), jnp.bfloat16)
    grad_out = jnp.concatenate([jnp.concatenate([grad_in[j, :, :] for j in range(4)], 0), lane_pad], 1)
    grad_turned = grad_out.astype(jnp.float32).T
    key_sum[...] = jnp.zeros(key_sum.shape, jnp.float32)
    value_sum[...] = jnp.zeros(value_sum.shape, jnp.float32)
    product = grad_turned * out_turned[...]
    lane = lax.broadcasted_iota(jnp.int32, (1, 256), 1)
    query_parts = []
    for q_start in range(0, 4 * block, 256):
        here = slice(q_start, q_start + 256)
        query_sum = jnp.zeros((256, 256), jnp.float32)
        sub = lax.broadcasted_iota(jnp.int32, (256, 1), 0)
        for head in range(3):
            query = query_in[here, :]
            query = jnp.where(head_select(256, head), query, jnp.zeros_like(query))
            head_grad = grad_out[q_start : q_start + 256, :]
            head_grad = jnp.where(lane // 64 == head, head_grad, jnp.zeros_like(head_grad))
            probs = jnp.exp(contract_cols(keys, query) - log_in[head : head + 1, here])
            delta = jnp.sum(product[head * 64 : (head + 1) * 64, here], 0, keepdims=True)
            grad_scores = (probs * (contract_cols(values, head_grad) - delta)).astype(jnp.bfloat16)
            value_sum[...] += dot_nn(probs.astype(jnp.bfloat16), head_grad)
            key_sum[...] += dot_nn(grad_scores, query)
            part = dot_nn(key_turned, grad_scores)
            query_sum = jnp.where((sub % 128) // 32 == head, part, query_sum)
        query_parts.append(query_sum.T * (HDIM ** (-0.5)))
    for j in range(4):
        rows = pl.ds(pl.multiple_of(((j >> 1) + (j & 1) * 2 * stride) * block, 128), block)
        q_part = query_parts[(j * block) // 256][(j * block) % 256 : (j * block) % 256 + block, :]
        first, second = q_part[:, 0:128], q_part[:, 128:256]
        turn_c, turn_s = cosine[rows, :], sine[rows, :]
        here = slice(j * block, (j + 1) * block)
        grad_packed[here, 0:128] = (first * turn_c + second * turn_s).astype(jnp.bfloat16)
        grad_packed[here, 128:256] = (second * turn_c - first * turn_s).astype(jnp.bfloat16)


def project_back_kernel(
    meta, norm, weight, chooser, columns, cosine, sine, grad_packed, key_sum, value_sum,
    own_rows, other_rows, grad_weight, sums, grad_queries, weight_sum, total
):
    step = pl.program_id(0)
    rows = norm.shape[0]

    @pl.when(step == 0)
    def _():
        block = grad_packed.shape[0] // 4
        stride = 1 + meta[64]
        grad_queries[...] = jnp.zeros(grad_queries.shape, jnp.bfloat16)
        for j in range(4):
            chosen = pl.ds(pl.multiple_of(((j >> 1) + (j & 1) * 2 * stride) * block, 128), block)
            grad_queries[chosen, :] = grad_packed[j * block : (j + 1) * block, :]
        weight_sum[...] = jnp.zeros(weight_sum.shape, jnp.float32)
        total[...] = jnp.zeros(total.shape, jnp.float32)

    first, second = key_sum[:, 0:128], key_sum[:, 128:256]
    turn_c, turn_s = cosine[...], sine[...]
    pair = jnp.concatenate(
        [first * turn_c + second * turn_s, second * turn_c - first * turn_s, value_sum[...]], 1
    ).astype(jnp.bfloat16)
    ones = jnp.ones((8, rows), jnp.bfloat16)

    @pl.when(step < 4)
    def _():
        query = grad_queries[pl.ds(pl.multiple_of(step * rows, 256), rows), :]
        triple = jnp.concatenate([query, pair], 1)
        own_rows[...] = contract_cols(triple, weight[...]).astype(jnp.bfloat16)
        weight_sum[...] += contract_rows(norm[...], triple)
        total[...] += dot_nn(ones, triple)

    @pl.when(step >= 4)
    def _():
        other_rows[...] = contract_cols(pair, weight[:, 256:768]).astype(jnp.bfloat16)
        weight_sum[:, 256:768] += contract_rows(norm[...], pair)
        total[:, 256:768] += dot_nn(ones, pair)

    @pl.when(step == pl.num_programs(0) - 1)
    def _():
        summed = total[0:1, :]
        whole = columns[:, 0:1] * weight_sum[...] + columns[:, 1:2] * summed
        grad_weight[...] = contract_cols(whole.astype(jnp.bfloat16), chooser[...]).astype(jnp.bfloat16)
        plain = weight[...].astype(jnp.float32)
        sums[:, 0:1] = jnp.sum(plain * summed, 1, keepdims=True)
        sums[:, 1:2] = jnp.sum(plain * weight_sum[...], 1, keepdims=True)


def middle_kernel(
    meta, attended, near_a, near_b, far_a, far_b, other_near, other_far, own_rows, vectors, projected_out, middle_out, low_out,
    weight_out
):
    core = meta[64]
    mine = pl.multiple_of(core * 384, 128)
    theirs = pl.multiple_of(384 - core * 384, 128)
    for slot in range(16):
        rows_a = pl.ds(pl.multiple_of(meta[slot] * 48, 16), 48)
        rows_b = pl.ds(pl.multiple_of(meta[16 + slot] * 48, 16), 48)
        rows_p = pl.ds(pl.multiple_of(meta[32 + slot] * 48, 16), 48)
        part_a, part_b, other = (near_a, near_b, other_near) if slot < 8 else (far_a, far_b, other_far)
        weight_out[rows_a, pl.ds(mine, 256)] = part_a[slot % 8, :, :]
        weight_out[rows_b, pl.ds(pl.multiple_of(mine + 256, 128), 128)] = part_b[slot % 8, :, :]
        weight_out[rows_p, pl.ds(theirs, 256)] = other[slot % 8, :, 0:256]
        weight_out[rows_b, pl.ds(pl.multiple_of(theirs + 256, 128), 128)] = other[slot % 8, :, 256:384]
    projected = dot_nn(attended[...], weight_out[...])
    projected_out[...] = projected
    middle = own_rows[...].astype(jnp.float32) + vectors[3:4, :] * projected
    middle_out[...] = middle
    low_out[...] = (row_norm(middle) * vectors[4:5, :] * vectors[5:6, :] + vectors[6:7, :]).astype(jnp.bfloat16)


def mlp_kernel(
    meta, low_own, low_other, grad_own, grad_other, near_a, near_b, far_a, far_b, bias, sums_own, sums_other,
    keep_a, keep_b, send_a, send_b, grad_bias, weight_in, weight_down, grad_in, grad_down, branch, back
):
    for slot in range(16):
        part_a, part_b = (near_a, near_b) if slot < 8 else (far_a, far_b)
        for lane_start, size, part, index in ((0, 256, part_a, meta[slot]), (256, 128, part_b, meta[16 + slot])):
            rows = pl.ds(pl.multiple_of(index * 48, 16), 48)
            for i in range(4):
                lanes = slice(i * 384 + lane_start, i * 384 + lane_start + size)
                weight_in[rows, lanes] = part[slot % 8, i * 48 : (i + 1) * 48, :]
            rows = pl.ds(pl.multiple_of(index * 96, 16), 96)
            for i in range(2):
                lanes = slice(i * 384 + lane_start, i * 384 + lane_start + size)
                weight_down[rows, lanes] = part[slot % 8, 192 + i * 96 : 192 + (i + 1) * 96, :]
    low = jnp.concatenate([low_own[...], low_other[...]], 0)
    grad = jnp.concatenate([grad_own[...], grad_other[...]], 0)
    tokens = low_own.shape[0]
    branch[...] = jnp.zeros(branch.shape, jnp.float32)
    back[...] = jnp.zeros(back.shape, jnp.float32)
    root, cubic = math.sqrt(2.0 / math.pi), 0.044715
    for i in range(4):
        hidden = slice(i * 384, (i + 1) * 384)
        pre_act = dot_nn(low, weight_in[:, hidden]) + bias[:, hidden]
        square = pre_act * pre_act
        bend = jnp.tanh(root * (pre_act + cubic * square * pre_act))
        active = (0.5 * pre_act * (1.0 + bend)).astype(jnp.bfloat16)
        slope = 0.5 * (1.0 + bend) + 0.5 * pre_act * (1.0 - bend * bend) * (root * (1.0 + 3.0 * cubic * square))
        branch[...] += dot_nn(active, weight_down[hidden, :])
        grad_pre = (contract_cols(grad, weight_down[hidden, :]) * slope).astype(jnp.bfloat16)
        grad_bias[:, hidden] = jnp.sum(grad_pre.astype(jnp.float32), 0, keepdims=True)
        back[...] += contract_cols(grad_pre, weight_in[:, hidden])
        grad_in[:, hidden] = contract_rows(low, grad_pre).astype(jnp.bfloat16)
        grad_down[hidden, :] = contract_rows(active, grad).astype(jnp.bfloat16)
    sums_own[0, :, :] = branch[:tokens, :]
    sums_other[0, :, :] = branch[tokens:, :]
    sums_own[1, :, :] = back[:tokens, :]
    sums_other[1, :, :] = back[tokens:, :]
    for slot in range(16):
        part_a, part_b = (keep_a, keep_b) if slot < 8 else (send_a, send_b)
        for lane_start, size, part, index in ((0, 256, part_a, meta[slot]), (256, 128, part_b, meta[16 + slot])):
            rows = pl.ds(pl.multiple_of(index * 48, 16), 48)
            for i in range(4):
                lanes = slice(i * 384 + lane_start, i * 384 + lane_start + size)
                part[slot % 8, i * 48 : (i + 1) * 48, :] = grad_in[rows, lanes]
            rows = pl.ds(pl.multiple_of(index * 96, 16), 96)
            for i in range(2):
                lanes = slice(i * 384 + lane_start, i * 384 + lane_start + size)
                part[slot % 8, 192 + i * 96 : 192 + (i + 1) * 96, :] = grad_down[rows, lanes]


def turn_kernel(
    meta, sums_own, sums_other, bias, middle_in, projected_in, cotangent, grad_branch, weight,
    attended, vectors, output, grad_middle_out, grad_attn_out, grad_weight, sums
):
    width = middle_in.shape[1]
    branch = sums_own[0, :, :] + sums_other[0, :, :] + bias[...]
    middle = middle_in[...]
    grad = cotangent[...].astype(jnp.float32)
    output[...] = (middle + vectors[7:8, :] * branch).astype(jnp.bfloat16)
    back = sums_own[1, :, :] + sums_other[1, :, :]
    center = middle - jnp.mean(middle, -1, keepdims=True)
    inverse = lax.rsqrt(jnp.mean(center * center, -1, keepdims=True) + 1e-05)
    norm = center * inverse
    scaled = back * vectors[5:6, :] * vectors[4:5, :]
    grad_middle = grad + inverse * (
        scaled - jnp.mean(scaled, -1, keepdims=True) - norm * jnp.mean(scaled * norm, -1, keepdims=True)
    )
    grad_middle_out[...] = grad_middle
    grad_proj = (vectors[3:4, :] * grad_middle).astype(jnp.bfloat16)
    grad_attn_out[...] = contract_cols(grad_proj, weight[...]).astype(jnp.bfloat16)
    grad_weight[...] = contract_rows(attended[...], grad_proj).astype(jnp.bfloat16)
    def total(values):
        return jnp.sum(values, 0, keepdims=True)

    sums[...] = jnp.concatenate(
        [
            total(grad_middle * projected_in[...]),
            total(back),
            total(back * norm),
            total(grad * branch),
            total(grad_branch[...].astype(jnp.float32)),
            jnp.zeros((3, width), jnp.float32),
        ],
        0,
    )


def call(body, outs, args, scratch=(), grid=None, blocks=(), out_blocks=(), flops=0, moved=0):
    if grid is None:
        whole = pl.BlockSpec(memory_space=pltpu.VMEM)
        in_specs, out_specs = [whole] * len(args), [whole] * len(outs)
    else:
        blocks, out_blocks = dict(blocks), dict(out_blocks)

        def spec(shape, block):
            return block or pl.BlockSpec(shape, lambda i: (0,) * len(shape))

        in_specs = [spec(member.shape, blocks.get(k)) for k, member in enumerate(args)]
        out_specs = [spec(member[0], out_blocks.get(k)) for k, member in enumerate(outs)]
    in_specs[0] = pl.BlockSpec(memory_space=pltpu.SMEM)
    return pl.pallas_call(
        body,
        grid=() if grid is None else grid,
        out_shape=[jax.ShapeDtypeStruct(*member) for member in outs],
        in_specs=in_specs,
        out_specs=out_specs,
        scratch_shapes=[pltpu.VMEM(*member) for member in scratch],
        compiler_params=pltpu.CompilerParams(vmem_limit_bytes=VMEM_LIMIT),
        cost_estimate=pl.CostEstimate(flops=flops, bytes_accessed=moved, transcendentals=0),
    )(*args)


def cube_local(
    hidden_in, time_index, cotangent, w_qkv, w_attn_out, w_mlp_in, w_mlp_out, w_ada, bias_ada, gain_attn, gain_mlp,
    bias_mlp_in, bias_mlp_out
):
    f32, bf16 = jnp.float32, jnp.bfloat16
    rows, width = hidden_in.shape[1:]
    tokens = 2 * rows
    place = lax.axis_index("fsdp")
    side = lax.axis_index("seq")
    device = side * 16 + place
    core, half, group = place & 1, place >> 3, (place >> 1) & 3
    x_own = jnp.concatenate(
        [pick(hidden_in, half), swap_bits(pick(hidden_in, 1 - half), HALF_BIT)], 0
    )
    cond = jax.nn.silu(time_features(time_index, w_ada.shape[1]))
    cond_parts, rest = [], cond
    for _ in range(3):
        cond_parts.append(lax.reduce_precision(rest, 8, 7))
        rest = rest - cond_parts[-1]
    cond_parts = jnp.concatenate(cond_parts, 0).astype(bf16)

    def double(values, bit):
        return jnp.concatenate([values, swap_bits(values, bit)], 0)

    x_own, w_ada, w_qkv, w_mlp_in, w_attn_out, w_mlp_out = lax.optimization_barrier(
        (x_own, w_ada, w_qkv, w_mlp_in, w_attn_out, w_mlp_out)
    )
    x_kept = x_own
    x_one = spread(x_own, TOKENS[:1])
    modulation = jnp.sum(contract_cols(cond_parts, w_ada).reshape(3, 2, -1), 0) + bias_ada.astype(f32)
    vector = jnp.concatenate(
        [modulation.reshape(1, -1)]
        + [member.astype(f32)[None] for member in (gain_attn, gain_mlp, bias_mlp_in, bias_mlp_out)],
        1,
    )
    came_qkv = swap_bits(w_qkv, HALF_BIT)
    in_columns = w_mlp_in.reshape(48, 8, 2, 192)

    def in_blocks(columns):
        return columns.reshape(48, 4, 384).transpose(1, 0, 2).reshape(192, 384)

    own_share = jnp.concatenate(
        [in_blocks(pick(in_columns, core, 2)), pick(w_attn_out.reshape(48, 2, 384), core, 1)], 0
    )
    sent_share = jnp.concatenate(
        [in_blocks(pick(in_columns, 1 - core, 2)), pick(w_attn_out.reshape(48, 2, 384), 1 - core, 1)], 0
    )
    down_share = pick(w_mlp_out.reshape(2, 96, 2, 384), side).transpose(1, 0, 2).reshape(192, 384)
    share = jnp.where(core == side, own_share, swap_bits(sent_share, CORE_BIT))
    share = jnp.concatenate([share[:192], down_share, share[192:]], 0)
    x_one, vector, share, place_kept = lax.optimization_barrier((x_one, vector, share, place))
    x_two = spread(x_one, TOKENS[1:2])
    vector = double(vector, HALF_BIT)
    came_share = swap_bits(share, HALF_BIT)
    x_two, vector, came_qkv = lax.optimization_barrier((x_two, vector, came_qkv))
    x_far = swap_bits(x_two, *TOKENS[2])
    other_two = swap_bits(x_two, CORE_BIT)
    vector = double(vector, ROW_BIT)
    both_qkv = jnp.stack([w_qkv, came_qkv])
    grouped = both_qkv.reshape(96, 3, 4, 192).transpose(2, 0, 1, 3).reshape(4, 96, 576)
    grouped = grouped[group ^ jnp.arange(4)].reshape(2, 2, 96, 576)
    grouped = jnp.stack([grouped[:, 0], swap_bits(grouped[:, 1], ROW_BIT)], 1)
    grouped, vector = lax.optimization_barrier((grouped, vector))
    grouped = jnp.stack([grouped[0], swap_bits(grouped[1], LOW_BIT)], 0).reshape(8, 48, 576)
    vector = double(vector, LOW_BIT)
    x_far, grouped, came_share, vector = lax.optimization_barrier((x_far, grouped, came_share, vector))
    other_far = swap_bits(x_far, CORE_BIT)
    came_grouped = swap_bits(grouped, CORE_BIT)
    vector = double(vector, CORE_BIT)
    share = jnp.stack([share, came_share])[None]
    part_a, part_b = spread(share[..., :256], STREAM[:1]), spread(share[..., 256:], SHARED[:1])
    apart = place ^ jnp.arange(16)
    vector = vector[(apart >> 3) | (apart & 6) | ((apart & 1) << 3)]
    parts, begin = [], 0
    for size in (288, 288, 48, 48, 192, 48):
        parts.append(vector[:, begin : begin + size])
        begin += size
    modulation = jnp.stack([parts[0].reshape(6, width), parts[1].reshape(6, width)])
    shift_attn, scale_attn, gate_attn, shift_mlp, scale_mlp, gate_mlp = [
        row for row in pick(modulation, half)
    ]
    full_gain_attn, full_gain_mlp = parts[2].reshape(-1), parts[3].reshape(-1)
    bias_in = pick(parts[4].reshape(8, 2, 192), core, 1).reshape(1, -1)
    bias_down = parts[5].reshape(1, -1)
    vectors = jnp.stack(
        [full_gain_attn, 1.0 + scale_attn, shift_attn, gate_attn, full_gain_mlp, 1.0 + scale_mlp, shift_mlp, gate_mlp]
        + [full_gain_attn * (1.0 + scale_attn)]
    )
    columns = jnp.stack([vectors[8], shift_attn], 1)
    place = place_kept
    device, core = side * 16 + place, place & 1
    stream_own, stream_other = slot_masks(STREAM, core), slot_masks(STREAM, 1 - core)
    shared = slot_masks(SHARED, core)

    def weight_slots(masks):
        moved = ((masks & 6) | (masks >> 4))[:, None] ^ jnp.array([0, 8], jnp.int32)[None]
        return (((place & 14) + side) ^ moved).reshape(-1)

    quad = jnp.array([0, ROW_BIT, LOW_BIT, LOW_BIT | ROW_BIT], jnp.int32)
    oct_masks = (quad[:, None] ^ jnp.array([0, HALF_BIT], jnp.int32)).reshape(-1)
    row_slots = place ^ jnp.concatenate([oct_masks, oct_masks ^ CORE_BIT])
    meta = jnp.concatenate(
        [weight_slots(stream_own), weight_slots(shared), weight_slots(stream_other), row_slots, core[None]]
    ).astype(jnp.int32)
    blocks = jnp.concatenate(
        [device ^ slot_masks(TOKENS, core), device ^ CORE_BIT ^ slot_masks(TOKENS, 1 - core)]
    )
    blocks = jnp.stack([blocks, blocks ^ HALF_BIT], 1)
    inverse = jnp.exp(-math.log(10000.0) * (2 * (jnp.arange(128) % 32)).astype(f32) / HDIM)
    begin_angles = (blocks.reshape(-1) * rows).astype(f32)[:, None, None] * inverse
    inner_angles = jnp.arange(rows, dtype=jnp.int32).astype(f32)[:, None] * inverse
    begin_c, begin_s, inner_c, inner_s = [
        lax.optimization_barrier(member)
        for member in (jnp.cos(begin_angles), jnp.sin(begin_angles), jnp.cos(inner_angles), jnp.sin(inner_angles))
    ]
    cosine = (begin_c * inner_c - begin_s * inner_s).reshape(-1, 128)
    sine = (begin_s * inner_c + begin_c * inner_s).reshape(-1, 128)
    lane = jnp.arange(768) + (place >> 4)
    inner = lane % 128
    wanted = jnp.where(
        lane < 512,
        jnp.where(inner < 96, (lane // 256) * 192 + (inner // 32) * 64 + ((lane % 256) // 128) * 32 + inner % 32, -1),
        jnp.where(lane < 704, lane - 128, -1),
    )
    chooser = (jnp.arange(576)[:, None] == wanted[None, :]).astype(bf16)
    (weight_qkv,) = call(
        order_weight_kernel,
        [((768, 768), bf16)],
        [meta, grouped, came_grouped, chooser],
        [((768, 576), bf16)],
        flops=2 * 768 * 768 * 576,
        moved=3_000_000,
    )
    span = 16 * tokens
    cosine, part_a, part_b = lax.optimization_barrier((cosine, part_a, part_b))
    part_a, part_b = spread(part_a, STREAM[1:2]), spread(part_b, SHARED[1:2])
    chunk = 256

    def part_of(number, size):
        return pl.BlockSpec((chunk, size), lambda i: (jnp.clip(i - number * 2, 0, 1), 0))

    def rows_of(size):
        return pl.BlockSpec((chunk, size), lambda i: (i, 0))

    queries, keys, values, norms = call(
        project_kernel,
        [((4 * tokens, 256), bf16), ((span, 256), bf16), ((span, 256), bf16), ((span, width), bf16)],
        [meta, x_two, x_far, other_two, other_far, weight_qkv, vectors, cosine, sine],
        [((8 * tokens, 256), bf16)],
        grid=(8,),
        blocks=[(1 + number, part_of(number, width)) for number in range(4)] + [(7, rows_of(128)), (8, rows_of(128))],
        out_blocks=[(1, rows_of(256)), (2, rows_of(256)), (3, rows_of(width))],
        flops=2_000_000_000,
        moved=8_000_000,
    )
    keys, part_a, part_b = lax.optimization_barrier((keys, part_a, part_b))
    far_a, far_b = swap_bits(part_a, *STREAM[2]), swap_bits(part_b, *SHARED[2])
    part_a, part_b = part_a.reshape(8, 432, 256), part_b.reshape(8, 432, 128)
    other_near = swap_bits(jnp.concatenate([part_a[:, 384:], part_b[:, 384:]], 2), CORE_BIT)
    out_turned, log_total, heads_out = call(
        attend_kernel,
        [((256, 4 * tokens), f32), ((8, 4 * tokens), f32), ((4, tokens, 192), bf16)],
        [meta, queries, keys, values],
        flops=8_000_000_000,
        moved=4_000_000,
    )
    heads_out = heads_out.reshape(2, 2, tokens, 192)
    came = swap_bits(heads_out[:, 1], ROW_BIT)
    came, far_a, far_b = lax.optimization_barrier((came, far_a, far_b))
    heads_out = jnp.stack([heads_out[:, 0], came], 1)
    by_group = jnp.stack([heads_out[0], swap_bits(heads_out[1], LOW_BIT)], 0).reshape(4, tokens, 192)
    attended = by_group[group ^ jnp.arange(4)].transpose(1, 0, 2).reshape(tokens, width)
    far_a, far_b = far_a.reshape(8, 432, 256), far_b.reshape(8, 432, 128)
    other_out = swap_bits(jnp.concatenate([far_a[:, 384:], far_b[:, 384:]], 2), CORE_BIT)
    projected, middle, mlp_own, weight_out = call(
        middle_kernel,
        [((tokens, width), f32), ((tokens, width), f32), ((tokens, width), bf16), ((768, 768), bf16)],
        [meta, attended, part_a[:, 384:], part_b[:, 384:], far_a[:, 384:], far_b[:, 384:], other_near, other_out]
        + [x_kept, vectors],
        flops=150_000_000,
        moved=3_000_000,
    )
    grad_own = jnp.concatenate(
        [pick(cotangent, half), swap_bits(pick(cotangent, 1 - half), HALF_BIT)], 0
    )
    branch_grad = (gate_mlp[None] * grad_own.astype(f32)).astype(bf16)
    branch_grad_other = swap_bits(branch_grad, CORE_BIT)
    mlp_other = swap_bits(mlp_own, CORE_BIT)
    sums_own, sums_sent, keep_a, keep_b, send_a, send_b, grad_bias_in = call(
        mlp_kernel,
        [((2, tokens, width), f32)] * 2
        + [((8, 384, 256), bf16), ((8, 384, 128), bf16)] * 2
        + [((1, 1536), f32)],
        [meta, mlp_own, mlp_other, branch_grad, branch_grad_other, part_a, part_b, far_a, far_b, bias_in],
        [((768, 1536), bf16), ((1536, 768), bf16), ((768, 1536), bf16), ((1536, 768), bf16)]
        + [((2 * tokens, width), f32)] * 2,
        flops=3_600_000_000,
        moved=12_000_000,
    )
    came = swap_bits(sums_sent, CORE_BIT)

    def plus(left, right):
        return (left.astype(f32) + right.astype(f32)).astype(bf16)

    sum_a = plus(keep_a, swap_bits(send_a, *STREAM[2])).reshape(4, 768, 256)
    sum_b = plus(keep_b, swap_bits(send_b, *SHARED[2])).reshape(4, 768, 128)
    output_rows, grad_middle, grad_attn, grad_w_out, sums_mlp = call(
        turn_kernel,
        [((tokens, width), bf16), ((tokens, width), f32), ((tokens, width), bf16), ((768, 768), bf16), ((8, width), f32)],
        [meta, sums_own, came, bias_down, middle, projected, grad_own, branch_grad, weight_out]
        + [attended, vectors],
        flops=300_000_000,
        moved=5_000_000,
    )

    grad_heads = grad_attn.reshape(tokens, 4, 192).transpose(1, 0, 2)[group ^ jnp.arange(4)]
    grad_heads = quad_exchange(grad_heads.reshape(2, 2, tokens, 192)).reshape(4, tokens, 192)
    by_core = grad_w_out.reshape(8, 2, 48, width)
    sum_out = plus(pick(by_core, core, 1), swap_bits(pick(by_core, 1 - core, 1), CORE_BIT))
    output = pair_up(output_rows[:rows], swap_bits(output_rows[rows:], HALF_BIT), half)
    grad_heads, sum_a, sum_b, sum_out, output = lax.optimization_barrier((grad_heads, sum_a, sum_b, sum_out, output))
    sum_a = collect([sum_a], STREAM[1:2])[0]
    sum_b = collect([sum_b], SHARED[1:2])[0]
    by_side = sum_out.reshape(8, 2, 24, width)
    sum_out = plus(pick(by_side, side, 1), swap_bits(pick(by_side, 1 - side, 1), SEQ_BIT))
    grad_packed, key_sum, value_sum = call(
        attend_back_kernel,
        [((4 * tokens, 256), bf16), ((span, 256), f32), ((span, 256), f32)],
        [meta, cosine, sine, queries, keys, values, out_turned, log_total, grad_heads],
        flops=14_000_000_000,
        moved=8_000_000,
    )
    key_sum, sum_a, sum_b, sum_out = lax.optimization_barrier((key_sum, sum_a, sum_b, sum_out))
    sum_a = collect([sum_a], STREAM[:1])[0]
    sum_b = collect([sum_b], SHARED[:1])[0]
    by_half = sum_out.reshape(2, 4, 24, width)
    sum_out = plus(pick(by_half, half), swap_bits(pick(by_half, 1 - half), HALF_BIT))
    own_rows, other_rows, grad_qkv, sums_attn = call(
        project_back_kernel,
        [((8 * tokens, width), bf16)] * 2 + [((768, 576), bf16), ((width, 2), f32)],
        [meta, norms, weight_qkv, chooser, columns, cosine, sine, grad_packed, key_sum, value_sum],
        [((8 * tokens, 256), bf16), ((width, width), f32), ((8, width), f32)],
        grid=(8,),
        blocks=[(1, rows_of(width)), (5, rows_of(128)), (6, rows_of(128)), (8, rows_of(256)), (9, rows_of(256))],
        out_blocks=[
            (0, pl.BlockSpec((chunk, width), lambda i: (jnp.minimum(i, 3), 0))),
            (1, pl.BlockSpec((chunk, width), lambda i: (jnp.maximum(i - 4, 0), 0))),
        ],
        flops=6_000_000_000,
        moved=16_000_000,
    )
    own_rows, other_rows, grad_qkv, sums_attn, sum_a, sum_b, sum_out = lax.optimization_barrier(
        (own_rows, other_rows, grad_qkv, sums_attn, sum_a, sum_b, sum_out)
    )
    own_rows = own_rows.reshape(8, tokens, width)
    came_rows = swap_bits(other_rows, CORE_BIT).reshape(8, tokens, width)
    small = jnp.concatenate([sums_attn.T, sums_mlp[0:5]], 0)
    small = jnp.concatenate([small + swap_bits(small, CORE_BIT), grad_bias_in.reshape(2, width)], 0)
    by_core = grad_qkv.reshape(8, 2, 48, 576)
    kept = plus(pick(by_core, core, 1), swap_bits(pick(by_core, 1 - core, 1), CORE_BIT))
    total = jnp.concatenate([sum_a.reshape(2, 384, 256), sum_b.reshape(2, 384, 128)], 2)

    def sum_step(own, came, small, order):
        half_way = own.shape[0] // 2
        sent = plus(own[half_way:], came[half_way:]).reshape(-1, width)
        high = jnp.pad(small, ((0, 7), (0, 0))).astype(bf16)
        low = (jnp.pad(small, ((0, 7), (0, 0))) - high.astype(f32)).astype(bf16)
        got = swap_bits(jnp.concatenate([sent, high, low], 0), *order)
        count = sent.shape[0]
        small = small + got[count : count + 9].astype(f32) + got[count + 16 : count + 25].astype(f32)
        return plus(own[:half_way], came[:half_way]), got[:count].reshape(half_way, tokens, width), small

    came_rows, small, kept = lax.optimization_barrier((came_rows, small, kept))
    came_total = swap_bits(total[1], HALF_BIT)
    own_rows, came_rows, small = sum_step(own_rows, came_rows, small, TOKENS[2])
    by_row = kept.reshape(2, 2, 2, 48, 576)
    out_row = sum_out.reshape(2, 2, 24, width)
    y = place & 2
    sent = jnp.concatenate(
        [
            pick(by_row, 1 - y // 2, 2).reshape(192, 576),
            pick(out_row, 1 - y // 2, 1).reshape(48, 4, 192).transpose(1, 0, 2).reshape(192, 192),
        ],
        1,
    )
    got = swap_bits(sent, ROW_BIT)
    by_row = jnp.stack([pick(by_row, y // 2, 2), got[:, :576].reshape(2, 2, 48, 576)])
    got = got[:, 576:].reshape(4, 48, 192).transpose(1, 0, 2).reshape(2, 24, width)
    sum_out = plus(pick(out_row, y // 2, 1), got)
    came_rows, by_row, sum_out, small, came_total = lax.optimization_barrier(
        (came_rows, by_row, sum_out, small, came_total)
    )
    own_rows, came_rows, small = sum_step(own_rows, came_rows, small, TOKENS[1])
    by_side = by_row.reshape(8, 2, 24, 576)
    kept = plus(pick(by_side, side, 1), swap_bits(pick(by_side, 1 - side, 1), SEQ_BIT))
    came_rows, kept, small = lax.optimization_barrier((came_rows, kept, small))
    own_rows, came_rows, small = sum_step(own_rows, came_rows, small, TOKENS[0])
    total = plus(total[0], came_total)
    across = swap_bits(total, SEQ_BIT)
    by_low = kept.reshape(2, 2, 2, 24, 576)
    z = (place >> 2) & 1
    sent = jnp.concatenate(
        [
            pick(by_low, 1 - z, 2).reshape(96, 576),
            pick(sum_out, 1 - z).reshape(24, 4, 192).transpose(1, 0, 2).reshape(96, 192),
        ],
        1,
    )
    got = swap_bits(sent, LOW_BIT)
    by_low = jnp.stack([pick(by_low, z, 2), got[:, :576].reshape(2, 2, 24, 576)])
    got = got[:, 576:].reshape(4, 24, 192).transpose(1, 0, 2).reshape(24, width)
    sum_out = plus(pick(sum_out, z), got)
    came_rows, by_low, sum_out, small, across = lax.optimization_barrier((came_rows, by_low, sum_out, small, across))
    own_sum = own_rows.astype(f32) + came_rows.astype(f32)
    grad_in = own_sum[0].astype(f32)
    source = x_kept.astype(f32)
    center = source - jnp.mean(source, -1, keepdims=True)
    inverse = lax.rsqrt(jnp.mean(center * center, -1, keepdims=True) + 1e-05)
    norm = center * inverse
    scaled = grad_in * vectors[1:2] * vectors[0:1]
    grad_hidden = grad_middle + inverse * (
        scaled - jnp.mean(scaled, -1, keepdims=True) - norm * jnp.mean(scaled * norm, -1, keepdims=True)
    )
    grad_hidden = pair_up(
        grad_hidden[:rows], swap_bits(grad_hidden[rows:].astype(bf16), HALF_BIT).astype(f32), half
    )

    grad_down = pair_up(total[192:], across[192:], side).reshape(2, 2, 96, 384)
    grad_down = grad_down.transpose(0, 2, 1, 3).reshape(192, 768).astype(f32)
    mine = jnp.where(core == side, total[:192], across[:192])
    theirs = swap_bits(jnp.where(core == side, across[:192], total[:192]), CORE_BIT)

    def in_columns_back(blocks):
        return blocks.reshape(4, 48, 384).transpose(1, 0, 2).reshape(48, 8, 192)

    grad_w_in = pair_up(in_columns_back(mine), in_columns_back(theirs), core)
    grad_w_in = grad_w_in.transpose(1, 2, 0, 3).reshape(48, 3072).astype(f32)
    by_half = by_low.reshape(4, 2, 24, 576)
    kept = plus(pick(by_half, half, 1), swap_bits(pick(by_half, 1 - half, 1), HALF_BIT))
    kept = kept[group ^ jnp.arange(4)].reshape(4, 24, 3, 192).transpose(1, 2, 0, 3).reshape(24, 2304)
    kept = jnp.concatenate([kept, sum_out], 1)
    kept = pair_up(kept, swap_bits(kept, SEQ_BIT), side).reshape(48, 3072).astype(f32)
    grad_w_qkv, grad_w_out = kept[:, :2304], kept[:, 2304:]
    both = pair_up(small, swap_bits(small, HALF_BIT), half)
    plus_scale = 1.0 + modulation[:, 1], 1.0 + modulation[:, 4]
    grad_mod = jnp.stack(
        [both[:, 0], both[:, 1] * full_gain_attn, both[:, 2], both[:, 3], both[:, 4] * full_gain_mlp, both[:, 5]], 1
    ).reshape(2, 16, 288)
    grad_mod = pick(grad_mod, place, 1)
    grad_ada = grad_mod[0][:, None] * cond[0][None] + grad_mod[1][:, None] * cond[1][None]
    gain_first = pick(jnp.sum(both[:, 1] * plus_scale[0], 0).reshape(16, 48), place)
    gain_second = pick(jnp.sum(both[:, 4] * plus_scale[1], 0).reshape(16, 48), place)
    summed = both[0] + both[1]
    bias_in_grad = pick(summed[7:9].reshape(8, 192), place >> 1)
    bias_down_grad = pick(summed[6].reshape(16, 48), place)
    return (
        output,
        grad_hidden,
        grad_w_qkv,
        grad_w_out,
        grad_w_in,
        grad_down,
        grad_ada,
        jnp.sum(grad_mod, 0),
        gain_first,
        gain_second,
        bias_in_grad,
        bias_down_grad,
    )


def solution(mesh):
    return jax.shard_map(
        cube_local if dict(mesh.shape) == {"seq": 2, "fsdp": 16} else local,
        mesh=mesh,
        in_specs=(
            P(None, ("seq", "fsdp"), None),
            P(),
            P(None, ("seq", "fsdp"), None),
            P("fsdp", None),
            P("fsdp", None),
            P("fsdp", None),
            P("fsdp", None),
            P("fsdp", None),
            P("fsdp"),
            P("fsdp"),
            P("fsdp"),
            P("fsdp"),
            P("fsdp"),
        ),
        out_specs=(
            P(None, ("seq", "fsdp"), None),
            P(None, ("seq", "fsdp"), None),
            P("fsdp", None),
            P("fsdp", None),
            P("fsdp", None),
            P("fsdp", None),
            P("fsdp", None),
            P("fsdp"),
            P("fsdp"),
            P("fsdp"),
            P("fsdp"),
            P("fsdp"),
        ),
        check_vma=False,
    )
```

```python
import math

import jax
import jax.numpy as jnp
from jax import lax
from jax.experimental import pallas as pl
from jax.experimental.pallas import tpu as pltpu
from jax.sharding import PartitionSpec as P

HEADS = 12
HDIM = 64


highest_precision = lax.Precision.HIGHEST


def normalize(values):
    center = values - jnp.mean(values, -1, keepdims=True)
    return center * lax.rsqrt(jnp.mean(center * center, -1, keepdims=True) + 1e-05)


def adapt(values, gain, shift, scale):
    return normalize(values) * gain * (1.0 + scale) + shift


def time_features(time_index, width):
    half_width = width // 2
    frequency = jnp.exp(-math.log(10000.0) * jnp.arange(half_width, dtype=jnp.float32) / half_width)
    angles = time_index.astype(jnp.float32)[:, None] * frequency[None, :]
    return jnp.concatenate([jnp.cos(angles), jnp.sin(angles)], -1)


def rotary_tables(positions, head_dim):
    inverse = jnp.exp(-math.log(10000.0) * jnp.arange(0, head_dim, 2, dtype=jnp.float32) / head_dim)
    angles = positions.astype(jnp.float32)[:, None] * inverse[None, :]
    angles = jnp.concatenate([angles, angles], -1)
    return (jnp.cos(angles), jnp.sin(angles))


def rotate(values, cosine, sine):
    first_half, second_half = jnp.split(values, 2, axis=-1)
    turned = jnp.concatenate([-second_half, first_half], -1)
    return values * cosine[:, None, :] + turned * sine[:, None, :]


def contract_rows(left_neighbor, right_neighbor):
    return lax.dot_general(
        left_neighbor, right_neighbor, (((0,), (0,)), ((), ())), preferred_element_type=jnp.float32
    )


def contract_cols(left_neighbor, right_neighbor):
    return lax.dot_general(
        left_neighbor, right_neighbor, (((1,), (1,)), ((), ())), preferred_element_type=jnp.float32
    )


def gelu_tanh(values):
    return jax.nn.gelu(values, approximate=True)


def local(
    hidden_in,
    time_index,
    cotangent,
    w_qkv,
    w_attn_out,
    w_mlp_in,
    w_mlp_out,
    w_ada,
    bias_ada,
    gain_attn,
    gain_mlp,
    bias_mlp_in,
    bias_mlp_out,
):
    seqs_here, row_count, width = hidden_in.shape
    flat_rows = seqs_here * row_count
    gathered = (
        lax.all_gather(w_qkv, "fsdp", axis=0, tiled=True),
        lax.all_gather(w_attn_out, "fsdp", axis=0, tiled=True),
        lax.all_gather(w_mlp_in, "fsdp", axis=0, tiled=True),
        lax.all_gather(w_mlp_out, "fsdp", axis=0, tiled=True),
        lax.all_gather(w_ada, "fsdp", axis=0, tiled=True),
        lax.all_gather(bias_ada, "fsdp", axis=0, tiled=True),
        lax.all_gather(gain_attn, "fsdp", axis=0, tiled=True),
        lax.all_gather(gain_mlp, "fsdp", axis=0, tiled=True),
        lax.all_gather(bias_mlp_in, "fsdp", axis=0, tiled=True),
        lax.all_gather(bias_mlp_out, "fsdp", axis=0, tiled=True),
    )
    (
        full_qkv,
        gathered_output,
        full_in,
        full_down,
        full_ada,
        full_bias_ada,
        full_gain_attn,
        full_gain_mlp,
        full_bias_in,
        full_bias_down,
    ) = gathered
    gain_first = full_gain_attn.astype(jnp.float32)
    gain_second = full_gain_mlp.astype(jnp.float32)
    cond = jax.nn.silu(time_features(time_index, full_ada.shape[1]))
    modulation = jnp.dot(
        cond, full_ada.astype(jnp.float32).T, precision=highest_precision
    ) + full_bias_ada.astype(jnp.float32)
    shift_attn, scale_attn, gate_attn, shift_mlp, scale_mlp, gate_mlp = jnp.split(
        modulation[:, None, :], 6, axis=-1
    )
    source = hidden_in.astype(jnp.float32)
    attn_in = adapt(source, gain_first, shift_attn, scale_attn)
    attn_low = attn_in.astype(jnp.bfloat16).reshape(flat_rows, width)
    qkv = jnp.dot(attn_low, full_qkv, preferred_element_type=jnp.float32).reshape(
        seqs_here, row_count, 3 * width
    )
    device_number = lax.axis_index("seq") * lax.axis_size("fsdp") + lax.axis_index("fsdp")
    positions = device_number * row_count + jnp.arange(row_count, dtype=jnp.int32)
    cosine, sine = rotary_tables(positions, HDIM)

    def turn_all(packed):
        split_three = packed.reshape(seqs_here, row_count, 3, HEADS, HDIM)
        query_turned = rotate(split_three[:, :, 0], cosine, sine).reshape(
            seqs_here, row_count, width
        )
        key_turned = rotate(split_three[:, :, 1], cosine, sine).reshape(seqs_here, row_count, width)
        return (query_turned, key_turned, split_three[:, :, 2].reshape(seqs_here, row_count, width))

    query_rot, key_rot, value_raw = turn_all(qkv)
    queries, keys, values = (
        lax.all_to_all(
            query_rot.astype(jnp.bfloat16), "seq", split_axis=2, concat_axis=1, tiled=True
        ),
        lax.all_to_all(
            key_rot.astype(jnp.bfloat16), "seq", split_axis=2, concat_axis=1, tiled=True
        ),
        lax.all_to_all(
            value_raw.astype(jnp.bfloat16), "seq", split_axis=2, concat_axis=1, tiled=True
        ),
    )
    local_heads = HEADS // lax.axis_size("seq")
    span = queries.shape[1]
    query_heads = queries.reshape(seqs_here, span, local_heads, HDIM)
    scale = HDIM ** (-0.5)

    def score_block(key_piece):
        key_heads = key_piece.reshape(seqs_here, key_piece.shape[1], local_heads, HDIM)
        logits = (
            jnp.einsum(
                "sqhd,skhd->shqk", query_heads, key_heads, preferred_element_type=jnp.float32
            )
            * scale
        )
        return (logits, key_heads)

    pieces = (
        lax.all_gather(keys, "fsdp", axis=1, tiled=True),
        lax.all_gather(values, "fsdp", axis=1, tiled=True),
    )
    best = jnp.full((seqs_here, local_heads, span), -1e30, jnp.float32)
    logits, unused = score_block(pieces[0])
    value_heads = pieces[1].reshape(seqs_here, pieces[1].shape[1], local_heads, HDIM)
    newest = jnp.maximum(best, jnp.max(logits, -1))
    raised = jnp.exp(logits - newest[..., None])
    total = jnp.sum(raised, -1)
    accum = jnp.einsum(
        "shqk,skhd->sqhd",
        raised.astype(jnp.bfloat16),
        value_heads,
        preferred_element_type=jnp.float32,
    )
    best, total, accum = (newest, total, accum)
    log_total = best + jnp.log(total)
    attended = accum / jnp.transpose(total, (0, 2, 1))[..., None]
    attended_low = attended.reshape(seqs_here, span, local_heads * HDIM).astype(jnp.bfloat16)
    attn_rows = lax.all_to_all(attended_low, "seq", split_axis=1, concat_axis=2, tiled=True)
    attn_flat = attn_rows.reshape(flat_rows, width)
    projected = jnp.dot(attn_flat, gathered_output, preferred_element_type=jnp.float32).reshape(
        seqs_here, row_count, width
    )
    middle = source + gate_attn * projected
    mlp_in = adapt(middle, gain_second, shift_mlp, scale_mlp)
    mlp_low = mlp_in.astype(jnp.bfloat16).reshape(flat_rows, width)
    pre_act = jnp.dot(mlp_low, full_in, preferred_element_type=jnp.float32) + full_bias_in.astype(
        jnp.float32
    )
    active = gelu_tanh(pre_act).astype(jnp.bfloat16)
    branch = (
        jnp.dot(active, full_down, preferred_element_type=jnp.float32)
        + full_bias_down.astype(jnp.float32)
    ).reshape(seqs_here, row_count, width)
    output = (middle + gate_mlp * branch).astype(jnp.bfloat16)
    grad_result = cotangent.astype(jnp.float32)
    grad_gate_mlp = jnp.sum(grad_result * branch, 1, keepdims=True)
    grad_branch = (gate_mlp * grad_result).astype(jnp.bfloat16).reshape(flat_rows, width)
    grad_bias_down = jnp.sum(grad_branch.astype(jnp.float32), 0)
    grad_down = contract_rows(active, grad_branch)
    grad_active = contract_cols(grad_branch, full_down)
    unused_gelu, gelu_back = jax.vjp(gelu_tanh, pre_act)
    grad_pre = gelu_back(grad_active)[0].astype(jnp.bfloat16)
    grad_bias_in = jnp.sum(grad_pre.astype(jnp.float32), 0)
    grad_in = contract_rows(mlp_low, grad_pre)
    grad_mlp_in = contract_cols(grad_pre, full_in).reshape(seqs_here, row_count, width)
    unused_second, second_back = jax.vjp(adapt, middle, gain_second, shift_mlp, scale_mlp)
    grad_middle_norm, grad_gain_mlp, grad_shift_mlp, grad_scale_mlp = second_back(grad_mlp_in)
    grad_middle = grad_result + grad_middle_norm
    grad_gate_attn = jnp.sum(grad_middle * projected, 1, keepdims=True)
    grad_proj = (gate_attn * grad_middle).astype(jnp.bfloat16).reshape(flat_rows, width)
    grad_attn_weight = contract_rows(attn_flat, grad_proj)
    grad_attn_rows = (
        contract_cols(grad_proj, gathered_output)
        .astype(jnp.bfloat16)
        .reshape(seqs_here, row_count, width)
    )
    grad_heads = lax.all_to_all(grad_attn_rows, "seq", split_axis=2, concat_axis=1, tiled=True)
    grad_head_parts = grad_heads.reshape(seqs_here, span, local_heads, HDIM)
    delta = jnp.transpose(jnp.sum(grad_head_parts.astype(jnp.float32) * attended, -1), (0, 2, 1))
    pieces = (
        lax.all_gather(keys, "fsdp", axis=1, tiled=True),
        lax.all_gather(values, "fsdp", axis=1, tiled=True),
    )
    logits, key_heads = score_block(pieces[0])
    piece_rows = pieces[1].shape[1]
    value_heads = pieces[1].reshape(seqs_here, piece_rows, local_heads, HDIM)
    probs = jnp.exp(logits - log_total[..., None])
    grad_weights = jnp.einsum(
        "sqhd,skhd->shqk", grad_head_parts, value_heads, preferred_element_type=jnp.float32
    )
    probs, grad_logits = (probs, (probs * (grad_weights - delta[..., None])).astype(jnp.bfloat16))
    grad_query = (
        jnp.einsum("shqk,skhd->sqhd", grad_logits, key_heads, preferred_element_type=jnp.float32)
        * scale
    )
    key_part = (
        jnp.einsum("shqk,sqhd->skhd", grad_logits, query_heads, preferred_element_type=jnp.float32)
        * scale
    )
    value_part = jnp.einsum(
        "shqk,sqhd->skhd",
        probs.astype(jnp.bfloat16),
        grad_head_parts,
        preferred_element_type=jnp.float32,
    )
    grad_key_all = key_part.reshape(seqs_here, piece_rows, local_heads * HDIM)
    grad_value_all = value_part.reshape(seqs_here, piece_rows, local_heads * HDIM)
    folded_rows = (grad_query, grad_key_all, grad_value_all)
    grad_query, grad_key_all, grad_value_all = folded_rows
    grad_keys, grad_values = (
        lax.psum_scatter(grad_key_all, "fsdp", scatter_dimension=1, tiled=True),
        lax.psum_scatter(grad_value_all, "fsdp", scatter_dimension=1, tiled=True),
    )
    grad_parts = (
        lax.all_to_all(
            grad_query.reshape(seqs_here, span, local_heads * HDIM).astype(jnp.bfloat16),
            "seq",
            split_axis=1,
            concat_axis=2,
            tiled=True,
        ),
        lax.all_to_all(
            grad_keys.astype(jnp.bfloat16), "seq", split_axis=1, concat_axis=2, tiled=True
        ),
        lax.all_to_all(
            grad_values.astype(jnp.bfloat16), "seq", split_axis=1, concat_axis=2, tiled=True
        ),
    )
    unused_turn, reverse_rotation = jax.vjp(turn_all, qkv)
    grad_qkv = (
        reverse_rotation(tuple((member.astype(jnp.float32) for member in grad_parts)))[0]
        .astype(jnp.bfloat16)
        .reshape(flat_rows, 3 * width)
    )
    grad_qkv_weight = contract_rows(attn_low, grad_qkv)
    grad_attn_in = contract_cols(grad_qkv, full_qkv).reshape(seqs_here, row_count, width)
    unused_first, first_back = jax.vjp(adapt, source, gain_first, shift_attn, scale_attn)
    grad_source_norm, grad_gain_attn, grad_shift_attn, grad_scale_attn = first_back(grad_attn_in)
    grad_hidden = grad_middle + grad_source_norm
    grad_mod = jnp.concatenate(
        [
            grad_shift_attn,
            grad_scale_attn,
            grad_gate_attn,
            grad_shift_mlp,
            grad_scale_mlp,
            grad_gate_mlp,
        ],
        -1,
    )[:, 0, :]
    grad_ada = jnp.dot(grad_mod.T, cond, precision=highest_precision)
    grad_bias_mod = jnp.sum(grad_mod, 0)
    summed = (
        lax.psum_scatter(grad_qkv_weight, "fsdp", scatter_dimension=0, tiled=True),
        lax.psum_scatter(grad_attn_weight, "fsdp", scatter_dimension=0, tiled=True),
        lax.psum_scatter(grad_in, "fsdp", scatter_dimension=0, tiled=True),
        lax.psum_scatter(grad_down, "fsdp", scatter_dimension=0, tiled=True),
        lax.psum_scatter(grad_ada, "fsdp", scatter_dimension=0, tiled=True),
        lax.psum_scatter(grad_bias_mod, "fsdp", scatter_dimension=0, tiled=True),
        lax.psum_scatter(grad_gain_attn, "fsdp", scatter_dimension=0, tiled=True),
        lax.psum_scatter(grad_gain_mlp, "fsdp", scatter_dimension=0, tiled=True),
        lax.psum_scatter(grad_bias_in, "fsdp", scatter_dimension=0, tiled=True),
        lax.psum_scatter(grad_bias_down, "fsdp", scatter_dimension=0, tiled=True),
    )
    totals = (
        lax.psum(summed[0].astype(jnp.bfloat16), "seq").astype(jnp.float32),
        lax.psum(summed[1].astype(jnp.bfloat16), "seq").astype(jnp.float32),
        lax.psum(summed[2].astype(jnp.bfloat16), "seq").astype(jnp.float32),
        lax.psum(summed[3].astype(jnp.bfloat16), "seq").astype(jnp.float32),
        lax.psum(summed[4].astype(jnp.bfloat16), "seq").astype(jnp.float32),
        lax.psum(summed[5].astype(jnp.bfloat16), "seq").astype(jnp.float32),
        lax.psum(summed[6].astype(jnp.bfloat16), "seq").astype(jnp.float32),
        lax.psum(summed[7].astype(jnp.bfloat16), "seq").astype(jnp.float32),
        lax.psum(summed[8].astype(jnp.bfloat16), "seq").astype(jnp.float32),
        lax.psum(summed[9].astype(jnp.bfloat16), "seq").astype(jnp.float32),
    )
    return (output, grad_hidden) + tuple(totals)


AXES = ("seq", "fsdp")
SEQ_BIT, HALF_BIT, LOW_BIT, ROW_BIT, CORE_BIT = 16, 8, 4, 2, 1
STREAM = ((ROW_BIT, SEQ_BIT), (LOW_BIT, ROW_BIT), (SEQ_BIT, LOW_BIT))
TOKENS = ((LOW_BIT, LOW_BIT), (ROW_BIT, SEQ_BIT), (SEQ_BIT, ROW_BIT))
SHARED = ((LOW_BIT, LOW_BIT), (SEQ_BIT, SEQ_BIT), (ROW_BIT, ROW_BIT))
VMEM_LIMIT = 62 * 1024 * 1024


def swap_bits(values, even, odd=None):
    odd = even if odd is None else odd
    return lax.ppermute(values, AXES, [(i, i ^ (odd if i & 1 else even)) for i in range(32)])


def spread(values, order):
    for even, odd in order:
        values = jnp.concatenate([values, swap_bits(values, even, odd)], 0)
    return values


def collect(arrays, order):
    for even, odd in reversed(order):
        half = arrays[0].shape[0] // 2
        sent = jnp.concatenate([member[half:] for member in arrays], 1) if len(arrays) > 1 else arrays[0][half:]
        came = swap_bits(sent, even, odd)
        begin, summed = 0, []
        for member in arrays:
            part = came[:, begin : begin + member.shape[1]]
            begin += member.shape[1]
            summed.append((member[:half].astype(jnp.float32) + part.astype(jnp.float32)).astype(jnp.bfloat16))
        arrays = summed
    return arrays


def slot_masks(order, core):
    masks = [jnp.int32(0)]
    for even, odd in order:
        step = jnp.where(core == 0, even, odd).astype(jnp.int32)
        masks = masks + [mask ^ step for mask in masks]
    return jnp.stack(masks)


def quad_exchange(parts):
    came = swap_bits(parts[:, 1], ROW_BIT)
    parts = jnp.stack([parts[:, 0], came], 1)
    came = swap_bits(parts[1], LOW_BIT)
    return jnp.stack([parts[0], came], 0)


def after(values, *others):
    return lax.optimization_barrier((values,) + others)[0]


def pick(values, index, axis=0):
    return lax.dynamic_index_in_dim(values, index, axis, keepdims=False)


def pair_up(mine, other, position):
    return jnp.where(position == 0, jnp.stack([mine, other]), jnp.stack([other, mine]))


def dot_nn(left, right):
    return lax.dot_general(left, right, (((1,), (0,)), ((), ())), preferred_element_type=jnp.float32)


def row_norm(values):
    center = values - jnp.mean(values, -1, keepdims=True)
    return center * lax.rsqrt(jnp.mean(center * center, -1, keepdims=True) + 1e-05)


def head_select(width, head):
    lane = lax.broadcasted_iota(jnp.int32, (1, width), 1)
    return (lane % 128) // 32 == head


def vector_kernel(meta, cond, w_ada, bias_ada, gain_attn, gain_mlp, bias_in, bias_down, out):
    part = contract_cols(cond[...], w_ada[...])
    rest = part[0:2] + part[2:4] + part[4:6] + bias_ada[...].astype(jnp.float32)
    out[...] = jnp.zeros(out.shape, jnp.bfloat16)
    for row in range(3):
        rounded = rest.astype(jnp.bfloat16)
        rest = rest - rounded.astype(jnp.float32)
        out[row : row + 1, 0 : rest.shape[1]] = rounded[0:1]
        out[row + 3 : row + 4, 0 : rest.shape[1]] = rounded[1:2]
    for row, member in enumerate((gain_attn, gain_mlp, bias_in, bias_down)):
        out[6 + row : 7 + row, 0 : member.shape[1]] = member[...]


def share_kernel(meta, w_in, w_out, w_down, own, sent):
    core, side = meta[0], meta[1]
    lane = lax.broadcasted_iota(jnp.int32, (768, 384), 1)
    source = lax.broadcasted_iota(jnp.int32, (768, 384), 0)
    for target, which in ((own, core), (sent, 1 - core)):
        wanted = jnp.where(lane < 192, lane, lane + 192) + which * 192
        chosen = (source == wanted).astype(jnp.float32).astype(jnp.bfloat16)
        for i in range(4):
            target[i * 48 : (i + 1) * 48, :] = dot_nn(w_in[:, i * 768 : (i + 1) * 768], chosen).astype(jnp.bfloat16)
        target[192:240, :] = w_out[:, pl.ds(pl.multiple_of(which * 384, 128), 384)]
    rows = pl.ds(pl.multiple_of(side * 96, 32), 96)
    own[240:336, :] = w_down[rows, 0:384]
    own[336:432, :] = w_down[rows, 384:768]


def finish_kernel(meta, kept, came, source, grad_middle, vectors, stays, leaves):
    grad = kept[...].astype(jnp.float32) + came[...].astype(jnp.float32)
    center = source[...].astype(jnp.float32)
    center = center - jnp.mean(center, -1, keepdims=True)
    inverse = lax.rsqrt(jnp.mean(center * center, -1, keepdims=True) + 1e-05)
    norm = center * inverse
    scaled = grad * vectors[1:2, :] * vectors[0:1, :]
    result = grad_middle[...] + inverse * (
        scaled - jnp.mean(scaled, -1, keepdims=True) - norm * jnp.mean(scaled * norm, -1, keepdims=True)
    )
    half_way = stays.shape[0]
    stays[...] = result[:half_way]
    leaves[...] = result[half_way:].astype(jnp.bfloat16)


def order_weight_kernel(meta, own, other, chooser, out, gathered):
    for slot in range(16):
        start = pl.multiple_of(meta[48 + slot] * 48, 16)
        first = (slot % 8) * 48
        gathered[pl.ds(start, 48), :] = (own if slot < 8 else other)[first : first + 48, :]
    out[...] = dot_nn(gathered[...], chooser[...]).astype(jnp.bfloat16)


def project_kernel(
    meta, near, far, other_near, other_far, weight, vectors, cosine, sine, query_out, key_out, value_out, norm_out, all_queries
):
    step = pl.program_id(0)
    rows = near.shape[0]

    def project(source):
        norm = row_norm(source[...].astype(jnp.float32))
        norm_out[...] = norm.astype(jnp.bfloat16)
        attn_in = (norm * vectors[8:9, :] + vectors[2:3, :]).astype(jnp.bfloat16)
        packed = dot_nn(attn_in, weight[:, 256:768])
        first, second = packed[:, 0:128], packed[:, 128:256]
        turn_c, turn_s = cosine[...], sine[...]
        key_out[:, 0:128] = (first * turn_c - second * turn_s).astype(jnp.bfloat16)
        key_out[:, 128:256] = (second * turn_c + first * turn_s).astype(jnp.bfloat16)
        value_out[...] = packed[:, 256:512].astype(jnp.bfloat16)
        return attn_in

    def project_queries(attn_in):
        packed = dot_nn(attn_in, weight[:, 0:256]) * (HDIM ** (-0.5))
        first, second = packed[:, 0:128], packed[:, 128:256]
        turn_c, turn_s = cosine[...], sine[...]
        here = pl.ds(pl.multiple_of(step * rows, 256), rows)
        all_queries[here, 0:128] = (first * turn_c - second * turn_s).astype(jnp.bfloat16)
        all_queries[here, 128:256] = (second * turn_c + first * turn_s).astype(jnp.bfloat16)

    for number, source in enumerate((near, far, other_near, other_far)):

        @pl.when(step // 2 == number)
        def _(number=number, source=source):
            attn_in = project(source)
            if number < 2:
                project_queries(attn_in)

    @pl.when(step == 3)
    def _():
        block = query_out.shape[0] // 4
        stride = 1 + meta[64]
        for j in range(4):
            chosen = pl.ds(pl.multiple_of(((j >> 1) + (j & 1) * 2 * stride) * block, 128), block)
            query_out[j * block : (j + 1) * block, :] = all_queries[chosen, :]


def attend_kernel(meta, query_in, key_in, value_in, out_turned, log_out, out):
    block = query_in.shape[0] // 4
    keys = key_in[...]
    value_turned = value_in[...].T
    log_out[...] = jnp.zeros(log_out.shape, jnp.float32)
    out_turned[...] = jnp.zeros(out_turned.shape, jnp.float32)
    for head in range(3):
        for q_start in range(0, 4 * block, 256):
            here = slice(q_start, q_start + 256)
            query = query_in[here, :]
            query = jnp.where(head_select(256, head), query, jnp.zeros_like(query))
            scores = contract_cols(keys, query)
            best = jnp.max(scores, 0, keepdims=True)
            raised = jnp.exp(scores - best)
            total = jnp.sum(raised, 0, keepdims=True)
            mixed = dot_nn(value_turned[head * 64 : (head + 1) * 64, :], raised.astype(jnp.bfloat16))
            out_turned[head * 64 : (head + 1) * 64, here] = mixed / total
            log_out[head : head + 1, here] = best + jnp.log(total)
    turned_back = out_turned[...].T.astype(jnp.bfloat16)
    for j in range(4):
        out[j, :, :] = turned_back[j * block : (j + 1) * block, 0:192]


def attend_back_kernel(
    meta, cosine, sine, query_in, key_in, value_in, out_turned, log_in, grad_in, grad_packed, key_sum, value_sum
):
    block = query_in.shape[0] // 4
    stride = 1 + meta[64]
    keys, values = key_in[...], value_in[...]
    key_turned = keys.T
    lane_pad = jnp.zeros((4 * block, 64), jnp.bfloat16)
    grad_out = jnp.concatenate([jnp.concatenate([grad_in[j, :, :] for j in range(4)], 0), lane_pad], 1)
    grad_turned = grad_out.astype(jnp.float32).T
    key_sum[...] = jnp.zeros(key_sum.shape, jnp.float32)
    value_sum[...] = jnp.zeros(value_sum.shape, jnp.float32)
    product = grad_turned * out_turned[...]
    lane = lax.broadcasted_iota(jnp.int32, (1, 256), 1)
    query_parts = []
    for q_start in range(0, 4 * block, 256):
        here = slice(q_start, q_start + 256)
        query_sum = jnp.zeros((256, 256), jnp.float32)
        sub = lax.broadcasted_iota(jnp.int32, (256, 1), 0)
        for head in range(3):
            query = query_in[here, :]
            query = jnp.where(head_select(256, head), query, jnp.zeros_like(query))
            head_grad = grad_out[q_start : q_start + 256, :]
            head_grad = jnp.where(lane // 64 == head, head_grad, jnp.zeros_like(head_grad))
            probs = jnp.exp(contract_cols(keys, query) - log_in[head : head + 1, here])
            delta = jnp.sum(product[head * 64 : (head + 1) * 64, here], 0, keepdims=True)
            grad_scores = (probs * (contract_cols(values, head_grad) - delta)).astype(jnp.bfloat16)
            value_sum[...] += dot_nn(probs.astype(jnp.bfloat16), head_grad)
            key_sum[...] += dot_nn(grad_scores, query)
            part = dot_nn(key_turned, grad_scores)
            query_sum = jnp.where((sub % 128) // 32 == head, part, query_sum)
        query_parts.append(query_sum.T * (HDIM ** (-0.5)))
    for j in range(4):
        rows = pl.ds(pl.multiple_of(((j >> 1) + (j & 1) * 2 * stride) * block, 128), block)
        q_part = query_parts[(j * block) // 256][(j * block) % 256 : (j * block) % 256 + block, :]
        first, second = q_part[:, 0:128], q_part[:, 128:256]
        turn_c, turn_s = cosine[rows, :], sine[rows, :]
        here = slice(j * block, (j + 1) * block)
        grad_packed[here, 0:128] = (first * turn_c + second * turn_s).astype(jnp.bfloat16)
        grad_packed[here, 128:256] = (second * turn_c - first * turn_s).astype(jnp.bfloat16)


def project_back_kernel(
    meta, norm, weight, chooser, columns, cosine, sine, grad_packed, key_sum, value_sum,
    own_rows, other_rows, grad_weight, sums, grad_queries, weight_sum, total
):
    step = pl.program_id(0)
    rows = norm.shape[0]

    @pl.when(step == 0)
    def _():
        block = grad_packed.shape[0] // 4
        stride = 1 + meta[64]
        grad_queries[...] = jnp.zeros(grad_queries.shape, jnp.bfloat16)
        for j in range(4):
            chosen = pl.ds(pl.multiple_of(((j >> 1) + (j & 1) * 2 * stride) * block, 128), block)
            grad_queries[chosen, :] = grad_packed[j * block : (j + 1) * block, :]
        weight_sum[...] = jnp.zeros(weight_sum.shape, jnp.float32)
        total[...] = jnp.zeros(total.shape, jnp.float32)

    first, second = key_sum[:, 0:128], key_sum[:, 128:256]
    turn_c, turn_s = cosine[...], sine[...]
    pair = jnp.concatenate(
        [first * turn_c + second * turn_s, second * turn_c - first * turn_s, value_sum[...]], 1
    ).astype(jnp.bfloat16)
    ones = jnp.ones((8, rows), jnp.bfloat16)

    @pl.when(step < 4)
    def _():
        query = grad_queries[pl.ds(pl.multiple_of(step * rows, 256), rows), :]
        triple = jnp.concatenate([query, pair], 1)
        own_rows[...] = contract_cols(triple, weight[...]).astype(jnp.bfloat16)
        weight_sum[...] += contract_rows(norm[...], triple)
        total[...] += dot_nn(ones, triple)

    @pl.when(step >= 4)
    def _():
        other_rows[...] = contract_cols(pair, weight[:, 256:768]).astype(jnp.bfloat16)
        weight_sum[:, 256:768] += contract_rows(norm[...], pair)
        total[:, 256:768] += dot_nn(ones, pair)

    @pl.when(step == pl.num_programs(0) - 1)
    def _():
        summed = total[0:1, :]
        whole = columns[:, 0:1] * weight_sum[...] + columns[:, 1:2] * summed
        grad_weight[...] = contract_cols(whole.astype(jnp.bfloat16), chooser[...]).astype(jnp.bfloat16)
        plain = weight[...].astype(jnp.float32)
        sums[:, 0:1] = jnp.sum(plain * summed, 1, keepdims=True)
        sums[:, 1:2] = jnp.sum(plain * weight_sum[...], 1, keepdims=True)


def middle_kernel(
    meta, attended, near_a, near_b, far_a, far_b, other_near, other_far, own_rows, vectors, projected_out, middle_out, low_out,
    weight_out
):
    core = meta[64]
    mine = pl.multiple_of(core * 384, 128)
    theirs = pl.multiple_of(384 - core * 384, 128)
    for slot in range(16):
        rows_a = pl.ds(pl.multiple_of(meta[slot] * 48, 16), 48)
        rows_b = pl.ds(pl.multiple_of(meta[16 + slot] * 48, 16), 48)
        rows_p = pl.ds(pl.multiple_of(meta[32 + slot] * 48, 16), 48)
        part_a, part_b, other = (near_a, near_b, other_near) if slot < 8 else (far_a, far_b, other_far)
        weight_out[rows_a, pl.ds(mine, 256)] = part_a[slot % 8, :, :]
        weight_out[rows_b, pl.ds(pl.multiple_of(mine + 256, 128), 128)] = part_b[slot % 8, :, :]
        weight_out[rows_p, pl.ds(theirs, 256)] = other[slot % 8, :, 0:256]
        weight_out[rows_b, pl.ds(pl.multiple_of(theirs + 256, 128), 128)] = other[slot % 8, :, 256:384]
    projected = dot_nn(attended[...], weight_out[...])
    projected_out[...] = projected
    middle = own_rows[...].astype(jnp.float32) + vectors[3:4, :] * projected
    middle_out[...] = middle
    low_out[...] = (row_norm(middle) * vectors[4:5, :] * vectors[5:6, :] + vectors[6:7, :]).astype(jnp.bfloat16)


def mlp_kernel(
    meta, low_own, low_other, grad_own, grad_other, near_a, near_b, far_a, far_b, bias, sums_own, sums_other,
    keep_a, keep_b, send_a, send_b, grad_bias, weight_in, weight_down, grad_in, grad_down, branch, back
):
    for slot in range(16):
        part_a, part_b = (near_a, near_b) if slot < 8 else (far_a, far_b)
        for lane_start, size, part, index in ((0, 256, part_a, meta[slot]), (256, 128, part_b, meta[16 + slot])):
            rows = pl.ds(pl.multiple_of(index * 48, 16), 48)
            for i in range(4):
                lanes = slice(i * 384 + lane_start, i * 384 + lane_start + size)
                weight_in[rows, lanes] = part[slot % 8, i * 48 : (i + 1) * 48, :]
            rows = pl.ds(pl.multiple_of(index * 96, 16), 96)
            for i in range(2):
                lanes = slice(i * 384 + lane_start, i * 384 + lane_start + size)
                weight_down[rows, lanes] = part[slot % 8, 192 + i * 96 : 192 + (i + 1) * 96, :]
    low = jnp.concatenate([low_own[...], low_other[...]], 0)
    grad = jnp.concatenate([grad_own[...], grad_other[...]], 0)
    tokens = low_own.shape[0]
    branch[...] = jnp.zeros(branch.shape, jnp.float32)
    back[...] = jnp.zeros(back.shape, jnp.float32)
    root, cubic = math.sqrt(2.0 / math.pi), 0.044715
    for i in range(4):
        hidden = slice(i * 384, (i + 1) * 384)
        pre_act = dot_nn(low, weight_in[:, hidden]) + bias[:, hidden]
        square = pre_act * pre_act
        bend = jnp.tanh(root * (pre_act + cubic * square * pre_act))
        active = (0.5 * pre_act * (1.0 + bend)).astype(jnp.bfloat16)
        slope = 0.5 * (1.0 + bend) + 0.5 * pre_act * (1.0 - bend * bend) * (root * (1.0 + 3.0 * cubic * square))
        branch[...] += dot_nn(active, weight_down[hidden, :])
        grad_pre = (contract_cols(grad, weight_down[hidden, :]) * slope).astype(jnp.bfloat16)
        grad_bias[:, hidden] = jnp.sum(grad_pre.astype(jnp.float32), 0, keepdims=True)
        back[...] += contract_cols(grad_pre, weight_in[:, hidden])
        grad_in[:, hidden] = contract_rows(low, grad_pre).astype(jnp.bfloat16)
        grad_down[hidden, :] = contract_rows(active, grad).astype(jnp.bfloat16)
    sums_own[0, :, :] = branch[:tokens, :]
    sums_other[0, :, :] = branch[tokens:, :]
    sums_own[1, :, :] = back[:tokens, :]
    sums_other[1, :, :] = back[tokens:, :]
    for slot in range(16):
        part_a, part_b = (keep_a, keep_b) if slot < 8 else (send_a, send_b)
        for lane_start, size, part, index in ((0, 256, part_a, meta[slot]), (256, 128, part_b, meta[16 + slot])):
            rows = pl.ds(pl.multiple_of(index * 48, 16), 48)
            for i in range(4):
                lanes = slice(i * 384 + lane_start, i * 384 + lane_start + size)
                part[slot % 8, i * 48 : (i + 1) * 48, :] = grad_in[rows, lanes]
            rows = pl.ds(pl.multiple_of(index * 96, 16), 96)
            for i in range(2):
                lanes = slice(i * 384 + lane_start, i * 384 + lane_start + size)
                part[slot % 8, 192 + i * 96 : 192 + (i + 1) * 96, :] = grad_down[rows, lanes]


def turn_kernel(
    meta, sums_own, sums_other, bias, middle_in, projected_in, cotangent, grad_branch, weight,
    attended, vectors, output, grad_middle_out, grad_attn_out, grad_weight, sums
):
    width = middle_in.shape[1]
    branch = sums_own[0, :, :] + sums_other[0, :, :] + bias[...]
    middle = middle_in[...]
    grad = cotangent[...].astype(jnp.float32)
    output[...] = (middle + vectors[7:8, :] * branch).astype(jnp.bfloat16)
    back = sums_own[1, :, :] + sums_other[1, :, :]
    center = middle - jnp.mean(middle, -1, keepdims=True)
    inverse = lax.rsqrt(jnp.mean(center * center, -1, keepdims=True) + 1e-05)
    norm = center * inverse
    scaled = back * vectors[5:6, :] * vectors[4:5, :]
    grad_middle = grad + inverse * (
        scaled - jnp.mean(scaled, -1, keepdims=True) - norm * jnp.mean(scaled * norm, -1, keepdims=True)
    )
    grad_middle_out[...] = grad_middle
    grad_proj = (vectors[3:4, :] * grad_middle).astype(jnp.bfloat16)
    grad_attn_out[...] = contract_cols(grad_proj, weight[...]).astype(jnp.bfloat16)
    grad_weight[...] = contract_rows(attended[...], grad_proj).astype(jnp.bfloat16)
    def total(values):
        return jnp.sum(values, 0, keepdims=True)

    sums[...] = jnp.concatenate(
        [
            total(grad_middle * projected_in[...]),
            total(back),
            total(back * norm),
            total(grad * branch),
            total(grad_branch[...].astype(jnp.float32)),
            jnp.zeros((3, width), jnp.float32),
        ],
        0,
    )


def call(body, outs, args, scratch=(), grid=None, blocks=(), out_blocks=(), flops=0, moved=0):
    if grid is None:
        whole = pl.BlockSpec(memory_space=pltpu.VMEM)
        in_specs, out_specs = [whole] * len(args), [whole] * len(outs)
    else:
        blocks, out_blocks = dict(blocks), dict(out_blocks)

        def spec(shape, block):
            return block or pl.BlockSpec(shape, lambda i: (0,) * len(shape))

        in_specs = [spec(member.shape, blocks.get(k)) for k, member in enumerate(args)]
        out_specs = [spec(member[0], out_blocks.get(k)) for k, member in enumerate(outs)]
    in_specs[0] = pl.BlockSpec(memory_space=pltpu.SMEM)
    return pl.pallas_call(
        body,
        grid=() if grid is None else grid,
        out_shape=[jax.ShapeDtypeStruct(*member) for member in outs],
        in_specs=in_specs,
        out_specs=out_specs,
        scratch_shapes=[pltpu.VMEM(*member) for member in scratch],
        compiler_params=pltpu.CompilerParams(vmem_limit_bytes=VMEM_LIMIT),
        cost_estimate=pl.CostEstimate(flops=flops, bytes_accessed=moved, transcendentals=0),
    )(*args)


def cube_local(
    hidden_in, time_index, cotangent, w_qkv, w_attn_out, w_mlp_in, w_mlp_out, w_ada, bias_ada, gain_attn, gain_mlp,
    bias_mlp_in, bias_mlp_out
):
    f32, bf16 = jnp.float32, jnp.bfloat16
    rows, width = hidden_in.shape[1:]
    tokens = 2 * rows
    place = lax.axis_index("fsdp")
    side = lax.axis_index("seq")
    device = side * 16 + place
    core, half, group = place & 1, place >> 3, (place >> 1) & 3
    x_own = jnp.concatenate(
        [pick(hidden_in, half), swap_bits(pick(hidden_in, 1 - half), HALF_BIT)], 0
    )
    cond = jax.nn.silu(time_features(time_index, w_ada.shape[1]))
    cond_parts, rest = [], cond
    for _ in range(3):
        cond_parts.append(lax.reduce_precision(rest, 8, 7))
        rest = rest - cond_parts[-1]
    cond_parts = jnp.concatenate(cond_parts + [jnp.zeros_like(cond)], 0).astype(bf16)

    def double(values, bit):
        return jnp.concatenate([values, swap_bits(values, bit)], 0)

    (vector,) = call(
        vector_kernel,
        [((16, 576), bf16)],
        [jnp.zeros((1,), jnp.int32), cond_parts, w_ada]
        + [member[None] for member in (bias_ada, gain_attn, gain_mlp, bias_mlp_in, bias_mlp_out)],
    )
    grouped = w_qkv.reshape(48, 3, 4, 192).transpose(2, 0, 1, 3).reshape(4, 48, 576)
    grouped = grouped[group ^ jnp.arange(4)].reshape(192, 576)
    grouped = jnp.concatenate([grouped, vector], 0)
    x_own, grouped, w_mlp_in, w_attn_out, w_mlp_out = lax.optimization_barrier(
        (x_own, grouped, w_mlp_in, w_attn_out, w_mlp_out)
    )
    x_kept = x_own
    x_one = spread(x_own, TOKENS[:1])
    came_qkv = swap_bits(grouped, HALF_BIT)
    own_share, sent_share = call(
        share_kernel,
        [((432, 384), bf16), ((240, 384), bf16)],
        [jnp.stack([core, side]).astype(jnp.int32), w_mlp_in, w_attn_out, w_mlp_out],
    )
    came_share = swap_bits(sent_share, CORE_BIT)
    share = jnp.where(core == side, own_share[:240], came_share)
    share = jnp.concatenate([share[:192], own_share[240:], share[192:]], 0)
    x_one, share, place_kept = lax.optimization_barrier((x_one, share, place))
    x_two = spread(x_one, TOKENS[1:2])
    came_share = swap_bits(share, HALF_BIT)
    x_two, grouped, came_qkv = lax.optimization_barrier((x_two, grouped, came_qkv))
    x_far = swap_bits(x_two, *TOKENS[2])
    other_two = swap_bits(x_two, CORE_BIT)
    both_qkv = jnp.stack([grouped[:192], came_qkv[:192]]).reshape(2, 2, 2, 48, 576)
    vector = jnp.concatenate([grouped[192:], came_qkv[192:]], 0)
    got = swap_bits(jnp.concatenate([both_qkv[:, :, 1].reshape(192, 576), vector], 0), ROW_BIT)
    got, came_share, cotangent = lax.optimization_barrier((got, came_share, cotangent))
    both_qkv = jnp.stack([both_qkv[:, :, 0], got[:192].reshape(2, 2, 48, 576)])
    vector = jnp.concatenate([vector, got[192:]], 0)
    got = swap_bits(jnp.concatenate([both_qkv[:, :, 1].reshape(192, 576), vector], 0), LOW_BIT)
    share = jnp.stack([share, came_share])[None]
    part_a, part_b = spread(share[..., :256], STREAM[:1]), spread(share[..., 256:], SHARED[:1])
    x_far, got, part_a, part_b = lax.optimization_barrier((x_far, got, part_a, part_b))
    grouped = jnp.concatenate([both_qkv[:, :, 0].reshape(192, 576), got[:192], vector, got[192:]], 0)
    came_grouped = swap_bits(grouped, CORE_BIT)
    other_far = swap_bits(x_far, CORE_BIT)
    came_a, came_b = swap_bits(part_a, *STREAM[1]), swap_bits(part_b, *SHARED[1])
    apart = place ^ jnp.arange(16)
    vector = jnp.concatenate([grouped[384:], came_grouped[384:]], 0).reshape(16, 16, 576).astype(f32)
    vector = vector[((apart & 1) << 3) | (apart & 4) | (apart & 2) | (apart >> 3)]
    parts = [jnp.sum(vector[:, row : row + 3, :288], 1) for row in (0, 3)]
    parts += [vector[:, 6 + row, :size] for row, size in enumerate((48, 48, 192, 48))]
    modulation = jnp.stack([parts[0].reshape(6, width), parts[1].reshape(6, width)])
    shift_attn, scale_attn, gate_attn, shift_mlp, scale_mlp, gate_mlp = [
        row for row in pick(modulation, half)
    ]
    full_gain_attn, full_gain_mlp = parts[2].reshape(-1), parts[3].reshape(-1)
    bias_in = pick(parts[4].reshape(8, 2, 192), core, 1).reshape(1, -1)
    bias_down = parts[5].reshape(1, -1)
    vectors = jnp.stack(
        [full_gain_attn, 1.0 + scale_attn, shift_attn, gate_attn, full_gain_mlp, 1.0 + scale_mlp, shift_mlp, gate_mlp]
        + [full_gain_attn * (1.0 + scale_attn)]
    )
    columns = jnp.stack([vectors[8], shift_attn], 1)
    place = place_kept
    device, core = side * 16 + place, place & 1
    stream_own, stream_other = slot_masks(STREAM, core), slot_masks(STREAM, 1 - core)
    shared = slot_masks(SHARED, core)

    def weight_slots(masks):
        moved = ((masks & 6) | (masks >> 4))[:, None] ^ jnp.array([0, 8], jnp.int32)[None]
        return (((place & 14) + side) ^ moved).reshape(-1)

    quad = jnp.array([0, ROW_BIT, LOW_BIT, LOW_BIT | ROW_BIT], jnp.int32)
    oct_masks = (quad[:, None] ^ jnp.array([0, HALF_BIT], jnp.int32)).reshape(-1)
    row_slots = place ^ jnp.concatenate([oct_masks, oct_masks ^ CORE_BIT])
    meta = jnp.concatenate(
        [weight_slots(stream_own), weight_slots(shared), weight_slots(stream_other), row_slots, core[None]]
    ).astype(jnp.int32)
    blocks = jnp.concatenate(
        [device ^ slot_masks(TOKENS, core), device ^ CORE_BIT ^ slot_masks(TOKENS, 1 - core)]
    )
    blocks = jnp.stack([blocks, blocks ^ HALF_BIT], 1)
    inverse = jnp.exp(-math.log(10000.0) * (2 * (jnp.arange(128) % 32)).astype(f32) / HDIM)
    begin_angles = (blocks.reshape(-1) * rows).astype(f32)[:, None, None] * inverse
    inner_angles = jnp.arange(rows, dtype=jnp.int32).astype(f32)[:, None] * inverse
    begin_c, begin_s, inner_c, inner_s = [
        lax.optimization_barrier(member)
        for member in (jnp.cos(begin_angles), jnp.sin(begin_angles), jnp.cos(inner_angles), jnp.sin(inner_angles))
    ]
    cosine = (begin_c * inner_c - begin_s * inner_s).reshape(-1, 128)
    sine = (begin_s * inner_c + begin_c * inner_s).reshape(-1, 128)
    lane = jnp.arange(768) + (place >> 4)
    inner = lane % 128
    wanted = jnp.where(
        lane < 512,
        jnp.where(inner < 96, (lane // 256) * 192 + (inner // 32) * 64 + ((lane % 256) // 128) * 32 + inner % 32, -1),
        jnp.where(lane < 704, lane - 128, -1),
    )
    chooser = (jnp.arange(576)[:, None] == wanted[None, :]).astype(bf16)
    (weight_qkv,) = call(
        order_weight_kernel,
        [((768, 768), bf16)],
        [meta, grouped, came_grouped, chooser],
        [((768, 576), bf16)],
        flops=2 * 768 * 768 * 576,
        moved=3_000_000,
    )
    span = 16 * tokens
    chunk = 256

    def part_of(number, size):
        return pl.BlockSpec((chunk, size), lambda i: (jnp.clip(i - number * 2, 0, 1), 0))

    def rows_of(size):
        return pl.BlockSpec((chunk, size), lambda i: (i, 0))

    queries, keys, values, norms = call(
        project_kernel,
        [((4 * tokens, 256), bf16), ((span, 256), bf16), ((span, 256), bf16), ((span, width), bf16)],
        [meta, x_two, x_far, other_two, other_far, weight_qkv, vectors, cosine, sine],
        [((8 * tokens, 256), bf16)],
        grid=(8,),
        blocks=[(1 + number, part_of(number, width)) for number in range(4)] + [(7, rows_of(128)), (8, rows_of(128))],
        out_blocks=[(1, rows_of(256)), (2, rows_of(256)), (3, rows_of(width))],
        flops=2_000_000_000,
        moved=8_000_000,
    )
    keys, came_a, came_b = lax.optimization_barrier((keys, came_a, came_b))
    part_a, part_b = jnp.concatenate([part_a, came_a], 0), jnp.concatenate([part_b, came_b], 0)
    far_a, far_b = swap_bits(part_a, *STREAM[2]), swap_bits(part_b, *SHARED[2])
    part_a, part_b = part_a.reshape(8, 432, 256), part_b.reshape(8, 432, 128)
    other_near = swap_bits(jnp.concatenate([part_a[:, 384:], part_b[:, 384:]], 2), CORE_BIT)
    out_turned, log_total, heads_out = call(
        attend_kernel,
        [((256, 4 * tokens), f32), ((8, 4 * tokens), f32), ((4, tokens, 192), bf16)],
        [meta, queries, keys, values],
        flops=8_000_000_000,
        moved=4_000_000,
    )
    heads_out = heads_out.reshape(2, 2, tokens, 192)
    came = swap_bits(heads_out[:, 1], ROW_BIT)
    came, far_a, far_b = lax.optimization_barrier((came, far_a, far_b))
    heads_out = jnp.stack([heads_out[:, 0], came], 1)
    by_group = jnp.stack([heads_out[0], swap_bits(heads_out[1], LOW_BIT)], 0).reshape(4, tokens, 192)
    attended = by_group[group ^ jnp.arange(4)].transpose(1, 0, 2).reshape(tokens, width)
    far_a, far_b = far_a.reshape(8, 432, 256), far_b.reshape(8, 432, 128)
    other_out = swap_bits(jnp.concatenate([far_a[:, 384:], far_b[:, 384:]], 2), CORE_BIT)
    projected, middle, mlp_own, weight_out = call(
        middle_kernel,
        [((tokens, width), f32), ((tokens, width), f32), ((tokens, width), bf16), ((768, 768), bf16)],
        [meta, attended, part_a[:, 384:], part_b[:, 384:], far_a[:, 384:], far_b[:, 384:], other_near, other_out]
        + [x_kept, vectors],
        flops=150_000_000,
        moved=3_000_000,
    )
    grad_own = jnp.concatenate(
        [pick(cotangent, half), swap_bits(pick(cotangent, 1 - half), HALF_BIT)], 0
    )
    branch_grad = (gate_mlp[None] * grad_own.astype(f32)).astype(bf16)
    branch_grad_other = swap_bits(branch_grad, CORE_BIT)
    mlp_other = swap_bits(mlp_own, CORE_BIT)
    sums_own, sums_sent, keep_a, keep_b, send_a, send_b, grad_bias_in = call(
        mlp_kernel,
        [((2, tokens, width), f32)] * 2
        + [((8, 384, 256), bf16), ((8, 384, 128), bf16)] * 2
        + [((1, 1536), f32)],
        [meta, mlp_own, mlp_other, branch_grad, branch_grad_other, part_a, part_b, far_a, far_b, bias_in],
        [((768, 1536), bf16), ((1536, 768), bf16), ((768, 1536), bf16), ((1536, 768), bf16)]
        + [((2 * tokens, width), f32)] * 2,
        flops=3_600_000_000,
        moved=12_000_000,
    )
    came = swap_bits(sums_sent, CORE_BIT)

    def plus(left, right):
        return (left.astype(f32) + right.astype(f32)).astype(bf16)

    came_a, came_b = swap_bits(send_a, *STREAM[2]), swap_bits(send_b, *SHARED[2])
    output_rows, grad_middle, grad_attn, grad_w_out, sums_mlp = call(
        turn_kernel,
        [((tokens, width), bf16), ((tokens, width), f32), ((tokens, width), bf16), ((768, 768), bf16), ((8, width), f32)],
        [meta, sums_own, came, bias_down, middle, projected, grad_own, branch_grad, weight_out]
        + [attended, vectors],
        flops=300_000_000,
        moved=5_000_000,
    )

    grad_heads = grad_attn.reshape(tokens, 4, 192).transpose(1, 0, 2)[group ^ jnp.arange(4)]
    grad_heads = quad_exchange(grad_heads.reshape(2, 2, tokens, 192)).reshape(4, tokens, 192)
    grad_heads, grad_w_out, output_rows = lax.optimization_barrier((grad_heads, grad_w_out, output_rows))
    by_core = grad_w_out.reshape(8, 2, 48, width)
    sum_out = plus(pick(by_core, core, 1), swap_bits(pick(by_core, 1 - core, 1), CORE_BIT))
    output = pair_up(output_rows[:rows], swap_bits(output_rows[rows:], HALF_BIT), half)
    grad_packed, key_sum, value_sum = call(
        attend_back_kernel,
        [((4 * tokens, 256), bf16), ((span, 256), f32), ((span, 256), f32)],
        [meta, cosine, sine, queries, keys, values, out_turned, log_total, grad_heads],
        flops=14_000_000_000,
        moved=8_000_000,
    )
    key_sum, came_a, came_b, sum_out, output = lax.optimization_barrier((key_sum, came_a, came_b, sum_out, output))
    sum_a = plus(keep_a, came_a).reshape(4, 768, 256)
    sum_b = plus(keep_b, came_b).reshape(4, 768, 128)
    came_a, came_b = swap_bits(sum_a[2:], *STREAM[1]), swap_bits(sum_b[2:], *SHARED[1])
    y, z = (place >> 1) & 1, (place >> 2) & 1
    out_row = sum_out.reshape(2, 2, 2, 48, width)
    came_out = swap_bits(pick(out_row, 1 - y, 2), ROW_BIT)
    own_rows, other_rows, grad_qkv, sums_attn = call(
        project_back_kernel,
        [((8 * tokens, width), bf16)] * 2 + [((768, 576), bf16), ((width, 2), f32)],
        [meta, norms, weight_qkv, chooser, columns, cosine, sine, grad_packed, key_sum, value_sum],
        [((8 * tokens, 256), bf16), ((width, width), f32), ((8, width), f32)],
        grid=(8,),
        blocks=[(1, rows_of(width)), (5, rows_of(128)), (6, rows_of(128)), (8, rows_of(256)), (9, rows_of(256))],
        out_blocks=[
            (0, pl.BlockSpec((chunk, width), lambda i: (jnp.minimum(i, 3), 0))),
            (1, pl.BlockSpec((chunk, width), lambda i: (jnp.maximum(i - 4, 0), 0))),
        ],
        flops=6_000_000_000,
        moved=16_000_000,
    )
    own_rows, other_rows, grad_qkv, sums_attn, came_a, came_b, came_out = lax.optimization_barrier(
        (own_rows, other_rows, grad_qkv, sums_attn, came_a, came_b, came_out)
    )
    own_rows = own_rows.reshape(8, tokens, width)
    came_rows = swap_bits(other_rows, CORE_BIT).reshape(8, tokens, width)
    small = jnp.concatenate([sums_attn.T, sums_mlp[0:5]], 0)
    small = jnp.concatenate([small + swap_bits(small, CORE_BIT), grad_bias_in.reshape(2, width)], 0)
    by_core = grad_qkv.reshape(8, 2, 48, 576)
    kept = plus(pick(by_core, core, 1), swap_bits(pick(by_core, 1 - core, 1), CORE_BIT))
    sum_a, sum_b = plus(sum_a[:2], came_a), plus(sum_b[:2], came_b)
    sum_out = plus(pick(out_row, y, 2), came_out)
    came_a, came_b = swap_bits(sum_a[1], *STREAM[0]), swap_bits(sum_b[1], *SHARED[0])

    def sum_step(own, came, small, order):
        half_way = own.shape[0] // 2
        sent = plus(own[half_way:], came[half_way:]).reshape(-1, width)
        high = jnp.pad(small, ((0, 7), (0, 0))).astype(bf16)
        low = (jnp.pad(small, ((0, 7), (0, 0))) - high.astype(f32)).astype(bf16)
        got = swap_bits(jnp.concatenate([sent, high, low], 0), *order)
        count = sent.shape[0]
        small = small + got[count : count + 9].astype(f32) + got[count + 16 : count + 25].astype(f32)
        return plus(own[:half_way], came[:half_way]), got[:count].reshape(half_way, tokens, width), small

    came_rows, small, kept, came_a, came_b = lax.optimization_barrier((came_rows, small, kept, came_a, came_b))
    own_rows, came_rows, small = sum_step(own_rows, came_rows, small, TOKENS[2])

    def with_out(of_qkv, of_out):
        count = of_qkv.size // 576
        blocks = count * width // of_out.size
        of_out = of_out.reshape(-1, blocks, width // blocks).transpose(1, 0, 2).reshape(count, -1)
        return jnp.concatenate([of_qkv.reshape(count, 576), of_out], 1)

    def without(got, of_qkv, of_out):
        blocks = width // (got.shape[1] - 576)
        out = got[:, 576:].reshape(blocks, -1, width // blocks).transpose(1, 0, 2).reshape(of_out.shape)
        return got[:, :576].reshape(of_qkv.shape), out

    sum_a, sum_b = plus(sum_a[0], came_a).reshape(2, 384, 256), plus(sum_b[0], came_b).reshape(2, 384, 128)
    total = jnp.concatenate([sum_a, sum_b], 2)
    came_total = swap_bits(total[1], HALF_BIT)
    by_row = kept.reshape(2, 2, 2, 48, 576)
    by_row = jnp.stack([pick(by_row, y, 2), swap_bits(pick(by_row, 1 - y, 2), ROW_BIT)])
    came_rows, by_row, sum_out, small, came_total = lax.optimization_barrier(
        (came_rows, by_row, sum_out, small, came_total)
    )
    total = plus(total[0], came_total)
    across = swap_bits(total, SEQ_BIT)
    own_rows, came_rows, small = sum_step(own_rows, came_rows, small, TOKENS[1])
    sent = pick(by_row, 1 - z, 2), pick(sum_out, 1 - z, 1)
    got = without(swap_bits(with_out(*sent), LOW_BIT), *sent)
    kept, sum_out = jnp.stack([pick(by_row, z, 2), got[0]]), plus(pick(sum_out, z, 1), got[1])
    came_rows, kept, small, sum_out, across = lax.optimization_barrier((came_rows, kept, small, sum_out, across))
    mine = jnp.where(core == side, total[:192], across[:192])
    theirs = swap_bits(jnp.where(core == side, across[:192], total[:192]), CORE_BIT)
    own_rows, came_rows, small = sum_step(own_rows, came_rows, small, TOKENS[0])
    by_half = kept.reshape(4, 2, 48, 576)
    sent = pick(by_half, 1 - half, 1), pick(sum_out, 1 - half)
    got = without(swap_bits(with_out(*sent), HALF_BIT), *sent)
    kept, sum_out = plus(pick(by_half, half, 1), got[0]), plus(pick(sum_out, half), got[1])
    came_rows, kept, sum_out, small, theirs = lax.optimization_barrier((came_rows, kept, sum_out, small, theirs))
    stays, leaves = call(
        finish_kernel,
        [((rows, width), f32), ((rows, width), bf16)],
        [jnp.zeros((1,), jnp.int32), own_rows[0], came_rows[0], x_kept, grad_middle, vectors],
    )
    grad_hidden = pair_up(stays, swap_bits(leaves, HALF_BIT).astype(f32), half)

    grad_down = pair_up(total[192:], across[192:], side).reshape(2, 2, 96, 384)
    grad_down = grad_down.transpose(0, 2, 1, 3).reshape(192, 768).astype(f32)
    def in_columns_back(blocks):
        return blocks.reshape(4, 48, 384).transpose(1, 0, 2).reshape(48, 8, 192)

    grad_w_in = pair_up(in_columns_back(mine), in_columns_back(theirs), core)
    grad_w_in = grad_w_in.transpose(1, 2, 0, 3).reshape(48, 3072).astype(f32)
    kept = kept[group ^ jnp.arange(4)].reshape(4, 48, 3, 192).transpose(1, 2, 0, 3).reshape(48, 2304)
    kept = jnp.concatenate([kept, sum_out], 1)
    came_kept, came_small = swap_bits(kept, SEQ_BIT), swap_bits(small, HALF_BIT)
    came_kept, came_small = lax.optimization_barrier((came_kept, came_small))
    kept = kept.astype(f32) + came_kept.astype(f32)
    grad_w_qkv, grad_w_out = kept[:, :2304], kept[:, 2304:]
    both = pair_up(small, came_small, half)
    plus_scale = 1.0 + modulation[:, 1], 1.0 + modulation[:, 4]
    grad_mod = jnp.stack(
        [both[:, 0], both[:, 1] * full_gain_attn, both[:, 2], both[:, 3], both[:, 4] * full_gain_mlp, both[:, 5]], 1
    ).reshape(2, 16, 288)
    grad_mod = pick(grad_mod, place, 1)
    grad_ada = grad_mod[0][:, None] * cond[0][None] + grad_mod[1][:, None] * cond[1][None]
    gain_first = pick(jnp.sum(both[:, 1] * plus_scale[0], 0).reshape(16, 48), place)
    gain_second = pick(jnp.sum(both[:, 4] * plus_scale[1], 0).reshape(16, 48), place)
    summed = both[0] + both[1]
    bias_in_grad = pick(summed[7:9].reshape(8, 192), place >> 1)
    bias_down_grad = pick(summed[6].reshape(16, 48), place)
    return (
        output,
        grad_hidden,
        grad_w_qkv,
        grad_w_out,
        grad_w_in,
        grad_down,
        grad_ada,
        jnp.sum(grad_mod, 0),
        gain_first,
        gain_second,
        bias_in_grad,
        bias_down_grad,
    )


def solution(mesh):
    return jax.shard_map(
        cube_local if dict(mesh.shape) == {"seq": 2, "fsdp": 16} else local,
        mesh=mesh,
        in_specs=(
            P(None, ("seq", "fsdp"), None),
            P(),
            P(None, ("seq", "fsdp"), None),
            P("fsdp", None),
            P("fsdp", None),
            P("fsdp", None),
            P("fsdp", None),
            P("fsdp", None),
            P("fsdp"),
            P("fsdp"),
            P("fsdp"),
            P("fsdp"),
            P("fsdp"),
        ),
        out_specs=(
            P(None, ("seq", "fsdp"), None),
            P(None, ("seq", "fsdp"), None),
            P("fsdp", None),
            P("fsdp", None),
            P("fsdp", None),
            P("fsdp", None),
            P("fsdp", None),
            P("fsdp"),
            P("fsdp"),
            P("fsdp"),
            P("fsdp"),
            P("fsdp"),
        ),
        check_vma=False,
    )
```

```python
import math

import jax
import jax.numpy as jnp
from jax import lax
from jax.experimental import pallas as pl
from jax.experimental.pallas import tpu as pltpu
from jax.sharding import PartitionSpec as P

HEADS = 12
HDIM = 64


highest_precision = lax.Precision.HIGHEST


def normalize(values):
    center = values - jnp.mean(values, -1, keepdims=True)
    return center * lax.rsqrt(jnp.mean(center * center, -1, keepdims=True) + 1e-05)


def adapt(values, gain, shift, scale):
    return normalize(values) * gain * (1.0 + scale) + shift


def time_features(time_index, width):
    half_width = width // 2
    frequency = jnp.exp(-math.log(10000.0) * jnp.arange(half_width, dtype=jnp.float32) / half_width)
    angles = time_index.astype(jnp.float32)[:, None] * frequency[None, :]
    return jnp.concatenate([jnp.cos(angles), jnp.sin(angles)], -1)


def rotary_tables(positions, head_dim):
    inverse = jnp.exp(-math.log(10000.0) * jnp.arange(0, head_dim, 2, dtype=jnp.float32) / head_dim)
    angles = positions.astype(jnp.float32)[:, None] * inverse[None, :]
    angles = jnp.concatenate([angles, angles], -1)
    return (jnp.cos(angles), jnp.sin(angles))


def rotate(values, cosine, sine):
    first_half, second_half = jnp.split(values, 2, axis=-1)
    turned = jnp.concatenate([-second_half, first_half], -1)
    return values * cosine[:, None, :] + turned * sine[:, None, :]


def contract_rows(left_neighbor, right_neighbor):
    return lax.dot_general(
        left_neighbor, right_neighbor, (((0,), (0,)), ((), ())), preferred_element_type=jnp.float32
    )


def contract_cols(left_neighbor, right_neighbor):
    return lax.dot_general(
        left_neighbor, right_neighbor, (((1,), (1,)), ((), ())), preferred_element_type=jnp.float32
    )


def gelu_tanh(values):
    return jax.nn.gelu(values, approximate=True)


def local(
    hidden_in,
    time_index,
    cotangent,
    w_qkv,
    w_attn_out,
    w_mlp_in,
    w_mlp_out,
    w_ada,
    bias_ada,
    gain_attn,
    gain_mlp,
    bias_mlp_in,
    bias_mlp_out,
):
    seqs_here, row_count, width = hidden_in.shape
    flat_rows = seqs_here * row_count
    gathered = (
        lax.all_gather(w_qkv, "fsdp", axis=0, tiled=True),
        lax.all_gather(w_attn_out, "fsdp", axis=0, tiled=True),
        lax.all_gather(w_mlp_in, "fsdp", axis=0, tiled=True),
        lax.all_gather(w_mlp_out, "fsdp", axis=0, tiled=True),
        lax.all_gather(w_ada, "fsdp", axis=0, tiled=True),
        lax.all_gather(bias_ada, "fsdp", axis=0, tiled=True),
        lax.all_gather(gain_attn, "fsdp", axis=0, tiled=True),
        lax.all_gather(gain_mlp, "fsdp", axis=0, tiled=True),
        lax.all_gather(bias_mlp_in, "fsdp", axis=0, tiled=True),
        lax.all_gather(bias_mlp_out, "fsdp", axis=0, tiled=True),
    )
    (
        full_qkv,
        gathered_output,
        full_in,
        full_down,
        full_ada,
        full_bias_ada,
        full_gain_attn,
        full_gain_mlp,
        full_bias_in,
        full_bias_down,
    ) = gathered
    gain_first = full_gain_attn.astype(jnp.float32)
    gain_second = full_gain_mlp.astype(jnp.float32)
    cond = jax.nn.silu(time_features(time_index, full_ada.shape[1]))
    modulation = jnp.dot(
        cond, full_ada.astype(jnp.float32).T, precision=highest_precision
    ) + full_bias_ada.astype(jnp.float32)
    shift_attn, scale_attn, gate_attn, shift_mlp, scale_mlp, gate_mlp = jnp.split(
        modulation[:, None, :], 6, axis=-1
    )
    source = hidden_in.astype(jnp.float32)
    attn_in = adapt(source, gain_first, shift_attn, scale_attn)
    attn_low = attn_in.astype(jnp.bfloat16).reshape(flat_rows, width)
    qkv = jnp.dot(attn_low, full_qkv, preferred_element_type=jnp.float32).reshape(
        seqs_here, row_count, 3 * width
    )
    device_number = lax.axis_index("seq") * lax.axis_size("fsdp") + lax.axis_index("fsdp")
    positions = device_number * row_count + jnp.arange(row_count, dtype=jnp.int32)
    cosine, sine = rotary_tables(positions, HDIM)

    def turn_all(packed):
        split_three = packed.reshape(seqs_here, row_count, 3, HEADS, HDIM)
        query_turned = rotate(split_three[:, :, 0], cosine, sine).reshape(
            seqs_here, row_count, width
        )
        key_turned = rotate(split_three[:, :, 1], cosine, sine).reshape(seqs_here, row_count, width)
        return (query_turned, key_turned, split_three[:, :, 2].reshape(seqs_here, row_count, width))

    query_rot, key_rot, value_raw = turn_all(qkv)
    queries, keys, values = (
        lax.all_to_all(
            query_rot.astype(jnp.bfloat16), "seq", split_axis=2, concat_axis=1, tiled=True
        ),
        lax.all_to_all(
            key_rot.astype(jnp.bfloat16), "seq", split_axis=2, concat_axis=1, tiled=True
        ),
        lax.all_to_all(
            value_raw.astype(jnp.bfloat16), "seq", split_axis=2, concat_axis=1, tiled=True
        ),
    )
    local_heads = HEADS // lax.axis_size("seq")
    span = queries.shape[1]
    query_heads = queries.reshape(seqs_here, span, local_heads, HDIM)
    scale = HDIM ** (-0.5)

    def score_block(key_piece):
        key_heads = key_piece.reshape(seqs_here, key_piece.shape[1], local_heads, HDIM)
        logits = (
            jnp.einsum(
                "sqhd,skhd->shqk", query_heads, key_heads, preferred_element_type=jnp.float32
            )
            * scale
        )
        return (logits, key_heads)

    pieces = (
        lax.all_gather(keys, "fsdp", axis=1, tiled=True),
        lax.all_gather(values, "fsdp", axis=1, tiled=True),
    )
    best = jnp.full((seqs_here, local_heads, span), -1e30, jnp.float32)
    logits, unused = score_block(pieces[0])
    value_heads = pieces[1].reshape(seqs_here, pieces[1].shape[1], local_heads, HDIM)
    newest = jnp.maximum(best, jnp.max(logits, -1))
    raised = jnp.exp(logits - newest[..., None])
    total = jnp.sum(raised, -1)
    accum = jnp.einsum(
        "shqk,skhd->sqhd",
        raised.astype(jnp.bfloat16),
        value_heads,
        preferred_element_type=jnp.float32,
    )
    best, total, accum = (newest, total, accum)
    log_total = best + jnp.log(total)
    attended = accum / jnp.transpose(total, (0, 2, 1))[..., None]
    attended_low = attended.reshape(seqs_here, span, local_heads * HDIM).astype(jnp.bfloat16)
    attn_rows = lax.all_to_all(attended_low, "seq", split_axis=1, concat_axis=2, tiled=True)
    attn_flat = attn_rows.reshape(flat_rows, width)
    projected = jnp.dot(attn_flat, gathered_output, preferred_element_type=jnp.float32).reshape(
        seqs_here, row_count, width
    )
    middle = source + gate_attn * projected
    mlp_in = adapt(middle, gain_second, shift_mlp, scale_mlp)
    mlp_low = mlp_in.astype(jnp.bfloat16).reshape(flat_rows, width)
    pre_act = jnp.dot(mlp_low, full_in, preferred_element_type=jnp.float32) + full_bias_in.astype(
        jnp.float32
    )
    active = gelu_tanh(pre_act).astype(jnp.bfloat16)
    branch = (
        jnp.dot(active, full_down, preferred_element_type=jnp.float32)
        + full_bias_down.astype(jnp.float32)
    ).reshape(seqs_here, row_count, width)
    output = (middle + gate_mlp * branch).astype(jnp.bfloat16)
    grad_result = cotangent.astype(jnp.float32)
    grad_gate_mlp = jnp.sum(grad_result * branch, 1, keepdims=True)
    grad_branch = (gate_mlp * grad_result).astype(jnp.bfloat16).reshape(flat_rows, width)
    grad_bias_down = jnp.sum(grad_branch.astype(jnp.float32), 0)
    grad_down = contract_rows(active, grad_branch)
    grad_active = contract_cols(grad_branch, full_down)
    unused_gelu, gelu_back = jax.vjp(gelu_tanh, pre_act)
    grad_pre = gelu_back(grad_active)[0].astype(jnp.bfloat16)
    grad_bias_in = jnp.sum(grad_pre.astype(jnp.float32), 0)
    grad_in = contract_rows(mlp_low, grad_pre)
    grad_mlp_in = contract_cols(grad_pre, full_in).reshape(seqs_here, row_count, width)
    unused_second, second_back = jax.vjp(adapt, middle, gain_second, shift_mlp, scale_mlp)
    grad_middle_norm, grad_gain_mlp, grad_shift_mlp, grad_scale_mlp = second_back(grad_mlp_in)
    grad_middle = grad_result + grad_middle_norm
    grad_gate_attn = jnp.sum(grad_middle * projected, 1, keepdims=True)
    grad_proj = (gate_attn * grad_middle).astype(jnp.bfloat16).reshape(flat_rows, width)
    grad_attn_weight = contract_rows(attn_flat, grad_proj)
    grad_attn_rows = (
        contract_cols(grad_proj, gathered_output)
        .astype(jnp.bfloat16)
        .reshape(seqs_here, row_count, width)
    )
    grad_heads = lax.all_to_all(grad_attn_rows, "seq", split_axis=2, concat_axis=1, tiled=True)
    grad_head_parts = grad_heads.reshape(seqs_here, span, local_heads, HDIM)
    delta = jnp.transpose(jnp.sum(grad_head_parts.astype(jnp.float32) * attended, -1), (0, 2, 1))
    pieces = (
        lax.all_gather(keys, "fsdp", axis=1, tiled=True),
        lax.all_gather(values, "fsdp", axis=1, tiled=True),
    )
    logits, key_heads = score_block(pieces[0])
    piece_rows = pieces[1].shape[1]
    value_heads = pieces[1].reshape(seqs_here, piece_rows, local_heads, HDIM)
    probs = jnp.exp(logits - log_total[..., None])
    grad_weights = jnp.einsum(
        "sqhd,skhd->shqk", grad_head_parts, value_heads, preferred_element_type=jnp.float32
    )
    probs, grad_logits = (probs, (probs * (grad_weights - delta[..., None])).astype(jnp.bfloat16))
    grad_query = (
        jnp.einsum("shqk,skhd->sqhd", grad_logits, key_heads, preferred_element_type=jnp.float32)
        * scale
    )
    key_part = (
        jnp.einsum("shqk,sqhd->skhd", grad_logits, query_heads, preferred_element_type=jnp.float32)
        * scale
    )
    value_part = jnp.einsum(
        "shqk,sqhd->skhd",
        probs.astype(jnp.bfloat16),
        grad_head_parts,
        preferred_element_type=jnp.float32,
    )
    grad_key_all = key_part.reshape(seqs_here, piece_rows, local_heads * HDIM)
    grad_value_all = value_part.reshape(seqs_here, piece_rows, local_heads * HDIM)
    folded_rows = (grad_query, grad_key_all, grad_value_all)
    grad_query, grad_key_all, grad_value_all = folded_rows
    grad_keys, grad_values = (
        lax.psum_scatter(grad_key_all, "fsdp", scatter_dimension=1, tiled=True),
        lax.psum_scatter(grad_value_all, "fsdp", scatter_dimension=1, tiled=True),
    )
    grad_parts = (
        lax.all_to_all(
            grad_query.reshape(seqs_here, span, local_heads * HDIM).astype(jnp.bfloat16),
            "seq",
            split_axis=1,
            concat_axis=2,
            tiled=True,
        ),
        lax.all_to_all(
            grad_keys.astype(jnp.bfloat16), "seq", split_axis=1, concat_axis=2, tiled=True
        ),
        lax.all_to_all(
            grad_values.astype(jnp.bfloat16), "seq", split_axis=1, concat_axis=2, tiled=True
        ),
    )
    unused_turn, reverse_rotation = jax.vjp(turn_all, qkv)
    grad_qkv = (
        reverse_rotation(tuple((member.astype(jnp.float32) for member in grad_parts)))[0]
        .astype(jnp.bfloat16)
        .reshape(flat_rows, 3 * width)
    )
    grad_qkv_weight = contract_rows(attn_low, grad_qkv)
    grad_attn_in = contract_cols(grad_qkv, full_qkv).reshape(seqs_here, row_count, width)
    unused_first, first_back = jax.vjp(adapt, source, gain_first, shift_attn, scale_attn)
    grad_source_norm, grad_gain_attn, grad_shift_attn, grad_scale_attn = first_back(grad_attn_in)
    grad_hidden = grad_middle + grad_source_norm
    grad_mod = jnp.concatenate(
        [
            grad_shift_attn,
            grad_scale_attn,
            grad_gate_attn,
            grad_shift_mlp,
            grad_scale_mlp,
            grad_gate_mlp,
        ],
        -1,
    )[:, 0, :]
    grad_ada = jnp.dot(grad_mod.T, cond, precision=highest_precision)
    grad_bias_mod = jnp.sum(grad_mod, 0)
    summed = (
        lax.psum_scatter(grad_qkv_weight, "fsdp", scatter_dimension=0, tiled=True),
        lax.psum_scatter(grad_attn_weight, "fsdp", scatter_dimension=0, tiled=True),
        lax.psum_scatter(grad_in, "fsdp", scatter_dimension=0, tiled=True),
        lax.psum_scatter(grad_down, "fsdp", scatter_dimension=0, tiled=True),
        lax.psum_scatter(grad_ada, "fsdp", scatter_dimension=0, tiled=True),
        lax.psum_scatter(grad_bias_mod, "fsdp", scatter_dimension=0, tiled=True),
        lax.psum_scatter(grad_gain_attn, "fsdp", scatter_dimension=0, tiled=True),
        lax.psum_scatter(grad_gain_mlp, "fsdp", scatter_dimension=0, tiled=True),
        lax.psum_scatter(grad_bias_in, "fsdp", scatter_dimension=0, tiled=True),
        lax.psum_scatter(grad_bias_down, "fsdp", scatter_dimension=0, tiled=True),
    )
    totals = (
        lax.psum(summed[0].astype(jnp.bfloat16), "seq").astype(jnp.float32),
        lax.psum(summed[1].astype(jnp.bfloat16), "seq").astype(jnp.float32),
        lax.psum(summed[2].astype(jnp.bfloat16), "seq").astype(jnp.float32),
        lax.psum(summed[3].astype(jnp.bfloat16), "seq").astype(jnp.float32),
        lax.psum(summed[4].astype(jnp.bfloat16), "seq").astype(jnp.float32),
        lax.psum(summed[5].astype(jnp.bfloat16), "seq").astype(jnp.float32),
        lax.psum(summed[6].astype(jnp.bfloat16), "seq").astype(jnp.float32),
        lax.psum(summed[7].astype(jnp.bfloat16), "seq").astype(jnp.float32),
        lax.psum(summed[8].astype(jnp.bfloat16), "seq").astype(jnp.float32),
        lax.psum(summed[9].astype(jnp.bfloat16), "seq").astype(jnp.float32),
    )
    return (output, grad_hidden) + tuple(totals)


AXES = ("seq", "fsdp")
SEQ_BIT, HALF_BIT, LOW_BIT, ROW_BIT, CORE_BIT = 16, 8, 4, 2, 1
STREAM = ((ROW_BIT, SEQ_BIT), (LOW_BIT, ROW_BIT), (SEQ_BIT, LOW_BIT))
TOKENS = ((LOW_BIT, LOW_BIT), (ROW_BIT, SEQ_BIT), (SEQ_BIT, ROW_BIT))
SHARED = ((LOW_BIT, LOW_BIT), (SEQ_BIT, SEQ_BIT), (ROW_BIT, ROW_BIT))
VMEM_LIMIT = 62 * 1024 * 1024


def swap_bits(values, even, odd=None):
    odd = even if odd is None else odd
    return lax.ppermute(values, AXES, [(i, i ^ (odd if i & 1 else even)) for i in range(32)])


def spread(values, order):
    for even, odd in order:
        values = jnp.concatenate([values, swap_bits(values, even, odd)], 0)
    return values


def collect(arrays, order):
    for even, odd in reversed(order):
        half = arrays[0].shape[0] // 2
        sent = jnp.concatenate([member[half:] for member in arrays], 1) if len(arrays) > 1 else arrays[0][half:]
        came = swap_bits(sent, even, odd)
        begin, summed = 0, []
        for member in arrays:
            part = came[:, begin : begin + member.shape[1]]
            begin += member.shape[1]
            summed.append((member[:half].astype(jnp.float32) + part.astype(jnp.float32)).astype(jnp.bfloat16))
        arrays = summed
    return arrays


def slot_masks(order, core):
    masks = [jnp.int32(0)]
    for even, odd in order:
        step = jnp.where(core == 0, even, odd).astype(jnp.int32)
        masks = masks + [mask ^ step for mask in masks]
    return jnp.stack(masks)


def quad_exchange(parts):
    came = swap_bits(parts[:, 1], ROW_BIT)
    parts = jnp.stack([parts[:, 0], came], 1)
    came = swap_bits(parts[1], LOW_BIT)
    return jnp.stack([parts[0], came], 0)


def after(values, *others):
    return lax.optimization_barrier((values,) + others)[0]


def pick(values, index, axis=0):
    return lax.dynamic_index_in_dim(values, index, axis, keepdims=False)


def pair_up(mine, other, position):
    return jnp.where(position == 0, jnp.stack([mine, other]), jnp.stack([other, mine]))


def dot_nn(left, right):
    return lax.dot_general(left, right, (((1,), (0,)), ((), ())), preferred_element_type=jnp.float32)


def row_norm(values):
    center = values - jnp.mean(values, -1, keepdims=True)
    return center * lax.rsqrt(jnp.mean(center * center, -1, keepdims=True) + 1e-05)


def head_select(width, head):
    lane = lax.broadcasted_iota(jnp.int32, (1, width), 1)
    return (lane % 128) // 32 == head


def vector_kernel(meta, cond, w_ada, bias_ada, gain_attn, gain_mlp, bias_in, bias_down, out):
    part = contract_cols(cond[...], w_ada[...])
    rest = part[0:2] + part[2:4] + part[4:6] + bias_ada[...].astype(jnp.float32)
    out[...] = jnp.zeros(out.shape, jnp.bfloat16)
    for row in range(3):
        rounded = rest.astype(jnp.bfloat16)
        rest = rest - rounded.astype(jnp.float32)
        out[row : row + 1, 0 : rest.shape[1]] = rounded[0:1]
        out[row + 3 : row + 4, 0 : rest.shape[1]] = rounded[1:2]
    for row, member in enumerate((gain_attn, gain_mlp, bias_in, bias_down)):
        out[6 + row : 7 + row, 0 : member.shape[1]] = member[...]


def share_kernel(meta, w_in, w_out, w_down, own, sent):
    core, side = meta[0], meta[1]
    lane = lax.broadcasted_iota(jnp.int32, (768, 384), 1)
    source = lax.broadcasted_iota(jnp.int32, (768, 384), 0)
    for target, which in ((own, core), (sent, 1 - core)):
        wanted = jnp.where(lane < 192, lane, lane + 192) + which * 192
        chosen = (source == wanted).astype(jnp.float32).astype(jnp.bfloat16)
        for i in range(4):
            target[i * 48 : (i + 1) * 48, :] = dot_nn(w_in[:, i * 768 : (i + 1) * 768], chosen).astype(jnp.bfloat16)
        target[192:240, :] = w_out[:, pl.ds(pl.multiple_of(which * 384, 128), 384)]
    rows = pl.ds(pl.multiple_of(side * 96, 32), 96)
    own[240:336, :] = w_down[rows, 0:384]
    own[336:432, :] = w_down[rows, 384:768]


def finish_kernel(meta, kept, came, source, grad_middle, vectors, stays, leaves):
    grad = kept[...].astype(jnp.float32) + came[...].astype(jnp.float32)
    center = source[...].astype(jnp.float32)
    center = center - jnp.mean(center, -1, keepdims=True)
    inverse = lax.rsqrt(jnp.mean(center * center, -1, keepdims=True) + 1e-05)
    norm = center * inverse
    scaled = grad * vectors[1:2, :] * vectors[0:1, :]
    result = grad_middle[...] + inverse * (
        scaled - jnp.mean(scaled, -1, keepdims=True) - norm * jnp.mean(scaled * norm, -1, keepdims=True)
    )
    half_way = stays.shape[0]
    stays[...] = result[:half_way]
    leaves[...] = result[half_way:].astype(jnp.bfloat16)


def order_weight_kernel(meta, own, other, chooser, out, gathered):
    for slot in range(16):
        start = pl.multiple_of(meta[48 + slot] * 48, 16)
        first = (slot % 8) * 48
        gathered[pl.ds(start, 48), :] = (own if slot < 8 else other)[first : first + 48, :]
    out[...] = dot_nn(gathered[...], chooser[...]).astype(jnp.bfloat16)


def project_kernel(
    meta, near, far, other_near, other_far, weight, vectors, cosine, sine, query_out, key_out, value_out, norm_out, all_queries
):
    step = pl.program_id(0)
    rows = near.shape[0]

    def project(source):
        norm = row_norm(source[...].astype(jnp.float32))
        norm_out[...] = norm.astype(jnp.bfloat16)
        attn_in = (norm * vectors[8:9, :] + vectors[2:3, :]).astype(jnp.bfloat16)
        packed = dot_nn(attn_in, weight[:, 256:768])
        first, second = packed[:, 0:128], packed[:, 128:256]
        turn_c, turn_s = cosine[...], sine[...]
        key_out[:, 0:128] = (first * turn_c - second * turn_s).astype(jnp.bfloat16)
        key_out[:, 128:256] = (second * turn_c + first * turn_s).astype(jnp.bfloat16)
        value_out[...] = packed[:, 256:512].astype(jnp.bfloat16)
        return attn_in

    def project_queries(attn_in):
        packed = dot_nn(attn_in, weight[:, 0:256]) * (HDIM ** (-0.5))
        first, second = packed[:, 0:128], packed[:, 128:256]
        turn_c, turn_s = cosine[...], sine[...]
        here = pl.ds(pl.multiple_of(step * rows, 256), rows)
        all_queries[here, 0:128] = (first * turn_c - second * turn_s).astype(jnp.bfloat16)
        all_queries[here, 128:256] = (second * turn_c + first * turn_s).astype(jnp.bfloat16)

    for number, source in enumerate((near, far, other_near, other_far)):

        @pl.when(step // 2 == number)
        def _(number=number, source=source):
            attn_in = project(source)
            if number < 2:
                project_queries(attn_in)

    @pl.when(step == 3)
    def _():
        block = query_out.shape[0] // 4
        stride = 1 + meta[64]
        for j in range(4):
            chosen = pl.ds(pl.multiple_of(((j >> 1) + (j & 1) * 2 * stride) * block, 128), block)
            query_out[j * block : (j + 1) * block, :] = all_queries[chosen, :]


def attend_kernel(meta, query_in, key_in, value_in, out_turned, log_out, out):
    block = query_in.shape[0] // 4
    keys = key_in[...]
    value_turned = value_in[...].T
    log_out[...] = jnp.zeros(log_out.shape, jnp.float32)
    out_turned[...] = jnp.zeros(out_turned.shape, jnp.float32)
    for head in range(3):
        for q_start in range(0, 4 * block, 256):
            here = slice(q_start, q_start + 256)
            query = query_in[here, :]
            query = jnp.where(head_select(256, head), query, jnp.zeros_like(query))
            scores = contract_cols(keys, query)
            best = jnp.max(scores, 0, keepdims=True)
            raised = jnp.exp(scores - best)
            total = jnp.sum(raised, 0, keepdims=True)
            mixed = dot_nn(value_turned[head * 64 : (head + 1) * 64, :], raised.astype(jnp.bfloat16))
            out_turned[head * 64 : (head + 1) * 64, here] = mixed / total
            log_out[head : head + 1, here] = best + jnp.log(total)
    turned_back = out_turned[...].T.astype(jnp.bfloat16)
    for j in range(4):
        out[j, :, :] = turned_back[j * block : (j + 1) * block, 0:192]


def attend_back_kernel(
    meta, cosine, sine, query_in, key_in, value_in, out_turned, log_in, grad_in, grad_packed, key_sum, value_sum
):
    block = query_in.shape[0] // 4
    stride = 1 + meta[64]
    keys, values = key_in[...], value_in[...]
    key_turned = keys.T
    lane_pad = jnp.zeros((4 * block, 64), jnp.bfloat16)
    grad_out = jnp.concatenate([jnp.concatenate([grad_in[j, :, :] for j in range(4)], 0), lane_pad], 1)
    grad_turned = grad_out.astype(jnp.float32).T
    key_sum[...] = jnp.zeros(key_sum.shape, jnp.float32)
    value_sum[...] = jnp.zeros(value_sum.shape, jnp.float32)
    product = grad_turned * out_turned[...]
    lane = lax.broadcasted_iota(jnp.int32, (1, 256), 1)
    query_parts = []
    for q_start in range(0, 4 * block, 256):
        here = slice(q_start, q_start + 256)
        query_sum = jnp.zeros((256, 256), jnp.float32)
        sub = lax.broadcasted_iota(jnp.int32, (256, 1), 0)
        for head in range(3):
            query = query_in[here, :]
            query = jnp.where(head_select(256, head), query, jnp.zeros_like(query))
            head_grad = grad_out[q_start : q_start + 256, :]
            head_grad = jnp.where(lane // 64 == head, head_grad, jnp.zeros_like(head_grad))
            probs = jnp.exp(contract_cols(keys, query) - log_in[head : head + 1, here])
            delta = jnp.sum(product[head * 64 : (head + 1) * 64, here], 0, keepdims=True)
            grad_scores = (probs * (contract_cols(values, head_grad) - delta)).astype(jnp.bfloat16)
            value_sum[...] += dot_nn(probs.astype(jnp.bfloat16), head_grad)
            key_sum[...] += dot_nn(grad_scores, query)
            part = dot_nn(key_turned, grad_scores)
            query_sum = jnp.where((sub % 128) // 32 == head, part, query_sum)
        query_parts.append(query_sum.T * (HDIM ** (-0.5)))
    for j in range(4):
        rows = pl.ds(pl.multiple_of(((j >> 1) + (j & 1) * 2 * stride) * block, 128), block)
        q_part = query_parts[(j * block) // 256][(j * block) % 256 : (j * block) % 256 + block, :]
        first, second = q_part[:, 0:128], q_part[:, 128:256]
        turn_c, turn_s = cosine[rows, :], sine[rows, :]
        here = slice(j * block, (j + 1) * block)
        grad_packed[here, 0:128] = (first * turn_c + second * turn_s).astype(jnp.bfloat16)
        grad_packed[here, 128:256] = (second * turn_c - first * turn_s).astype(jnp.bfloat16)


def project_back_kernel(
    meta, norm, weight, chooser, columns, cosine, sine, grad_packed, key_sum, value_sum,
    own_rows, other_rows, grad_weight, sums, grad_queries, weight_sum, total
):
    step = pl.program_id(0)
    rows = norm.shape[0]

    @pl.when(step == 0)
    def _():
        block = grad_packed.shape[0] // 4
        stride = 1 + meta[64]
        grad_queries[...] = jnp.zeros(grad_queries.shape, jnp.bfloat16)
        for j in range(4):
            chosen = pl.ds(pl.multiple_of(((j >> 1) + (j & 1) * 2 * stride) * block, 128), block)
            grad_queries[chosen, :] = grad_packed[j * block : (j + 1) * block, :]
        weight_sum[...] = jnp.zeros(weight_sum.shape, jnp.float32)
        total[...] = jnp.zeros(total.shape, jnp.float32)

    first, second = key_sum[:, 0:128], key_sum[:, 128:256]
    turn_c, turn_s = cosine[...], sine[...]
    pair = jnp.concatenate(
        [first * turn_c + second * turn_s, second * turn_c - first * turn_s, value_sum[...]], 1
    ).astype(jnp.bfloat16)
    ones = jnp.ones((8, rows), jnp.bfloat16)

    @pl.when(step < 4)
    def _():
        query = grad_queries[pl.ds(pl.multiple_of(step * rows, 256), rows), :]
        triple = jnp.concatenate([query, pair], 1)
        own_rows[...] = contract_cols(triple, weight[...]).astype(jnp.bfloat16)
        weight_sum[...] += contract_rows(norm[...], triple)
        total[...] += dot_nn(ones, triple)

    @pl.when(step >= 4)
    def _():
        other_rows[...] = contract_cols(pair, weight[:, 256:768]).astype(jnp.bfloat16)
        weight_sum[:, 256:768] += contract_rows(norm[...], pair)
        total[:, 256:768] += dot_nn(ones, pair)

    @pl.when(step == pl.num_programs(0) - 1)
    def _():
        summed = total[0:1, :]
        whole = columns[:, 0:1] * weight_sum[...] + columns[:, 1:2] * summed
        grad_weight[...] = contract_cols(whole.astype(jnp.bfloat16), chooser[...]).astype(jnp.bfloat16)
        plain = weight[...].astype(jnp.float32)
        sums[:, 0:1] = jnp.sum(plain * summed, 1, keepdims=True)
        sums[:, 1:2] = jnp.sum(plain * weight_sum[...], 1, keepdims=True)


def middle_kernel(
    meta, attended, near_a, near_b, far_a, far_b, other_near, other_far, own_rows, vectors, projected_out, middle_out, low_out,
    weight_out
):
    core = meta[64]
    mine = pl.multiple_of(core * 384, 128)
    theirs = pl.multiple_of(384 - core * 384, 128)
    for slot in range(16):
        rows_a = pl.ds(pl.multiple_of(meta[slot] * 48, 16), 48)
        rows_b = pl.ds(pl.multiple_of(meta[16 + slot] * 48, 16), 48)
        rows_p = pl.ds(pl.multiple_of(meta[32 + slot] * 48, 16), 48)
        part_a, part_b, other = (near_a, near_b, other_near) if slot < 8 else (far_a, far_b, other_far)
        weight_out[rows_a, pl.ds(mine, 256)] = part_a[slot % 8, :, :]
        weight_out[rows_b, pl.ds(pl.multiple_of(mine + 256, 128), 128)] = part_b[slot % 8, :, :]
        weight_out[rows_p, pl.ds(theirs, 256)] = other[slot % 8, :, 0:256]
        weight_out[rows_b, pl.ds(pl.multiple_of(theirs + 256, 128), 128)] = other[slot % 8, :, 256:384]
    projected = dot_nn(attended[...], weight_out[...])
    projected_out[...] = projected
    middle = own_rows[...].astype(jnp.float32) + vectors[3:4, :] * projected
    middle_out[...] = middle
    low_out[...] = (row_norm(middle) * vectors[4:5, :] * vectors[5:6, :] + vectors[6:7, :]).astype(jnp.bfloat16)


def mlp_kernel(
    meta, low_own, low_other, grad_own, grad_other, near_a, near_b, far_a, far_b, bias, sums_own, sums_other,
    keep_a, keep_b, send_a, send_b, grad_bias, weight_in, weight_down, grad_in, grad_down, branch, back
):
    for slot in range(16):
        part_a, part_b = (near_a, near_b) if slot < 8 else (far_a, far_b)
        for lane_start, size, part, index in ((0, 256, part_a, meta[slot]), (256, 128, part_b, meta[16 + slot])):
            rows = pl.ds(pl.multiple_of(index * 48, 16), 48)
            for i in range(4):
                lanes = slice(i * 384 + lane_start, i * 384 + lane_start + size)
                weight_in[rows, lanes] = part[slot % 8, i * 48 : (i + 1) * 48, :]
            rows = pl.ds(pl.multiple_of(index * 96, 16), 96)
            for i in range(2):
                lanes = slice(i * 384 + lane_start, i * 384 + lane_start + size)
                weight_down[rows, lanes] = part[slot % 8, 192 + i * 96 : 192 + (i + 1) * 96, :]
    low = jnp.concatenate([low_own[...], low_other[...]], 0)
    grad = jnp.concatenate([grad_own[...], grad_other[...]], 0)
    tokens = low_own.shape[0]
    branch[...] = jnp.zeros(branch.shape, jnp.float32)
    back[...] = jnp.zeros(back.shape, jnp.float32)
    root, cubic = math.sqrt(2.0 / math.pi), 0.044715
    for i in range(4):
        hidden = slice(i * 384, (i + 1) * 384)
        pre_act = dot_nn(low, weight_in[:, hidden]) + bias[:, hidden]
        square = pre_act * pre_act
        bend = jnp.tanh(root * (pre_act + cubic * square * pre_act))
        active = (0.5 * pre_act * (1.0 + bend)).astype(jnp.bfloat16)
        slope = 0.5 * (1.0 + bend) + 0.5 * pre_act * (1.0 - bend * bend) * (root * (1.0 + 3.0 * cubic * square))
        branch[...] += dot_nn(active, weight_down[hidden, :])
        grad_pre = (contract_cols(grad, weight_down[hidden, :]) * slope).astype(jnp.bfloat16)
        grad_bias[:, hidden] = jnp.sum(grad_pre.astype(jnp.float32), 0, keepdims=True)
        back[...] += contract_cols(grad_pre, weight_in[:, hidden])
        grad_in[:, hidden] = contract_rows(low, grad_pre).astype(jnp.bfloat16)
        grad_down[hidden, :] = contract_rows(active, grad).astype(jnp.bfloat16)
    sums_own[0, :, :] = branch[:tokens, :]
    sums_other[0, :, :] = branch[tokens:, :]
    sums_own[1, :, :] = back[:tokens, :]
    sums_other[1, :, :] = back[tokens:, :]
    for slot in range(16):
        part_a, part_b = (keep_a, keep_b) if slot < 8 else (send_a, send_b)
        for lane_start, size, part, index in ((0, 256, part_a, meta[slot]), (256, 128, part_b, meta[16 + slot])):
            rows = pl.ds(pl.multiple_of(index * 48, 16), 48)
            for i in range(4):
                lanes = slice(i * 384 + lane_start, i * 384 + lane_start + size)
                part[slot % 8, i * 48 : (i + 1) * 48, :] = grad_in[rows, lanes]
            rows = pl.ds(pl.multiple_of(index * 96, 16), 96)
            for i in range(2):
                lanes = slice(i * 384 + lane_start, i * 384 + lane_start + size)
                part[slot % 8, 192 + i * 96 : 192 + (i + 1) * 96, :] = grad_down[rows, lanes]


def turn_kernel(
    meta, sums_own, sums_other, bias, middle_in, projected_in, cotangent, grad_branch, weight,
    attended, vectors, output, grad_middle_out, grad_attn_out, grad_weight, sums
):
    width = middle_in.shape[1]
    branch = sums_own[0, :, :] + sums_other[0, :, :] + bias[...]
    middle = middle_in[...]
    grad = cotangent[...].astype(jnp.float32)
    output[...] = (middle + vectors[7:8, :] * branch).astype(jnp.bfloat16)
    back = sums_own[1, :, :] + sums_other[1, :, :]
    center = middle - jnp.mean(middle, -1, keepdims=True)
    inverse = lax.rsqrt(jnp.mean(center * center, -1, keepdims=True) + 1e-05)
    norm = center * inverse
    scaled = back * vectors[5:6, :] * vectors[4:5, :]
    grad_middle = grad + inverse * (
        scaled - jnp.mean(scaled, -1, keepdims=True) - norm * jnp.mean(scaled * norm, -1, keepdims=True)
    )
    grad_middle_out[...] = grad_middle
    grad_proj = (vectors[3:4, :] * grad_middle).astype(jnp.bfloat16)
    grad_attn_out[...] = contract_cols(grad_proj, weight[...]).astype(jnp.bfloat16)
    grad_weight[...] = contract_rows(attended[...], grad_proj).astype(jnp.bfloat16)
    def total(values):
        return jnp.sum(values, 0, keepdims=True)

    sums[...] = jnp.concatenate(
        [
            total(grad_middle * projected_in[...]),
            total(back),
            total(back * norm),
            total(grad * branch),
            total(grad_branch[...].astype(jnp.float32)),
            jnp.zeros((3, width), jnp.float32),
        ],
        0,
    )


def call(body, outs, args, scratch=(), grid=None, blocks=(), out_blocks=(), flops=0, moved=0):
    if grid is None:
        whole = pl.BlockSpec(memory_space=pltpu.VMEM)
        in_specs, out_specs = [whole] * len(args), [whole] * len(outs)
    else:
        blocks, out_blocks = dict(blocks), dict(out_blocks)

        def spec(shape, block):
            return block or pl.BlockSpec(shape, lambda i: (0,) * len(shape))

        in_specs = [spec(member.shape, blocks.get(k)) for k, member in enumerate(args)]
        out_specs = [spec(member[0], out_blocks.get(k)) for k, member in enumerate(outs)]
    in_specs[0] = pl.BlockSpec(memory_space=pltpu.SMEM)
    return pl.pallas_call(
        body,
        grid=() if grid is None else grid,
        out_shape=[jax.ShapeDtypeStruct(*member) for member in outs],
        in_specs=in_specs,
        out_specs=out_specs,
        scratch_shapes=[pltpu.VMEM(*member) for member in scratch],
        compiler_params=pltpu.CompilerParams(vmem_limit_bytes=VMEM_LIMIT),
        cost_estimate=pl.CostEstimate(flops=flops, bytes_accessed=moved, transcendentals=0),
    )(*args)


def cube_local(
    hidden_in, time_index, cotangent, w_qkv, w_attn_out, w_mlp_in, w_mlp_out, w_ada, bias_ada, gain_attn, gain_mlp,
    bias_mlp_in, bias_mlp_out
):
    f32, bf16 = jnp.float32, jnp.bfloat16
    rows, width = hidden_in.shape[1:]
    tokens = 2 * rows
    place = lax.axis_index("fsdp")
    side = lax.axis_index("seq")
    device = side * 16 + place
    core, half, group = place & 1, place >> 3, (place >> 1) & 3
    x_own = jnp.concatenate(
        [pick(hidden_in, half), swap_bits(pick(hidden_in, 1 - half), HALF_BIT)], 0
    )
    cond = jax.nn.silu(time_features(time_index, w_ada.shape[1]))
    cond_parts, rest = [], cond
    for _ in range(3):
        cond_parts.append(lax.reduce_precision(rest, 8, 7))
        rest = rest - cond_parts[-1]
    cond_parts = jnp.concatenate(cond_parts + [jnp.zeros_like(cond)], 0).astype(bf16)

    def double(values, bit):
        return jnp.concatenate([values, swap_bits(values, bit)], 0)

    (vector,) = call(
        vector_kernel,
        [((16, 576), bf16)],
        [jnp.zeros((1,), jnp.int32), cond_parts, w_ada]
        + [member[None] for member in (bias_ada, gain_attn, gain_mlp, bias_mlp_in, bias_mlp_out)],
    )
    grouped = w_qkv.reshape(48, 3, 4, 192).transpose(2, 0, 1, 3).reshape(4, 48, 576)
    grouped = grouped[group ^ jnp.arange(4)].reshape(192, 576)
    grouped = jnp.concatenate([grouped, vector], 0)
    x_own, grouped, w_mlp_in, w_attn_out, w_mlp_out = lax.optimization_barrier(
        (x_own, grouped, w_mlp_in, w_attn_out, w_mlp_out)
    )
    x_kept = x_own
    x_one = spread(x_own, TOKENS[:1])
    came_qkv = swap_bits(grouped, HALF_BIT)
    own_share, sent_share = call(
        share_kernel,
        [((432, 384), bf16), ((240, 384), bf16)],
        [jnp.stack([core, side]).astype(jnp.int32), w_mlp_in, w_attn_out, w_mlp_out],
    )
    came_share = swap_bits(sent_share, CORE_BIT)
    share = jnp.where(core == side, own_share[:240], came_share)
    share = jnp.concatenate([share[:192], own_share[240:], share[192:]], 0)
    x_one, share, place_kept = lax.optimization_barrier((x_one, share, place))
    x_two = spread(x_one, TOKENS[1:2])
    came_share = swap_bits(share, HALF_BIT)
    place = place_kept
    device, core = side * 16 + place, place & 1
    stream_own, stream_other = slot_masks(STREAM, core), slot_masks(STREAM, 1 - core)
    shared = slot_masks(SHARED, core)

    def weight_slots(masks):
        moved = ((masks & 6) | (masks >> 4))[:, None] ^ jnp.array([0, 8], jnp.int32)[None]
        return (((place & 14) + side) ^ moved).reshape(-1)

    quad = jnp.array([0, ROW_BIT, LOW_BIT, LOW_BIT | ROW_BIT], jnp.int32)
    oct_masks = (quad[:, None] ^ jnp.array([0, HALF_BIT], jnp.int32)).reshape(-1)
    row_slots = place ^ jnp.concatenate([oct_masks, oct_masks ^ CORE_BIT])
    meta = jnp.concatenate(
        [weight_slots(stream_own), weight_slots(shared), weight_slots(stream_other), row_slots, core[None]]
    ).astype(jnp.int32)
    blocks = jnp.concatenate(
        [device ^ slot_masks(TOKENS, core), device ^ CORE_BIT ^ slot_masks(TOKENS, 1 - core)]
    )
    blocks = jnp.stack([blocks, blocks ^ HALF_BIT], 1)
    inverse = jnp.exp(-math.log(10000.0) * (2 * (jnp.arange(128) % 32)).astype(f32) / HDIM)
    begin_angles = (blocks.reshape(-1) * rows).astype(f32)[:, None, None] * inverse
    inner_angles = jnp.arange(rows, dtype=jnp.int32).astype(f32)[:, None] * inverse
    begin_c, begin_s, inner_c, inner_s = [
        lax.optimization_barrier(member)
        for member in (jnp.cos(begin_angles), jnp.sin(begin_angles), jnp.cos(inner_angles), jnp.sin(inner_angles))
    ]
    cosine = (begin_c * inner_c - begin_s * inner_s).reshape(-1, 128)
    sine = (begin_s * inner_c + begin_c * inner_s).reshape(-1, 128)
    lane = jnp.arange(768) + (place >> 4)
    inner = lane % 128
    wanted = jnp.where(
        lane < 512,
        jnp.where(inner < 96, (lane // 256) * 192 + (inner // 32) * 64 + ((lane % 256) // 128) * 32 + inner % 32, -1),
        jnp.where(lane < 704, lane - 128, -1),
    )
    chooser = (jnp.arange(576)[:, None] == wanted[None, :]).astype(bf16)
    x_two, grouped, came_qkv, meta, cosine, sine, chooser = lax.optimization_barrier(
        (x_two, grouped, came_qkv, meta, cosine, sine, chooser)
    )
    x_far = swap_bits(x_two, *TOKENS[2])
    other_two = swap_bits(x_two, CORE_BIT)
    both_qkv = jnp.stack([grouped[:192], came_qkv[:192]]).reshape(2, 2, 2, 48, 576)
    vector = jnp.concatenate([grouped[192:], came_qkv[192:]], 0)
    got = swap_bits(jnp.concatenate([both_qkv[:, :, 1].reshape(192, 576), vector], 0), ROW_BIT)
    got, came_share, cotangent = lax.optimization_barrier((got, came_share, cotangent))
    both_qkv = jnp.stack([both_qkv[:, :, 0], got[:192].reshape(2, 2, 48, 576)])
    vector = jnp.concatenate([vector, got[192:]], 0)
    got = swap_bits(jnp.concatenate([both_qkv[:, :, 1].reshape(192, 576), vector], 0), LOW_BIT)
    share = jnp.stack([share, came_share])[None]
    part_a, part_b = spread(share[..., :256], STREAM[:1]), spread(share[..., 256:], SHARED[:1])
    x_far, got, part_a, part_b = lax.optimization_barrier((x_far, got, part_a, part_b))
    grouped = jnp.concatenate([both_qkv[:, :, 0].reshape(192, 576), got[:192], vector, got[192:]], 0)
    came_grouped = swap_bits(grouped, CORE_BIT)
    other_far = swap_bits(x_far, CORE_BIT)
    came_a, came_b = swap_bits(part_a, *STREAM[1]), swap_bits(part_b, *SHARED[1])
    apart = place ^ jnp.arange(16)
    vector = jnp.concatenate([grouped[384:], came_grouped[384:]], 0).reshape(16, 16, 576).astype(f32)
    vector = vector[((apart & 1) << 3) | (apart & 4) | (apart & 2) | (apart >> 3)]
    parts = [jnp.sum(vector[:, row : row + 3, :288], 1) for row in (0, 3)]
    parts += [vector[:, 6 + row, :size] for row, size in enumerate((48, 48, 192, 48))]
    modulation = jnp.stack([parts[0].reshape(6, width), parts[1].reshape(6, width)])
    shift_attn, scale_attn, gate_attn, shift_mlp, scale_mlp, gate_mlp = [
        row for row in pick(modulation, half)
    ]
    full_gain_attn, full_gain_mlp = parts[2].reshape(-1), parts[3].reshape(-1)
    bias_in = pick(parts[4].reshape(8, 2, 192), core, 1).reshape(1, -1)
    bias_down = parts[5].reshape(1, -1)
    vectors = jnp.stack(
        [full_gain_attn, 1.0 + scale_attn, shift_attn, gate_attn, full_gain_mlp, 1.0 + scale_mlp, shift_mlp, gate_mlp]
        + [full_gain_attn * (1.0 + scale_attn)]
    )
    columns = jnp.stack([vectors[8], shift_attn], 1)
    (weight_qkv,) = call(
        order_weight_kernel,
        [((768, 768), bf16)],
        [meta, grouped, came_grouped, chooser],
        [((768, 576), bf16)],
        flops=2 * 768 * 768 * 576,
        moved=3_000_000,
    )
    span = 16 * tokens
    chunk = 256

    def part_of(number, size):
        return pl.BlockSpec((chunk, size), lambda i: (jnp.clip(i - number * 2, 0, 1), 0))

    def rows_of(size):
        return pl.BlockSpec((chunk, size), lambda i: (i, 0))

    queries, keys, values, norms = call(
        project_kernel,
        [((4 * tokens, 256), bf16), ((span, 256), bf16), ((span, 256), bf16), ((span, width), bf16)],
        [meta, x_two, x_far, other_two, other_far, weight_qkv, vectors, cosine, sine],
        [((8 * tokens, 256), bf16)],
        grid=(8,),
        blocks=[(1 + number, part_of(number, width)) for number in range(4)] + [(7, rows_of(128)), (8, rows_of(128))],
        out_blocks=[(1, rows_of(256)), (2, rows_of(256)), (3, rows_of(width))],
        flops=2_000_000_000,
        moved=8_000_000,
    )
    keys, came_a, came_b = lax.optimization_barrier((keys, came_a, came_b))
    part_a, part_b = jnp.concatenate([part_a, came_a], 0), jnp.concatenate([part_b, came_b], 0)
    far_a, far_b = swap_bits(part_a, *STREAM[2]), swap_bits(part_b, *SHARED[2])
    part_a, part_b = part_a.reshape(8, 432, 256), part_b.reshape(8, 432, 128)
    other_near = swap_bits(jnp.concatenate([part_a[:, 384:], part_b[:, 384:]], 2), CORE_BIT)
    out_turned, log_total, heads_out = call(
        attend_kernel,
        [((256, 4 * tokens), f32), ((8, 4 * tokens), f32), ((4, tokens, 192), bf16)],
        [meta, queries, keys, values],
        flops=8_000_000_000,
        moved=4_000_000,
    )
    heads_out = heads_out.reshape(2, 2, tokens, 192)
    came = swap_bits(heads_out[:, 1], ROW_BIT)
    came, far_a, far_b = lax.optimization_barrier((came, far_a, far_b))
    heads_out = jnp.stack([heads_out[:, 0], came], 1)
    by_group = jnp.stack([heads_out[0], swap_bits(heads_out[1], LOW_BIT)], 0).reshape(4, tokens, 192)
    attended = by_group[group ^ jnp.arange(4)].transpose(1, 0, 2).reshape(tokens, width)
    far_a, far_b = far_a.reshape(8, 432, 256), far_b.reshape(8, 432, 128)
    other_out = swap_bits(jnp.concatenate([far_a[:, 384:], far_b[:, 384:]], 2), CORE_BIT)
    projected, middle, mlp_own, weight_out = call(
        middle_kernel,
        [((tokens, width), f32), ((tokens, width), f32), ((tokens, width), bf16), ((768, 768), bf16)],
        [meta, attended, part_a[:, 384:], part_b[:, 384:], far_a[:, 384:], far_b[:, 384:], other_near, other_out]
        + [x_kept, vectors],
        flops=150_000_000,
        moved=3_000_000,
    )
    grad_own = jnp.concatenate(
        [pick(cotangent, half), swap_bits(pick(cotangent, 1 - half), HALF_BIT)], 0
    )
    branch_grad = (gate_mlp[None] * grad_own.astype(f32)).astype(bf16)
    branch_grad_other = swap_bits(branch_grad, CORE_BIT)
    mlp_other = swap_bits(mlp_own, CORE_BIT)
    sums_own, sums_sent, keep_a, keep_b, send_a, send_b, grad_bias_in = call(
        mlp_kernel,
        [((2, tokens, width), f32)] * 2
        + [((8, 384, 256), bf16), ((8, 384, 128), bf16)] * 2
        + [((1, 1536), f32)],
        [meta, mlp_own, mlp_other, branch_grad, branch_grad_other, part_a, part_b, far_a, far_b, bias_in],
        [((768, 1536), bf16), ((1536, 768), bf16), ((768, 1536), bf16), ((1536, 768), bf16)]
        + [((2 * tokens, width), f32)] * 2,
        flops=3_600_000_000,
        moved=12_000_000,
    )
    came = swap_bits(sums_sent, CORE_BIT)

    def plus(left, right):
        return (left.astype(f32) + right.astype(f32)).astype(bf16)

    came_a, came_b = swap_bits(send_a, *STREAM[2]), swap_bits(send_b, *SHARED[2])
    output_rows, grad_middle, grad_attn, grad_w_out, sums_mlp = call(
        turn_kernel,
        [((tokens, width), bf16), ((tokens, width), f32), ((tokens, width), bf16), ((768, 768), bf16), ((8, width), f32)],
        [meta, sums_own, came, bias_down, middle, projected, grad_own, branch_grad, weight_out]
        + [attended, vectors],
        flops=300_000_000,
        moved=5_000_000,
    )

    grad_heads = grad_attn.reshape(tokens, 4, 192).transpose(1, 0, 2)[group ^ jnp.arange(4)]
    grad_heads = quad_exchange(grad_heads.reshape(2, 2, tokens, 192)).reshape(4, tokens, 192)
    grad_heads, grad_w_out, output_rows = lax.optimization_barrier((grad_heads, grad_w_out, output_rows))
    by_core = grad_w_out.reshape(8, 2, 48, width)
    sum_out = plus(pick(by_core, core, 1), swap_bits(pick(by_core, 1 - core, 1), CORE_BIT))
    output = pair_up(output_rows[:rows], swap_bits(output_rows[rows:], HALF_BIT), half)
    grad_packed, key_sum, value_sum = call(
        attend_back_kernel,
        [((4 * tokens, 256), bf16), ((span, 256), f32), ((span, 256), f32)],
        [meta, cosine, sine, queries, keys, values, out_turned, log_total, grad_heads],
        flops=14_000_000_000,
        moved=8_000_000,
    )
    key_sum, came_a, came_b, sum_out, output = lax.optimization_barrier((key_sum, came_a, came_b, sum_out, output))
    sum_a = plus(keep_a, came_a).reshape(4, 768, 256)
    sum_b = plus(keep_b, came_b).reshape(4, 768, 128)
    came_a, came_b = swap_bits(sum_a[2:], *STREAM[1]), swap_bits(sum_b[2:], *SHARED[1])
    y, z = (place >> 1) & 1, (place >> 2) & 1
    out_row = sum_out.reshape(2, 2, 2, 48, width)
    came_out = swap_bits(pick(out_row, 1 - y, 2), ROW_BIT)
    own_rows, other_rows, grad_qkv, sums_attn = call(
        project_back_kernel,
        [((8 * tokens, width), bf16)] * 2 + [((768, 576), bf16), ((width, 2), f32)],
        [meta, norms, weight_qkv, chooser, columns, cosine, sine, grad_packed, key_sum, value_sum],
        [((8 * tokens, 256), bf16), ((width, width), f32), ((8, width), f32)],
        grid=(8,),
        blocks=[(1, rows_of(width)), (5, rows_of(128)), (6, rows_of(128)), (8, rows_of(256)), (9, rows_of(256))],
        out_blocks=[
            (0, pl.BlockSpec((chunk, width), lambda i: (jnp.minimum(i, 3), 0))),
            (1, pl.BlockSpec((chunk, width), lambda i: (jnp.maximum(i - 4, 0), 0))),
        ],
        flops=6_000_000_000,
        moved=16_000_000,
    )
    own_rows, other_rows, grad_qkv, sums_attn, came_a, came_b, came_out = lax.optimization_barrier(
        (own_rows, other_rows, grad_qkv, sums_attn, came_a, came_b, came_out)
    )
    own_rows = own_rows.reshape(8, tokens, width)
    came_rows = swap_bits(other_rows, CORE_BIT).reshape(8, tokens, width)
    small = jnp.concatenate([sums_attn.T, sums_mlp[0:5]], 0)
    small = jnp.concatenate([small + swap_bits(small, CORE_BIT), grad_bias_in.reshape(2, width)], 0)
    by_core = grad_qkv.reshape(8, 2, 48, 576)
    kept = plus(pick(by_core, core, 1), swap_bits(pick(by_core, 1 - core, 1), CORE_BIT))
    sum_a, sum_b = plus(sum_a[:2], came_a), plus(sum_b[:2], came_b)
    sum_out = plus(pick(out_row, y, 2), came_out)
    came_a, came_b = swap_bits(sum_a[1], *STREAM[0]), swap_bits(sum_b[1], *SHARED[0])

    def sum_step(own, came, small, order):
        half_way = own.shape[0] // 2
        sent = plus(own[half_way:], came[half_way:]).reshape(-1, width)
        high = jnp.pad(small, ((0, 7), (0, 0))).astype(bf16)
        low = (jnp.pad(small, ((0, 7), (0, 0))) - high.astype(f32)).astype(bf16)
        got = swap_bits(jnp.concatenate([sent, high, low], 0), *order)
        count = sent.shape[0]
        small = small + got[count : count + 9].astype(f32) + got[count + 16 : count + 25].astype(f32)
        return plus(own[:half_way], came[:half_way]), got[:count].reshape(half_way, tokens, width), small

    came_rows, small, kept, came_a, came_b = lax.optimization_barrier((came_rows, small, kept, came_a, came_b))
    own_rows, came_rows, small = sum_step(own_rows, came_rows, small, TOKENS[2])

    def with_out(of_qkv, of_out):
        count = of_qkv.size // 576
        blocks = count * width // of_out.size
        of_out = of_out.reshape(-1, blocks, width // blocks).transpose(1, 0, 2).reshape(count, -1)
        return jnp.concatenate([of_qkv.reshape(count, 576), of_out], 1)

    def without(got, of_qkv, of_out):
        blocks = width // (got.shape[1] - 576)
        out = got[:, 576:].reshape(blocks, -1, width // blocks).transpose(1, 0, 2).reshape(of_out.shape)
        return got[:, :576].reshape(of_qkv.shape), out

    sum_a, sum_b = plus(sum_a[0], came_a).reshape(2, 384, 256), plus(sum_b[0], came_b).reshape(2, 384, 128)
    total = jnp.concatenate([sum_a, sum_b], 2)
    came_total = swap_bits(total[1], HALF_BIT)
    by_row = kept.reshape(2, 2, 2, 48, 576)
    by_row = jnp.stack([pick(by_row, y, 2), swap_bits(pick(by_row, 1 - y, 2), ROW_BIT)])
    came_rows, by_row, sum_out, small, came_total = lax.optimization_barrier(
        (came_rows, by_row, sum_out, small, came_total)
    )
    total = plus(total[0], came_total)
    across = swap_bits(total, SEQ_BIT)
    own_rows, came_rows, small = sum_step(own_rows, came_rows, small, TOKENS[1])
    sent = pick(by_row, 1 - z, 2), pick(sum_out, 1 - z, 1)
    got = without(swap_bits(with_out(*sent), LOW_BIT), *sent)
    kept, sum_out = jnp.stack([pick(by_row, z, 2), got[0]]), plus(pick(sum_out, z, 1), got[1])
    came_rows, kept, small, sum_out, across = lax.optimization_barrier((came_rows, kept, small, sum_out, across))
    mine = jnp.where(core == side, total[:192], across[:192])
    theirs = swap_bits(jnp.where(core == side, across[:192], total[:192]), CORE_BIT)
    own_rows, came_rows, small = sum_step(own_rows, came_rows, small, TOKENS[0])
    by_half = kept.reshape(4, 2, 48, 576)
    sent = pick(by_half, 1 - half, 1), pick(sum_out, 1 - half)
    got = without(swap_bits(with_out(*sent), HALF_BIT), *sent)
    kept, sum_out = plus(pick(by_half, half, 1), got[0]), plus(pick(sum_out, half), got[1])
    came_rows, small, theirs = lax.optimization_barrier((came_rows, small, theirs))
    stays, leaves = call(
        finish_kernel,
        [((rows, width), f32), ((rows, width), bf16)],
        [jnp.zeros((1,), jnp.int32), own_rows[0], came_rows[0], x_kept, grad_middle, vectors],
    )
    leaves_came = swap_bits(leaves, HALF_BIT)

    grad_down = pair_up(total[192:], across[192:], side).reshape(2, 2, 96, 384)
    grad_down = grad_down.transpose(0, 2, 1, 3).reshape(192, 768).astype(f32)
    def in_columns_back(blocks):
        return blocks.reshape(4, 48, 384).transpose(1, 0, 2).reshape(48, 8, 192)

    grad_w_in = pair_up(in_columns_back(mine), in_columns_back(theirs), core)
    grad_w_in = grad_w_in.transpose(1, 2, 0, 3).reshape(48, 3072).astype(f32)
    kept = kept[group ^ jnp.arange(4)].reshape(4, 48, 3, 192).transpose(1, 2, 0, 3).reshape(48, 2304)
    kept = jnp.concatenate([kept, sum_out], 1)
    kept, came_small, leaves_came = lax.optimization_barrier((kept, swap_bits(small, HALF_BIT), leaves_came))
    grad_hidden = pair_up(stays, leaves_came.astype(f32), half)
    came_kept = swap_bits(kept, SEQ_BIT)
    kept = kept.astype(f32) + came_kept.astype(f32)
    grad_w_qkv, grad_w_out = kept[:, :2304], kept[:, 2304:]
    both = pair_up(small, came_small, half)
    plus_scale = 1.0 + modulation[:, 1], 1.0 + modulation[:, 4]
    grad_mod = jnp.stack(
        [both[:, 0], both[:, 1] * full_gain_attn, both[:, 2], both[:, 3], both[:, 4] * full_gain_mlp, both[:, 5]], 1
    ).reshape(2, 16, 288)
    grad_mod = pick(grad_mod, place, 1)
    grad_ada = grad_mod[0][:, None] * cond[0][None] + grad_mod[1][:, None] * cond[1][None]
    gain_first = pick(jnp.sum(both[:, 1] * plus_scale[0], 0).reshape(16, 48), place)
    gain_second = pick(jnp.sum(both[:, 4] * plus_scale[1], 0).reshape(16, 48), place)
    summed = both[0] + both[1]
    bias_in_grad = pick(summed[7:9].reshape(8, 192), place >> 1)
    bias_down_grad = pick(summed[6].reshape(16, 48), place)
    return (
        output,
        grad_hidden,
        grad_w_qkv,
        grad_w_out,
        grad_w_in,
        grad_down,
        grad_ada,
        jnp.sum(grad_mod, 0),
        gain_first,
        gain_second,
        bias_in_grad,
        bias_down_grad,
    )


def solution(mesh):
    return jax.shard_map(
        cube_local if dict(mesh.shape) == {"seq": 2, "fsdp": 16} else local,
        mesh=mesh,
        in_specs=(
            P(None, ("seq", "fsdp"), None),
            P(),
            P(None, ("seq", "fsdp"), None),
            P("fsdp", None),
            P("fsdp", None),
            P("fsdp", None),
            P("fsdp", None),
            P("fsdp", None),
            P("fsdp"),
            P("fsdp"),
            P("fsdp"),
            P("fsdp"),
            P("fsdp"),
        ),
        out_specs=(
            P(None, ("seq", "fsdp"), None),
            P(None, ("seq", "fsdp"), None),
            P("fsdp", None),
            P("fsdp", None),
            P("fsdp", None),
            P("fsdp", None),
            P("fsdp", None),
            P("fsdp"),
            P("fsdp"),
            P("fsdp"),
            P("fsdp"),
            P("fsdp"),
        ),
        check_vma=False,
    )
```

```python
import math

import jax
import jax.numpy as jnp
from jax import lax
from jax.experimental import pallas as pl
from jax.experimental.pallas import tpu as pltpu
from jax.sharding import PartitionSpec as P

HEADS = 12
HDIM = 64


highest_precision = lax.Precision.HIGHEST


def normalize(values):
    center = values - jnp.mean(values, -1, keepdims=True)
    return center * lax.rsqrt(jnp.mean(center * center, -1, keepdims=True) + 1e-05)


def adapt(values, gain, shift, scale):
    return normalize(values) * gain * (1.0 + scale) + shift


def time_features(time_index, width):
    half_width = width // 2
    frequency = jnp.exp(-math.log(10000.0) * jnp.arange(half_width, dtype=jnp.float32) / half_width)
    angles = time_index.astype(jnp.float32)[:, None] * frequency[None, :]
    return jnp.concatenate([jnp.cos(angles), jnp.sin(angles)], -1)


def rotary_tables(positions, head_dim):
    inverse = jnp.exp(-math.log(10000.0) * jnp.arange(0, head_dim, 2, dtype=jnp.float32) / head_dim)
    angles = positions.astype(jnp.float32)[:, None] * inverse[None, :]
    angles = jnp.concatenate([angles, angles], -1)
    return (jnp.cos(angles), jnp.sin(angles))


def rotate(values, cosine, sine):
    first_half, second_half = jnp.split(values, 2, axis=-1)
    turned = jnp.concatenate([-second_half, first_half], -1)
    return values * cosine[:, None, :] + turned * sine[:, None, :]


def contract_rows(left_neighbor, right_neighbor):
    return lax.dot_general(
        left_neighbor, right_neighbor, (((0,), (0,)), ((), ())), preferred_element_type=jnp.float32
    )


def contract_cols(left_neighbor, right_neighbor):
    return lax.dot_general(
        left_neighbor, right_neighbor, (((1,), (1,)), ((), ())), preferred_element_type=jnp.float32
    )


def gelu_tanh(values):
    return jax.nn.gelu(values, approximate=True)


def local(
    hidden_in,
    time_index,
    cotangent,
    w_qkv,
    w_attn_out,
    w_mlp_in,
    w_mlp_out,
    w_ada,
    bias_ada,
    gain_attn,
    gain_mlp,
    bias_mlp_in,
    bias_mlp_out,
):
    seqs_here, row_count, width = hidden_in.shape
    flat_rows = seqs_here * row_count
    gathered = (
        lax.all_gather(w_qkv, "fsdp", axis=0, tiled=True),
        lax.all_gather(w_attn_out, "fsdp", axis=0, tiled=True),
        lax.all_gather(w_mlp_in, "fsdp", axis=0, tiled=True),
        lax.all_gather(w_mlp_out, "fsdp", axis=0, tiled=True),
        lax.all_gather(w_ada, "fsdp", axis=0, tiled=True),
        lax.all_gather(bias_ada, "fsdp", axis=0, tiled=True),
        lax.all_gather(gain_attn, "fsdp", axis=0, tiled=True),
        lax.all_gather(gain_mlp, "fsdp", axis=0, tiled=True),
        lax.all_gather(bias_mlp_in, "fsdp", axis=0, tiled=True),
        lax.all_gather(bias_mlp_out, "fsdp", axis=0, tiled=True),
    )
    (
        full_qkv,
        gathered_output,
        full_in,
        full_down,
        full_ada,
        full_bias_ada,
        full_gain_attn,
        full_gain_mlp,
        full_bias_in,
        full_bias_down,
    ) = gathered
    gain_first = full_gain_attn.astype(jnp.float32)
    gain_second = full_gain_mlp.astype(jnp.float32)
    cond = jax.nn.silu(time_features(time_index, full_ada.shape[1]))
    modulation = jnp.dot(
        cond, full_ada.astype(jnp.float32).T, precision=highest_precision
    ) + full_bias_ada.astype(jnp.float32)
    shift_attn, scale_attn, gate_attn, shift_mlp, scale_mlp, gate_mlp = jnp.split(
        modulation[:, None, :], 6, axis=-1
    )
    source = hidden_in.astype(jnp.float32)
    attn_in = adapt(source, gain_first, shift_attn, scale_attn)
    attn_low = attn_in.astype(jnp.bfloat16).reshape(flat_rows, width)
    qkv = jnp.dot(attn_low, full_qkv, preferred_element_type=jnp.float32).reshape(
        seqs_here, row_count, 3 * width
    )
    device_number = lax.axis_index("seq") * lax.axis_size("fsdp") + lax.axis_index("fsdp")
    positions = device_number * row_count + jnp.arange(row_count, dtype=jnp.int32)
    cosine, sine = rotary_tables(positions, HDIM)

    def turn_all(packed):
        split_three = packed.reshape(seqs_here, row_count, 3, HEADS, HDIM)
        query_turned = rotate(split_three[:, :, 0], cosine, sine).reshape(
            seqs_here, row_count, width
        )
        key_turned = rotate(split_three[:, :, 1], cosine, sine).reshape(seqs_here, row_count, width)
        return (query_turned, key_turned, split_three[:, :, 2].reshape(seqs_here, row_count, width))

    query_rot, key_rot, value_raw = turn_all(qkv)
    queries, keys, values = (
        lax.all_to_all(
            query_rot.astype(jnp.bfloat16), "seq", split_axis=2, concat_axis=1, tiled=True
        ),
        lax.all_to_all(
            key_rot.astype(jnp.bfloat16), "seq", split_axis=2, concat_axis=1, tiled=True
        ),
        lax.all_to_all(
            value_raw.astype(jnp.bfloat16), "seq", split_axis=2, concat_axis=1, tiled=True
        ),
    )
    local_heads = HEADS // lax.axis_size("seq")
    span = queries.shape[1]
    query_heads = queries.reshape(seqs_here, span, local_heads, HDIM)
    scale = HDIM ** (-0.5)

    def score_block(key_piece):
        key_heads = key_piece.reshape(seqs_here, key_piece.shape[1], local_heads, HDIM)
        logits = (
            jnp.einsum(
                "sqhd,skhd->shqk", query_heads, key_heads, preferred_element_type=jnp.float32
            )
            * scale
        )
        return (logits, key_heads)

    pieces = (
        lax.all_gather(keys, "fsdp", axis=1, tiled=True),
        lax.all_gather(values, "fsdp", axis=1, tiled=True),
    )
    best = jnp.full((seqs_here, local_heads, span), -1e30, jnp.float32)
    logits, unused = score_block(pieces[0])
    value_heads = pieces[1].reshape(seqs_here, pieces[1].shape[1], local_heads, HDIM)
    newest = jnp.maximum(best, jnp.max(logits, -1))
    raised = jnp.exp(logits - newest[..., None])
    total = jnp.sum(raised, -1)
    accum = jnp.einsum(
        "shqk,skhd->sqhd",
        raised.astype(jnp.bfloat16),
        value_heads,
        preferred_element_type=jnp.float32,
    )
    best, total, accum = (newest, total, accum)
    log_total = best + jnp.log(total)
    attended = accum / jnp.transpose(total, (0, 2, 1))[..., None]
    attended_low = attended.reshape(seqs_here, span, local_heads * HDIM).astype(jnp.bfloat16)
    attn_rows = lax.all_to_all(attended_low, "seq", split_axis=1, concat_axis=2, tiled=True)
    attn_flat = attn_rows.reshape(flat_rows, width)
    projected = jnp.dot(attn_flat, gathered_output, preferred_element_type=jnp.float32).reshape(
        seqs_here, row_count, width
    )
    middle = source + gate_attn * projected
    mlp_in = adapt(middle, gain_second, shift_mlp, scale_mlp)
    mlp_low = mlp_in.astype(jnp.bfloat16).reshape(flat_rows, width)
    pre_act = jnp.dot(mlp_low, full_in, preferred_element_type=jnp.float32) + full_bias_in.astype(
        jnp.float32
    )
    active = gelu_tanh(pre_act).astype(jnp.bfloat16)
    branch = (
        jnp.dot(active, full_down, preferred_element_type=jnp.float32)
        + full_bias_down.astype(jnp.float32)
    ).reshape(seqs_here, row_count, width)
    output = (middle + gate_mlp * branch).astype(jnp.bfloat16)
    grad_result = cotangent.astype(jnp.float32)
    grad_gate_mlp = jnp.sum(grad_result * branch, 1, keepdims=True)
    grad_branch = (gate_mlp * grad_result).astype(jnp.bfloat16).reshape(flat_rows, width)
    grad_bias_down = jnp.sum(grad_branch.astype(jnp.float32), 0)
    grad_down = contract_rows(active, grad_branch)
    grad_active = contract_cols(grad_branch, full_down)
    unused_gelu, gelu_back = jax.vjp(gelu_tanh, pre_act)
    grad_pre = gelu_back(grad_active)[0].astype(jnp.bfloat16)
    grad_bias_in = jnp.sum(grad_pre.astype(jnp.float32), 0)
    grad_in = contract_rows(mlp_low, grad_pre)
    grad_mlp_in = contract_cols(grad_pre, full_in).reshape(seqs_here, row_count, width)
    unused_second, second_back = jax.vjp(adapt, middle, gain_second, shift_mlp, scale_mlp)
    grad_middle_norm, grad_gain_mlp, grad_shift_mlp, grad_scale_mlp = second_back(grad_mlp_in)
    grad_middle = grad_result + grad_middle_norm
    grad_gate_attn = jnp.sum(grad_middle * projected, 1, keepdims=True)
    grad_proj = (gate_attn * grad_middle).astype(jnp.bfloat16).reshape(flat_rows, width)
    grad_attn_weight = contract_rows(attn_flat, grad_proj)
    grad_attn_rows = (
        contract_cols(grad_proj, gathered_output)
        .astype(jnp.bfloat16)
        .reshape(seqs_here, row_count, width)
    )
    grad_heads = lax.all_to_all(grad_attn_rows, "seq", split_axis=2, concat_axis=1, tiled=True)
    grad_head_parts = grad_heads.reshape(seqs_here, span, local_heads, HDIM)
    delta = jnp.transpose(jnp.sum(grad_head_parts.astype(jnp.float32) * attended, -1), (0, 2, 1))
    pieces = (
        lax.all_gather(keys, "fsdp", axis=1, tiled=True),
        lax.all_gather(values, "fsdp", axis=1, tiled=True),
    )
    logits, key_heads = score_block(pieces[0])
    piece_rows = pieces[1].shape[1]
    value_heads = pieces[1].reshape(seqs_here, piece_rows, local_heads, HDIM)
    probs = jnp.exp(logits - log_total[..., None])
    grad_weights = jnp.einsum(
        "sqhd,skhd->shqk", grad_head_parts, value_heads, preferred_element_type=jnp.float32
    )
    probs, grad_logits = (probs, (probs * (grad_weights - delta[..., None])).astype(jnp.bfloat16))
    grad_query = (
        jnp.einsum("shqk,skhd->sqhd", grad_logits, key_heads, preferred_element_type=jnp.float32)
        * scale
    )
    key_part = (
        jnp.einsum("shqk,sqhd->skhd", grad_logits, query_heads, preferred_element_type=jnp.float32)
        * scale
    )
    value_part = jnp.einsum(
        "shqk,sqhd->skhd",
        probs.astype(jnp.bfloat16),
        grad_head_parts,
        preferred_element_type=jnp.float32,
    )
    grad_key_all = key_part.reshape(seqs_here, piece_rows, local_heads * HDIM)
    grad_value_all = value_part.reshape(seqs_here, piece_rows, local_heads * HDIM)
    folded_rows = (grad_query, grad_key_all, grad_value_all)
    grad_query, grad_key_all, grad_value_all = folded_rows
    grad_keys, grad_values = (
        lax.psum_scatter(grad_key_all, "fsdp", scatter_dimension=1, tiled=True),
        lax.psum_scatter(grad_value_all, "fsdp", scatter_dimension=1, tiled=True),
    )
    grad_parts = (
        lax.all_to_all(
            grad_query.reshape(seqs_here, span, local_heads * HDIM).astype(jnp.bfloat16),
            "seq",
            split_axis=1,
            concat_axis=2,
            tiled=True,
        ),
        lax.all_to_all(
            grad_keys.astype(jnp.bfloat16), "seq", split_axis=1, concat_axis=2, tiled=True
        ),
        lax.all_to_all(
            grad_values.astype(jnp.bfloat16), "seq", split_axis=1, concat_axis=2, tiled=True
        ),
    )
    unused_turn, reverse_rotation = jax.vjp(turn_all, qkv)
    grad_qkv = (
        reverse_rotation(tuple((member.astype(jnp.float32) for member in grad_parts)))[0]
        .astype(jnp.bfloat16)
        .reshape(flat_rows, 3 * width)
    )
    grad_qkv_weight = contract_rows(attn_low, grad_qkv)
    grad_attn_in = contract_cols(grad_qkv, full_qkv).reshape(seqs_here, row_count, width)
    unused_first, first_back = jax.vjp(adapt, source, gain_first, shift_attn, scale_attn)
    grad_source_norm, grad_gain_attn, grad_shift_attn, grad_scale_attn = first_back(grad_attn_in)
    grad_hidden = grad_middle + grad_source_norm
    grad_mod = jnp.concatenate(
        [
            grad_shift_attn,
            grad_scale_attn,
            grad_gate_attn,
            grad_shift_mlp,
            grad_scale_mlp,
            grad_gate_mlp,
        ],
        -1,
    )[:, 0, :]
    grad_ada = jnp.dot(grad_mod.T, cond, precision=highest_precision)
    grad_bias_mod = jnp.sum(grad_mod, 0)
    summed = (
        lax.psum_scatter(grad_qkv_weight, "fsdp", scatter_dimension=0, tiled=True),
        lax.psum_scatter(grad_attn_weight, "fsdp", scatter_dimension=0, tiled=True),
        lax.psum_scatter(grad_in, "fsdp", scatter_dimension=0, tiled=True),
        lax.psum_scatter(grad_down, "fsdp", scatter_dimension=0, tiled=True),
        lax.psum_scatter(grad_ada, "fsdp", scatter_dimension=0, tiled=True),
        lax.psum_scatter(grad_bias_mod, "fsdp", scatter_dimension=0, tiled=True),
        lax.psum_scatter(grad_gain_attn, "fsdp", scatter_dimension=0, tiled=True),
        lax.psum_scatter(grad_gain_mlp, "fsdp", scatter_dimension=0, tiled=True),
        lax.psum_scatter(grad_bias_in, "fsdp", scatter_dimension=0, tiled=True),
        lax.psum_scatter(grad_bias_down, "fsdp", scatter_dimension=0, tiled=True),
    )
    totals = (
        lax.psum(summed[0].astype(jnp.bfloat16), "seq").astype(jnp.float32),
        lax.psum(summed[1].astype(jnp.bfloat16), "seq").astype(jnp.float32),
        lax.psum(summed[2].astype(jnp.bfloat16), "seq").astype(jnp.float32),
        lax.psum(summed[3].astype(jnp.bfloat16), "seq").astype(jnp.float32),
        lax.psum(summed[4].astype(jnp.bfloat16), "seq").astype(jnp.float32),
        lax.psum(summed[5].astype(jnp.bfloat16), "seq").astype(jnp.float32),
        lax.psum(summed[6].astype(jnp.bfloat16), "seq").astype(jnp.float32),
        lax.psum(summed[7].astype(jnp.bfloat16), "seq").astype(jnp.float32),
        lax.psum(summed[8].astype(jnp.bfloat16), "seq").astype(jnp.float32),
        lax.psum(summed[9].astype(jnp.bfloat16), "seq").astype(jnp.float32),
    )
    return (output, grad_hidden) + tuple(totals)


AXES = ("seq", "fsdp")
SEQ_BIT, HALF_BIT, LOW_BIT, ROW_BIT, CORE_BIT = 16, 8, 4, 2, 1
STREAM = ((ROW_BIT, SEQ_BIT), (LOW_BIT, ROW_BIT), (SEQ_BIT, LOW_BIT))
TOKENS = ((LOW_BIT, LOW_BIT), (ROW_BIT, SEQ_BIT), (SEQ_BIT, ROW_BIT))
SHARED = ((LOW_BIT, LOW_BIT), (SEQ_BIT, SEQ_BIT), (ROW_BIT, ROW_BIT))
VMEM_LIMIT = 62 * 1024 * 1024


def swap_bits(values, even, odd=None):
    odd = even if odd is None else odd
    return lax.ppermute(values, AXES, [(i, i ^ (odd if i & 1 else even)) for i in range(32)])


def spread(values, order):
    for even, odd in order:
        values = jnp.concatenate([values, swap_bits(values, even, odd)], 0)
    return values


def collect(arrays, order):
    for even, odd in reversed(order):
        half = arrays[0].shape[0] // 2
        sent = jnp.concatenate([member[half:] for member in arrays], 1) if len(arrays) > 1 else arrays[0][half:]
        came = swap_bits(sent, even, odd)
        begin, summed = 0, []
        for member in arrays:
            part = came[:, begin : begin + member.shape[1]]
            begin += member.shape[1]
            summed.append((member[:half].astype(jnp.float32) + part.astype(jnp.float32)).astype(jnp.bfloat16))
        arrays = summed
    return arrays


def slot_masks(order, core):
    masks = [jnp.int32(0)]
    for even, odd in order:
        step = jnp.where(core == 0, even, odd).astype(jnp.int32)
        masks = masks + [mask ^ step for mask in masks]
    return jnp.stack(masks)


def quad_exchange(parts):
    came = swap_bits(parts[:, 1], ROW_BIT)
    parts = jnp.stack([parts[:, 0], came], 1)
    came = swap_bits(parts[1], LOW_BIT)
    return jnp.stack([parts[0], came], 0)


def after(values, *others):
    return lax.optimization_barrier((values,) + others)[0]


def pick(values, index, axis=0):
    return lax.dynamic_index_in_dim(values, index, axis, keepdims=False)


def pair_up(mine, other, position):
    return jnp.where(position == 0, jnp.stack([mine, other]), jnp.stack([other, mine]))


def dot_nn(left, right):
    return lax.dot_general(left, right, (((1,), (0,)), ((), ())), preferred_element_type=jnp.float32)


def row_norm(values):
    center = values - jnp.mean(values, -1, keepdims=True)
    return center * lax.rsqrt(jnp.mean(center * center, -1, keepdims=True) + 1e-05)


def head_select(width, head):
    lane = lax.broadcasted_iota(jnp.int32, (1, width), 1)
    return (lane % 128) // 32 == head


def vector_kernel(meta, cond, w_ada, bias_ada, gain_attn, gain_mlp, bias_in, bias_down, out):
    part = contract_cols(cond[...], w_ada[...])
    rest = part[0:2] + part[2:4] + part[4:6] + bias_ada[...].astype(jnp.float32)
    out[...] = jnp.zeros(out.shape, jnp.bfloat16)
    for row in range(3):
        rounded = rest.astype(jnp.bfloat16)
        rest = rest - rounded.astype(jnp.float32)
        out[row : row + 1, 0 : rest.shape[1]] = rounded[0:1]
        out[row + 3 : row + 4, 0 : rest.shape[1]] = rounded[1:2]
    for row, member in enumerate((gain_attn, gain_mlp, bias_in, bias_down)):
        out[6 + row : 7 + row, 0 : member.shape[1]] = member[...]


def share_kernel(meta, w_in, w_out, w_down, own, sent):
    core, side = meta[0], meta[1]
    lane = lax.broadcasted_iota(jnp.int32, (768, 384), 1)
    source = lax.broadcasted_iota(jnp.int32, (768, 384), 0)
    for target, which in ((own, core), (sent, 1 - core)):
        wanted = jnp.where(lane < 192, lane, lane + 192) + which * 192
        chosen = (source == wanted).astype(jnp.float32).astype(jnp.bfloat16)
        for i in range(4):
            target[i * 48 : (i + 1) * 48, :] = dot_nn(w_in[:, i * 768 : (i + 1) * 768], chosen).astype(jnp.bfloat16)
        target[192:240, :] = w_out[:, pl.ds(pl.multiple_of(which * 384, 128), 384)]
    rows = pl.ds(pl.multiple_of(side * 96, 32), 96)
    own[240:336, :] = w_down[rows, 0:384]
    own[336:432, :] = w_down[rows, 384:768]


def finish_kernel(meta, kept, came, source, grad_middle, vectors, stays, leaves):
    grad = kept[...].astype(jnp.float32) + came[...].astype(jnp.float32)
    center = source[...].astype(jnp.float32)
    center = center - jnp.mean(center, -1, keepdims=True)
    inverse = lax.rsqrt(jnp.mean(center * center, -1, keepdims=True) + 1e-05)
    norm = center * inverse
    scaled = grad * vectors[1:2, :] * vectors[0:1, :]
    result = grad_middle[...] + inverse * (
        scaled - jnp.mean(scaled, -1, keepdims=True) - norm * jnp.mean(scaled * norm, -1, keepdims=True)
    )
    half_way = stays.shape[0]
    stays[...] = result[:half_way]
    leaves[...] = result[half_way:].astype(jnp.bfloat16)


def order_weight_kernel(meta, own, other, chooser, out, gathered):
    for slot in range(16):
        start = pl.multiple_of(meta[48 + slot] * 48, 16)
        first = (slot % 8) * 48
        gathered[pl.ds(start, 48), :] = (own if slot < 8 else other)[first : first + 48, :]
    out[...] = dot_nn(gathered[...], chooser[...]).astype(jnp.bfloat16)


def project_kernel(
    meta, near, far, other_near, other_far, weight, vectors, cosine, sine, query_out, key_out, value_out, norm_out, all_queries
):
    step = pl.program_id(0)
    rows = near.shape[0]

    def project(source):
        norm = row_norm(source[...].astype(jnp.float32))
        norm_out[...] = norm.astype(jnp.bfloat16)
        attn_in = (norm * vectors[8:9, :] + vectors[2:3, :]).astype(jnp.bfloat16)
        packed = dot_nn(attn_in, weight[:, 256:768])
        first, second = packed[:, 0:128], packed[:, 128:256]
        turn_c, turn_s = cosine[...], sine[...]
        key_out[:, 0:128] = (first * turn_c - second * turn_s).astype(jnp.bfloat16)
        key_out[:, 128:256] = (second * turn_c + first * turn_s).astype(jnp.bfloat16)
        value_out[...] = packed[:, 256:512].astype(jnp.bfloat16)
        return attn_in

    def project_queries(attn_in):
        packed = dot_nn(attn_in, weight[:, 0:256]) * (HDIM ** (-0.5))
        first, second = packed[:, 0:128], packed[:, 128:256]
        turn_c, turn_s = cosine[...], sine[...]
        here = pl.ds(pl.multiple_of(step * rows, 256), rows)
        all_queries[here, 0:128] = (first * turn_c - second * turn_s).astype(jnp.bfloat16)
        all_queries[here, 128:256] = (second * turn_c + first * turn_s).astype(jnp.bfloat16)

    for number, source in enumerate((near, far, other_near, other_far)):

        @pl.when(step // 2 == number)
        def _(number=number, source=source):
            attn_in = project(source)
            if number < 2:
                project_queries(attn_in)

    @pl.when(step == 3)
    def _():
        block = query_out.shape[0] // 4
        stride = 1 + meta[64]
        for j in range(4):
            chosen = pl.ds(pl.multiple_of(((j >> 1) + (j & 1) * 2 * stride) * block, 128), block)
            query_out[j * block : (j + 1) * block, :] = all_queries[chosen, :]


def attend_kernel(meta, query_in, key_in, value_in, out_turned, log_out, out, value_turned):
    block = query_in.shape[0] // 4
    keys = key_in[...]
    value_turned[...] = value_in[...].T
    log_out[...] = jnp.zeros(log_out.shape, jnp.float32)
    out_turned[...] = jnp.zeros(out_turned.shape, jnp.float32)

    def body(number, carry):
        head = number % 3
        here = pl.ds(pl.multiple_of(number // 3 * 256, 256), 256)
        of_head = pl.ds(pl.multiple_of(head * 64, 64), 64)
        query = query_in[here, :]
        query = jnp.where(head_select(256, head), query, jnp.zeros_like(query))
        scores = contract_cols(keys, query)
        best = jnp.max(scores, 0, keepdims=True)
        raised = jnp.exp(scores - best)
        total = jnp.sum(raised, 0, keepdims=True)
        mixed = dot_nn(value_turned[of_head, :], raised.astype(jnp.bfloat16))
        out_turned[of_head, here] = mixed / total
        log_out[pl.ds(head, 1), here] = best + jnp.log(total)
        return carry

    lax.fori_loop(0, 3 * 4 * block // 256, body, 0)
    turned_back = out_turned[...].T.astype(jnp.bfloat16)
    for j in range(4):
        out[j, :, :] = turned_back[j * block : (j + 1) * block, 0:192]


def attend_back_kernel(
    meta, cosine, sine, query_in, key_in, value_in, out_turned, log_in, grad_in, grad_packed, key_sum, value_sum,
    product, grad_out, query_sums
):
    block = query_in.shape[0] // 4
    stride = 1 + meta[64]
    keys, values = key_in[...], value_in[...]
    key_turned = keys.T
    lane_pad = jnp.zeros((4 * block, 64), jnp.bfloat16)
    grad_out[...] = jnp.concatenate([jnp.concatenate([grad_in[j, :, :] for j in range(4)], 0), lane_pad], 1)
    key_sum[...] = jnp.zeros(key_sum.shape, jnp.float32)
    value_sum[...] = jnp.zeros(value_sum.shape, jnp.float32)
    product[...] = grad_out[...].astype(jnp.float32).T * out_turned[...]
    lane = lax.broadcasted_iota(jnp.int32, (1, 256), 1)

    def body(number, carry):
        head = number % 3
        here = pl.ds(pl.multiple_of(number // 3 * 256, 256), 256)
        query = query_in[here, :]
        query = jnp.where(head_select(256, head), query, jnp.zeros_like(query))
        head_grad = grad_out[here, :]
        head_grad = jnp.where(lane // 64 == head, head_grad, jnp.zeros_like(head_grad))
        probs = jnp.exp(contract_cols(keys, query) - log_in[pl.ds(head, 1), here])
        delta = jnp.sum(product[pl.ds(pl.multiple_of(head * 64, 64), 64), here], 0, keepdims=True)
        grad_scores = (probs * (contract_cols(values, head_grad) - delta)).astype(jnp.bfloat16)
        value_sum[...] += dot_nn(probs.astype(jnp.bfloat16), head_grad)
        key_sum[...] += dot_nn(grad_scores, query)
        part = dot_nn(key_turned, grad_scores).T * (HDIM ** (-0.5))
        query_sums[here, :] = jnp.where(head_select(256, head), part, query_sums[here, :])
        return carry

    query_sums[...] = jnp.zeros(query_sums.shape, jnp.float32)
    lax.fori_loop(0, 3 * 4 * block // 256, body, 0)
    for j in range(4):
        rows = pl.ds(pl.multiple_of(((j >> 1) + (j & 1) * 2 * stride) * block, 128), block)
        q_part = query_sums[j * block : (j + 1) * block, :]
        first, second = q_part[:, 0:128], q_part[:, 128:256]
        turn_c, turn_s = cosine[rows, :], sine[rows, :]
        here = slice(j * block, (j + 1) * block)
        grad_packed[here, 0:128] = (first * turn_c + second * turn_s).astype(jnp.bfloat16)
        grad_packed[here, 128:256] = (second * turn_c - first * turn_s).astype(jnp.bfloat16)


def project_back_kernel(
    meta, norm, weight, chooser, columns, cosine, sine, grad_packed, key_sum, value_sum,
    own_rows, other_rows, grad_weight, sums, grad_queries, weight_sum, total
):
    step = pl.program_id(0)
    rows = norm.shape[0]

    @pl.when(step == 0)
    def _():
        block = grad_packed.shape[0] // 4
        stride = 1 + meta[64]
        grad_queries[...] = jnp.zeros(grad_queries.shape, jnp.bfloat16)
        for j in range(4):
            chosen = pl.ds(pl.multiple_of(((j >> 1) + (j & 1) * 2 * stride) * block, 128), block)
            grad_queries[chosen, :] = grad_packed[j * block : (j + 1) * block, :]
        weight_sum[...] = jnp.zeros(weight_sum.shape, jnp.float32)
        total[...] = jnp.zeros(total.shape, jnp.float32)

    first, second = key_sum[:, 0:128], key_sum[:, 128:256]
    turn_c, turn_s = cosine[...], sine[...]
    pair = jnp.concatenate(
        [first * turn_c + second * turn_s, second * turn_c - first * turn_s, value_sum[...]], 1
    ).astype(jnp.bfloat16)
    ones = jnp.ones((8, rows), jnp.bfloat16)

    @pl.when(step < 4)
    def _():
        query = grad_queries[pl.ds(pl.multiple_of(step * rows, 256), rows), :]
        triple = jnp.concatenate([query, pair], 1)
        own_rows[...] = contract_cols(triple, weight[...]).astype(jnp.bfloat16)
        weight_sum[...] += contract_rows(norm[...], triple)
        total[...] += dot_nn(ones, triple)

    @pl.when(step >= 4)
    def _():
        other_rows[...] = contract_cols(pair, weight[:, 256:768]).astype(jnp.bfloat16)
        weight_sum[:, 256:768] += contract_rows(norm[...], pair)
        total[:, 256:768] += dot_nn(ones, pair)

    @pl.when(step == pl.num_programs(0) - 1)
    def _():
        summed = total[0:1, :]
        whole = columns[:, 0:1] * weight_sum[...] + columns[:, 1:2] * summed
        grad_weight[...] = contract_cols(whole.astype(jnp.bfloat16), chooser[...]).astype(jnp.bfloat16)
        plain = weight[...].astype(jnp.float32)
        sums[:, 0:1] = jnp.sum(plain * summed, 1, keepdims=True)
        sums[:, 1:2] = jnp.sum(plain * weight_sum[...], 1, keepdims=True)


def middle_kernel(
    meta, attended, near_a, near_b, far_a, far_b, other_near, other_far, own_rows, vectors, projected_out, middle_out, low_out,
    weight_out
):
    core = meta[64]
    mine = pl.multiple_of(core * 384, 128)
    theirs = pl.multiple_of(384 - core * 384, 128)
    for slot in range(16):
        rows_a = pl.ds(pl.multiple_of(meta[slot] * 48, 16), 48)
        rows_b = pl.ds(pl.multiple_of(meta[16 + slot] * 48, 16), 48)
        rows_p = pl.ds(pl.multiple_of(meta[32 + slot] * 48, 16), 48)
        part_a, part_b, other = (near_a, near_b, other_near) if slot < 8 else (far_a, far_b, other_far)
        weight_out[rows_a, pl.ds(mine, 256)] = part_a[slot % 8, :, :]
        weight_out[rows_b, pl.ds(pl.multiple_of(mine + 256, 128), 128)] = part_b[slot % 8, :, :]
        weight_out[rows_p, pl.ds(theirs, 256)] = other[slot % 8, :, 0:256]
        weight_out[rows_b, pl.ds(pl.multiple_of(theirs + 256, 128), 128)] = other[slot % 8, :, 256:384]
    projected = dot_nn(attended[...], weight_out[...])
    projected_out[...] = projected
    middle = own_rows[...].astype(jnp.float32) + vectors[3:4, :] * projected
    middle_out[...] = middle
    low_out[...] = (row_norm(middle) * vectors[4:5, :] * vectors[5:6, :] + vectors[6:7, :]).astype(jnp.bfloat16)


def mlp_kernel(
    meta, low_own, low_other, grad_own, grad_other, near_a, near_b, far_a, far_b, bias, sums_own, sums_other,
    keep_a, keep_b, send_a, send_b, grad_bias, weight_in, weight_down, grad_in, grad_down, branch, back
):
    def each_piece(base, part_a, part_b, move):
        def body(slot, carry):
            places = (0, 256, part_a, meta[base + slot]), (256, 128, part_b, meta[base + slot + 16])
            for lane_start, size, part, index in places:
                rows = pl.ds(pl.multiple_of(index * 48, 16), 48)
                for i in range(4):
                    lanes = slice(i * 384 + lane_start, i * 384 + lane_start + size)
                    move(part, (slot, pl.ds(i * 48, 48)), False, (rows, lanes))
                rows = pl.ds(pl.multiple_of(index * 96, 16), 96)
                for i in range(2):
                    lanes = slice(i * 384 + lane_start, i * 384 + lane_start + size)
                    move(part, (slot, pl.ds(192 + i * 96, 96)), True, (rows, lanes))
            return carry

        lax.fori_loop(0, 8, body, 0)

    def gather(part, piece, down, place):
        (weight_down if down else weight_in)[place] = part[piece]

    def scatter(part, piece, down, place):
        part[piece] = (grad_down if down else grad_in)[place]

    each_piece(0, near_a, near_b, gather)
    each_piece(8, far_a, far_b, gather)
    low = jnp.concatenate([low_own[...], low_other[...]], 0)
    grad = jnp.concatenate([grad_own[...], grad_other[...]], 0)
    tokens = low_own.shape[0]
    branch[...] = jnp.zeros(branch.shape, jnp.float32)
    back[...] = jnp.zeros(back.shape, jnp.float32)
    root, cubic = math.sqrt(2.0 / math.pi), 0.044715

    def body(number, carry):
        hidden = pl.ds(pl.multiple_of(number * 384, 128), 384)
        pre_act = dot_nn(low, weight_in[:, hidden]) + bias[:, hidden]
        square = pre_act * pre_act
        bend = jnp.tanh(root * (pre_act + cubic * square * pre_act))
        active = (0.5 * pre_act * (1.0 + bend)).astype(jnp.bfloat16)
        slope = 0.5 * (1.0 + bend) + 0.5 * pre_act * (1.0 - bend * bend) * (root * (1.0 + 3.0 * cubic * square))
        branch[...] += dot_nn(active, weight_down[hidden, :])
        grad_pre = (contract_cols(grad, weight_down[hidden, :]) * slope).astype(jnp.bfloat16)
        grad_bias[:, hidden] = jnp.sum(grad_pre.astype(jnp.float32), 0, keepdims=True)
        back[...] += contract_cols(grad_pre, weight_in[:, hidden])
        grad_in[:, hidden] = contract_rows(low, grad_pre).astype(jnp.bfloat16)
        grad_down[hidden, :] = contract_rows(active, grad).astype(jnp.bfloat16)
        return carry

    lax.fori_loop(0, 4, body, 0)
    sums_own[0, :, :] = branch[:tokens, :]
    sums_other[0, :, :] = branch[tokens:, :]
    sums_own[1, :, :] = back[:tokens, :]
    sums_other[1, :, :] = back[tokens:, :]
    each_piece(0, keep_a, keep_b, scatter)
    each_piece(8, send_a, send_b, scatter)


def turn_kernel(
    meta, sums_own, sums_other, bias, middle_in, projected_in, cotangent, grad_branch, weight,
    attended, vectors, output, grad_middle_out, grad_attn_out, grad_weight, sums
):
    width = middle_in.shape[1]
    branch = sums_own[0, :, :] + sums_other[0, :, :] + bias[...]
    middle = middle_in[...]
    grad = cotangent[...].astype(jnp.float32)
    output[...] = (middle + vectors[7:8, :] * branch).astype(jnp.bfloat16)
    back = sums_own[1, :, :] + sums_other[1, :, :]
    center = middle - jnp.mean(middle, -1, keepdims=True)
    inverse = lax.rsqrt(jnp.mean(center * center, -1, keepdims=True) + 1e-05)
    norm = center * inverse
    scaled = back * vectors[5:6, :] * vectors[4:5, :]
    grad_middle = grad + inverse * (
        scaled - jnp.mean(scaled, -1, keepdims=True) - norm * jnp.mean(scaled * norm, -1, keepdims=True)
    )
    grad_middle_out[...] = grad_middle
    grad_proj = (vectors[3:4, :] * grad_middle).astype(jnp.bfloat16)
    grad_attn_out[...] = contract_cols(grad_proj, weight[...]).astype(jnp.bfloat16)
    grad_weight[...] = contract_rows(attended[...], grad_proj).astype(jnp.bfloat16)
    def total(values):
        return jnp.sum(values, 0, keepdims=True)

    sums[...] = jnp.concatenate(
        [
            total(grad_middle * projected_in[...]),
            total(back),
            total(back * norm),
            total(grad * branch),
            total(grad_branch[...].astype(jnp.float32)),
            jnp.zeros((3, width), jnp.float32),
        ],
        0,
    )


def call(body, outs, args, scratch=(), grid=None, blocks=(), out_blocks=(), flops=0, moved=0):
    if grid is None:
        whole = pl.BlockSpec(memory_space=pltpu.VMEM)
        in_specs, out_specs = [whole] * len(args), [whole] * len(outs)
    else:
        blocks, out_blocks = dict(blocks), dict(out_blocks)

        def spec(shape, block):
            return block or pl.BlockSpec(shape, lambda i: (0,) * len(shape))

        in_specs = [spec(member.shape, blocks.get(k)) for k, member in enumerate(args)]
        out_specs = [spec(member[0], out_blocks.get(k)) for k, member in enumerate(outs)]
    in_specs[0] = pl.BlockSpec(memory_space=pltpu.SMEM)
    return pl.pallas_call(
        body,
        grid=() if grid is None else grid,
        out_shape=[jax.ShapeDtypeStruct(*member) for member in outs],
        in_specs=in_specs,
        out_specs=out_specs,
        scratch_shapes=[pltpu.VMEM(*member) for member in scratch],
        compiler_params=pltpu.CompilerParams(vmem_limit_bytes=VMEM_LIMIT),
        cost_estimate=pl.CostEstimate(flops=flops, bytes_accessed=moved, transcendentals=0),
    )(*args)


def cube_local(
    hidden_in, time_index, cotangent, w_qkv, w_attn_out, w_mlp_in, w_mlp_out, w_ada, bias_ada, gain_attn, gain_mlp,
    bias_mlp_in, bias_mlp_out
):
    f32, bf16 = jnp.float32, jnp.bfloat16
    rows, width = hidden_in.shape[1:]
    tokens = 2 * rows
    place = lax.axis_index("fsdp")
    side = lax.axis_index("seq")
    device = side * 16 + place
    core, half, group = place & 1, place >> 3, (place >> 1) & 3
    x_own = jnp.concatenate(
        [pick(hidden_in, half), swap_bits(pick(hidden_in, 1 - half), HALF_BIT)], 0
    )
    cond = jax.nn.silu(time_features(time_index, w_ada.shape[1]))
    cond_parts, rest = [], cond
    for _ in range(3):
        cond_parts.append(lax.reduce_precision(rest, 8, 7))
        rest = rest - cond_parts[-1]
    cond_parts = jnp.concatenate(cond_parts + [jnp.zeros_like(cond)], 0).astype(bf16)

    def double(values, bit):
        return jnp.concatenate([values, swap_bits(values, bit)], 0)

    (vector,) = call(
        vector_kernel,
        [((16, 576), bf16)],
        [jnp.zeros((1,), jnp.int32), cond_parts, w_ada]
        + [member[None] for member in (bias_ada, gain_attn, gain_mlp, bias_mlp_in, bias_mlp_out)],
    )
    grouped = w_qkv.reshape(48, 3, 4, 192).transpose(2, 0, 1, 3).reshape(4, 48, 576)
    grouped = grouped[group ^ jnp.arange(4)].reshape(192, 576)
    grouped = jnp.concatenate([grouped, vector], 0)
    x_own, grouped, w_mlp_in, w_attn_out, w_mlp_out = lax.optimization_barrier(
        (x_own, grouped, w_mlp_in, w_attn_out, w_mlp_out)
    )
    x_kept = x_own
    x_one = spread(x_own, TOKENS[:1])
    came_qkv = swap_bits(grouped, HALF_BIT)
    own_share, sent_share = call(
        share_kernel,
        [((432, 384), bf16), ((240, 384), bf16)],
        [jnp.stack([core, side]).astype(jnp.int32), w_mlp_in, w_attn_out, w_mlp_out],
    )
    came_share = swap_bits(sent_share, CORE_BIT)
    share = jnp.where(core == side, own_share[:240], came_share)
    share = jnp.concatenate([share[:192], own_share[240:], share[192:]], 0)
    x_one, share, place_kept = lax.optimization_barrier((x_one, share, place))
    x_two = spread(x_one, TOKENS[1:2])
    came_share = swap_bits(share, HALF_BIT)
    place = place_kept
    device, core = side * 16 + place, place & 1
    stream_own, stream_other = slot_masks(STREAM, core), slot_masks(STREAM, 1 - core)
    shared = slot_masks(SHARED, core)

    def weight_slots(masks):
        moved = ((masks & 6) | (masks >> 4))[:, None] ^ jnp.array([0, 8], jnp.int32)[None]
        return (((place & 14) + side) ^ moved).reshape(-1)

    quad = jnp.array([0, ROW_BIT, LOW_BIT, LOW_BIT | ROW_BIT], jnp.int32)
    oct_masks = (quad[:, None] ^ jnp.array([0, HALF_BIT], jnp.int32)).reshape(-1)
    row_slots = place ^ jnp.concatenate([oct_masks, oct_masks ^ CORE_BIT])
    meta = jnp.concatenate(
        [weight_slots(stream_own), weight_slots(shared), weight_slots(stream_other), row_slots, core[None]]
    ).astype(jnp.int32)
    blocks = jnp.concatenate(
        [device ^ slot_masks(TOKENS, core), device ^ CORE_BIT ^ slot_masks(TOKENS, 1 - core)]
    )
    blocks = jnp.stack([blocks, blocks ^ HALF_BIT], 1)
    inverse = jnp.exp(-math.log(10000.0) * (2 * (jnp.arange(128) % 32)).astype(f32) / HDIM)
    begin_angles = (blocks.reshape(-1) * rows).astype(f32)[:, None, None] * inverse
    inner_angles = jnp.arange(rows, dtype=jnp.int32).astype(f32)[:, None] * inverse
    begin_c, begin_s, inner_c, inner_s = [
        lax.optimization_barrier(member)
        for member in (jnp.cos(begin_angles), jnp.sin(begin_angles), jnp.cos(inner_angles), jnp.sin(inner_angles))
    ]
    cosine = (begin_c * inner_c - begin_s * inner_s).reshape(-1, 128)
    sine = (begin_s * inner_c + begin_c * inner_s).reshape(-1, 128)
    lane = jnp.arange(768) + (place >> 4)
    inner = lane % 128
    wanted = jnp.where(
        lane < 512,
        jnp.where(inner < 96, (lane // 256) * 192 + (inner // 32) * 64 + ((lane % 256) // 128) * 32 + inner % 32, -1),
        jnp.where(lane < 704, lane - 128, -1),
    )
    chooser = (jnp.arange(576)[:, None] == wanted[None, :]).astype(bf16)
    x_two, grouped, came_qkv, meta, cosine, sine, chooser = lax.optimization_barrier(
        (x_two, grouped, came_qkv, meta, cosine, sine, chooser)
    )
    x_far = swap_bits(x_two, *TOKENS[2])
    other_two = swap_bits(x_two, CORE_BIT)
    both_qkv = jnp.stack([grouped[:192], came_qkv[:192]]).reshape(2, 2, 2, 48, 576)
    vector = jnp.concatenate([grouped[192:], came_qkv[192:]], 0)
    got = swap_bits(jnp.concatenate([both_qkv[:, :, 1].reshape(192, 576), vector], 0), ROW_BIT)
    got, came_share, cotangent = lax.optimization_barrier((got, came_share, cotangent))
    both_qkv = jnp.stack([both_qkv[:, :, 0], got[:192].reshape(2, 2, 48, 576)])
    vector = jnp.concatenate([vector, got[192:]], 0)
    got = swap_bits(jnp.concatenate([both_qkv[:, :, 1].reshape(192, 576), vector], 0), LOW_BIT)
    share = jnp.stack([share, came_share])[None]
    part_a, part_b = spread(share[..., :256], STREAM[:1]), spread(share[..., 256:], SHARED[:1])
    x_far, got, part_a, part_b = lax.optimization_barrier((x_far, got, part_a, part_b))
    grouped = jnp.concatenate([both_qkv[:, :, 0].reshape(192, 576), got[:192], vector, got[192:]], 0)
    came_grouped = swap_bits(grouped, CORE_BIT)
    other_far = swap_bits(x_far, CORE_BIT)
    came_a, came_b = swap_bits(part_a, *STREAM[1]), swap_bits(part_b, *SHARED[1])
    apart = place ^ jnp.arange(16)
    vector = jnp.concatenate([grouped[384:], came_grouped[384:]], 0).reshape(16, 16, 576).astype(f32)
    vector = vector[((apart & 1) << 3) | (apart & 4) | (apart & 2) | (apart >> 3)]
    parts = [jnp.sum(vector[:, row : row + 3, :288], 1) for row in (0, 3)]
    parts += [vector[:, 6 + row, :size] for row, size in enumerate((48, 48, 192, 48))]
    modulation = jnp.stack([parts[0].reshape(6, width), parts[1].reshape(6, width)])
    shift_attn, scale_attn, gate_attn, shift_mlp, scale_mlp, gate_mlp = [
        row for row in pick(modulation, half)
    ]
    full_gain_attn, full_gain_mlp = parts[2].reshape(-1), parts[3].reshape(-1)
    bias_in = pick(parts[4].reshape(8, 2, 192), core, 1).reshape(1, -1)
    bias_down = parts[5].reshape(1, -1)
    vectors = jnp.stack(
        [full_gain_attn, 1.0 + scale_attn, shift_attn, gate_attn, full_gain_mlp, 1.0 + scale_mlp, shift_mlp, gate_mlp]
        + [full_gain_attn * (1.0 + scale_attn)]
    )
    columns = jnp.stack([vectors[8], shift_attn], 1)
    (weight_qkv,) = call(
        order_weight_kernel,
        [((768, 768), bf16)],
        [meta, grouped, came_grouped, chooser],
        [((768, 576), bf16)],
        flops=2 * 768 * 768 * 576,
        moved=3_000_000,
    )
    span = 16 * tokens
    chunk = 256

    def part_of(number, size):
        return pl.BlockSpec((chunk, size), lambda i: (jnp.clip(i - number * 2, 0, 1), 0))

    def rows_of(size):
        return pl.BlockSpec((chunk, size), lambda i: (i, 0))

    queries, keys, values, norms = call(
        project_kernel,
        [((4 * tokens, 256), bf16), ((span, 256), bf16), ((span, 256), bf16), ((span, width), bf16)],
        [meta, x_two, x_far, other_two, other_far, weight_qkv, vectors, cosine, sine],
        [((8 * tokens, 256), bf16)],
        grid=(8,),
        blocks=[(1 + number, part_of(number, width)) for number in range(4)] + [(7, rows_of(128)), (8, rows_of(128))],
        out_blocks=[(1, rows_of(256)), (2, rows_of(256)), (3, rows_of(width))],
        flops=2_000_000_000,
        moved=8_000_000,
    )
    keys, came_a, came_b = lax.optimization_barrier((keys, came_a, came_b))
    part_a, part_b = jnp.concatenate([part_a, came_a], 0), jnp.concatenate([part_b, came_b], 0)
    far_a, far_b = swap_bits(part_a, *STREAM[2]), swap_bits(part_b, *SHARED[2])
    part_a, part_b = part_a.reshape(8, 432, 256), part_b.reshape(8, 432, 128)
    other_near = swap_bits(jnp.concatenate([part_a[:, 384:], part_b[:, 384:]], 2), CORE_BIT)
    out_turned, log_total, heads_out = call(
        attend_kernel,
        [((256, 4 * tokens), f32), ((8, 4 * tokens), f32), ((4, tokens, 192), bf16)],
        [meta, queries, keys, values],
        [((256, span), bf16)],
        flops=8_000_000_000,
        moved=4_000_000,
    )
    heads_out = heads_out.reshape(2, 2, tokens, 192)
    came = swap_bits(heads_out[:, 1], ROW_BIT)
    came, far_a, far_b = lax.optimization_barrier((came, far_a, far_b))
    heads_out = jnp.stack([heads_out[:, 0], came], 1)
    by_group = jnp.stack([heads_out[0], swap_bits(heads_out[1], LOW_BIT)], 0).reshape(4, tokens, 192)
    attended = by_group[group ^ jnp.arange(4)].transpose(1, 0, 2).reshape(tokens, width)
    far_a, far_b = far_a.reshape(8, 432, 256), far_b.reshape(8, 432, 128)
    other_out = swap_bits(jnp.concatenate([far_a[:, 384:], far_b[:, 384:]], 2), CORE_BIT)
    projected, middle, mlp_own, weight_out = call(
        middle_kernel,
        [((tokens, width), f32), ((tokens, width), f32), ((tokens, width), bf16), ((768, 768), bf16)],
        [meta, attended, part_a[:, 384:], part_b[:, 384:], far_a[:, 384:], far_b[:, 384:], other_near, other_out]
        + [x_kept, vectors],
        flops=150_000_000,
        moved=3_000_000,
    )
    grad_own = jnp.concatenate(
        [pick(cotangent, half), swap_bits(pick(cotangent, 1 - half), HALF_BIT)], 0
    )
    branch_grad = (gate_mlp[None] * grad_own.astype(f32)).astype(bf16)
    branch_grad_other = swap_bits(branch_grad, CORE_BIT)
    mlp_other = swap_bits(mlp_own, CORE_BIT)
    sums_own, sums_sent, keep_a, keep_b, send_a, send_b, grad_bias_in = call(
        mlp_kernel,
        [((2, tokens, width), f32)] * 2
        + [((8, 384, 256), bf16), ((8, 384, 128), bf16)] * 2
        + [((1, 1536), f32)],
        [meta, mlp_own, mlp_other, branch_grad, branch_grad_other, part_a, part_b, far_a, far_b, bias_in],
        [((768, 1536), bf16), ((1536, 768), bf16), ((768, 1536), bf16), ((1536, 768), bf16)]
        + [((2 * tokens, width), f32)] * 2,
        flops=3_600_000_000,
        moved=12_000_000,
    )
    came = swap_bits(sums_sent, CORE_BIT)

    def plus(left, right):
        return (left.astype(f32) + right.astype(f32)).astype(bf16)

    came_a, came_b = swap_bits(send_a, *STREAM[2]), swap_bits(send_b, *SHARED[2])
    output_rows, grad_middle, grad_attn, grad_w_out, sums_mlp = call(
        turn_kernel,
        [((tokens, width), bf16), ((tokens, width), f32), ((tokens, width), bf16), ((768, 768), bf16), ((8, width), f32)],
        [meta, sums_own, came, bias_down, middle, projected, grad_own, branch_grad, weight_out]
        + [attended, vectors],
        flops=300_000_000,
        moved=5_000_000,
    )

    grad_heads = grad_attn.reshape(tokens, 4, 192).transpose(1, 0, 2)[group ^ jnp.arange(4)]
    grad_heads = quad_exchange(grad_heads.reshape(2, 2, tokens, 192)).reshape(4, tokens, 192)
    grad_heads, grad_w_out, output_rows = lax.optimization_barrier((grad_heads, grad_w_out, output_rows))
    by_core = grad_w_out.reshape(8, 2, 48, width)
    sum_out = plus(pick(by_core, core, 1), swap_bits(pick(by_core, 1 - core, 1), CORE_BIT))
    output = pair_up(output_rows[:rows], swap_bits(output_rows[rows:], HALF_BIT), half)
    grad_packed, key_sum, value_sum = call(
        attend_back_kernel,
        [((4 * tokens, 256), bf16), ((span, 256), f32), ((span, 256), f32)],
        [meta, cosine, sine, queries, keys, values, out_turned, log_total, grad_heads],
        [((256, 4 * tokens), f32), ((4 * tokens, 256), bf16), ((4 * tokens, 256), f32)],
        flops=14_000_000_000,
        moved=8_000_000,
    )
    key_sum, came_a, came_b, sum_out, output = lax.optimization_barrier((key_sum, came_a, came_b, sum_out, output))
    sum_a = plus(keep_a, came_a).reshape(4, 768, 256)
    sum_b = plus(keep_b, came_b).reshape(4, 768, 128)
    came_a, came_b = swap_bits(sum_a[2:], *STREAM[1]), swap_bits(sum_b[2:], *SHARED[1])
    y, z = (place >> 1) & 1, (place >> 2) & 1
    out_row = sum_out.reshape(2, 2, 2, 48, width)
    came_out = swap_bits(pick(out_row, 1 - y, 2), ROW_BIT)
    own_rows, other_rows, grad_qkv, sums_attn = call(
        project_back_kernel,
        [((8 * tokens, width), bf16)] * 2 + [((768, 576), bf16), ((width, 2), f32)],
        [meta, norms, weight_qkv, chooser, columns, cosine, sine, grad_packed, key_sum, value_sum],
        [((8 * tokens, 256), bf16), ((width, width), f32), ((8, width), f32)],
        grid=(8,),
        blocks=[(1, rows_of(width)), (5, rows_of(128)), (6, rows_of(128)), (8, rows_of(256)), (9, rows_of(256))],
        out_blocks=[
            (0, pl.BlockSpec((chunk, width), lambda i: (jnp.minimum(i, 3), 0))),
            (1, pl.BlockSpec((chunk, width), lambda i: (jnp.maximum(i - 4, 0), 0))),
        ],
        flops=6_000_000_000,
        moved=16_000_000,
    )
    own_rows, other_rows, grad_qkv, sums_attn, came_a, came_b, came_out = lax.optimization_barrier(
        (own_rows, other_rows, grad_qkv, sums_attn, came_a, came_b, came_out)
    )
    own_rows = own_rows.reshape(8, tokens, width)
    came_rows = swap_bits(other_rows, CORE_BIT).reshape(8, tokens, width)
    small = jnp.concatenate([sums_attn.T, sums_mlp[0:5]], 0)
    small = jnp.concatenate([small + swap_bits(small, CORE_BIT), grad_bias_in.reshape(2, width)], 0)
    by_core = grad_qkv.reshape(8, 2, 48, 576)
    kept = plus(pick(by_core, core, 1), swap_bits(pick(by_core, 1 - core, 1), CORE_BIT))
    sum_a, sum_b = plus(sum_a[:2], came_a), plus(sum_b[:2], came_b)
    sum_out = plus(pick(out_row, y, 2), came_out)
    came_a, came_b = swap_bits(sum_a[1], *STREAM[0]), swap_bits(sum_b[1], *SHARED[0])

    def sum_step(own, came, small, order):
        half_way = own.shape[0] // 2
        sent = plus(own[half_way:], came[half_way:]).reshape(-1, width)
        high = jnp.pad(small, ((0, 7), (0, 0))).astype(bf16)
        low = (jnp.pad(small, ((0, 7), (0, 0))) - high.astype(f32)).astype(bf16)
        got = swap_bits(jnp.concatenate([sent, high, low], 0), *order)
        count = sent.shape[0]
        small = small + got[count : count + 9].astype(f32) + got[count + 16 : count + 25].astype(f32)
        return plus(own[:half_way], came[:half_way]), got[:count].reshape(half_way, tokens, width), small

    came_rows, small, kept, came_a, came_b = lax.optimization_barrier((came_rows, small, kept, came_a, came_b))
    own_rows, came_rows, small = sum_step(own_rows, came_rows, small, TOKENS[2])

    def with_out(of_qkv, of_out):
        count = of_qkv.size // 576
        blocks = count * width // of_out.size
        of_out = of_out.reshape(-1, blocks, width // blocks).transpose(1, 0, 2).reshape(count, -1)
        return jnp.concatenate([of_qkv.reshape(count, 576), of_out], 1)

    def without(got, of_qkv, of_out):
        blocks = width // (got.shape[1] - 576)
        out = got[:, 576:].reshape(blocks, -1, width // blocks).transpose(1, 0, 2).reshape(of_out.shape)
        return got[:, :576].reshape(of_qkv.shape), out

    sum_a, sum_b = plus(sum_a[0], came_a).reshape(2, 384, 256), plus(sum_b[0], came_b).reshape(2, 384, 128)
    total = jnp.concatenate([sum_a, sum_b], 2)
    came_total = swap_bits(total[1], HALF_BIT)
    by_row = kept.reshape(2, 2, 2, 48, 576)
    by_row = jnp.stack([pick(by_row, y, 2), swap_bits(pick(by_row, 1 - y, 2), ROW_BIT)])
    came_rows, by_row, sum_out, small, came_total = lax.optimization_barrier(
        (came_rows, by_row, sum_out, small, came_total)
    )
    total = plus(total[0], came_total)
    across = swap_bits(total, SEQ_BIT)
    own_rows, came_rows, small = sum_step(own_rows, came_rows, small, TOKENS[1])
    sent = pick(by_row, 1 - z, 2), pick(sum_out, 1 - z, 1)
    got = without(swap_bits(with_out(*sent), LOW_BIT), *sent)
    kept, sum_out = jnp.stack([pick(by_row, z, 2), got[0]]), plus(pick(sum_out, z, 1), got[1])
    came_rows, kept, small, sum_out, across = lax.optimization_barrier((came_rows, kept, small, sum_out, across))
    mine = jnp.where(core == side, total[:192], across[:192])
    theirs = swap_bits(jnp.where(core == side, across[:192], total[:192]), CORE_BIT)
    own_rows, came_rows, small = sum_step(own_rows, came_rows, small, TOKENS[0])
    by_half = kept.reshape(4, 2, 48, 576)
    sent = pick(by_half, 1 - half, 1), pick(sum_out, 1 - half)
    got = without(swap_bits(with_out(*sent), HALF_BIT), *sent)
    kept, sum_out = plus(pick(by_half, half, 1), got[0]), plus(pick(sum_out, half), got[1])
    came_rows, small, theirs = lax.optimization_barrier((came_rows, small, theirs))
    stays, leaves = call(
        finish_kernel,
        [((rows, width), f32), ((rows, width), bf16)],
        [jnp.zeros((1,), jnp.int32), own_rows[0], came_rows[0], x_kept, grad_middle, vectors],
    )
    leaves_came = swap_bits(leaves, HALF_BIT)

    grad_down = pair_up(total[192:], across[192:], side).reshape(2, 2, 96, 384)
    grad_down = grad_down.transpose(0, 2, 1, 3).reshape(192, 768).astype(f32)
    def in_columns_back(blocks):
        return blocks.reshape(4, 48, 384).transpose(1, 0, 2).reshape(48, 8, 192)

    grad_w_in = pair_up(in_columns_back(mine), in_columns_back(theirs), core)
    grad_w_in = grad_w_in.transpose(1, 2, 0, 3).reshape(48, 3072).astype(f32)
    kept = kept[group ^ jnp.arange(4)].reshape(4, 48, 3, 192).transpose(1, 2, 0, 3).reshape(48, 2304)
    kept = jnp.concatenate([kept, sum_out], 1)
    kept, came_small, leaves_came = lax.optimization_barrier((kept, swap_bits(small, HALF_BIT), leaves_came))
    grad_hidden = pair_up(stays, leaves_came.astype(f32), half)
    came_kept = swap_bits(kept, SEQ_BIT)
    kept = kept.astype(f32) + came_kept.astype(f32)
    grad_w_qkv, grad_w_out = kept[:, :2304], kept[:, 2304:]
    both = pair_up(small, came_small, half)
    plus_scale = 1.0 + modulation[:, 1], 1.0 + modulation[:, 4]
    grad_mod = jnp.stack(
        [both[:, 0], both[:, 1] * full_gain_attn, both[:, 2], both[:, 3], both[:, 4] * full_gain_mlp, both[:, 5]], 1
    ).reshape(2, 16, 288)
    grad_mod = pick(grad_mod, place, 1)
    grad_ada = grad_mod[0][:, None] * cond[0][None] + grad_mod[1][:, None] * cond[1][None]
    gain_first = pick(jnp.sum(both[:, 1] * plus_scale[0], 0).reshape(16, 48), place)
    gain_second = pick(jnp.sum(both[:, 4] * plus_scale[1], 0).reshape(16, 48), place)
    summed = both[0] + both[1]
    bias_in_grad = pick(summed[7:9].reshape(8, 192), place >> 1)
    bias_down_grad = pick(summed[6].reshape(16, 48), place)
    return (
        output,
        grad_hidden,
        grad_w_qkv,
        grad_w_out,
        grad_w_in,
        grad_down,
        grad_ada,
        jnp.sum(grad_mod, 0),
        gain_first,
        gain_second,
        bias_in_grad,
        bias_down_grad,
    )


def solution(mesh):
    return jax.shard_map(
        cube_local if dict(mesh.shape) == {"seq": 2, "fsdp": 16} else local,
        mesh=mesh,
        in_specs=(
            P(None, ("seq", "fsdp"), None),
            P(),
            P(None, ("seq", "fsdp"), None),
            P("fsdp", None),
            P("fsdp", None),
            P("fsdp", None),
            P("fsdp", None),
            P("fsdp", None),
            P("fsdp"),
            P("fsdp"),
            P("fsdp"),
            P("fsdp"),
            P("fsdp"),
        ),
        out_specs=(
            P(None, ("seq", "fsdp"), None),
            P(None, ("seq", "fsdp"), None),
            P("fsdp", None),
            P("fsdp", None),
            P("fsdp", None),
            P("fsdp", None),
            P("fsdp", None),
            P("fsdp"),
            P("fsdp"),
            P("fsdp"),
            P("fsdp"),
            P("fsdp"),
        ),
        check_vma=False,
    )
```

```python
import math

import jax
import jax.numpy as jnp
from jax import lax
from jax.experimental import pallas as pl
from jax.experimental.pallas import tpu as pltpu
from jax.sharding import PartitionSpec as P

HEADS = 12
HDIM = 64


highest_precision = lax.Precision.HIGHEST


def normalize(values):
    center = values - jnp.mean(values, -1, keepdims=True)
    return center * lax.rsqrt(jnp.mean(center * center, -1, keepdims=True) + 1e-05)


def adapt(values, gain, shift, scale):
    return normalize(values) * gain * (1.0 + scale) + shift


def time_features(time_index, width):
    half_width = width // 2
    frequency = jnp.exp(-math.log(10000.0) * jnp.arange(half_width, dtype=jnp.float32) / half_width)
    angles = time_index.astype(jnp.float32)[:, None] * frequency[None, :]
    return jnp.concatenate([jnp.cos(angles), jnp.sin(angles)], -1)


def rotary_tables(positions, head_dim):
    inverse = jnp.exp(-math.log(10000.0) * jnp.arange(0, head_dim, 2, dtype=jnp.float32) / head_dim)
    angles = positions.astype(jnp.float32)[:, None] * inverse[None, :]
    angles = jnp.concatenate([angles, angles], -1)
    return (jnp.cos(angles), jnp.sin(angles))


def rotate(values, cosine, sine):
    first_half, second_half = jnp.split(values, 2, axis=-1)
    turned = jnp.concatenate([-second_half, first_half], -1)
    return values * cosine[:, None, :] + turned * sine[:, None, :]


def contract_rows(left_neighbor, right_neighbor):
    return lax.dot_general(
        left_neighbor, right_neighbor, (((0,), (0,)), ((), ())), preferred_element_type=jnp.float32
    )


def contract_cols(left_neighbor, right_neighbor):
    return lax.dot_general(
        left_neighbor, right_neighbor, (((1,), (1,)), ((), ())), preferred_element_type=jnp.float32
    )


def gelu_tanh(values):
    return jax.nn.gelu(values, approximate=True)


def local(
    hidden_in,
    time_index,
    cotangent,
    w_qkv,
    w_attn_out,
    w_mlp_in,
    w_mlp_out,
    w_ada,
    bias_ada,
    gain_attn,
    gain_mlp,
    bias_mlp_in,
    bias_mlp_out,
):
    seqs_here, row_count, width = hidden_in.shape
    flat_rows = seqs_here * row_count
    gathered = (
        lax.all_gather(w_qkv, "fsdp", axis=0, tiled=True),
        lax.all_gather(w_attn_out, "fsdp", axis=0, tiled=True),
        lax.all_gather(w_mlp_in, "fsdp", axis=0, tiled=True),
        lax.all_gather(w_mlp_out, "fsdp", axis=0, tiled=True),
        lax.all_gather(w_ada, "fsdp", axis=0, tiled=True),
        lax.all_gather(bias_ada, "fsdp", axis=0, tiled=True),
        lax.all_gather(gain_attn, "fsdp", axis=0, tiled=True),
        lax.all_gather(gain_mlp, "fsdp", axis=0, tiled=True),
        lax.all_gather(bias_mlp_in, "fsdp", axis=0, tiled=True),
        lax.all_gather(bias_mlp_out, "fsdp", axis=0, tiled=True),
    )
    (
        full_qkv,
        gathered_output,
        full_in,
        full_down,
        full_ada,
        full_bias_ada,
        full_gain_attn,
        full_gain_mlp,
        full_bias_in,
        full_bias_down,
    ) = gathered
    gain_first = full_gain_attn.astype(jnp.float32)
    gain_second = full_gain_mlp.astype(jnp.float32)
    cond = jax.nn.silu(time_features(time_index, full_ada.shape[1]))
    modulation = jnp.dot(
        cond, full_ada.astype(jnp.float32).T, precision=highest_precision
    ) + full_bias_ada.astype(jnp.float32)
    shift_attn, scale_attn, gate_attn, shift_mlp, scale_mlp, gate_mlp = jnp.split(
        modulation[:, None, :], 6, axis=-1
    )
    source = hidden_in.astype(jnp.float32)
    attn_in = adapt(source, gain_first, shift_attn, scale_attn)
    attn_low = attn_in.astype(jnp.bfloat16).reshape(flat_rows, width)
    qkv = jnp.dot(attn_low, full_qkv, preferred_element_type=jnp.float32).reshape(
        seqs_here, row_count, 3 * width
    )
    device_number = lax.axis_index("seq") * lax.axis_size("fsdp") + lax.axis_index("fsdp")
    positions = device_number * row_count + jnp.arange(row_count, dtype=jnp.int32)
    cosine, sine = rotary_tables(positions, HDIM)

    def turn_all(packed):
        split_three = packed.reshape(seqs_here, row_count, 3, HEADS, HDIM)
        query_turned = rotate(split_three[:, :, 0], cosine, sine).reshape(
            seqs_here, row_count, width
        )
        key_turned = rotate(split_three[:, :, 1], cosine, sine).reshape(seqs_here, row_count, width)
        return (query_turned, key_turned, split_three[:, :, 2].reshape(seqs_here, row_count, width))

    query_rot, key_rot, value_raw = turn_all(qkv)
    queries, keys, values = (
        lax.all_to_all(
            query_rot.astype(jnp.bfloat16), "seq", split_axis=2, concat_axis=1, tiled=True
        ),
        lax.all_to_all(
            key_rot.astype(jnp.bfloat16), "seq", split_axis=2, concat_axis=1, tiled=True
        ),
        lax.all_to_all(
            value_raw.astype(jnp.bfloat16), "seq", split_axis=2, concat_axis=1, tiled=True
        ),
    )
    local_heads = HEADS // lax.axis_size("seq")
    span = queries.shape[1]
    query_heads = queries.reshape(seqs_here, span, local_heads, HDIM)
    scale = HDIM ** (-0.5)

    def score_block(key_piece):
        key_heads = key_piece.reshape(seqs_here, key_piece.shape[1], local_heads, HDIM)
        logits = (
            jnp.einsum(
                "sqhd,skhd->shqk", query_heads, key_heads, preferred_element_type=jnp.float32
            )
            * scale
        )
        return (logits, key_heads)

    pieces = (
        lax.all_gather(keys, "fsdp", axis=1, tiled=True),
        lax.all_gather(values, "fsdp", axis=1, tiled=True),
    )
    best = jnp.full((seqs_here, local_heads, span), -1e30, jnp.float32)
    logits, unused = score_block(pieces[0])
    value_heads = pieces[1].reshape(seqs_here, pieces[1].shape[1], local_heads, HDIM)
    newest = jnp.maximum(best, jnp.max(logits, -1))
    raised = jnp.exp(logits - newest[..., None])
    total = jnp.sum(raised, -1)
    accum = jnp.einsum(
        "shqk,skhd->sqhd",
        raised.astype(jnp.bfloat16),
        value_heads,
        preferred_element_type=jnp.float32,
    )
    best, total, accum = (newest, total, accum)
    log_total = best + jnp.log(total)
    attended = accum / jnp.transpose(total, (0, 2, 1))[..., None]
    attended_low = attended.reshape(seqs_here, span, local_heads * HDIM).astype(jnp.bfloat16)
    attn_rows = lax.all_to_all(attended_low, "seq", split_axis=1, concat_axis=2, tiled=True)
    attn_flat = attn_rows.reshape(flat_rows, width)
    projected = jnp.dot(attn_flat, gathered_output, preferred_element_type=jnp.float32).reshape(
        seqs_here, row_count, width
    )
    middle = source + gate_attn * projected
    mlp_in = adapt(middle, gain_second, shift_mlp, scale_mlp)
    mlp_low = mlp_in.astype(jnp.bfloat16).reshape(flat_rows, width)
    pre_act = jnp.dot(mlp_low, full_in, preferred_element_type=jnp.float32) + full_bias_in.astype(
        jnp.float32
    )
    active = gelu_tanh(pre_act).astype(jnp.bfloat16)
    branch = (
        jnp.dot(active, full_down, preferred_element_type=jnp.float32)
        + full_bias_down.astype(jnp.float32)
    ).reshape(seqs_here, row_count, width)
    output = (middle + gate_mlp * branch).astype(jnp.bfloat16)
    grad_result = cotangent.astype(jnp.float32)
    grad_gate_mlp = jnp.sum(grad_result * branch, 1, keepdims=True)
    grad_branch = (gate_mlp * grad_result).astype(jnp.bfloat16).reshape(flat_rows, width)
    grad_bias_down = jnp.sum(grad_branch.astype(jnp.float32), 0)
    grad_down = contract_rows(active, grad_branch)
    grad_active = contract_cols(grad_branch, full_down)
    unused_gelu, gelu_back = jax.vjp(gelu_tanh, pre_act)
    grad_pre = gelu_back(grad_active)[0].astype(jnp.bfloat16)
    grad_bias_in = jnp.sum(grad_pre.astype(jnp.float32), 0)
    grad_in = contract_rows(mlp_low, grad_pre)
    grad_mlp_in = contract_cols(grad_pre, full_in).reshape(seqs_here, row_count, width)
    unused_second, second_back = jax.vjp(adapt, middle, gain_second, shift_mlp, scale_mlp)
    grad_middle_norm, grad_gain_mlp, grad_shift_mlp, grad_scale_mlp = second_back(grad_mlp_in)
    grad_middle = grad_result + grad_middle_norm
    grad_gate_attn = jnp.sum(grad_middle * projected, 1, keepdims=True)
    grad_proj = (gate_attn * grad_middle).astype(jnp.bfloat16).reshape(flat_rows, width)
    grad_attn_weight = contract_rows(attn_flat, grad_proj)
    grad_attn_rows = (
        contract_cols(grad_proj, gathered_output)
        .astype(jnp.bfloat16)
        .reshape(seqs_here, row_count, width)
    )
    grad_heads = lax.all_to_all(grad_attn_rows, "seq", split_axis=2, concat_axis=1, tiled=True)
    grad_head_parts = grad_heads.reshape(seqs_here, span, local_heads, HDIM)
    delta = jnp.transpose(jnp.sum(grad_head_parts.astype(jnp.float32) * attended, -1), (0, 2, 1))
    pieces = (
        lax.all_gather(keys, "fsdp", axis=1, tiled=True),
        lax.all_gather(values, "fsdp", axis=1, tiled=True),
    )
    logits, key_heads = score_block(pieces[0])
    piece_rows = pieces[1].shape[1]
    value_heads = pieces[1].reshape(seqs_here, piece_rows, local_heads, HDIM)
    probs = jnp.exp(logits - log_total[..., None])
    grad_weights = jnp.einsum(
        "sqhd,skhd->shqk", grad_head_parts, value_heads, preferred_element_type=jnp.float32
    )
    probs, grad_logits = (probs, (probs * (grad_weights - delta[..., None])).astype(jnp.bfloat16))
    grad_query = (
        jnp.einsum("shqk,skhd->sqhd", grad_logits, key_heads, preferred_element_type=jnp.float32)
        * scale
    )
    key_part = (
        jnp.einsum("shqk,sqhd->skhd", grad_logits, query_heads, preferred_element_type=jnp.float32)
        * scale
    )
    value_part = jnp.einsum(
        "shqk,sqhd->skhd",
        probs.astype(jnp.bfloat16),
        grad_head_parts,
        preferred_element_type=jnp.float32,
    )
    grad_key_all = key_part.reshape(seqs_here, piece_rows, local_heads * HDIM)
    grad_value_all = value_part.reshape(seqs_here, piece_rows, local_heads * HDIM)
    folded_rows = (grad_query, grad_key_all, grad_value_all)
    grad_query, grad_key_all, grad_value_all = folded_rows
    grad_keys, grad_values = (
        lax.psum_scatter(grad_key_all, "fsdp", scatter_dimension=1, tiled=True),
        lax.psum_scatter(grad_value_all, "fsdp", scatter_dimension=1, tiled=True),
    )
    grad_parts = (
        lax.all_to_all(
            grad_query.reshape(seqs_here, span, local_heads * HDIM).astype(jnp.bfloat16),
            "seq",
            split_axis=1,
            concat_axis=2,
            tiled=True,
        ),
        lax.all_to_all(
            grad_keys.astype(jnp.bfloat16), "seq", split_axis=1, concat_axis=2, tiled=True
        ),
        lax.all_to_all(
            grad_values.astype(jnp.bfloat16), "seq", split_axis=1, concat_axis=2, tiled=True
        ),
    )
    unused_turn, reverse_rotation = jax.vjp(turn_all, qkv)
    grad_qkv = (
        reverse_rotation(tuple((member.astype(jnp.float32) for member in grad_parts)))[0]
        .astype(jnp.bfloat16)
        .reshape(flat_rows, 3 * width)
    )
    grad_qkv_weight = contract_rows(attn_low, grad_qkv)
    grad_attn_in = contract_cols(grad_qkv, full_qkv).reshape(seqs_here, row_count, width)
    unused_first, first_back = jax.vjp(adapt, source, gain_first, shift_attn, scale_attn)
    grad_source_norm, grad_gain_attn, grad_shift_attn, grad_scale_attn = first_back(grad_attn_in)
    grad_hidden = grad_middle + grad_source_norm
    grad_mod = jnp.concatenate(
        [
            grad_shift_attn,
            grad_scale_attn,
            grad_gate_attn,
            grad_shift_mlp,
            grad_scale_mlp,
            grad_gate_mlp,
        ],
        -1,
    )[:, 0, :]
    grad_ada = jnp.dot(grad_mod.T, cond, precision=highest_precision)
    grad_bias_mod = jnp.sum(grad_mod, 0)
    summed = (
        lax.psum_scatter(grad_qkv_weight, "fsdp", scatter_dimension=0, tiled=True),
        lax.psum_scatter(grad_attn_weight, "fsdp", scatter_dimension=0, tiled=True),
        lax.psum_scatter(grad_in, "fsdp", scatter_dimension=0, tiled=True),
        lax.psum_scatter(grad_down, "fsdp", scatter_dimension=0, tiled=True),
        lax.psum_scatter(grad_ada, "fsdp", scatter_dimension=0, tiled=True),
        lax.psum_scatter(grad_bias_mod, "fsdp", scatter_dimension=0, tiled=True),
        lax.psum_scatter(grad_gain_attn, "fsdp", scatter_dimension=0, tiled=True),
        lax.psum_scatter(grad_gain_mlp, "fsdp", scatter_dimension=0, tiled=True),
        lax.psum_scatter(grad_bias_in, "fsdp", scatter_dimension=0, tiled=True),
        lax.psum_scatter(grad_bias_down, "fsdp", scatter_dimension=0, tiled=True),
    )
    totals = (
        lax.psum(summed[0].astype(jnp.bfloat16), "seq").astype(jnp.float32),
        lax.psum(summed[1].astype(jnp.bfloat16), "seq").astype(jnp.float32),
        lax.psum(summed[2].astype(jnp.bfloat16), "seq").astype(jnp.float32),
        lax.psum(summed[3].astype(jnp.bfloat16), "seq").astype(jnp.float32),
        lax.psum(summed[4].astype(jnp.bfloat16), "seq").astype(jnp.float32),
        lax.psum(summed[5].astype(jnp.bfloat16), "seq").astype(jnp.float32),
        lax.psum(summed[6].astype(jnp.bfloat16), "seq").astype(jnp.float32),
        lax.psum(summed[7].astype(jnp.bfloat16), "seq").astype(jnp.float32),
        lax.psum(summed[8].astype(jnp.bfloat16), "seq").astype(jnp.float32),
        lax.psum(summed[9].astype(jnp.bfloat16), "seq").astype(jnp.float32),
    )
    return (output, grad_hidden) + tuple(totals)


AXES = ("seq", "fsdp")
SEQ_BIT, HALF_BIT, LOW_BIT, ROW_BIT, CORE_BIT = 16, 8, 4, 2, 1
STREAM = ((ROW_BIT, SEQ_BIT), (LOW_BIT, ROW_BIT), (SEQ_BIT, LOW_BIT))
TOKENS = ((LOW_BIT, LOW_BIT), (ROW_BIT, SEQ_BIT), (SEQ_BIT, ROW_BIT))
SHARED = ((LOW_BIT, LOW_BIT), (SEQ_BIT, SEQ_BIT), (ROW_BIT, ROW_BIT))
VMEM_LIMIT = 62 * 1024 * 1024


def swap_bits(values, even, odd=None):
    odd = even if odd is None else odd
    return lax.ppermute(values, AXES, [(i, i ^ (odd if i & 1 else even)) for i in range(32)])


def spread(values, order):
    for even, odd in order:
        values = jnp.concatenate([values, swap_bits(values, even, odd)], 0)
    return values


def collect(arrays, order):
    for even, odd in reversed(order):
        half = arrays[0].shape[0] // 2
        sent = jnp.concatenate([member[half:] for member in arrays], 1) if len(arrays) > 1 else arrays[0][half:]
        came = swap_bits(sent, even, odd)
        begin, summed = 0, []
        for member in arrays:
            part = came[:, begin : begin + member.shape[1]]
            begin += member.shape[1]
            summed.append((member[:half].astype(jnp.float32) + part.astype(jnp.float32)).astype(jnp.bfloat16))
        arrays = summed
    return arrays


def slot_masks(order, core):
    masks = [jnp.int32(0)]
    for even, odd in order:
        step = jnp.where(core == 0, even, odd).astype(jnp.int32)
        masks = masks + [mask ^ step for mask in masks]
    return jnp.stack(masks)


def quad_exchange(parts):
    came = swap_bits(parts[:, 1], ROW_BIT)
    parts = jnp.stack([parts[:, 0], came], 1)
    came = swap_bits(parts[1], LOW_BIT)
    return jnp.stack([parts[0], came], 0)


def after(values, *others):
    return lax.optimization_barrier((values,) + others)[0]


def pick(values, index, axis=0):
    return lax.dynamic_index_in_dim(values, index, axis, keepdims=False)


def pair_up(mine, other, position):
    return jnp.where(position == 0, jnp.stack([mine, other]), jnp.stack([other, mine]))


def dot_nn(left, right):
    return lax.dot_general(left, right, (((1,), (0,)), ((), ())), preferred_element_type=jnp.float32)


def row_norm(values):
    center = values - jnp.mean(values, -1, keepdims=True)
    return center * lax.rsqrt(jnp.mean(center * center, -1, keepdims=True) + 1e-05)


def head_select(width, head):
    lane = lax.broadcasted_iota(jnp.int32, (1, width), 1)
    return (lane % 128) // 32 == head


def vector_kernel(meta, cond, w_ada, bias_ada, gain_attn, gain_mlp, bias_in, bias_down, out):
    part = contract_cols(cond[...], w_ada[...])
    rest = part[0:2] + part[2:4] + part[4:6] + bias_ada[...].astype(jnp.float32)
    out[...] = jnp.zeros(out.shape, jnp.bfloat16)
    for row in range(3):
        rounded = rest.astype(jnp.bfloat16)
        rest = rest - rounded.astype(jnp.float32)
        out[row : row + 1, 0 : rest.shape[1]] = rounded[0:1]
        out[row + 3 : row + 4, 0 : rest.shape[1]] = rounded[1:2]
    for row, member in enumerate((gain_attn, gain_mlp, bias_in, bias_down)):
        out[6 + row : 7 + row, 0 : member.shape[1]] = member[...]


def share_kernel(meta, w_in, w_out, w_down, own, sent):
    core, side = meta[0], meta[1]
    lane = lax.broadcasted_iota(jnp.int32, (768, 384), 1)
    source = lax.broadcasted_iota(jnp.int32, (768, 384), 0)
    for target, which in ((own, core), (sent, 1 - core)):
        wanted = jnp.where(lane < 192, lane, lane + 192) + which * 192
        chosen = (source == wanted).astype(jnp.float32).astype(jnp.bfloat16)

        def body(i, carry, target=target, chosen=chosen):
            columns = w_in[:, pl.ds(pl.multiple_of(i * 768, 128), 768)]
            target[pl.ds(pl.multiple_of(i * 48, 16), 48), :] = dot_nn(columns, chosen).astype(jnp.bfloat16)
            return carry

        lax.fori_loop(0, 4, body, 0)
        target[192:240, :] = w_out[:, pl.ds(pl.multiple_of(which * 384, 128), 384)]
    rows = pl.ds(pl.multiple_of(side * 96, 32), 96)
    own[240:336, :] = w_down[rows, 0:384]
    own[336:432, :] = w_down[rows, 384:768]


def finish_kernel(meta, kept, came, source, grad_middle, vectors, stays, leaves):
    grad = kept[...].astype(jnp.float32) + came[...].astype(jnp.float32)
    center = source[...].astype(jnp.float32)
    center = center - jnp.mean(center, -1, keepdims=True)
    inverse = lax.rsqrt(jnp.mean(center * center, -1, keepdims=True) + 1e-05)
    norm = center * inverse
    scaled = grad * vectors[1:2, :] * vectors[0:1, :]
    result = grad_middle[...] + inverse * (
        scaled - jnp.mean(scaled, -1, keepdims=True) - norm * jnp.mean(scaled * norm, -1, keepdims=True)
    )
    half_way = stays.shape[0]
    stays[...] = result[:half_way]
    leaves[...] = result[half_way:].astype(jnp.bfloat16)


def order_weight_kernel(meta, own, other, chooser, out, gathered):
    for base, source in ((48, own), (56, other)):

        def body(slot, carry, base=base, source=source):
            start = pl.multiple_of(meta[base + slot] * 48, 16)
            gathered[pl.ds(start, 48), :] = source[pl.ds(pl.multiple_of(slot * 48, 16), 48), :]
            return carry

        lax.fori_loop(0, 8, body, 0)
    out[...] = dot_nn(gathered[...], chooser[...]).astype(jnp.bfloat16)


def project_kernel(
    meta, near, far, other_near, other_far, weight, vectors, cosine, sine, query_out, key_out, value_out, norm_out, all_queries, chunk
):
    step = pl.program_id(0)
    rows = near.shape[0]

    for number, source in enumerate((near, far, other_near, other_far)):

        @pl.when(step // 2 == number)
        def _(source=source):
            chunk[...] = source[...]

    norm = row_norm(chunk[...].astype(jnp.float32))
    norm_out[...] = norm.astype(jnp.bfloat16)
    attn_in = (norm * vectors[8:9, :] + vectors[2:3, :]).astype(jnp.bfloat16)
    turn_c, turn_s = cosine[...], sine[...]
    packed = dot_nn(attn_in, weight[:, 256:768])
    first, second = packed[:, 0:128], packed[:, 128:256]
    key_out[:, 0:128] = (first * turn_c - second * turn_s).astype(jnp.bfloat16)
    key_out[:, 128:256] = (second * turn_c + first * turn_s).astype(jnp.bfloat16)
    value_out[...] = packed[:, 256:512].astype(jnp.bfloat16)

    @pl.when(step < 4)
    def _():
        packed = dot_nn(attn_in, weight[:, 0:256]) * (HDIM ** (-0.5))
        first, second = packed[:, 0:128], packed[:, 128:256]
        here = pl.ds(pl.multiple_of(step * rows, 256), rows)
        all_queries[here, 0:128] = (first * turn_c - second * turn_s).astype(jnp.bfloat16)
        all_queries[here, 128:256] = (second * turn_c + first * turn_s).astype(jnp.bfloat16)

    @pl.when(step == 3)
    def _():
        block = query_out.shape[0] // 4
        stride = 1 + meta[64]
        for j in range(4):
            chosen = pl.ds(pl.multiple_of(((j >> 1) + (j & 1) * 2 * stride) * block, 128), block)
            query_out[j * block : (j + 1) * block, :] = all_queries[chosen, :]


def attend_kernel(meta, query_in, key_in, value_in, out_turned, log_out, out, value_turned):
    block = query_in.shape[0] // 4
    keys = key_in[...]
    value_turned[...] = value_in[...].T
    log_out[...] = jnp.zeros(log_out.shape, jnp.float32)
    out_turned[...] = jnp.zeros(out_turned.shape, jnp.float32)

    def body(number, carry):
        head = number % 3
        here = pl.ds(pl.multiple_of(number // 3 * 256, 256), 256)
        of_head = pl.ds(pl.multiple_of(head * 64, 64), 64)
        query = query_in[here, :]
        query = jnp.where(head_select(256, head), query, jnp.zeros_like(query))
        scores = contract_cols(keys, query)
        best = jnp.max(scores, 0, keepdims=True)
        raised = jnp.exp(scores - best)
        total = jnp.sum(raised, 0, keepdims=True)
        mixed = dot_nn(value_turned[of_head, :], raised.astype(jnp.bfloat16))
        out_turned[of_head, here] = mixed / total
        log_out[pl.ds(head, 1), here] = best + jnp.log(total)
        return carry

    lax.fori_loop(0, 3 * 4 * block // 256, body, 0)
    turned_back = out_turned[...].T.astype(jnp.bfloat16)
    for j in range(4):
        out[j, :, :] = turned_back[j * block : (j + 1) * block, 0:192]


def attend_back_kernel(
    meta, cosine, sine, query_in, key_in, value_in, out_turned, log_in, grad_in, grad_packed, key_sum, value_sum,
    product, grad_out, query_sums
):
    block = query_in.shape[0] // 4
    stride = 1 + meta[64]
    keys, values = key_in[...], value_in[...]
    key_turned = keys.T
    lane_pad = jnp.zeros((4 * block, 64), jnp.bfloat16)
    grad_out[...] = jnp.concatenate([jnp.concatenate([grad_in[j, :, :] for j in range(4)], 0), lane_pad], 1)
    key_sum[...] = jnp.zeros(key_sum.shape, jnp.float32)
    value_sum[...] = jnp.zeros(value_sum.shape, jnp.float32)
    product[...] = grad_out[...].astype(jnp.float32).T * out_turned[...]
    lane = lax.broadcasted_iota(jnp.int32, (1, 256), 1)

    def body(number, carry):
        here = pl.ds(pl.multiple_of(number * 256, 256), 256)
        query_sum = jnp.zeros((256, 256), jnp.float32)
        for head in range(3):
            query = query_in[here, :]
            query = jnp.where(head_select(256, head), query, jnp.zeros_like(query))
            head_grad = grad_out[here, :]
            head_grad = jnp.where(lane // 64 == head, head_grad, jnp.zeros_like(head_grad))
            probs = jnp.exp(contract_cols(keys, query) - log_in[head : head + 1, here])
            delta = jnp.sum(product[head * 64 : (head + 1) * 64, here], 0, keepdims=True)
            grad_scores = (probs * (contract_cols(values, head_grad) - delta)).astype(jnp.bfloat16)
            value_sum[...] += dot_nn(probs.astype(jnp.bfloat16), head_grad)
            key_sum[...] += dot_nn(grad_scores, query)
            part = dot_nn(key_turned, grad_scores)
            query_sum = jnp.where((sub % 128) // 32 == head, part, query_sum)
        query_sums[here, :] = query_sum.T * (HDIM ** (-0.5))
        return carry

    sub = lax.broadcasted_iota(jnp.int32, (256, 1), 0)
    lax.fori_loop(0, 4 * block // 256, body, 0)
    for j in range(4):
        rows = pl.ds(pl.multiple_of(((j >> 1) + (j & 1) * 2 * stride) * block, 128), block)
        q_part = query_sums[j * block : (j + 1) * block, :]
        first, second = q_part[:, 0:128], q_part[:, 128:256]
        turn_c, turn_s = cosine[rows, :], sine[rows, :]
        here = slice(j * block, (j + 1) * block)
        grad_packed[here, 0:128] = (first * turn_c + second * turn_s).astype(jnp.bfloat16)
        grad_packed[here, 128:256] = (second * turn_c - first * turn_s).astype(jnp.bfloat16)


def project_back_kernel(
    meta, norm, weight, chooser, columns, cosine, sine, grad_packed, key_sum, value_sum,
    own_rows, other_rows, grad_weight, sums, grad_queries, weight_sum, total
):
    step = pl.program_id(0)
    rows = norm.shape[0]

    @pl.when(step == 0)
    def _():
        block = grad_packed.shape[0] // 4
        stride = 1 + meta[64]
        grad_queries[...] = jnp.zeros(grad_queries.shape, jnp.bfloat16)
        for j in range(4):
            chosen = pl.ds(pl.multiple_of(((j >> 1) + (j & 1) * 2 * stride) * block, 128), block)
            grad_queries[chosen, :] = grad_packed[j * block : (j + 1) * block, :]
        weight_sum[...] = jnp.zeros(weight_sum.shape, jnp.float32)
        total[...] = jnp.zeros(total.shape, jnp.float32)

    first, second = key_sum[:, 0:128], key_sum[:, 128:256]
    turn_c, turn_s = cosine[...], sine[...]
    pair = jnp.concatenate(
        [first * turn_c + second * turn_s, second * turn_c - first * turn_s, value_sum[...]], 1
    ).astype(jnp.bfloat16)
    ones = jnp.ones((8, rows), jnp.bfloat16)

    @pl.when(step < 4)
    def _():
        query = grad_queries[pl.ds(pl.multiple_of(step * rows, 256), rows), :]
        triple = jnp.concatenate([query, pair], 1)
        own_rows[...] = contract_cols(triple, weight[...]).astype(jnp.bfloat16)
        weight_sum[...] += contract_rows(norm[...], triple)
        total[...] += dot_nn(ones, triple)

    @pl.when(step >= 4)
    def _():
        other_rows[...] = contract_cols(pair, weight[:, 256:768]).astype(jnp.bfloat16)
        weight_sum[:, 256:768] += contract_rows(norm[...], pair)
        total[:, 256:768] += dot_nn(ones, pair)

    @pl.when(step == pl.num_programs(0) - 1)
    def _():
        def body(i, carry):
            here = pl.ds(pl.multiple_of(i * 256, 256), 256)
            summed = total[0:1, :]
            part = weight_sum[here, :]
            whole = columns[here, 0:1] * part + columns[here, 1:2] * summed
            grad_weight[here, :] = contract_cols(whole.astype(jnp.bfloat16), chooser[...]).astype(jnp.bfloat16)
            plain = weight[here, :].astype(jnp.float32)
            sums[here, 0:1] = jnp.sum(plain * summed, 1, keepdims=True)
            sums[here, 1:2] = jnp.sum(plain * part, 1, keepdims=True)
            return carry

        lax.fori_loop(0, weight.shape[0] // 256, body, 0)


def middle_kernel(
    meta, attended, near_a, near_b, far_a, far_b, other_near, other_far, own_rows, vectors, projected_out, middle_out, low_out,
    weight_out
):
    core = meta[64]
    mine = pl.multiple_of(core * 384, 128)
    theirs = pl.multiple_of(384 - core * 384, 128)
    for base, part_a, part_b, other in ((0, near_a, near_b, other_near), (8, far_a, far_b, other_far)):

        def body(slot, carry, base=base, part_a=part_a, part_b=part_b, other=other):
            rows_a = pl.ds(pl.multiple_of(meta[base + slot] * 48, 16), 48)
            rows_b = pl.ds(pl.multiple_of(meta[base + slot + 16] * 48, 16), 48)
            rows_p = pl.ds(pl.multiple_of(meta[base + slot + 32] * 48, 16), 48)
            weight_out[rows_a, pl.ds(mine, 256)] = part_a[slot]
            weight_out[rows_b, pl.ds(pl.multiple_of(mine + 256, 128), 128)] = part_b[slot]
            weight_out[rows_p, pl.ds(theirs, 256)] = other[slot, :, 0:256]
            weight_out[rows_b, pl.ds(pl.multiple_of(theirs + 256, 128), 128)] = other[slot, :, 256:384]
            return carry

        lax.fori_loop(0, 8, body, 0)
    projected = dot_nn(attended[...], weight_out[...])
    projected_out[...] = projected
    middle = own_rows[...].astype(jnp.float32) + vectors[3:4, :] * projected
    middle_out[...] = middle
    low_out[...] = (row_norm(middle) * vectors[4:5, :] * vectors[5:6, :] + vectors[6:7, :]).astype(jnp.bfloat16)


def mlp_kernel(
    meta, low_own, low_other, grad_own, grad_other, near_a, near_b, far_a, far_b, bias, sums_own, sums_other,
    keep_a, keep_b, send_a, send_b, grad_bias, weight_in, weight_down, grad_in, grad_down, branch, back
):
    def each_piece(base, part_a, part_b, move):
        def body(slot, carry):
            places = (0, 256, part_a, meta[base + slot]), (256, 128, part_b, meta[base + slot + 16])
            for lane_start, size, part, index in places:
                rows = pl.ds(pl.multiple_of(index * 48, 16), 48)
                for i in range(4):
                    lanes = slice(i * 384 + lane_start, i * 384 + lane_start + size)
                    move(part, (slot, pl.ds(i * 48, 48)), False, (rows, lanes))
                rows = pl.ds(pl.multiple_of(index * 96, 16), 96)
                for i in range(2):
                    lanes = slice(i * 384 + lane_start, i * 384 + lane_start + size)
                    move(part, (slot, pl.ds(192 + i * 96, 96)), True, (rows, lanes))
            return carry

        lax.fori_loop(0, 8, body, 0)

    def gather(part, piece, down, place):
        (weight_down if down else weight_in)[place] = part[piece]

    def scatter(part, piece, down, place):
        part[piece] = (grad_down if down else grad_in)[place]

    each_piece(0, near_a, near_b, gather)
    each_piece(8, far_a, far_b, gather)
    low = jnp.concatenate([low_own[...], low_other[...]], 0)
    grad = jnp.concatenate([grad_own[...], grad_other[...]], 0)
    tokens = low_own.shape[0]
    branch[...] = jnp.zeros(branch.shape, jnp.float32)
    back[...] = jnp.zeros(back.shape, jnp.float32)
    root, cubic = math.sqrt(2.0 / math.pi), 0.044715

    def body(number, carry):
        hidden = pl.ds(pl.multiple_of(number * 384, 128), 384)
        pre_act = dot_nn(low, weight_in[:, hidden]) + bias[:, hidden]
        square = pre_act * pre_act
        bend = jnp.tanh(root * (pre_act + cubic * square * pre_act))
        active = (0.5 * pre_act * (1.0 + bend)).astype(jnp.bfloat16)
        slope = 0.5 * (1.0 + bend) + 0.5 * pre_act * (1.0 - bend * bend) * (root * (1.0 + 3.0 * cubic * square))
        branch[...] += dot_nn(active, weight_down[hidden, :])
        grad_pre = (contract_cols(grad, weight_down[hidden, :]) * slope).astype(jnp.bfloat16)
        grad_bias[:, hidden] = jnp.sum(grad_pre.astype(jnp.float32), 0, keepdims=True)
        back[...] += contract_cols(grad_pre, weight_in[:, hidden])
        grad_in[:, hidden] = contract_rows(low, grad_pre).astype(jnp.bfloat16)
        grad_down[hidden, :] = contract_rows(active, grad).astype(jnp.bfloat16)
        return carry

    lax.fori_loop(0, 4, body, 0)
    sums_own[0, :, :] = branch[:tokens, :]
    sums_other[0, :, :] = branch[tokens:, :]
    sums_own[1, :, :] = back[:tokens, :]
    sums_other[1, :, :] = back[tokens:, :]
    each_piece(0, keep_a, keep_b, scatter)
    each_piece(8, send_a, send_b, scatter)


def turn_kernel(
    meta, sums_own, sums_other, bias, middle_in, projected_in, cotangent, grad_branch, weight,
    attended, vectors, output, grad_middle_out, grad_attn_out, grad_weight, sums
):
    width = middle_in.shape[1]
    branch = sums_own[0, :, :] + sums_other[0, :, :] + bias[...]
    middle = middle_in[...]
    grad = cotangent[...].astype(jnp.float32)
    output[...] = (middle + vectors[7:8, :] * branch).astype(jnp.bfloat16)
    back = sums_own[1, :, :] + sums_other[1, :, :]
    center = middle - jnp.mean(middle, -1, keepdims=True)
    inverse = lax.rsqrt(jnp.mean(center * center, -1, keepdims=True) + 1e-05)
    norm = center * inverse
    scaled = back * vectors[5:6, :] * vectors[4:5, :]
    grad_middle = grad + inverse * (
        scaled - jnp.mean(scaled, -1, keepdims=True) - norm * jnp.mean(scaled * norm, -1, keepdims=True)
    )
    grad_middle_out[...] = grad_middle
    grad_proj = (vectors[3:4, :] * grad_middle).astype(jnp.bfloat16)
    grad_attn_out[...] = contract_cols(grad_proj, weight[...]).astype(jnp.bfloat16)
    grad_weight[...] = contract_rows(attended[...], grad_proj).astype(jnp.bfloat16)
    def total(values):
        return jnp.sum(values, 0, keepdims=True)

    sums[...] = jnp.concatenate(
        [
            total(grad_middle * projected_in[...]),
            total(back),
            total(back * norm),
            total(grad * branch),
            total(grad_branch[...].astype(jnp.float32)),
            jnp.zeros((3, width), jnp.float32),
        ],
        0,
    )


def call(body, outs, args, scratch=(), grid=None, blocks=(), out_blocks=(), flops=0, moved=0):
    if grid is None:
        whole = pl.BlockSpec(memory_space=pltpu.VMEM)
        in_specs, out_specs = [whole] * len(args), [whole] * len(outs)
    else:
        blocks, out_blocks = dict(blocks), dict(out_blocks)

        def spec(shape, block):
            return block or pl.BlockSpec(shape, lambda i: (0,) * len(shape))

        in_specs = [spec(member.shape, blocks.get(k)) for k, member in enumerate(args)]
        out_specs = [spec(member[0], out_blocks.get(k)) for k, member in enumerate(outs)]
    in_specs[0] = pl.BlockSpec(memory_space=pltpu.SMEM)
    return pl.pallas_call(
        body,
        grid=() if grid is None else grid,
        out_shape=[jax.ShapeDtypeStruct(*member) for member in outs],
        in_specs=in_specs,
        out_specs=out_specs,
        scratch_shapes=[pltpu.VMEM(*member) for member in scratch],
        compiler_params=pltpu.CompilerParams(vmem_limit_bytes=VMEM_LIMIT),
        cost_estimate=pl.CostEstimate(flops=flops, bytes_accessed=moved, transcendentals=0),
    )(*args)


def cube_local(
    hidden_in, time_index, cotangent, w_qkv, w_attn_out, w_mlp_in, w_mlp_out, w_ada, bias_ada, gain_attn, gain_mlp,
    bias_mlp_in, bias_mlp_out
):
    f32, bf16 = jnp.float32, jnp.bfloat16
    rows, width = hidden_in.shape[1:]
    tokens = 2 * rows
    place = lax.axis_index("fsdp")
    side = lax.axis_index("seq")
    device = side * 16 + place
    core, half, group = place & 1, place >> 3, (place >> 1) & 3
    x_own = jnp.concatenate(
        [pick(hidden_in, half), swap_bits(pick(hidden_in, 1 - half), HALF_BIT)], 0
    )
    cond = jax.nn.silu(time_features(time_index, w_ada.shape[1]))
    cond_parts, rest = [], cond
    for _ in range(3):
        cond_parts.append(lax.reduce_precision(rest, 8, 7))
        rest = rest - cond_parts[-1]
    cond_parts = jnp.concatenate(cond_parts + [jnp.zeros_like(cond)], 0).astype(bf16)

    def double(values, bit):
        return jnp.concatenate([values, swap_bits(values, bit)], 0)

    (vector,) = call(
        vector_kernel,
        [((16, 576), bf16)],
        [jnp.zeros((1,), jnp.int32), cond_parts, w_ada]
        + [member[None] for member in (bias_ada, gain_attn, gain_mlp, bias_mlp_in, bias_mlp_out)],
    )
    grouped = w_qkv.reshape(48, 3, 4, 192).transpose(2, 0, 1, 3).reshape(4, 48, 576)
    grouped = grouped[group ^ jnp.arange(4)].reshape(192, 576)
    grouped = jnp.concatenate([grouped, vector], 0)
    x_own, grouped, w_mlp_in, w_attn_out, w_mlp_out = lax.optimization_barrier(
        (x_own, grouped, w_mlp_in, w_attn_out, w_mlp_out)
    )
    x_kept = x_own
    x_one = spread(x_own, TOKENS[:1])
    came_qkv = swap_bits(grouped, HALF_BIT)
    own_share, sent_share = call(
        share_kernel,
        [((432, 384), bf16), ((240, 384), bf16)],
        [jnp.stack([core, side]).astype(jnp.int32), w_mlp_in, w_attn_out, w_mlp_out],
    )
    came_share = swap_bits(sent_share, CORE_BIT)
    share = jnp.where(core == side, own_share[:240], came_share)
    share = jnp.concatenate([share[:192], own_share[240:], share[192:]], 0)
    x_one, share, place_kept = lax.optimization_barrier((x_one, share, place))
    x_two = spread(x_one, TOKENS[1:2])
    came_share = swap_bits(share, HALF_BIT)
    place = place_kept
    device, core = side * 16 + place, place & 1
    stream_own, stream_other = slot_masks(STREAM, core), slot_masks(STREAM, 1 - core)
    shared = slot_masks(SHARED, core)

    def weight_slots(masks):
        moved = ((masks & 6) | (masks >> 4))[:, None] ^ jnp.array([0, 8], jnp.int32)[None]
        return (((place & 14) + side) ^ moved).reshape(-1)

    quad = jnp.array([0, ROW_BIT, LOW_BIT, LOW_BIT | ROW_BIT], jnp.int32)
    oct_masks = (quad[:, None] ^ jnp.array([0, HALF_BIT], jnp.int32)).reshape(-1)
    row_slots = place ^ jnp.concatenate([oct_masks, oct_masks ^ CORE_BIT])
    meta = jnp.concatenate(
        [weight_slots(stream_own), weight_slots(shared), weight_slots(stream_other), row_slots, core[None]]
    ).astype(jnp.int32)
    blocks = jnp.concatenate(
        [device ^ slot_masks(TOKENS, core), device ^ CORE_BIT ^ slot_masks(TOKENS, 1 - core)]
    )
    blocks = jnp.stack([blocks, blocks ^ HALF_BIT], 1)
    inverse = jnp.exp(-math.log(10000.0) * (2 * (jnp.arange(128) % 32)).astype(f32) / HDIM)
    begin_angles = (blocks.reshape(-1) * rows).astype(f32)[:, None, None] * inverse
    inner_angles = jnp.arange(rows, dtype=jnp.int32).astype(f32)[:, None] * inverse
    begin_c, begin_s, inner_c, inner_s = [
        lax.optimization_barrier(member)
        for member in (jnp.cos(begin_angles), jnp.sin(begin_angles), jnp.cos(inner_angles), jnp.sin(inner_angles))
    ]
    cosine = (begin_c * inner_c - begin_s * inner_s).reshape(-1, 128)
    sine = (begin_s * inner_c + begin_c * inner_s).reshape(-1, 128)
    lane = jnp.arange(768) + (place >> 4)
    inner = lane % 128
    wanted = jnp.where(
        lane < 512,
        jnp.where(inner < 96, (lane // 256) * 192 + (inner // 32) * 64 + ((lane % 256) // 128) * 32 + inner % 32, -1),
        jnp.where(lane < 704, lane - 128, -1),
    )
    chooser = (jnp.arange(576)[:, None] == wanted[None, :]).astype(bf16)
    x_two, grouped, came_qkv, meta, cosine, sine, chooser = lax.optimization_barrier(
        (x_two, grouped, came_qkv, meta, cosine, sine, chooser)
    )
    x_far = swap_bits(x_two, *TOKENS[2])
    other_two = swap_bits(x_two, CORE_BIT)
    both_qkv = jnp.stack([grouped[:192], came_qkv[:192]]).reshape(2, 2, 2, 48, 576)
    vector = jnp.concatenate([grouped[192:], came_qkv[192:]], 0)
    got = swap_bits(jnp.concatenate([both_qkv[:, :, 1].reshape(192, 576), vector], 0), ROW_BIT)
    got, came_share, cotangent = lax.optimization_barrier((got, came_share, cotangent))
    both_qkv = jnp.stack([both_qkv[:, :, 0], got[:192].reshape(2, 2, 48, 576)])
    vector = jnp.concatenate([vector, got[192:]], 0)
    got = swap_bits(jnp.concatenate([both_qkv[:, :, 1].reshape(192, 576), vector], 0), LOW_BIT)
    share = jnp.stack([share, came_share])[None]
    part_a, part_b = spread(share[..., :256], STREAM[:1]), spread(share[..., 256:], SHARED[:1])
    x_far, got, part_a, part_b = lax.optimization_barrier((x_far, got, part_a, part_b))
    grouped = jnp.concatenate([both_qkv[:, :, 0].reshape(192, 576), got[:192], vector, got[192:]], 0)
    came_grouped = swap_bits(grouped, CORE_BIT)
    other_far = swap_bits(x_far, CORE_BIT)
    came_a, came_b = swap_bits(part_a, *STREAM[1]), swap_bits(part_b, *SHARED[1])
    apart = place ^ jnp.arange(16)
    vector = jnp.concatenate([grouped[384:], came_grouped[384:]], 0).reshape(16, 16, 576).astype(f32)
    vector = vector[((apart & 1) << 3) | (apart & 4) | (apart & 2) | (apart >> 3)]
    parts = [jnp.sum(vector[:, row : row + 3, :288], 1) for row in (0, 3)]
    parts += [vector[:, 6 + row, :size] for row, size in enumerate((48, 48, 192, 48))]
    modulation = jnp.stack([parts[0].reshape(6, width), parts[1].reshape(6, width)])
    shift_attn, scale_attn, gate_attn, shift_mlp, scale_mlp, gate_mlp = [
        row for row in pick(modulation, half)
    ]
    full_gain_attn, full_gain_mlp = parts[2].reshape(-1), parts[3].reshape(-1)
    bias_in = pick(parts[4].reshape(8, 2, 192), core, 1).reshape(1, -1)
    bias_down = parts[5].reshape(1, -1)
    vectors = jnp.stack(
        [full_gain_attn, 1.0 + scale_attn, shift_attn, gate_attn, full_gain_mlp, 1.0 + scale_mlp, shift_mlp, gate_mlp]
        + [full_gain_attn * (1.0 + scale_attn)]
    )
    columns = jnp.stack([vectors[8], shift_attn], 1)
    (weight_qkv,) = call(
        order_weight_kernel,
        [((768, 768), bf16)],
        [meta, grouped, came_grouped, chooser],
        [((768, 576), bf16)],
        flops=2 * 768 * 768 * 576,
        moved=3_000_000,
    )
    span = 16 * tokens
    chunk = 256

    def part_of(number, size):
        return pl.BlockSpec((chunk, size), lambda i: (jnp.clip(i - number * 2, 0, 1), 0))

    def rows_of(size):
        return pl.BlockSpec((chunk, size), lambda i: (i, 0))

    queries, keys, values, norms = call(
        project_kernel,
        [((4 * tokens, 256), bf16), ((span, 256), bf16), ((span, 256), bf16), ((span, width), bf16)],
        [meta, x_two, x_far, other_two, other_far, weight_qkv, vectors, cosine, sine],
        [((8 * tokens, 256), bf16), ((chunk, width), bf16)],
        grid=(8,),
        blocks=[(1 + number, part_of(number, width)) for number in range(4)] + [(7, rows_of(128)), (8, rows_of(128))],
        out_blocks=[(1, rows_of(256)), (2, rows_of(256)), (3, rows_of(width))],
        flops=2_000_000_000,
        moved=8_000_000,
    )
    keys, came_a, came_b = lax.optimization_barrier((keys, came_a, came_b))
    part_a, part_b = jnp.concatenate([part_a, came_a], 0), jnp.concatenate([part_b, came_b], 0)
    far_a, far_b = swap_bits(part_a, *STREAM[2]), swap_bits(part_b, *SHARED[2])
    part_a, part_b = part_a.reshape(8, 432, 256), part_b.reshape(8, 432, 128)
    other_near = swap_bits(jnp.concatenate([part_a[:, 384:], part_b[:, 384:]], 2), CORE_BIT)
    out_turned, log_total, heads_out = call(
        attend_kernel,
        [((256, 4 * tokens), f32), ((8, 4 * tokens), f32), ((4, tokens, 192), bf16)],
        [meta, queries, keys, values],
        [((256, span), bf16)],
        flops=8_000_000_000,
        moved=4_000_000,
    )
    heads_out = heads_out.reshape(2, 2, tokens, 192)
    came = swap_bits(heads_out[:, 1], ROW_BIT)
    came, far_a, far_b = lax.optimization_barrier((came, far_a, far_b))
    heads_out = jnp.stack([heads_out[:, 0], came], 1)
    by_group = jnp.stack([heads_out[0], swap_bits(heads_out[1], LOW_BIT)], 0).reshape(4, tokens, 192)
    attended = by_group[group ^ jnp.arange(4)].transpose(1, 0, 2).reshape(tokens, width)
    far_a, far_b = far_a.reshape(8, 432, 256), far_b.reshape(8, 432, 128)
    other_out = swap_bits(jnp.concatenate([far_a[:, 384:], far_b[:, 384:]], 2), CORE_BIT)
    projected, middle, mlp_own, weight_out = call(
        middle_kernel,
        [((tokens, width), f32), ((tokens, width), f32), ((tokens, width), bf16), ((768, 768), bf16)],
        [meta, attended, part_a[:, 384:], part_b[:, 384:], far_a[:, 384:], far_b[:, 384:], other_near, other_out]
        + [x_kept, vectors],
        flops=150_000_000,
        moved=3_000_000,
    )
    grad_own = jnp.concatenate(
        [pick(cotangent, half), swap_bits(pick(cotangent, 1 - half), HALF_BIT)], 0
    )
    branch_grad = (gate_mlp[None] * grad_own.astype(f32)).astype(bf16)
    branch_grad_other = swap_bits(branch_grad, CORE_BIT)
    mlp_other = swap_bits(mlp_own, CORE_BIT)
    sums_own, sums_sent, keep_a, keep_b, send_a, send_b, grad_bias_in = call(
        mlp_kernel,
        [((2, tokens, width), f32)] * 2
        + [((8, 384, 256), bf16), ((8, 384, 128), bf16)] * 2
        + [((1, 1536), f32)],
        [meta, mlp_own, mlp_other, branch_grad, branch_grad_other, part_a, part_b, far_a, far_b, bias_in],
        [((768, 1536), bf16), ((1536, 768), bf16), ((768, 1536), bf16), ((1536, 768), bf16)]
        + [((2 * tokens, width), f32)] * 2,
        flops=3_600_000_000,
        moved=12_000_000,
    )
    came = swap_bits(sums_sent, CORE_BIT)

    def plus(left, right):
        return (left.astype(f32) + right.astype(f32)).astype(bf16)

    came_a, came_b = swap_bits(send_a, *STREAM[2]), swap_bits(send_b, *SHARED[2])
    output_rows, grad_middle, grad_attn, grad_w_out, sums_mlp = call(
        turn_kernel,
        [((tokens, width), bf16), ((tokens, width), f32), ((tokens, width), bf16), ((768, 768), bf16), ((8, width), f32)],
        [meta, sums_own, came, bias_down, middle, projected, grad_own, branch_grad, weight_out]
        + [attended, vectors],
        flops=300_000_000,
        moved=5_000_000,
    )

    grad_heads = grad_attn.reshape(tokens, 4, 192).transpose(1, 0, 2)[group ^ jnp.arange(4)]
    grad_heads = quad_exchange(grad_heads.reshape(2, 2, tokens, 192)).reshape(4, tokens, 192)
    grad_heads, grad_w_out, output_rows = lax.optimization_barrier((grad_heads, grad_w_out, output_rows))
    by_core = grad_w_out.reshape(8, 2, 48, width)
    sum_out = plus(pick(by_core, core, 1), swap_bits(pick(by_core, 1 - core, 1), CORE_BIT))
    output = pair_up(output_rows[:rows], swap_bits(output_rows[rows:], HALF_BIT), half)
    grad_packed, key_sum, value_sum = call(
        attend_back_kernel,
        [((4 * tokens, 256), bf16), ((span, 256), f32), ((span, 256), f32)],
        [meta, cosine, sine, queries, keys, values, out_turned, log_total, grad_heads],
        [((256, 4 * tokens), f32), ((4 * tokens, 256), bf16), ((4 * tokens, 256), f32)],
        flops=14_000_000_000,
        moved=8_000_000,
    )
    key_sum, came_a, came_b, sum_out, output = lax.optimization_barrier((key_sum, came_a, came_b, sum_out, output))
    sum_a = plus(keep_a, came_a).reshape(4, 768, 256)
    sum_b = plus(keep_b, came_b).reshape(4, 768, 128)
    came_a, came_b = swap_bits(sum_a[2:], *STREAM[1]), swap_bits(sum_b[2:], *SHARED[1])
    y, z = (place >> 1) & 1, (place >> 2) & 1
    out_row = sum_out.reshape(2, 2, 2, 48, width)
    came_out = swap_bits(pick(out_row, 1 - y, 2), ROW_BIT)
    own_rows, other_rows, grad_qkv, sums_attn = call(
        project_back_kernel,
        [((8 * tokens, width), bf16)] * 2 + [((768, 576), bf16), ((width, 2), f32)],
        [meta, norms, weight_qkv, chooser, columns, cosine, sine, grad_packed, key_sum, value_sum],
        [((8 * tokens, 256), bf16), ((width, width), f32), ((8, width), f32)],
        grid=(8,),
        blocks=[(1, rows_of(width)), (5, rows_of(128)), (6, rows_of(128)), (8, rows_of(256)), (9, rows_of(256))],
        out_blocks=[
            (0, pl.BlockSpec((chunk, width), lambda i: (jnp.minimum(i, 3), 0))),
            (1, pl.BlockSpec((chunk, width), lambda i: (jnp.maximum(i - 4, 0), 0))),
        ],
        flops=6_000_000_000,
        moved=16_000_000,
    )
    own_rows, other_rows, grad_qkv, sums_attn, came_a, came_b, came_out = lax.optimization_barrier(
        (own_rows, other_rows, grad_qkv, sums_attn, came_a, came_b, came_out)
    )
    own_rows = own_rows.reshape(8, tokens, width)
    came_rows = swap_bits(other_rows, CORE_BIT).reshape(8, tokens, width)
    small = jnp.concatenate([sums_attn.T, sums_mlp[0:5]], 0)
    small = jnp.concatenate([small + swap_bits(small, CORE_BIT), grad_bias_in.reshape(2, width)], 0)
    by_core = grad_qkv.reshape(8, 2, 48, 576)
    kept = plus(pick(by_core, core, 1), swap_bits(pick(by_core, 1 - core, 1), CORE_BIT))
    sum_a, sum_b = plus(sum_a[:2], came_a), plus(sum_b[:2], came_b)
    sum_out = plus(pick(out_row, y, 2), came_out)
    came_a, came_b = swap_bits(sum_a[1], *STREAM[0]), swap_bits(sum_b[1], *SHARED[0])

    def sum_step(own, came, small, order):
        half_way = own.shape[0] // 2
        sent = plus(own[half_way:], came[half_way:]).reshape(-1, width)
        high = jnp.pad(small, ((0, 7), (0, 0))).astype(bf16)
        low = (jnp.pad(small, ((0, 7), (0, 0))) - high.astype(f32)).astype(bf16)
        got = swap_bits(jnp.concatenate([sent, high, low], 0), *order)
        count = sent.shape[0]
        small = small + got[count : count + 9].astype(f32) + got[count + 16 : count + 25].astype(f32)
        return plus(own[:half_way], came[:half_way]), got[:count].reshape(half_way, tokens, width), small

    came_rows, small, kept, came_a, came_b = lax.optimization_barrier((came_rows, small, kept, came_a, came_b))
    own_rows, came_rows, small = sum_step(own_rows, came_rows, small, TOKENS[2])

    def with_out(of_qkv, of_out):
        count = of_qkv.size // 576
        blocks = count * width // of_out.size
        of_out = of_out.reshape(-1, blocks, width // blocks).transpose(1, 0, 2).reshape(count, -1)
        return jnp.concatenate([of_qkv.reshape(count, 576), of_out], 1)

    def without(got, of_qkv, of_out):
        blocks = width // (got.shape[1] - 576)
        out = got[:, 576:].reshape(blocks, -1, width // blocks).transpose(1, 0, 2).reshape(of_out.shape)
        return got[:, :576].reshape(of_qkv.shape), out

    sum_a, sum_b = plus(sum_a[0], came_a).reshape(2, 384, 256), plus(sum_b[0], came_b).reshape(2, 384, 128)
    total = jnp.concatenate([sum_a, sum_b], 2)
    came_total = swap_bits(total[1], HALF_BIT)
    by_row = kept.reshape(2, 2, 2, 48, 576)
    by_row = jnp.stack([pick(by_row, y, 2), swap_bits(pick(by_row, 1 - y, 2), ROW_BIT)])
    came_rows, by_row, sum_out, small, came_total = lax.optimization_barrier(
        (came_rows, by_row, sum_out, small, came_total)
    )
    total = plus(total[0], came_total)
    across = swap_bits(total, SEQ_BIT)
    own_rows, came_rows, small = sum_step(own_rows, came_rows, small, TOKENS[1])
    sent = pick(by_row, 1 - z, 2), pick(sum_out, 1 - z, 1)
    got = without(swap_bits(with_out(*sent), LOW_BIT), *sent)
    kept, sum_out = jnp.stack([pick(by_row, z, 2), got[0]]), plus(pick(sum_out, z, 1), got[1])
    came_rows, kept, small, sum_out, across = lax.optimization_barrier((came_rows, kept, small, sum_out, across))
    mine = jnp.where(core == side, total[:192], across[:192])
    theirs = swap_bits(jnp.where(core == side, across[:192], total[:192]), CORE_BIT)
    own_rows, came_rows, small = sum_step(own_rows, came_rows, small, TOKENS[0])
    by_half = kept.reshape(4, 2, 48, 576)
    sent = pick(by_half, 1 - half, 1), pick(sum_out, 1 - half)
    got = without(swap_bits(with_out(*sent), HALF_BIT), *sent)
    kept, sum_out = plus(pick(by_half, half, 1), got[0]), plus(pick(sum_out, half), got[1])
    came_rows, small, theirs = lax.optimization_barrier((came_rows, small, theirs))
    stays, leaves = call(
        finish_kernel,
        [((rows, width), f32), ((rows, width), bf16)],
        [jnp.zeros((1,), jnp.int32), own_rows[0], came_rows[0], x_kept, grad_middle, vectors],
    )
    leaves_came = swap_bits(leaves, HALF_BIT)

    grad_down = pair_up(total[192:], across[192:], side).reshape(2, 2, 96, 384)
    grad_down = grad_down.transpose(0, 2, 1, 3).reshape(192, 768).astype(f32)
    def in_columns_back(blocks):
        return blocks.reshape(4, 48, 384).transpose(1, 0, 2).reshape(48, 8, 192)

    grad_w_in = pair_up(in_columns_back(mine), in_columns_back(theirs), core)
    grad_w_in = grad_w_in.transpose(1, 2, 0, 3).reshape(48, 3072).astype(f32)
    kept = kept[group ^ jnp.arange(4)].reshape(4, 48, 3, 192).transpose(1, 2, 0, 3).reshape(48, 2304)
    kept = jnp.concatenate([kept, sum_out], 1)
    kept, came_small, leaves_came = lax.optimization_barrier((kept, swap_bits(small, HALF_BIT), leaves_came))
    grad_hidden = pair_up(stays, leaves_came.astype(f32), half)
    came_kept = swap_bits(kept, SEQ_BIT)
    kept = kept.astype(f32) + came_kept.astype(f32)
    grad_w_qkv, grad_w_out = kept[:, :2304], kept[:, 2304:]
    both = pair_up(small, came_small, half)
    plus_scale = 1.0 + modulation[:, 1], 1.0 + modulation[:, 4]
    grad_mod = jnp.stack(
        [both[:, 0], both[:, 1] * full_gain_attn, both[:, 2], both[:, 3], both[:, 4] * full_gain_mlp, both[:, 5]], 1
    ).reshape(2, 16, 288)
    grad_mod = pick(grad_mod, place, 1)
    grad_ada = grad_mod[0][:, None] * cond[0][None] + grad_mod[1][:, None] * cond[1][None]
    gain_first = pick(jnp.sum(both[:, 1] * plus_scale[0], 0).reshape(16, 48), place)
    gain_second = pick(jnp.sum(both[:, 4] * plus_scale[1], 0).reshape(16, 48), place)
    summed = both[0] + both[1]
    bias_in_grad = pick(summed[7:9].reshape(8, 192), place >> 1)
    bias_down_grad = pick(summed[6].reshape(16, 48), place)
    return (
        output,
        grad_hidden,
        grad_w_qkv,
        grad_w_out,
        grad_w_in,
        grad_down,
        grad_ada,
        jnp.sum(grad_mod, 0),
        gain_first,
        gain_second,
        bias_in_grad,
        bias_down_grad,
    )


def solution(mesh):
    return jax.shard_map(
        cube_local if dict(mesh.shape) == {"seq": 2, "fsdp": 16} else local,
        mesh=mesh,
        in_specs=(
            P(None, ("seq", "fsdp"), None),
            P(),
            P(None, ("seq", "fsdp"), None),
            P("fsdp", None),
            P("fsdp", None),
            P("fsdp", None),
            P("fsdp", None),
            P("fsdp", None),
            P("fsdp"),
            P("fsdp"),
            P("fsdp"),
            P("fsdp"),
            P("fsdp"),
        ),
        out_specs=(
            P(None, ("seq", "fsdp"), None),
            P(None, ("seq", "fsdp"), None),
            P("fsdp", None),
            P("fsdp", None),
            P("fsdp", None),
            P("fsdp", None),
            P("fsdp", None),
            P("fsdp"),
            P("fsdp"),
            P("fsdp"),
            P("fsdp"),
            P("fsdp"),
        ),
        check_vma=False,
    )
```
